32 devices in a mesh: dp: 8 (over y, x, core), tensor: 4 (over z).
Axes of the slice: x: 2, y: 2, z: 4, core: 2. Of those that a mesh axis runs over, the one named last changes fastest.
Arguments:
- activations: bfloat16 [8192, 1024], P(('dp', 'tensor')), may hold values from -6 to 6
- segments: int32 [8192], P('dp'), may hold values from 0 to 31, as said below
- attn_weight: bfloat16 [1, 3, 1024, 1024], P(None, None, 'dp', 'tensor'), may hold values from -0.1875 to 0.1875
- out_weight: bfloat16 [1, 1024, 1024], P(None, 'tensor', 'dp'), may hold values from -0.75 to 0.75
- up_weight: bfloat16 [1, 1024, 4096], P(None, 'dp', 'tensor'), may hold values from -0.1875 to 0.1875
- down_weight: bfloat16 [1, 4096, 1024], P(None, 'tensor', 'dp'), may hold values from -0.09375 to 0.09375
- norm_gains: bfloat16 [1, 2, 1024], P(None, None, 'dp'), may hold values from 0.5 to 1.5
- bias_rows: bfloat16 [1, 10, 1024], P(None, None, 'dp'), may hold values from -1 to 1
- cotangent: float32 [8192, 1024], P(('dp', 'tensor')), may hold values from -6 to 6
Outputs:
- layer_output: float32 [8192, 1024], P(('dp', 'tensor'))
- input_grad: float32 [8192, 1024], P(('dp', 'tensor'))
- attn_weight_grad: float32 [1, 3, 1024, 1024], P(None, None, 'dp', 'tensor')
- out_weight_grad: float32 [1, 1024, 1024], P(None, 'tensor', 'dp')
- up_weight_grad: float32 [1, 1024, 4096], P(None, 'dp', 'tensor')
- down_weight_grad: float32 [1, 4096, 1024], P(None, 'tensor', 'dp')
- gain_grad: float32 [1, 2, 1024], P(None, None, 'dp')
- bias_grad: float32 [1, 10, 1024], P(None, None, 'dp')
The draws below stay inside these ranges and needn't reach their ends.
Inputs may be any that keep to these rules, and one draw needn't show every extreme that they name: `segments`: within each sequence of 1024 tokens ids never fall; every document has 200 tokens or more; sequences share no id; the last document of sequence j has id 4 j + 3 and ids of sequence j lie in 4 j to 4 j + 3.
All inputs are finite; a program needn't handle non-finite values.
Results may differ from the reference program's by a relative error of at most 0.018.
Values may be sent and summed in bfloat16 or wider, within the bound.
A program may use at most 128 MiB of HBM per device.

```python
import jax
import jax.numpy as jnp
from jax import lax

D = 1024
HEADS = 16
HD = 64
FF = 4096
LAYERS = 1
SEQS = 1
DOC_MIN = 200
SEQ = 1024
TOK = 1024
TOKENS = 8192
N_DP = 8


def draw_segments(key, part):
    sequences = TOKENS // SEQ
    first_key, second_key = jax.random.split(jax.random.fold_in(key, 7))
    spare_room = SEQ - 4 * DOC_MIN
    offsets = jnp.sort(jax.random.randint(first_key, (sequences, 3), 0, spare_room + 1), axis=1)
    starts = (jnp.arange(1, 4) * DOC_MIN)[None, :] + offsets
    kept_bound = jax.random.randint(second_key, (sequences, 3), 0, 2)
    position = jnp.arange(SEQ)
    later_count = jnp.sum(jnp.where(starts[:, None, :] > position[None, :, None], kept_bound[:, None, :], 0), axis=2)
    last_id = jnp.arange(sequences)[:, None] * 4 + 3
    return (last_id - later_count).reshape(TOKENS).astype(jnp.int32)


def spiked(values, key, source, target, shards_of, factor):
    def block_of(axis_at):
        return (jnp.arange(values.shape[axis_at]) // (values.shape[axis_at] // shards_of)).reshape((-1,) + (1,) * (values.ndim - 1 - axis_at))

    near = jax.random.permutation(key, shards_of)[block_of(target)]
    other_side = (block_of(target) + shards_of // 2) % shards_of
    return jnp.where((block_of(source) == near) | (block_of(source) == other_side), factor * values, values)


def level_of(key, dims, pieces, low, top_value):
    def one(dim, blocks):
        heights = jax.random.uniform(jax.random.fold_in(jax.random.fold_in(key, 6), dim), (blocks,), jnp.float32, low / len(pieces), top_value / len(pieces))
        return jnp.repeat(jnp.exp(heights), dims[dim] // blocks).reshape((-1,) + (1,) * (len(dims) - dim - 1))

    gain = one(*pieces[0])
    for cut in pieces[1:]:
        gain = gain * one(*cut)
    return gain


def bell_draw(rng, extent, scale, most, cuts=(), kind=jnp.bfloat16):
    entries = jax.random.normal(rng, extent, jnp.float32) * scale
    if len(cuts) > 0:
        entries = level_of(rng, extent, cuts, -0.22, 0.18) * entries
    return jnp.clip(entries, min=-most, max=most).astype(kind)


def gaussian_with(rng, dims, scale, limit, cuts, heavy, kind=jnp.bfloat16):
    array = scale * jax.random.normal(rng, dims, jnp.float32)
    if cuts:
        array = array * level_of(rng, dims, cuts, -0.22, 0.18)
    return jnp.clip(spiked(array, jax.random.fold_in(rng, 3), *heavy), -limit, limit).astype(kind)


def setup_inputs(seed: int = 0) -> dict:
    seeds = jax.random.split(jax.random.key(seed), 10)
    return {
        "activations": gaussian_with(seeds[0], (TOKENS, D), 1.0, 6.0, ((0, 32),), (0, 1, 32, 2.75)),
        "segments": draw_segments(jax.random.fold_in(seeds[9], 71), 0),
        "attn_weight": bell_draw(seeds[2], (LAYERS, 3, D, D), D ** -0.5, 0.1875, ((2, 8), (3, 4))),
        "out_weight": bell_draw(seeds[3], (LAYERS, D, D), (D // 16) ** -0.5, 0.75, ((1, 4), (2, 8))),
        "up_weight": bell_draw(seeds[4], (LAYERS, D, FF), D ** -0.5, 0.1875, ((1, 8), (2, 4))),
        "down_weight": bell_draw(seeds[5], (LAYERS, FF, D), FF ** -0.5, 0.09375, ((1, 4), (2, 8))),
        "norm_gains": jnp.clip(1.0 + 0.1 * jax.random.normal(seeds[6], (LAYERS, 2, D), jnp.float32), 0.5, 1.5).astype(jnp.bfloat16),
        "bias_rows": bell_draw(seeds[7], (LAYERS, 10, D), 0.2, 1.0, ((2, 8),)),
        "cotangent": gaussian_with(seeds[8], (TOKENS, D), 1.0, 6.0, ((0, 32),), (0, 1, 32, 2.75), jnp.float32),
    }


@jax.custom_vjp
def low(v):
    return lax.optimization_barrier(v.astype(jnp.bfloat16)).astype(jnp.float32)

@jax.custom_vjp
def low_back(v):
    return v

def low_keep(v):
    return (low(v), None)

def low_pass(kept, grad):
    return (grad,)

def back_keep(v):
    return (v, None)

def back_low(kept, grad):
    return (low(grad),)
low.defvjp(low_keep, low_pass)
low_back.defvjp(back_keep, back_low)
MASKED = -1e+30
EPSILON = 1e-05
HIGHEST = lax.Precision.HIGHEST

def layer_norm(values, gain_row, shift_row):
    center = values - lax.optimization_barrier(jnp.mean(values, axis=-1, keepdims=True))
    spread = lax.optimization_barrier(jnp.mean(center * center, axis=-1, keepdims=True))
    return center * lax.rsqrt(spread + EPSILON) * gain_row + shift_row

def layer_forward(residual, params, seg_ids):
    attn_w, out_w, up_w, down_w, gain_rows, bias_rows = params
    normed = low(layer_norm(residual, gain_rows[0], bias_rows[0]))
    bias_three = jnp.stack([bias_rows[1], jnp.zeros_like(bias_rows[1]), bias_rows[2]])
    project = jnp.einsum('td,cde->tce', normed, attn_w, precision=HIGHEST) + bias_three[None]
    project = low_back(low(project))
    shaped = project.reshape(SEQS, SEQ, 3, HEADS, HD)
    queries = shaped[:, :, 0]
    key_vecs = shaped[:, :, 1]
    value_vecs = shaped[:, :, 2]
    scores = jnp.einsum('sqhd,skhd->shqk', queries, key_vecs, precision=HIGHEST) * HD ** (-0.5)
    scores = low_back(scores)
    position = jnp.arange(SEQ)
    causal = position[None, :] <= position[:, None]
    seg_seq = seg_ids.reshape(SEQS, SEQ)
    visible = causal[None] & (seg_seq[:, :, None] == seg_seq[:, None, :])
    scores = jnp.where(visible[:, None], scores, MASKED)
    prob_rows = low(jax.nn.softmax(scores, axis=-1))
    attended = jnp.einsum('shqk,skhd->sqhd', prob_rows, value_vecs, precision=HIGHEST).reshape(TOK, D)
    attended = low_back(low(attended))
    attn_branch = low_back(jnp.dot(attended, out_w, precision=HIGHEST) + bias_rows[3])
    middle = residual + attn_branch
    normed_two = low(layer_norm(middle, gain_rows[1], bias_rows[4]))
    hidden = low_back(jnp.dot(normed_two, up_w, precision=HIGHEST) + bias_rows[6:10].reshape(FF))
    active = low(jax.nn.gelu(hidden, approximate=True))
    mlp_branch = low_back(jnp.dot(active, down_w, precision=HIGHEST) + bias_rows[5])
    return middle + mlp_branch

def stack_forward(residual, params, seg_ids):
    for layer_index in range(LAYERS):
        layer_params = tuple((member[layer_index] for member in params))
        residual = layer_forward(residual, layer_params, seg_ids)
    return residual

def reference(activations, segments, attn_weight, out_weight, up_weight, down_weight, norm_gains, bias_rows, cotangent):
    params = tuple((member.astype(jnp.float32) for member in (attn_weight, out_weight, up_weight, down_weight, norm_gains, bias_rows)))
    inputs = activations.astype(jnp.float32).reshape(N_DP, TOK, D)
    seg_groups = segments.reshape(N_DP, TOK)
    grad_groups = cotangent.reshape(N_DP, TOK, D)

    def one_group(totals, member):
        residual, seg_group, grad_group = member
        result, pullback = jax.vjp(lambda values, weights: stack_forward(values, weights, seg_group), residual, params)
        grad_in, grad_params = pullback(grad_group)
        return (jax.tree.map(jnp.add, totals, grad_params), (result, grad_in))
    zero_grads = jax.tree.map(jnp.zeros_like, params)
    totals, (results, grads_in) = lax.scan(one_group, zero_grads, (inputs, seg_groups, grad_groups))
    return (results.reshape(TOKENS, D), grads_in.reshape(TOKENS, D), totals[0], totals[1], totals[2], totals[3], totals[4], totals[5])
```

```python
import functools

import jax
import jax.numpy as jnp
from jax import lax
from jax.experimental import pallas as pl
from jax.experimental.pallas import tpu as pltpu
from jax.sharding import PartitionSpec as P

HD = 64
SEQ = 1024
EPSILON = 1e-05
MASKED = -1e30
MESH_ID = pl.DeviceIdType.MESH
BF = jnp.bfloat16
F32 = jnp.float32
ANY = pl.BlockSpec(memory_space=pl.ANY)
VM = pl.BlockSpec(memory_space=pltpu.VMEM)


def layer_norm(values, gain_row, shift_row):
    center = values - jnp.mean(values, axis=-1, keepdims=True)
    spread = jnp.mean(center * center, axis=-1, keepdims=True)
    return center * lax.rsqrt(spread + EPSILON) * gain_row + shift_row


def norm_stats(values):
    center = values - jnp.mean(values, axis=-1, keepdims=True)
    spread = jnp.mean(center * center, axis=-1, keepdims=True)
    scale = lax.rsqrt(spread + EPSILON)
    return center * scale, scale


def norm_back(grad, unit, scale, gain_row):
    u = grad * gain_row
    mean_u = jnp.mean(u, axis=-1, keepdims=True)
    mean_ux = jnp.mean(u * unit, axis=-1, keepdims=True)
    return scale * (u - mean_u - unit * mean_ux)


def gelu_tanh(values):
    return jax.nn.gelu(values, approximate=True)


class Geometry:
    def __init__(self, dp, tensor):
        self.dp, self.tensor = dp, tensor
        self.c_size = 2
        rest = dp // 2
        self.a_size = 1
        while self.a_size * self.a_size < rest:
            self.a_size *= 2
        self.b_size = rest // self.a_size
        assert self.a_size * self.b_size * 2 == dp

    def bind(self):
        spot = Spot()
        spot.geo = self
        spot.d = lax.axis_index("dp")
        spot.t = lax.axis_index("tensor")
        spot.c = lax.rem(spot.d, 2)
        half = lax.div(spot.d, 2)
        spot.a = lax.rem(half, self.a_size)
        spot.b = lax.div(half, self.a_size)
        return spot


class Spot:
    def rank(self, b, a, c):
        return (b * self.geo.a_size + a) * 2 + c

    def at_t(self, t):
        return (self.d, t)

    def at_d(self, d):
        return (d, self.t)


def ring_next(rank, step, size):
    return lax.rem(rank + step, size)


def ring_prev(rank, step, size):
    return lax.rem(rank + size - step, size)


class Wire:
    def __init__(self, send, recv):
        self.send_sems, self.recv_sems = send, recv
        self.count = 0
        self.pending = []

    def take(self, n):
        first = self.count
        self.count += n
        return first

    def copy(self, i, src, dst, device):
        return pltpu.make_async_remote_copy(
            src_ref=src, dst_ref=dst, send_sem=self.send_sems.at[i], recv_sem=self.recv_sems.at[i],
            device_id=device, device_id_type=MESH_ID)

    def start(self, i, src, dst, device, when=None):
        copy = self.copy(i, src, dst, device)
        if when is None:
            copy.start()
        else:
            pl.when(when)(copy.start)
        self.pending.append((copy, when))

    def landed(self, i, dst, device, when=None):
        copy = self.copy(i, dst, dst, device)
        if when is None:
            copy.wait_recv()
        else:
            pl.when(when)(copy.wait_recv)

    def drain(self):
        for copy, when in self.pending:
            if when is None:
                copy.wait_send()
            else:
                pl.when(when)(copy.wait_send)
        self.pending = []


def greet(spot, with_dp=True):
    geo = spot.geo
    barrier = pltpu.get_barrier_semaphore()
    total = 0
    for step in range(1, geo.tensor):
        pl.semaphore_signal(barrier, inc=1, device_id=spot.at_t(ring_next(spot.t, step, geo.tensor)), device_id_type=MESH_ID)
        total += 1
    for step in range(1, geo.dp):
        pl.semaphore_signal(barrier, inc=1, device_id=spot.at_d(ring_next(spot.d, step, geo.dp)), device_id_type=MESH_ID)
        total += 1
    pl.semaphore_wait(barrier, total)


class LineGather:
    def __init__(self, spot, wire, src, slot):
        self.spot, self.wire, self.src, self.slot = spot, wire, src, slot
        self.size = spot.geo.tensor
        self.line = self.size == 4
        self.first = wire.take(6 if self.line else self.size - 1)

    def start(self):
        spot, t = self.spot, self.spot.t
        if not self.line:
            for step in range(1, self.size):
                self.wire.start(self.first + step - 1, self.src, self.slot(t), spot.at_t(ring_next(t, step, self.size)))
            return
        for k, delta in enumerate((2, -2, 1, -1)):
            to = t + delta
            ok = (to >= 0) & (to < self.size)
            self.wire.start(self.first + k, self.src, self.slot(t), spot.at_t(to), when=ok)

    def forward(self):
        if not self.line:
            return
        spot, t = self.spot, self.spot.t
        self.wire.landed(self.first + 0, self.slot(t - 2), spot.at_t(t - 2), when=t == 2)
        self.wire.start(self.first + 4, self.slot(t - 2), self.slot(t - 2), spot.at_t(t + 1), when=t == 2)
        self.wire.landed(self.first + 1, self.slot(t + 2), spot.at_t(t + 2), when=t == 1)
        self.wire.start(self.first + 5, self.slot(t + 2), self.slot(t + 2), spot.at_t(t - 1), when=t == 1)

    def finish(self):
        spot, t = self.spot, self.spot.t
        if not self.line:
            for step in range(1, self.size):
                source = ring_prev(t, step, self.size)
                self.wire.landed(self.first + step - 1, self.slot(source), spot.at_t(source))
            return
        self.wire.landed(self.first + 0, self.slot(t - 2), spot.at_t(t - 2), when=t == 3)
        self.wire.landed(self.first + 1, self.slot(t + 2), spot.at_t(t + 2), when=t == 0)
        self.wire.landed(self.first + 2, self.slot(t - 1), spot.at_t(t - 1), when=t >= 1)
        self.wire.landed(self.first + 3, self.slot(t + 1), spot.at_t(t + 1), when=t <= 2)
        self.wire.landed(self.first + 4, self.slot(t - 3), spot.at_t(t - 1), when=t == 3)
        self.wire.landed(self.first + 5, self.slot(t + 3), spot.at_t(t + 1), when=t == 0)


class LineScatter:
    def __init__(self, spot, wire, part, land, add):
        self.spot, self.wire, self.part, self.land, self.add = spot, wire, part, land, add
        self.size = spot.geo.tensor
        self.line = self.size == 4
        self.first = wire.take(6 if self.line else self.size - 1)

    def start(self):
        spot, t = self.spot, self.spot.t
        if not self.line:
            for step in range(1, self.size):
                to = ring_next(t, step, self.size)
                self.wire.start(self.first + step - 1, self.part(to), self.land(step - 1), spot.at_t(to))
            return
        self.wire.start(self.first + 4, self.part(3), self.land(4), spot.at_t(1), when=t == 0)
        self.wire.start(self.first + 5, self.part(0), self.land(4), spot.at_t(2), when=t == 3)
        self.wire.start(self.first + 0, self.part(2), self.land(0), spot.at_t(2), when=t == 0)
        self.wire.start(self.first + 1, self.part(1), self.land(1), spot.at_t(1), when=t == 3)
        self.wire.start(self.first + 2, self.part(jnp.minimum(t + 1, 3)), self.land(2), spot.at_t(t + 1), when=t <= 2)
        self.wire.start(self.first + 3, self.part(jnp.maximum(t - 1, 0)), self.land(3), spot.at_t(t - 1), when=t >= 1)

    def forward(self):
        if not self.line:
            return
        spot, t = self.spot, self.spot.t

        @pl.when(t == 1)
        def _():
            self.wire.landed(self.first + 4, self.land(4), spot.at_t(0))
            self.add(self.part(3), self.land(4))

        @pl.when(t == 2)
        def _():
            self.wire.landed(self.first + 5, self.land(4), spot.at_t(3))
            self.add(self.part(0), self.land(4))

        self.wire.start(self.first + 0, self.part(3), self.land(0), spot.at_t(3), when=t == 1)
        self.wire.start(self.first + 1, self.part(0), self.land(1), spot.at_t(0), when=t == 2)

    def finish(self, total):
        spot, t = self.spot, self.spot.t
        if not self.line:
            for step in range(1, self.size):
                self.wire.landed(self.first + step - 1, self.land(step - 1), spot.at_t(ring_prev(t, step, self.size)))
                total(self.land(step - 1))
            return
        for k, delta in enumerate((2, -2, 1, -1)):
            source = t - delta

            @pl.when((source >= 0) & (source < self.size))
            def _():
                self.wire.landed(self.first + k, self.land(k), spot.at_t(source))
                total(self.land(k))


def add_into(rows):
    def add(dst, src):
        dst[...] = (dst[...].astype(F32) + src[...].astype(F32)).astype(dst.dtype)

    return add


def add_tiled(dst, src, tile):
    count = dst.shape[0] // tile

    def step(i, carry):
        rows = pl.ds(pl.multiple_of(i * tile, tile), tile)
        dst[rows] = (dst[rows].astype(F32) + src[rows].astype(F32)).astype(dst.dtype)
        return carry

    lax.fori_loop(0, count, step, 0)


def k1_body(geo, x_ref, w_ref, s_ref, xf, wf, sf, send, recv, local):
    spot = geo.bind()
    wire = Wire(send, recv)
    rows = x_ref.shape[0]
    wrows = w_ref.shape[1]

    def slot(t):
        return xf.at[pl.ds(pl.multiple_of(t * rows, rows), rows)]

    def wslot(d):
        return wf.at[:, pl.ds(pl.multiple_of(d * wrows, wrows), wrows)]

    own = [
        pltpu.make_async_copy(x_ref, slot(spot.t), local.at[0]),
        pltpu.make_async_copy(w_ref, wslot(spot.d), local.at[1]),
        pltpu.make_async_copy(s_ref, sf.at[spot.d], local.at[2]),
    ]
    for copy in own:
        copy.start()
    greet(spot)
    gather = LineGather(spot, wire, x_ref, slot)
    gather.start()
    small = wire.take(geo.dp - 1)
    big = wire.take(geo.dp - 1)
    for step in range(1, geo.dp):
        to = ring_next(spot.d, step, geo.dp)
        wire.start(small + step - 1, s_ref, sf.at[spot.d], spot.at_d(to))
        wire.start(big + step - 1, w_ref, wslot(spot.d), spot.at_d(to))
    gather.forward()
    for step in range(1, geo.dp):
        source = ring_prev(spot.d, step, geo.dp)
        wire.landed(small + step - 1, sf.at[source], spot.at_d(source))
        wire.landed(big + step - 1, wslot(source), spot.at_d(source))
    gather.finish()
    wire.drain()
    for copy in own:
        copy.wait()


def k1(geo, x, w4, small):
    sems = 6 + 2 * geo.dp + geo.tensor
    return pl.pallas_call(
        functools.partial(k1_body, geo),
        out_shape=(
            jax.ShapeDtypeStruct((geo.tensor * x.shape[0], x.shape[1]), BF),
            jax.ShapeDtypeStruct((w4.shape[0], geo.dp * w4.shape[1], w4.shape[2]), BF),
            jax.ShapeDtypeStruct((geo.dp,) + small.shape, small.dtype),
        ),
        in_specs=[ANY] * 3,
        out_specs=(ANY, ANY, ANY),
        scratch_shapes=[pltpu.SemaphoreType.DMA((sems,)), pltpu.SemaphoreType.DMA((sems,)), pltpu.SemaphoreType.DMA((3,))],
        compiler_params=pltpu.CompilerParams(collective_id=1, has_side_effects=True),
        name="k1",
    )(x, w4, small)


class WeightGather:
    def __init__(self, spot, wire, piece, full):
        geo = spot.geo
        self.spot, self.wire, self.piece, self.full = spot, wire, piece, full
        self.rows = piece.shape[0]
        self.line = LineGather(spot, wire, piece, lambda t: full.at[t, self.span(spot.d)])
        self.one_a = wire.take(geo.a_size - 1)
        self.one_b = wire.take(geo.b_size - 1)
        self.two_a = wire.take((geo.b_size - 1) * geo.a_size)
        self.two_b = wire.take((geo.a_size - 1) * geo.b_size)
        self.last = wire.take(geo.a_size * geo.b_size)
        self.half = geo.tensor // 2

    def span(self, d):
        return pl.ds(pl.multiple_of(d * self.rows, self.rows), self.rows)

    def low(self, d):
        return self.full.at[pl.ds(0, self.half), self.span(d)]

    def high(self, d):
        return self.full.at[pl.ds(self.half, self.spot.geo.tensor - self.half), self.span(d)]

    def both(self, d):
        return self.full.at[:, self.span(d)]

    def first(self):
        spot, geo = self.spot, self.spot.geo
        mine = spot.d
        for j in range(1, geo.a_size):
            to = spot.rank(spot.b, ring_next(spot.a, j, geo.a_size), spot.c)
            self.wire.start(self.one_a + j - 1, self.low(mine), self.low(mine), spot.at_d(to))
        for j in range(1, geo.b_size):
            to = spot.rank(ring_next(spot.b, j, geo.b_size), spot.a, spot.c)
            self.wire.start(self.one_b + j - 1, self.high(mine), self.high(mine), spot.at_d(to))
        sibling = spot.rank(spot.b, spot.a, 1 - spot.c)
        self.wire.start(self.last, self.both(mine), self.both(mine), spot.at_d(sibling))

    def second(self):
        spot, geo = self.spot, self.spot.geo
        for i in range(geo.a_size):
            held = spot.rank(spot.b, ring_prev(spot.a, i, geo.a_size), spot.c)
            if i:
                self.wire.landed(self.one_a + i - 1, self.low(held), spot.at_d(held))
            for j in range(1, geo.b_size):
                to = spot.rank(ring_next(spot.b, j, geo.b_size), spot.a, spot.c)
                self.wire.start(self.two_a + (j - 1) * geo.a_size + i, self.low(held), self.low(held), spot.at_d(to))
        for i in range(geo.b_size):
            held = spot.rank(ring_prev(spot.b, i, geo.b_size), spot.a, spot.c)
            if i:
                self.wire.landed(self.one_b + i - 1, self.high(held), spot.at_d(held))
            for j in range(1, geo.a_size):
                to = spot.rank(spot.b, ring_next(spot.a, j, geo.a_size), spot.c)
                self.wire.start(self.two_b + (j - 1) * geo.b_size + i, self.high(held), self.high(held), spot.at_d(to))

    def third(self):
        spot, geo = self.spot, self.spot.geo
        for j in range(1, geo.b_size):
            for i in range(geo.a_size):
                held = spot.rank(ring_prev(spot.b, j, geo.b_size), ring_prev(spot.a, i, geo.a_size), spot.c)
                source = spot.rank(ring_prev(spot.b, j, geo.b_size), spot.a, spot.c)
                self.wire.landed(self.two_a + (j - 1) * geo.a_size + i, self.low(held), spot.at_d(source))
        for j in range(1, geo.a_size):
            for i in range(geo.b_size):
                held = spot.rank(ring_prev(spot.b, i, geo.b_size), ring_prev(spot.a, j, geo.a_size), spot.c)
                source = spot.rank(spot.b, ring_prev(spot.a, j, geo.a_size), spot.c)
                self.wire.landed(self.two_b + (j - 1) * geo.b_size + i, self.high(held), spot.at_d(source))
        sibling = spot.rank(spot.b, spot.a, 1 - spot.c)
        for j in range(geo.b_size):
            for i in range(geo.a_size):
                if i or j:
                    held = spot.rank(ring_prev(spot.b, j, geo.b_size), ring_prev(spot.a, i, geo.a_size), spot.c)
                    self.wire.start(self.last + j * geo.a_size + i, self.both(held), self.both(held), spot.at_d(sibling))

    def fourth(self):
        spot, geo = self.spot, self.spot.geo
        sibling = spot.rank(spot.b, spot.a, 1 - spot.c)
        for j in range(geo.b_size):
            for i in range(geo.a_size):
                held = spot.rank(ring_prev(spot.b, j, geo.b_size), ring_prev(spot.a, i, geo.a_size), 1 - spot.c)
                self.wire.landed(self.last + j * geo.a_size + i, self.both(held), spot.at_d(sibling))


def gather_sems(geo):
    ab = geo.a_size * geo.b_size
    return 6 + geo.tensor + geo.a_size + geo.b_size + 3 * ab


def k2_body(geo, part, m_ref, total, full, land, send, recv, local):
    spot = geo.bind()
    wire = Wire(send, recv)
    rows = total.shape[0]
    mrows = m_ref.shape[1]

    def block(t):
        return part.at[pl.ds(pl.multiple_of(t * rows, rows), rows)]

    own = []
    for k in range(2):
        span = pl.ds(pl.multiple_of(spot.d * mrows, mrows), mrows)
        copy = pltpu.make_async_copy(m_ref.at[k], full.at[k, spot.t, span], local.at[k])
        copy.start()
        own.append(copy)
    greet(spot)
    scatter = LineScatter(spot, wire, block, lambda k: land.at[k], lambda dst, src: add_tiled(dst, src, 64))
    gathers = [WeightGather(spot, wire, m_ref.at[k], full.at[k]) for k in range(2)]
    gathers[0].line.start()
    scatter.start()
    gathers[1].line.start()
    gathers[0].line.forward()
    scatter.forward()
    own[0].wait()
    gathers[0].line.finish()
    gathers[0].first()
    gathers[1].line.forward()
    own[1].wait()
    gathers[1].line.finish()
    gathers[1].first()
    gathers[0].second()
    gathers[1].second()

    mine = block(spot.t)

    def set_total(i, carry):
        span = pl.ds(pl.multiple_of(i * 64, 64), 64)
        total[span] = mine[span].astype(F32)
        return carry

    lax.fori_loop(0, rows // 64, set_total, 0)
    scatter.finish(lambda ref: add_tiled(total, ref, 64))
    gathers[0].third()
    gathers[1].third()
    gathers[0].fourth()
    gathers[1].fourth()
    wire.drain()


def k2(geo, part, m2):
    sems = 6 + geo.tensor + 2 * gather_sems(geo)
    rows = part.shape[0] // geo.tensor
    width = part.shape[1]
    return pl.pallas_call(
        functools.partial(k2_body, geo),
        out_shape=(
            jax.ShapeDtypeStruct((rows, width), F32),
            jax.ShapeDtypeStruct((2, geo.tensor, geo.dp * m2.shape[1], m2.shape[2]), BF),
        ),
        in_specs=[VM, ANY],
        out_specs=(VM, ANY),
        scratch_shapes=[
            pltpu.VMEM((max(5, geo.tensor - 1), rows, width), BF),
            pltpu.SemaphoreType.DMA((sems,)), pltpu.SemaphoreType.DMA((sems,)), pltpu.SemaphoreType.DMA((2,))],
        compiler_params=pltpu.CompilerParams(collective_id=2, has_side_effects=True, vmem_limit_bytes=32 * 2**20),
        name="k2",
    )(part, m2)


class WeightScatter:
    def __init__(self, spot, wire, part, held, mine, one_a, one_b, two_a, two_b, land, sem):
        geo = spot.geo
        self.spot, self.wire, self.part, self.held, self.mine = spot, wire, part, held, mine
        self.one_a_buf, self.one_b_buf, self.two_a_buf, self.two_b_buf = one_a, one_b, two_a, two_b
        self.sem = sem
        self.rows = held.shape[3]
        self.half = geo.tensor // 2
        ab = geo.a_size * geo.b_size
        self.zero = wire.take(ab)
        self.one_a = wire.take(geo.a_size - 1)
        self.one_b = wire.take(geo.b_size - 1)
        self.two_a = wire.take(geo.b_size - 1)
        self.two_b = wire.take(geo.a_size - 1)
        here = held.at[spot.b, spot.a]
        self.line = LineScatter(spot, wire, lambda t: here.at[t], lambda k: land.at[k], lambda dst, src: add_tiled(dst, src, min(64, self.rows)))

    def span(self, d):
        return pl.ds(pl.multiple_of(d * self.rows, self.rows), self.rows)

    def start(self):
        spot, geo = self.spot, self.spot.geo
        sibling = spot.rank(spot.b, spot.a, 1 - spot.c)
        self.loads = []
        for b in range(geo.b_size):
            for a in range(geo.a_size):
                theirs = self.part.at[:, self.span(spot.rank(b, a, 1 - spot.c))]
                self.wire.start(self.zero + b * geo.a_size + a, theirs, self.held.at[b, a], spot.at_d(sibling))
                ours = self.part.at[:, self.span(spot.rank(b, a, spot.c))]
                load = pltpu.make_async_copy(ours, self.mine.at[b, a], self.sem.at[b * geo.a_size + a])
                load.start()
                self.loads.append(load)

    def add(self, dst, src):
        n = dst.shape[0]
        tile = min(64, self.rows)
        per = self.rows // tile

        def step(i, carry):
            rows = pl.ds(pl.multiple_of(lax.rem(i, per) * tile, tile), tile)
            j = lax.div(i, per)
            dst[j, rows] = (dst[j, rows].astype(F32) + src[j, rows].astype(F32)).astype(dst.dtype)
            return carry

        lax.fori_loop(0, n * per, step, 0)

    def first(self):
        spot, geo = self.spot, self.spot.geo
        sibling = spot.rank(spot.b, spot.a, 1 - spot.c)
        for b in range(geo.b_size):
            for a in range(geo.a_size):
                i = b * geo.a_size + a
                self.loads[i].wait()
                self.wire.landed(self.zero + i, self.held.at[b, a], spot.at_d(sibling))
                self.add(self.held.at[b, a], self.mine.at[b, a])
        for j in range(1, geo.a_size):
            a = ring_next(spot.a, j, geo.a_size)
            to = spot.rank(spot.b, a, spot.c)
            self.wire.start(self.one_a + j - 1, self.held.at[:, a, pl.ds(0, self.half)], self.one_a_buf.at[j - 1], spot.at_d(to))
        for j in range(1, geo.b_size):
            b = ring_next(spot.b, j, geo.b_size)
            to = spot.rank(b, spot.a, spot.c)
            self.wire.start(self.one_b + j - 1, self.held.at[b, :, pl.ds(self.half, self.half)], self.one_b_buf.at[j - 1], spot.at_d(to))

    def second(self):
        spot, geo = self.spot, self.spot.geo
        low, high = pl.ds(0, self.half), pl.ds(self.half, self.half)
        for j in range(1, geo.a_size):
            self.wire.landed(self.one_a + j - 1, self.one_a_buf.at[j - 1], spot.at_d(spot.rank(spot.b, ring_prev(spot.a, j, geo.a_size), spot.c)))
            for b in range(geo.b_size):
                self.add(self.held.at[b, spot.a, low], self.one_a_buf.at[j - 1, b])
        for j in range(1, geo.b_size):
            b = ring_next(spot.b, j, geo.b_size)
            self.wire.start(self.two_a + j - 1, self.held.at[b, spot.a, low], self.two_a_buf.at[j - 1], spot.at_d(spot.rank(b, spot.a, spot.c)))
        for j in range(1, geo.b_size):
            self.wire.landed(self.one_b + j - 1, self.one_b_buf.at[j - 1], spot.at_d(spot.rank(ring_prev(spot.b, j, geo.b_size), spot.a, spot.c)))
            for a in range(geo.a_size):
                self.add(self.held.at[spot.b, a, high], self.one_b_buf.at[j - 1, a])
        for j in range(1, geo.a_size):
            a = ring_next(spot.a, j, geo.a_size)
            self.wire.start(self.two_b + j - 1, self.held.at[spot.b, a, high], self.two_b_buf.at[j - 1], spot.at_d(spot.rank(spot.b, a, spot.c)))

    def third(self):
        spot, geo = self.spot, self.spot.geo
        low, high = pl.ds(0, self.half), pl.ds(self.half, self.half)
        for j in range(1, geo.b_size):
            self.wire.landed(self.two_a + j - 1, self.two_a_buf.at[j - 1], spot.at_d(spot.rank(ring_prev(spot.b, j, geo.b_size), spot.a, spot.c)))
            self.add(self.held.at[spot.b, spot.a, low], self.two_a_buf.at[j - 1])
        for j in range(1, geo.a_size):
            self.wire.landed(self.two_b + j - 1, self.two_b_buf.at[j - 1], spot.at_d(spot.rank(spot.b, ring_prev(spot.a, j, geo.a_size), spot.c)))
            self.add(self.held.at[spot.b, spot.a, high], self.two_b_buf.at[j - 1])
        self.line.start()

    def fourth(self, out):
        spot = self.spot
        self.line.forward()
        here = self.held.at[spot.b, spot.a, spot.t]
        tile = min(64, self.rows)

        def step(i, carry):
            rows = pl.ds(pl.multiple_of(i * tile, tile), tile)
            out[rows] = here[rows].astype(F32)
            return carry

        lax.fori_loop(0, self.rows // tile, step, 0)
        self.line.finish(lambda ref: add_tiled(out, ref, tile))


def k3_body(geo, ga_ref, g_ref, gaf, out, *rest):
    *bufs, send, recv, local, loads = rest
    spot = geo.bind()
    wire = Wire(send, recv)
    rows = ga_ref.shape[0]

    def slot(t):
        return gaf.at[pl.ds(pl.multiple_of(t * rows, rows), rows)]

    own = pltpu.make_async_copy(ga_ref, slot(spot.t), local.at[0])
    own.start()
    greet(spot)
    gather = LineGather(spot, wire, ga_ref, slot)
    scatters = [WeightScatter(spot, wire, g_ref.at[k], *(buf.at[k] for buf in bufs), loads.at[k]) for k in range(2)]
    scatters[1].start()
    scatters[0].start()
    gather.start()
    scatters[1].first()
    scatters[0].first()
    gather.forward()
    scatters[1].second()
    scatters[0].second()
    scatters[1].third()
    scatters[0].third()
    gather.finish()
    scatters[1].fourth(out.at[1])
    scatters[0].fourth(out.at[0])
    wire.drain()
    own.wait()


def k3(geo, ga, grads):
    rows = grads.shape[2] // geo.dp
    width = grads.shape[3]
    t, a, b = geo.tensor, geo.a_size, geo.b_size
    ab = a * b
    half = t // 2
    sems = 12 + 2 * t + 2 * (ab + 2 * a + 2 * b + 6)
    return pl.pallas_call(
        functools.partial(k3_body, geo),
        out_shape=(
            jax.ShapeDtypeStruct((t * ga.shape[0], ga.shape[1]), BF),
            jax.ShapeDtypeStruct((2, rows, width), F32),
        ),
        in_specs=[ANY, ANY],
        out_specs=(ANY, VM),
        scratch_shapes=[
            pltpu.VMEM((2, b, a, t, rows, width), BF),
            pltpu.VMEM((2, b, a, t, rows, width), BF),
            pltpu.VMEM((2, a - 1, b, half, rows, width), BF),
            pltpu.VMEM((2, b - 1, a, half, rows, width), BF),
            pltpu.VMEM((2, b - 1, half, rows, width), BF),
            pltpu.VMEM((2, a - 1, half, rows, width), BF),
            pltpu.VMEM((2, max(5, t - 1), rows, width), BF),
            pltpu.SemaphoreType.DMA((sems,)), pltpu.SemaphoreType.DMA((sems,)),
            pltpu.SemaphoreType.DMA((1,)), pltpu.SemaphoreType.DMA((2, ab))],
        compiler_params=pltpu.CompilerParams(collective_id=3, has_side_effects=True, vmem_limit_bytes=56 * 2**20),
        name="k3",
    )(ga, grads)


def k4_body(geo, part, w_ref, s_ref, total, wout, sout, land, wland, sland, stot, tland, send, recv):
    spot = geo.bind()
    wire = Wire(send, recv)
    rows = total.shape[0]
    wrows = wout.shape[1]
    greet(spot)

    def block(t):
        return part.at[pl.ds(pl.multiple_of(t * rows, rows), rows)]

    def wblock(d):
        return w_ref.at[:, pl.ds(pl.multiple_of(d * wrows, wrows), wrows)]

    small = wire.take(geo.dp - 1)
    big = wire.take(geo.dp - 1)
    last = wire.take(geo.tensor - 1)
    scatter = LineScatter(spot, wire, block, lambda k: land.at[k], lambda dst, src: add_tiled(dst, src, 64))
    scatter.start()
    for step in range(1, geo.dp):
        to = ring_next(spot.d, step, geo.dp)
        wire.start(small + step - 1, s_ref.at[to], sland.at[step - 1], spot.at_d(to))
    for step in range(1, geo.dp):
        to = ring_next(spot.d, step, geo.dp)
        wire.start(big + step - 1, wblock(to), wland.at[step - 1], spot.at_d(to))
    stot[...] = s_ref[spot.d]
    for step in range(1, geo.dp):
        wire.landed(small + step - 1, sland.at[step - 1], spot.at_d(ring_prev(spot.d, step, geo.dp)))
        stot[...] += sland[step - 1]
    for step in range(1, geo.tensor):
        wire.start(last + step - 1, stot, tland.at[step - 1], spot.at_t(ring_next(spot.t, step, geo.tensor)))
    scatter.forward()
    own = wblock(spot.d)
    for k in range(w_ref.shape[0]):
        wout[k] = own[k].astype(F32)
    for step in range(1, geo.dp):
        wire.landed(big + step - 1, wland.at[step - 1], spot.at_d(ring_prev(spot.d, step, geo.dp)))

        def add(k, carry):
            wout[k] += wland[step - 1, k].astype(F32)
            return carry

        lax.fori_loop(0, w_ref.shape[0], add, 0)
    sout[...] = stot[...]
    for step in range(1, geo.tensor):
        wire.landed(last + step - 1, tland.at[step - 1], spot.at_t(ring_prev(spot.t, step, geo.tensor)))
        sout[...] += tland[step - 1]
    mine = block(spot.t)

    def set_total(i, carry):
        span = pl.ds(pl.multiple_of(i * 64, 64), 64)
        total[span] = mine[span].astype(F32)
        return carry

    lax.fori_loop(0, rows // 64, set_total, 0)
    scatter.finish(lambda ref: add_tiled(total, ref, 64))
    wire.drain()


def k4(geo, part, wgrad, small):
    rows = part.shape[0] // geo.tensor
    width = part.shape[1]
    wshape = (wgrad.shape[0], wgrad.shape[1] // geo.dp, wgrad.shape[2])
    sshape = small.shape[1:]
    sems = 6 + 2 * geo.tensor + 2 * geo.dp
    return pl.pallas_call(
        functools.partial(k4_body, geo),
        out_shape=(
            jax.ShapeDtypeStruct((rows, width), F32),
            jax.ShapeDtypeStruct(wshape, F32),
            jax.ShapeDtypeStruct(sshape, F32),
        ),
        in_specs=[VM, VM, VM],
        out_specs=(VM, VM, VM),
        scratch_shapes=[
            pltpu.VMEM((max(5, geo.tensor - 1), rows, width), BF),
            pltpu.VMEM((geo.dp - 1,) + wshape, BF),
            pltpu.VMEM((geo.dp - 1,) + sshape, F32),
            pltpu.VMEM(sshape, F32),
            pltpu.VMEM((geo.tensor - 1,) + sshape, F32),
            pltpu.SemaphoreType.DMA((sems,)), pltpu.SemaphoreType.DMA((sems,))],
        compiler_params=pltpu.CompilerParams(collective_id=4, has_side_effects=True, vmem_limit_bytes=48 * 2**20),
        name="k4",
    )(part, wgrad, small)


def visible_mask(segments, first_row, block_rows):
    query_pos = first_row + jnp.arange(block_rows)
    key_pos = jnp.arange(SEQ)
    query_seg = lax.dynamic_slice_in_dim(segments, first_row, block_rows, 0)
    return (key_pos[None, :] <= query_pos[:, None]) & (query_seg[:, None] == segments[None, :])


def block_scores(project, segments, first_row, block_rows):
    head_count = project.shape[2] // HD
    query_rows = lax.dynamic_slice_in_dim(project, first_row, block_rows, 1)[0].reshape(block_rows, head_count, HD)
    key_vecs = project[1].reshape(SEQ, head_count, HD)
    value_vecs = project[2].reshape(SEQ, head_count, HD)
    scores = jnp.einsum("qhd,khd->hqk", query_rows, key_vecs, preferred_element_type=F32) * HD ** (-0.5)
    visible = visible_mask(segments, first_row, block_rows)
    scores = jnp.where(visible[None], scores, MASKED)
    return (query_rows, key_vecs, value_vecs, scores)


def attend(project, segments):
    block_rows = 512

    def one(block_index):
        first_row = block_index * block_rows
        query_rows, key_vecs, value_vecs, scores = block_scores(project, segments, first_row, block_rows)
        row_max = jnp.max(scores, axis=-1, keepdims=True)
        raised = jnp.exp(scores - row_max)
        row_total = jnp.sum(raised, axis=-1, keepdims=True)
        prob_rows = (raised / row_total).astype(BF)
        attended = jnp.einsum("hqk,khd->qhd", prob_rows, value_vecs, preferred_element_type=F32)
        return attended.reshape(block_rows, -1).astype(BF), (row_max + jnp.log(row_total))[:, :, 0]

    attended, log_total = lax.map(one, jnp.arange(SEQ // block_rows))
    return (attended.reshape(SEQ, -1), log_total)


def attend_back(project, segments, log_total, attended_grad):
    head_width = project.shape[2]
    head_count = head_width // HD
    block_rows = 512
    factor = HD ** (-0.5)

    def one(totals, index):
        key_total, value_total = totals
        first_row = index * block_rows
        query_rows, key_vecs, value_vecs, scores = block_scores(project, segments, first_row, block_rows)
        prob_rows = jnp.exp(scores - log_total[index][:, :, None])
        grad_rows = lax.dynamic_slice_in_dim(attended_grad, first_row, block_rows, 0).reshape(block_rows, head_count, HD)
        prob_grad = jnp.einsum("qhd,khd->hqk", grad_rows, value_vecs, preferred_element_type=F32)
        inner_sum = jnp.sum(prob_rows * prob_grad, axis=-1, keepdims=True)
        score_grad = (prob_rows * (prob_grad - inner_sum)).astype(BF)
        query_grad = jnp.einsum("hqk,khd->qhd", score_grad, key_vecs, preferred_element_type=F32) * factor
        key_total = key_total + jnp.einsum("hqk,qhd->khd", score_grad, query_rows, preferred_element_type=F32) * factor
        value_total = value_total + jnp.einsum("hqk,qhd->khd", prob_rows.astype(BF), grad_rows, preferred_element_type=F32)
        return ((key_total, value_total), query_grad)

    zero = jnp.zeros((SEQ, head_count, HD), F32)
    (key_total, value_total), query_grads = lax.scan(one, (zero, zero), jnp.arange(SEQ // block_rows))
    stacked = jnp.stack([query_grads.reshape(SEQ, head_width), key_total.reshape(SEQ, head_width), value_total.reshape(SEQ, head_width)])
    return stacked.astype(BF)


def dot_nt(x, w):
    return lax.dot_general(x, w, (((1,), (1,)), ((), ())), preferred_element_type=F32)


def dot_tn(x, w):
    return lax.dot_general(x, w, (((0,), (0,)), ((), ())), preferred_element_type=F32)


def per_device(geo, activations, segments, attn_weight, out_weight, up_weight, down_weight, norm_gains, bias_rows, cotangent):
    tensor_rank = lax.axis_index("tensor")
    width = activations.shape[1]
    head_width = attn_weight.shape[3]
    w4 = jnp.concatenate([attn_weight[0], out_weight.transpose(0, 2, 1)], axis=0)
    m2 = jnp.concatenate([up_weight, down_weight.transpose(0, 2, 1)], axis=0)
    small = jnp.concatenate([norm_gains[0], bias_rows[0]], axis=0)
    x_full, w_full, small_full = k1(geo, activations, w4, small)
    rows12 = small_full.transpose(1, 0, 2).reshape(12, width).astype(F32)
    gains, biases = rows12[:2], rows12[2:]
    column = tensor_rank * head_width

    normed_full = layer_norm(x_full.astype(F32), gains[0], biases[0]).astype(BF)
    query_bias = lax.dynamic_slice_in_dim(biases[1], column, head_width, 0)
    value_bias = lax.dynamic_slice_in_dim(biases[2], column, head_width, 0)
    bias_three = jnp.stack([query_bias, jnp.zeros_like(query_bias), value_bias])
    project = (jnp.einsum("td,cde->cte", normed_full, w_full[:3], preferred_element_type=F32) + bias_three[:, None]).astype(BF)
    attended, log_total = attend(project, segments)
    attn_part = dot_nt(attended, w_full[3]).astype(BF)
    attn_sum, m_full = k2(geo, attn_part, m2)

    residual = activations.astype(F32)
    middle = residual + (attn_sum + biases[3])
    unit_two, scale_two = norm_stats(middle)
    normed_two = (unit_two * gains[1] + biases[4]).astype(BF)
    up_full, down_full = m_full[0], m_full[1]
    tensor = up_full.shape[0]
    unit_width = up_full.shape[2]
    up_bias = biases[6:10].reshape(1, -1)
    hidden = jnp.concatenate([jnp.dot(normed_two, up_full[s], preferred_element_type=F32) for s in range(tensor)], axis=1) + up_bias
    active = gelu_tanh(hidden).astype(BF)
    branch = cotangent.astype(BF)
    ff = sum(dot_nt(active[:, s * unit_width:(s + 1) * unit_width], down_full[s]) for s in range(tensor))
    output = middle + (ff + biases[5])
    active_grad = jnp.concatenate([jnp.dot(branch, down_full[s], preferred_element_type=F32) for s in range(tensor)], axis=1)
    hidden_grad = jax.vjp(gelu_tanh, hidden)[1](active_grad)[0].astype(BF)
    up_bias_grad = jnp.sum(hidden_grad.astype(F32), axis=0).reshape(4, width)
    grads = jnp.stack([
        jnp.stack([dot_tn(normed_two, hidden_grad[:, s * unit_width:(s + 1) * unit_width]).astype(BF) for s in range(tensor)]),
        jnp.stack([dot_tn(branch, active[:, s * unit_width:(s + 1) * unit_width]).astype(BF) for s in range(tensor)]),
    ])
    normed_two_grad = sum(dot_nt(hidden_grad[:, s * unit_width:(s + 1) * unit_width], up_full[s]) for s in range(tensor))
    middle_grad = cotangent + norm_back(normed_two_grad, unit_two, scale_two, gains[1])
    attn_branch = middle_grad.astype(BF)
    ga_full, mlp_grads = k3(geo, attn_branch, grads)

    attended_grad = jnp.dot(ga_full, w_full[3], preferred_element_type=F32).astype(BF)
    project_grad = attend_back(project, segments, log_total, attended_grad)
    dn_part = sum(dot_nt(project_grad[j], w_full[j]) for j in range(3)).astype(BF)
    w_grads = jnp.stack([dot_tn(normed_full, project_grad[j]).astype(BF) for j in range(3)] + [dot_tn(ga_full, attended).astype(BF)])

    query_bias_grad = jnp.sum(project_grad[0].astype(F32), axis=0)
    value_bias_grad = jnp.sum(project_grad[2].astype(F32), axis=0)
    zeros = jnp.zeros((width,), F32)
    dn_total, w_out, small_one = k4_call(geo, dn_part, w_grads, jnp.stack([
        jnp.sum(normed_two_grad * unit_two, axis=0),
        lax.dynamic_update_slice_in_dim(zeros, query_bias_grad, column, 0),
        lax.dynamic_update_slice_in_dim(zeros, value_bias_grad, column, 0),
        jnp.sum(attn_branch.astype(F32), axis=0),
        jnp.sum(normed_two_grad, axis=0),
        jnp.sum(branch.astype(F32), axis=0),
        up_bias_grad[0], up_bias_grad[1], up_bias_grad[2], up_bias_grad[3],
    ]))
    unit_one, scale_one = norm_stats(residual)
    input_grad = middle_grad + norm_back(dn_total, unit_one, scale_one, gains[0])
    late = jnp.stack([jnp.sum(dn_total * unit_one, axis=0), jnp.sum(dn_total, axis=0)])
    late_sum = k5(geo, split_dp(geo, late))
    gain_grad = jnp.stack([late_sum[0], small_one[0]])[None]
    bias_grad = jnp.concatenate([late_sum[1:2], small_one[1:10]], axis=0)[None]
    return (
        output, input_grad, w_out[None, :3], w_out[3].T[None], mlp_grads[0][None], mlp_grads[1].T[None], gain_grad, bias_grad)


def split_dp(geo, rows):
    n, width = rows.shape
    pad = -n % 8
    rows = jnp.pad(rows, ((0, pad), (0, 0)))
    return rows.reshape(n + pad, geo.dp, width // geo.dp).transpose(1, 0, 2)


def k4_call(geo, part, wgrad, small):
    return k4(geo, part, wgrad, split_dp(geo, small))


def k5_body(geo, s_ref, sout, sland, stot, tland, send, recv):
    spot = geo.bind()
    wire = Wire(send, recv)
    greet(spot)
    small = wire.take(geo.dp - 1)
    last = wire.take(geo.tensor - 1)
    for step in range(1, geo.dp):
        to = ring_next(spot.d, step, geo.dp)
        wire.start(small + step - 1, s_ref.at[to], sland.at[step - 1], spot.at_d(to))
    stot[...] = s_ref[spot.d]
    for step in range(1, geo.dp):
        wire.landed(small + step - 1, sland.at[step - 1], spot.at_d(ring_prev(spot.d, step, geo.dp)))
        stot[...] += sland[step - 1]
    for step in range(1, geo.tensor):
        wire.start(last + step - 1, stot, tland.at[step - 1], spot.at_t(ring_next(spot.t, step, geo.tensor)))
    sout[...] = stot[...]
    for step in range(1, geo.tensor):
        wire.landed(last + step - 1, tland.at[step - 1], spot.at_t(ring_prev(spot.t, step, geo.tensor)))
        sout[...] += tland[step - 1]
    wire.drain()


def k5(geo, small):
    sshape = small.shape[1:]
    sems = geo.tensor + geo.dp
    return pl.pallas_call(
        functools.partial(k5_body, geo),
        out_shape=jax.ShapeDtypeStruct(sshape, F32),
        in_specs=[VM],
        out_specs=VM,
        scratch_shapes=[
            pltpu.VMEM((geo.dp - 1,) + sshape, F32),
            pltpu.VMEM(sshape, F32),
            pltpu.VMEM((geo.tensor - 1,) + sshape, F32),
            pltpu.SemaphoreType.DMA((sems,)), pltpu.SemaphoreType.DMA((sems,))],
        compiler_params=pltpu.CompilerParams(collective_id=5, has_side_effects=True),
        name="k5",
    )(small)


def solution(mesh):
    geo = Geometry(mesh.shape["dp"], mesh.shape["tensor"])
    return jax.shard_map(
        functools.partial(per_device, geo),
        mesh=mesh,
        in_specs=(
            P(("dp", "tensor"), None),
            P("dp"),
            P(None, None, "dp", "tensor"),
            P(None, "tensor", "dp"),
            P(None, "dp", "tensor"),
            P(None, "tensor", "dp"),
            P(None, None, "dp"),
            P(None, None, "dp"),
            P(("dp", "tensor"), None),
        ),
        out_specs=(
            P(("dp", "tensor"), None),
            P(("dp", "tensor"), None),
            P(None, None, "dp", "tensor"),
            P(None, "tensor", "dp"),
            P(None, "dp", "tensor"),
            P(None, "tensor", "dp"),
            P(None, None, "dp"),
            P(None, None, "dp"),
        ),
        check_vma=False,
    )
```

```python
import functools

import jax
import jax.numpy as jnp
from jax import lax
from jax.experimental import pallas as pl
from jax.experimental.pallas import tpu as pltpu
from jax.sharding import PartitionSpec as P

HD = 64
SEQ = 1024
EPSILON = 1e-05
MASKED = -1e30
MESH_ID = pl.DeviceIdType.MESH
BF = jnp.bfloat16
F32 = jnp.float32
ANY = pl.BlockSpec(memory_space=pl.ANY)
VM = pl.BlockSpec(memory_space=pltpu.VMEM)


def layer_norm(values, gain_row, shift_row):
    center = values - jnp.mean(values, axis=-1, keepdims=True)
    spread = jnp.mean(center * center, axis=-1, keepdims=True)
    return center * lax.rsqrt(spread + EPSILON) * gain_row + shift_row


def norm_stats(values):
    center = values - jnp.mean(values, axis=-1, keepdims=True)
    spread = jnp.mean(center * center, axis=-1, keepdims=True)
    scale = lax.rsqrt(spread + EPSILON)
    return center * scale, scale


def norm_back(grad, unit, scale, gain_row):
    u = grad * gain_row
    mean_u = jnp.mean(u, axis=-1, keepdims=True)
    mean_ux = jnp.mean(u * unit, axis=-1, keepdims=True)
    return scale * (u - mean_u - unit * mean_ux)


def gelu_tanh(values):
    return jax.nn.gelu(values, approximate=True)


class Geometry:
    def __init__(self, dp, tensor):
        self.dp, self.tensor = dp, tensor
        self.c_size = 2
        rest = dp // 2
        self.a_size = 1
        while self.a_size * self.a_size < rest:
            self.a_size *= 2
        self.b_size = rest // self.a_size
        assert self.a_size * self.b_size * 2 == dp

    def bind(self):
        spot = Spot()
        spot.geo = self
        spot.d = lax.axis_index("dp")
        spot.t = lax.axis_index("tensor")
        spot.c = lax.rem(spot.d, 2)
        half = lax.div(spot.d, 2)
        spot.a = lax.rem(half, self.a_size)
        spot.b = lax.div(half, self.a_size)
        return spot


class Spot:
    def rank(self, b, a, c):
        return (b * self.geo.a_size + a) * 2 + c

    def at_t(self, t):
        return (self.d, t)

    def at_d(self, d):
        return (d, self.t)


def ring_next(rank, step, size):
    return lax.rem(rank + step, size)


def ring_prev(rank, step, size):
    return lax.rem(rank + size - step, size)


class Wire:
    def __init__(self, send, recv):
        self.send_sems, self.recv_sems = send, recv
        self.count = 0
        self.pending = []

    def take(self, n):
        first = self.count
        self.count += n
        return first

    def copy(self, i, src, dst, device):
        return pltpu.make_async_remote_copy(
            src_ref=src, dst_ref=dst, send_sem=self.send_sems.at[i], recv_sem=self.recv_sems.at[i],
            device_id=device, device_id_type=MESH_ID)

    def start(self, i, src, dst, device, when=None):
        copy = self.copy(i, src, dst, device)
        if when is None:
            copy.start()
        else:
            pl.when(when)(copy.start)
        self.pending.append((copy, when))

    def landed(self, i, dst, device, when=None):
        copy = self.copy(i, dst, dst, device)
        if when is None:
            copy.wait_recv()
        else:
            pl.when(when)(copy.wait_recv)

    def drain(self):
        for copy, when in self.pending:
            if when is None:
                copy.wait_send()
            else:
                pl.when(when)(copy.wait_send)
        self.pending = []


def greet(spot, with_dp=True):
    geo = spot.geo
    barrier = pltpu.get_barrier_semaphore()
    total = 0
    for step in range(1, geo.tensor):
        pl.semaphore_signal(barrier, inc=1, device_id=spot.at_t(ring_next(spot.t, step, geo.tensor)), device_id_type=MESH_ID)
        total += 1
    for step in range(1, geo.dp):
        pl.semaphore_signal(barrier, inc=1, device_id=spot.at_d(ring_next(spot.d, step, geo.dp)), device_id_type=MESH_ID)
        total += 1
    pl.semaphore_wait(barrier, total)


class LineGather:
    def __init__(self, spot, wire, src, slot):
        self.spot, self.wire, self.src, self.slot = spot, wire, src, slot
        self.size = spot.geo.tensor
        self.line = self.size == 4
        self.first = wire.take(6 if self.line else self.size - 1)

    def start(self):
        spot, t = self.spot, self.spot.t
        if not self.line:
            for step in range(1, self.size):
                self.wire.start(self.first + step - 1, self.src, self.slot(t), spot.at_t(ring_next(t, step, self.size)))
            return
        for k, delta in enumerate((2, -2, 1, -1)):
            to = t + delta
            ok = (to >= 0) & (to < self.size)
            self.wire.start(self.first + k, self.src, self.slot(t), spot.at_t(to), when=ok)

    def forward(self):
        if not self.line:
            return
        spot, t = self.spot, self.spot.t
        self.wire.landed(self.first + 0, self.slot(t - 2), spot.at_t(t - 2), when=t == 2)
        self.wire.start(self.first + 4, self.slot(t - 2), self.slot(t - 2), spot.at_t(t + 1), when=t == 2)
        self.wire.landed(self.first + 1, self.slot(t + 2), spot.at_t(t + 2), when=t == 1)
        self.wire.start(self.first + 5, self.slot(t + 2), self.slot(t + 2), spot.at_t(t - 1), when=t == 1)

    def finish(self):
        spot, t = self.spot, self.spot.t
        if not self.line:
            for step in range(1, self.size):
                source = ring_prev(t, step, self.size)
                self.wire.landed(self.first + step - 1, self.slot(source), spot.at_t(source))
            return
        self.wire.landed(self.first + 0, self.slot(t - 2), spot.at_t(t - 2), when=t == 3)
        self.wire.landed(self.first + 1, self.slot(t + 2), spot.at_t(t + 2), when=t == 0)
        self.wire.landed(self.first + 2, self.slot(t - 1), spot.at_t(t - 1), when=t >= 1)
        self.wire.landed(self.first + 3, self.slot(t + 1), spot.at_t(t + 1), when=t <= 2)
        self.wire.landed(self.first + 4, self.slot(t - 3), spot.at_t(t - 1), when=t == 3)
        self.wire.landed(self.first + 5, self.slot(t + 3), spot.at_t(t + 1), when=t == 0)


class LineScatter:
    def __init__(self, spot, wire, part, land, add):
        self.spot, self.wire, self.part, self.land, self.add = spot, wire, part, land, add
        self.size = spot.geo.tensor
        self.line = self.size == 4
        self.first = wire.take(6 if self.line else self.size - 1)

    def start(self):
        spot, t = self.spot, self.spot.t
        if not self.line:
            for step in range(1, self.size):
                to = ring_next(t, step, self.size)
                self.wire.start(self.first + step - 1, self.part(to), self.land(step - 1), spot.at_t(to))
            return
        self.wire.start(self.first + 4, self.part(3), self.land(4), spot.at_t(1), when=t == 0)
        self.wire.start(self.first + 5, self.part(0), self.land(4), spot.at_t(2), when=t == 3)
        self.wire.start(self.first + 0, self.part(2), self.land(0), spot.at_t(2), when=t == 0)
        self.wire.start(self.first + 1, self.part(1), self.land(1), spot.at_t(1), when=t == 3)
        self.wire.start(self.first + 2, self.part(jnp.minimum(t + 1, 3)), self.land(2), spot.at_t(t + 1), when=t <= 2)
        self.wire.start(self.first + 3, self.part(jnp.maximum(t - 1, 0)), self.land(3), spot.at_t(t - 1), when=t >= 1)

    def forward(self):
        if not self.line:
            return
        spot, t = self.spot, self.spot.t

        @pl.when(t == 1)
        def _():
            self.wire.landed(self.first + 4, self.land(4), spot.at_t(0))
            self.add(self.part(3), self.land(4))

        @pl.when(t == 2)
        def _():
            self.wire.landed(self.first + 5, self.land(4), spot.at_t(3))
            self.add(self.part(0), self.land(4))

        self.wire.start(self.first + 0, self.part(3), self.land(0), spot.at_t(3), when=t == 1)
        self.wire.start(self.first + 1, self.part(0), self.land(1), spot.at_t(0), when=t == 2)

    def finish(self, total):
        spot, t = self.spot, self.spot.t
        if not self.line:
            for step in range(1, self.size):
                self.wire.landed(self.first + step - 1, self.land(step - 1), spot.at_t(ring_prev(t, step, self.size)))
                total(self.land(step - 1))
            return
        for k, delta in enumerate((2, -2, 1, -1)):
            source = t - delta

            @pl.when((source >= 0) & (source < self.size))
            def _():
                self.wire.landed(self.first + k, self.land(k), spot.at_t(source))
                total(self.land(k))


def add_into(rows):
    def add(dst, src):
        dst[...] = (dst[...].astype(F32) + src[...].astype(F32)).astype(dst.dtype)

    return add


def add_tiled(dst, src, tile):
    count = dst.shape[0] // tile

    def step(i, carry):
        rows = pl.ds(pl.multiple_of(i * tile, tile), tile)
        dst[rows] = (dst[rows].astype(F32) + src[rows].astype(F32)).astype(dst.dtype)
        return carry

    lax.fori_loop(0, count, step, 0)


def k1_body(geo, x_ref, w_ref, s_ref, xf, wf, sf, send, recv, local):
    spot = geo.bind()
    wire = Wire(send, recv)
    rows = x_ref.shape[0]
    wrows = w_ref.shape[1]

    def slot(t):
        return xf.at[pl.ds(pl.multiple_of(t * rows, rows), rows)]

    def wslot(d):
        return wf.at[:, pl.ds(pl.multiple_of(d * wrows, wrows), wrows)]

    own = [
        pltpu.make_async_copy(x_ref, slot(spot.t), local.at[0]),
        pltpu.make_async_copy(w_ref, wslot(spot.d), local.at[1]),
        pltpu.make_async_copy(s_ref, sf.at[spot.d], local.at[2]),
    ]
    for copy in own:
        copy.start()
    greet(spot)
    gather = LineGather(spot, wire, x_ref, slot)
    gather.start()
    small = wire.take(geo.dp - 1)
    big = wire.take(geo.dp - 1)
    for step in range(1, geo.dp):
        to = ring_next(spot.d, step, geo.dp)
        wire.start(small + step - 1, s_ref, sf.at[spot.d], spot.at_d(to))
        wire.start(big + step - 1, w_ref, wslot(spot.d), spot.at_d(to))
    gather.forward()
    for step in range(1, geo.dp):
        source = ring_prev(spot.d, step, geo.dp)
        wire.landed(small + step - 1, sf.at[source], spot.at_d(source))
        wire.landed(big + step - 1, wslot(source), spot.at_d(source))
    gather.finish()
    wire.drain()
    for copy in own:
        copy.wait()


def k1(geo, x, w4, small):
    sems = 6 + 2 * geo.dp + geo.tensor
    return pl.pallas_call(
        functools.partial(k1_body, geo),
        out_shape=(
            jax.ShapeDtypeStruct((geo.tensor * x.shape[0], x.shape[1]), BF),
            jax.ShapeDtypeStruct((w4.shape[0], geo.dp * w4.shape[1], w4.shape[2]), BF),
            jax.ShapeDtypeStruct((geo.dp,) + small.shape, small.dtype),
        ),
        in_specs=[ANY] * 3,
        out_specs=(ANY, ANY, ANY),
        scratch_shapes=[pltpu.SemaphoreType.DMA((sems,)), pltpu.SemaphoreType.DMA((sems,)), pltpu.SemaphoreType.DMA((3,))],
        compiler_params=pltpu.CompilerParams(collective_id=1, has_side_effects=True),
        name="k1",
    )(x, w4, small)


class WeightGather:
    def __init__(self, spot, wire, piece, full):
        geo = spot.geo
        self.spot, self.wire, self.piece, self.full = spot, wire, piece, full
        self.rows = piece.shape[0]
        self.line = LineGather(spot, wire, piece, lambda t: full.at[t, self.span(spot.d)])
        self.one_a = wire.take(geo.a_size - 1)
        self.one_b = wire.take(geo.b_size - 1)
        self.two_a = wire.take((geo.b_size - 1) * geo.a_size)
        self.two_b = wire.take((geo.a_size - 1) * geo.b_size)
        self.last = wire.take(geo.a_size * geo.b_size)
        self.half = geo.tensor // 2

    def span(self, d):
        return pl.ds(pl.multiple_of(d * self.rows, self.rows), self.rows)

    def low(self, d):
        return self.full.at[pl.ds(0, self.half), self.span(d)]

    def high(self, d):
        return self.full.at[pl.ds(self.half, self.spot.geo.tensor - self.half), self.span(d)]

    def both(self, d):
        return self.full.at[:, self.span(d)]

    def first(self):
        spot, geo = self.spot, self.spot.geo
        mine = spot.d
        for j in range(1, geo.a_size):
            to = spot.rank(spot.b, ring_next(spot.a, j, geo.a_size), spot.c)
            self.wire.start(self.one_a + j - 1, self.low(mine), self.low(mine), spot.at_d(to))
        for j in range(1, geo.b_size):
            to = spot.rank(ring_next(spot.b, j, geo.b_size), spot.a, spot.c)
            self.wire.start(self.one_b + j - 1, self.high(mine), self.high(mine), spot.at_d(to))
        sibling = spot.rank(spot.b, spot.a, 1 - spot.c)
        self.wire.start(self.last, self.both(mine), self.both(mine), spot.at_d(sibling))

    def second(self):
        spot, geo = self.spot, self.spot.geo
        for i in range(geo.a_size):
            held = spot.rank(spot.b, ring_prev(spot.a, i, geo.a_size), spot.c)
            if i:
                self.wire.landed(self.one_a + i - 1, self.low(held), spot.at_d(held))
            for j in range(1, geo.b_size):
                to = spot.rank(ring_next(spot.b, j, geo.b_size), spot.a, spot.c)
                self.wire.start(self.two_a + (j - 1) * geo.a_size + i, self.low(held), self.low(held), spot.at_d(to))
        for i in range(geo.b_size):
            held = spot.rank(ring_prev(spot.b, i, geo.b_size), spot.a, spot.c)
            if i:
                self.wire.landed(self.one_b + i - 1, self.high(held), spot.at_d(held))
            for j in range(1, geo.a_size):
                to = spot.rank(spot.b, ring_next(spot.a, j, geo.a_size), spot.c)
                self.wire.start(self.two_b + (j - 1) * geo.b_size + i, self.high(held), self.high(held), spot.at_d(to))

    def third(self):
        spot, geo = self.spot, self.spot.geo
        for j in range(1, geo.b_size):
            for i in range(geo.a_size):
                held = spot.rank(ring_prev(spot.b, j, geo.b_size), ring_prev(spot.a, i, geo.a_size), spot.c)
                source = spot.rank(ring_prev(spot.b, j, geo.b_size), spot.a, spot.c)
                self.wire.landed(self.two_a + (j - 1) * geo.a_size + i, self.low(held), spot.at_d(source))
        for j in range(1, geo.a_size):
            for i in range(geo.b_size):
                held = spot.rank(ring_prev(spot.b, i, geo.b_size), ring_prev(spot.a, j, geo.a_size), spot.c)
                source = spot.rank(spot.b, ring_prev(spot.a, j, geo.a_size), spot.c)
                self.wire.landed(self.two_b + (j - 1) * geo.b_size + i, self.high(held), spot.at_d(source))
        sibling = spot.rank(spot.b, spot.a, 1 - spot.c)
        for j in range(geo.b_size):
            for i in range(geo.a_size):
                if i or j:
                    held = spot.rank(ring_prev(spot.b, j, geo.b_size), ring_prev(spot.a, i, geo.a_size), spot.c)
                    self.wire.start(self.last + j * geo.a_size + i, self.both(held), self.both(held), spot.at_d(sibling))

    def fourth(self):
        spot, geo = self.spot, self.spot.geo
        sibling = spot.rank(spot.b, spot.a, 1 - spot.c)
        for j in range(geo.b_size):
            for i in range(geo.a_size):
                held = spot.rank(ring_prev(spot.b, j, geo.b_size), ring_prev(spot.a, i, geo.a_size), 1 - spot.c)
                self.wire.landed(self.last + j * geo.a_size + i, self.both(held), spot.at_d(sibling))


def gather_sems(geo):
    ab = geo.a_size * geo.b_size
    return 6 + geo.tensor + geo.a_size + geo.b_size + 3 * ab


def k2_body(geo, part, m_ref, total, full, land, send, recv, local):
    spot = geo.bind()
    wire = Wire(send, recv)
    rows = total.shape[0]
    mrows = m_ref.shape[1]

    def block(t):
        return part.at[pl.ds(pl.multiple_of(t * rows, rows), rows)]

    own = []
    for k in range(2):
        span = pl.ds(pl.multiple_of(spot.d * mrows, mrows), mrows)
        copy = pltpu.make_async_copy(m_ref.at[k], full.at[k, spot.t, span], local.at[k])
        copy.start()
        own.append(copy)
    greet(spot)
    scatter = LineScatter(spot, wire, block, lambda k: land.at[k], lambda dst, src: add_tiled(dst, src, 64))
    gathers = [WeightGather(spot, wire, m_ref.at[k], full.at[k]) for k in range(2)]
    gathers[0].line.start()
    scatter.start()
    gathers[1].line.start()
    gathers[0].line.forward()
    scatter.forward()
    own[0].wait()
    gathers[0].line.finish()
    gathers[0].first()
    gathers[1].line.forward()
    own[1].wait()
    gathers[1].line.finish()
    gathers[1].first()
    gathers[0].second()
    gathers[1].second()

    mine = block(spot.t)

    def set_total(i, carry):
        span = pl.ds(pl.multiple_of(i * 64, 64), 64)
        total[span] = mine[span].astype(F32)
        return carry

    lax.fori_loop(0, rows // 64, set_total, 0)
    scatter.finish(lambda ref: add_tiled(total, ref, 64))
    gathers[0].third()
    gathers[1].third()
    gathers[0].fourth()
    gathers[1].fourth()
    wire.drain()


def k2(geo, part, m2):
    sems = 6 + geo.tensor + 2 * gather_sems(geo)
    rows = part.shape[0] // geo.tensor
    width = part.shape[1]
    return pl.pallas_call(
        functools.partial(k2_body, geo),
        out_shape=(
            jax.ShapeDtypeStruct((rows, width), F32),
            jax.ShapeDtypeStruct((2, geo.tensor, geo.dp * m2.shape[1], m2.shape[2]), BF),
        ),
        in_specs=[VM, ANY],
        out_specs=(VM, ANY),
        scratch_shapes=[
            pltpu.VMEM((max(5, geo.tensor - 1), rows, width), BF),
            pltpu.SemaphoreType.DMA((sems,)), pltpu.SemaphoreType.DMA((sems,)), pltpu.SemaphoreType.DMA((2,))],
        compiler_params=pltpu.CompilerParams(collective_id=2, has_side_effects=True, vmem_limit_bytes=32 * 2**20),
        name="k2",
    )(part, m2)


class WeightScatter:
    def __init__(self, spot, wire, part, held, mine, one_a, one_b, two_a, two_b, land, sem):
        geo = spot.geo
        self.spot, self.wire, self.part, self.held, self.mine = spot, wire, part, held, mine
        self.one_a_buf, self.one_b_buf, self.two_a_buf, self.two_b_buf = one_a, one_b, two_a, two_b
        self.sem = sem
        self.rows = held.shape[3]
        self.half = geo.tensor // 2
        ab = geo.a_size * geo.b_size
        self.zero = wire.take(ab)
        self.one_a = wire.take(geo.a_size - 1)
        self.one_b = wire.take(geo.b_size - 1)
        self.two_a = wire.take(geo.b_size - 1)
        self.two_b = wire.take(geo.a_size - 1)
        here = held.at[spot.b, spot.a]
        self.line = LineScatter(spot, wire, lambda t: here.at[t], lambda k: land.at[k], lambda dst, src: add_tiled(dst, src, min(64, self.rows)))

    def span(self, d):
        return pl.ds(pl.multiple_of(d * self.rows, self.rows), self.rows)

    def start(self):
        spot, geo = self.spot, self.spot.geo
        sibling = spot.rank(spot.b, spot.a, 1 - spot.c)
        self.loads = []
        for b in range(geo.b_size):
            for a in range(geo.a_size):
                theirs = self.part.at[:, self.span(spot.rank(b, a, 1 - spot.c))]
                self.wire.start(self.zero + b * geo.a_size + a, theirs, self.held.at[b, a], spot.at_d(sibling))
                ours = self.part.at[:, self.span(spot.rank(b, a, spot.c))]
                load = pltpu.make_async_copy(ours, self.mine.at[b, a], self.sem.at[b * geo.a_size + a])
                load.start()
                self.loads.append(load)

    def add(self, dst, src):
        n = dst.shape[0]
        tile = min(64, self.rows)
        per = self.rows // tile

        def step(i, carry):
            rows = pl.ds(pl.multiple_of(lax.rem(i, per) * tile, tile), tile)
            j = lax.div(i, per)
            dst[j, rows] = (dst[j, rows].astype(F32) + src[j, rows].astype(F32)).astype(dst.dtype)
            return carry

        lax.fori_loop(0, n * per, step, 0)

    def first(self):
        spot, geo = self.spot, self.spot.geo
        sibling = spot.rank(spot.b, spot.a, 1 - spot.c)
        for b in range(geo.b_size):
            for a in range(geo.a_size):
                i = b * geo.a_size + a
                self.loads[i].wait()
                self.wire.landed(self.zero + i, self.held.at[b, a], spot.at_d(sibling))
                self.add(self.held.at[b, a], self.mine.at[b, a])
        for j in range(1, geo.a_size):
            a = ring_next(spot.a, j, geo.a_size)
            to = spot.rank(spot.b, a, spot.c)
            self.wire.start(self.one_a + j - 1, self.held.at[:, a, pl.ds(0, self.half)], self.one_a_buf.at[j - 1], spot.at_d(to))
        for j in range(1, geo.b_size):
            b = ring_next(spot.b, j, geo.b_size)
            to = spot.rank(b, spot.a, spot.c)
            self.wire.start(self.one_b + j - 1, self.held.at[b, :, pl.ds(self.half, self.half)], self.one_b_buf.at[j - 1], spot.at_d(to))

    def second(self):
        spot, geo = self.spot, self.spot.geo
        low, high = pl.ds(0, self.half), pl.ds(self.half, self.half)
        for j in range(1, geo.a_size):
            self.wire.landed(self.one_a + j - 1, self.one_a_buf.at[j - 1], spot.at_d(spot.rank(spot.b, ring_prev(spot.a, j, geo.a_size), spot.c)))
            for b in range(geo.b_size):
                self.add(self.held.at[b, spot.a, low], self.one_a_buf.at[j - 1, b])
        for j in range(1, geo.b_size):
            b = ring_next(spot.b, j, geo.b_size)
            self.wire.start(self.two_a + j - 1, self.held.at[b, spot.a, low], self.two_a_buf.at[j - 1], spot.at_d(spot.rank(b, spot.a, spot.c)))
        for j in range(1, geo.b_size):
            self.wire.landed(self.one_b + j - 1, self.one_b_buf.at[j - 1], spot.at_d(spot.rank(ring_prev(spot.b, j, geo.b_size), spot.a, spot.c)))
            for a in range(geo.a_size):
                self.add(self.held.at[spot.b, a, high], self.one_b_buf.at[j - 1, a])
        for j in range(1, geo.a_size):
            a = ring_next(spot.a, j, geo.a_size)
            self.wire.start(self.two_b + j - 1, self.held.at[spot.b, a, high], self.two_b_buf.at[j - 1], spot.at_d(spot.rank(spot.b, a, spot.c)))

    def third(self):
        spot, geo = self.spot, self.spot.geo
        low, high = pl.ds(0, self.half), pl.ds(self.half, self.half)
        for j in range(1, geo.b_size):
            self.wire.landed(self.two_a + j - 1, self.two_a_buf.at[j - 1], spot.at_d(spot.rank(ring_prev(spot.b, j, geo.b_size), spot.a, spot.c)))
            self.add(self.held.at[spot.b, spot.a, low], self.two_a_buf.at[j - 1])
        for j in range(1, geo.a_size):
            self.wire.landed(self.two_b + j - 1, self.two_b_buf.at[j - 1], spot.at_d(spot.rank(spot.b, ring_prev(spot.a, j, geo.a_size), spot.c)))
            self.add(self.held.at[spot.b, spot.a, high], self.two_b_buf.at[j - 1])
        self.line.start()

    def fourth(self, out):
        spot = self.spot
        self.line.forward()
        here = self.held.at[spot.b, spot.a, spot.t]
        tile = min(64, self.rows)

        def step(i, carry):
            rows = pl.ds(pl.multiple_of(i * tile, tile), tile)
            out[rows] = here[rows].astype(F32)
            return carry

        lax.fori_loop(0, self.rows // tile, step, 0)
        self.line.finish(lambda ref: add_tiled(out, ref, tile))


def k3_body(geo, ga_ref, g_ref, gaf, out, *rest):
    *bufs, send, recv, local, loads = rest
    spot = geo.bind()
    wire = Wire(send, recv)
    rows = ga_ref.shape[0]

    def slot(t):
        return gaf.at[pl.ds(pl.multiple_of(t * rows, rows), rows)]

    own = pltpu.make_async_copy(ga_ref, slot(spot.t), local.at[0])
    own.start()
    greet(spot)
    gather = LineGather(spot, wire, ga_ref, slot)
    scatters = [WeightScatter(spot, wire, g_ref.at[k], *(buf.at[k] for buf in bufs), loads.at[k]) for k in range(2)]
    scatters[1].start()
    scatters[0].start()
    gather.start()
    scatters[1].first()
    scatters[0].first()
    gather.forward()
    scatters[1].second()
    scatters[0].second()
    scatters[1].third()
    scatters[0].third()
    gather.finish()
    scatters[1].fourth(out.at[1])
    scatters[0].fourth(out.at[0])
    wire.drain()
    own.wait()


def k3(geo, ga, grads):
    rows = grads.shape[2] // geo.dp
    width = grads.shape[3]
    t, a, b = geo.tensor, geo.a_size, geo.b_size
    ab = a * b
    half = t // 2
    sems = 12 + 2 * t + 2 * (ab + 2 * a + 2 * b + 6)
    return pl.pallas_call(
        functools.partial(k3_body, geo),
        out_shape=(
            jax.ShapeDtypeStruct((t * ga.shape[0], ga.shape[1]), BF),
            jax.ShapeDtypeStruct((2, rows, width), F32),
        ),
        in_specs=[ANY, ANY],
        out_specs=(ANY, VM),
        scratch_shapes=[
            pltpu.VMEM((2, b, a, t, rows, width), BF),
            pltpu.VMEM((2, b, a, t, rows, width), BF),
            pltpu.VMEM((2, a - 1, b, half, rows, width), BF),
            pltpu.VMEM((2, b - 1, a, half, rows, width), BF),
            pltpu.VMEM((2, b - 1, half, rows, width), BF),
            pltpu.VMEM((2, a - 1, half, rows, width), BF),
            pltpu.VMEM((2, max(5, t - 1), rows, width), BF),
            pltpu.SemaphoreType.DMA((sems,)), pltpu.SemaphoreType.DMA((sems,)),
            pltpu.SemaphoreType.DMA((1,)), pltpu.SemaphoreType.DMA((2, ab))],
        compiler_params=pltpu.CompilerParams(collective_id=3, has_side_effects=True, vmem_limit_bytes=56 * 2**20),
        name="k3",
    )(ga, grads)


def k4_body(geo, part, w_ref, s_ref, total, wout, sout, land, wland, sland, stot, tland, send, recv):
    spot = geo.bind()
    wire = Wire(send, recv)
    rows = total.shape[0]
    wrows = wout.shape[1]
    greet(spot)

    def block(t):
        return part.at[pl.ds(pl.multiple_of(t * rows, rows), rows)]

    def wblock(d):
        return w_ref.at[:, pl.ds(pl.multiple_of(d * wrows, wrows), wrows)]

    small = wire.take(geo.dp - 1)
    big = wire.take(geo.dp - 1)
    last = wire.take(geo.tensor - 1)
    scatter = LineScatter(spot, wire, block, lambda k: land.at[k], lambda dst, src: add_tiled(dst, src, 64))
    scatter.start()
    for step in range(1, geo.dp):
        to = ring_next(spot.d, step, geo.dp)
        wire.start(small + step - 1, s_ref.at[to], sland.at[step - 1], spot.at_d(to))
    for step in range(1, geo.dp):
        to = ring_next(spot.d, step, geo.dp)
        wire.start(big + step - 1, wblock(to), wland.at[step - 1], spot.at_d(to))
    stot[...] = s_ref[spot.d]
    for step in range(1, geo.dp):
        wire.landed(small + step - 1, sland.at[step - 1], spot.at_d(ring_prev(spot.d, step, geo.dp)))
        stot[...] += sland[step - 1]
    for step in range(1, geo.tensor):
        wire.start(last + step - 1, stot, tland.at[step - 1], spot.at_t(ring_next(spot.t, step, geo.tensor)))
    scatter.forward()
    own = wblock(spot.d)
    for k in range(w_ref.shape[0]):
        wout[k] = own[k].astype(F32)
    for step in range(1, geo.dp):
        wire.landed(big + step - 1, wland.at[step - 1], spot.at_d(ring_prev(spot.d, step, geo.dp)))

        def add(k, carry):
            wout[k] += wland[step - 1, k].astype(F32)
            return carry

        lax.fori_loop(0, w_ref.shape[0], add, 0)
    sout[...] = stot[...]
    for step in range(1, geo.tensor):
        wire.landed(last + step - 1, tland.at[step - 1], spot.at_t(ring_prev(spot.t, step, geo.tensor)))
        sout[...] += tland[step - 1]
    mine = block(spot.t)

    def set_total(i, carry):
        span = pl.ds(pl.multiple_of(i * 64, 64), 64)
        total[span] = mine[span].astype(F32)
        return carry

    lax.fori_loop(0, rows // 64, set_total, 0)
    scatter.finish(lambda ref: add_tiled(total, ref, 64))
    wire.drain()


def k4(geo, part, wgrad, small):
    rows = part.shape[0] // geo.tensor
    width = part.shape[1]
    wshape = (wgrad.shape[0], wgrad.shape[1] // geo.dp, wgrad.shape[2])
    sshape = small.shape[1:]
    sems = 6 + 2 * geo.tensor + 2 * geo.dp
    return pl.pallas_call(
        functools.partial(k4_body, geo),
        out_shape=(
            jax.ShapeDtypeStruct((rows, width), F32),
            jax.ShapeDtypeStruct(wshape, F32),
            jax.ShapeDtypeStruct(sshape, F32),
        ),
        in_specs=[VM, VM, VM],
        out_specs=(VM, VM, VM),
        scratch_shapes=[
            pltpu.VMEM((max(5, geo.tensor - 1), rows, width), BF),
            pltpu.VMEM((geo.dp - 1,) + wshape, BF),
            pltpu.VMEM((geo.dp - 1,) + sshape, F32),
            pltpu.VMEM(sshape, F32),
            pltpu.VMEM((geo.tensor - 1,) + sshape, F32),
            pltpu.SemaphoreType.DMA((sems,)), pltpu.SemaphoreType.DMA((sems,))],
        compiler_params=pltpu.CompilerParams(collective_id=4, has_side_effects=True, vmem_limit_bytes=48 * 2**20),
        name="k4",
    )(part, wgrad, small)


PAIR = 2 * HD


def nt(x, w):
    return lax.dot_general(x, w, (((1,), (1,)), ((), ())), preferred_element_type=F32)


def nn(x, w):
    return lax.dot_general(x, w, (((1,), (0,)), ((), ())), preferred_element_type=F32)


def tn(x, w):
    return lax.dot_general(x, w, (((0,), (0,)), ((), ())), preferred_element_type=F32)


def block_bias(seg_col, seg_row, bias, start, rows, keys):
    query = seg_col[start:start + rows, :]
    for first in range(0, keys, rows):
        key = seg_row[:, first:first + rows]
        seen = query == key
        if first + rows > start:
            q_pos = start + lax.broadcasted_iota(jnp.int32, (rows, rows), 0)
            k_pos = first + lax.broadcasted_iota(jnp.int32, (rows, rows), 1)
            seen = seen & (k_pos <= q_pos)
        bias[:, first:first + rows] = jnp.where(seen, 0.0, MASKED).astype(F32)


def one_head(pair, head):
    lane = lax.broadcasted_iota(jnp.int32, pair.shape, 1)
    return jnp.where((lane < HD) if head == 0 else (lane >= HD), pair, jnp.zeros_like(pair))


def attend_block(qkv, bias, att, lse, start, rows):
    keys = start + rows
    width = qkv.shape[2]
    stat_lane = lax.broadcasted_iota(jnp.int32, (rows, 128), 1)
    stats = jnp.zeros((rows, 128), F32)
    for p in range(width // PAIR):
        lanes = slice(p * PAIR, (p + 1) * PAIR)
        query = qkv[0, start:keys, lanes]
        outs = []
        for head in range(2):
            s = nt(one_head(query, head), qkv[1, 0:keys, lanes]) + bias[:, 0:keys]
            top = jnp.max(s, axis=1, keepdims=True)
            e = jnp.exp(s - top)
            total = jnp.sum(e, axis=1, keepdims=True)
            prob = (e * (1.0 / total)).astype(BF)
            outs.append(nn(prob, qkv[2, 0:keys, lanes]))
            stats = jnp.where(stat_lane == 2 * p + head, top + jnp.log(total), stats)
        lane = lax.broadcasted_iota(jnp.int32, outs[0].shape, 1)
        att[start:keys, lanes] = jnp.where(lane < HD, outs[0], outs[1]).astype(BF)
    lse[start:keys, :] = stats


def attend_block_back(qkv, bias, lse, do, dq, dk, dv, start, rows):
    keys = start + rows
    width = qkv.shape[2]
    stat_lane = lax.broadcasted_iota(jnp.int32, (rows, 128), 1)
    stats = lse[start:keys, :]
    for p in range(width // PAIR):
        lanes = slice(p * PAIR, (p + 1) * PAIR)
        query = qkv[0, start:keys, lanes]
        grad = do[start:keys, lanes]
        dqs, dks, dvs = [], [], []
        for head in range(2):
            level = jnp.sum(jnp.where(stat_lane == 2 * p + head, stats, 0.0), axis=1, keepdims=True)
            s = nt(one_head(query, head), qkv[1, 0:keys, lanes]) + bias[:, 0:keys]
            prob = jnp.exp(s - level)
            d_prob = nt(one_head(grad, head), qkv[2, 0:keys, lanes])
            mixed = prob * d_prob
            ds = (mixed - prob * jnp.sum(mixed, axis=1, keepdims=True)).astype(BF)
            dqs.append(nn(ds, qkv[1, 0:keys, lanes]))
            dks.append(tn(ds, query))
            dvs.append(tn(prob.astype(BF), grad))
        lane = lax.broadcasted_iota(jnp.int32, dqs[0].shape, 1)
        dq[start:keys, lanes] = (jnp.where(lane < HD, dqs[0], dqs[1]) * (HD ** -0.5)).astype(dq.dtype)
        lane = lax.broadcasted_iota(jnp.int32, dks[0].shape, 1)
        dk[0:keys, lanes] += jnp.where(lane < HD, dks[0], dks[1])
        dv[0:keys, lanes] += jnp.where(lane < HD, dvs[0], dvs[1])


def attend_body(qkv, seg_col, seg_row, att, lse, bias):
    rows = 256
    for start in range(0, SEQ, rows):
        block_bias(seg_col, seg_row, bias, start, rows, start + rows)
        attend_block(qkv, bias, att, lse, start, rows)


def attend(qkv, seg_col, seg_row):
    return pl.pallas_call(
        attend_body,
        out_shape=(jax.ShapeDtypeStruct(qkv.shape[1:], BF), jax.ShapeDtypeStruct((qkv.shape[1], 128), F32)),
        in_specs=[VM] * 3, out_specs=(VM, VM),
        scratch_shapes=[pltpu.VMEM((256, SEQ), F32)],
        compiler_params=pltpu.CompilerParams(vmem_limit_bytes=40 * 2**20),
        name="attend",
    )(qkv, seg_col, seg_row)


def attend_back_body(qkv, seg_col, seg_row, lse, do, dqkv, bias, dk, dv):
    rows = 256
    dk[...] = jnp.zeros_like(dk)
    dv[...] = jnp.zeros_like(dv)
    for start in range(SEQ - rows, -1, -rows):
        block_bias(seg_col, seg_row, bias, start, rows, start + rows)
        attend_block_back(qkv, bias, lse, do, dqkv.at[0], dk, dv, start, rows)
        dqkv[1, start:start + rows, :] = dk[start:start + rows, :].astype(BF)
        dqkv[2, start:start + rows, :] = dv[start:start + rows, :].astype(BF)


def attend_back(qkv, seg_col, seg_row, lse, do):
    return pl.pallas_call(
        attend_back_body,
        out_shape=jax.ShapeDtypeStruct(qkv.shape, BF),
        in_specs=[VM] * 5, out_specs=VM,
        scratch_shapes=[pltpu.VMEM((256, SEQ), F32), pltpu.VMEM(qkv.shape[1:], F32), pltpu.VMEM(qkv.shape[1:], F32)],
        compiler_params=pltpu.CompilerParams(vmem_limit_bytes=40 * 2**20),
        name="attend_back",
    )(qkv, seg_col, seg_row, lse, do)


def dot_nt(x, w):
    return lax.dot_general(x, w, (((1,), (1,)), ((), ())), preferred_element_type=F32)


def dot_tn(x, w):
    return lax.dot_general(x, w, (((0,), (0,)), ((), ())), preferred_element_type=F32)


def per_device(geo, activations, segments, attn_weight, out_weight, up_weight, down_weight, norm_gains, bias_rows, cotangent):
    tensor_rank = lax.axis_index("tensor")
    width = activations.shape[1]
    head_width = attn_weight.shape[3]
    w4 = jnp.concatenate([attn_weight[0], out_weight.transpose(0, 2, 1)], axis=0)
    m2 = jnp.concatenate([up_weight, down_weight.transpose(0, 2, 1)], axis=0)
    small = jnp.concatenate([norm_gains[0], bias_rows[0]], axis=0)
    x_full, w_full, small_full = k1(geo, activations, w4, small)
    rows12 = small_full.transpose(1, 0, 2).reshape(12, width).astype(F32)
    gains, biases = rows12[:2], rows12[2:]
    column = tensor_rank * head_width

    normed_full = layer_norm(x_full.astype(F32), gains[0], biases[0]).astype(BF)
    query_bias = lax.dynamic_slice_in_dim(biases[1], column, head_width, 0)
    value_bias = lax.dynamic_slice_in_dim(biases[2], column, head_width, 0)
    bias_three = jnp.stack([query_bias, jnp.zeros_like(query_bias), value_bias])
    project = (jnp.einsum("td,cde->cte", normed_full, w_full[:3], preferred_element_type=F32) + bias_three[:, None]).astype(BF)
    project = project * jnp.array([HD ** -0.5, 1, 1], BF)[:, None, None]
    seg_col, seg_row = segments[:, None], segments[None, :]
    attended, log_total = attend(project, seg_col, seg_row)
    attn_part = dot_nt(attended, w_full[3]).astype(BF)
    attn_sum, m_full = k2(geo, attn_part, m2)

    residual = activations.astype(F32)
    middle = residual + (attn_sum + biases[3])
    unit_two, scale_two = norm_stats(middle)
    normed_two = (unit_two * gains[1] + biases[4]).astype(BF)
    up_full, down_full = m_full[0], m_full[1]
    tensor = up_full.shape[0]
    unit_width = up_full.shape[2]
    up_bias = biases[6:10].reshape(1, -1)
    hidden = jnp.concatenate([jnp.dot(normed_two, up_full[s], preferred_element_type=F32) for s in range(tensor)], axis=1) + up_bias
    active = gelu_tanh(hidden).astype(BF)
    branch = cotangent.astype(BF)
    ff = sum(dot_nt(active[:, s * unit_width:(s + 1) * unit_width], down_full[s]) for s in range(tensor))
    output = middle + (ff + biases[5])
    active_grad = jnp.concatenate([jnp.dot(branch, down_full[s], preferred_element_type=F32) for s in range(tensor)], axis=1)
    hidden_grad = jax.vjp(gelu_tanh, hidden)[1](active_grad)[0].astype(BF)
    up_bias_grad = jnp.sum(hidden_grad.astype(F32), axis=0).reshape(4, width)
    grads = jnp.stack([
        jnp.stack([dot_tn(normed_two, hidden_grad[:, s * unit_width:(s + 1) * unit_width]).astype(BF) for s in range(tensor)]),
        jnp.stack([dot_tn(branch, active[:, s * unit_width:(s + 1) * unit_width]).astype(BF) for s in range(tensor)]),
    ])
    normed_two_grad = sum(dot_nt(hidden_grad[:, s * unit_width:(s + 1) * unit_width], up_full[s]) for s in range(tensor))
    middle_grad = cotangent + norm_back(normed_two_grad, unit_two, scale_two, gains[1])
    attn_branch = middle_grad.astype(BF)
    ga_full, mlp_grads = k3(geo, attn_branch, grads)

    attended_grad = jnp.dot(ga_full, w_full[3], preferred_element_type=F32).astype(BF)
    project_grad = attend_back(project, seg_col, seg_row, log_total, attended_grad)
    dn_part = sum(dot_nt(project_grad[j], w_full[j]) for j in range(3))
    w_grads = jnp.stack([dot_tn(normed_full, project_grad[j]).astype(BF) for j in range(3)] + [dot_tn(ga_full, attended).astype(BF)])

    query_bias_grad = jnp.sum(project_grad[0].astype(F32), axis=0)
    value_bias_grad = jnp.sum(project_grad[2].astype(F32), axis=0)
    zeros = jnp.zeros((width,), F32)
    unit_full, _ = norm_stats(x_full.astype(F32))
    dn_total, w_out, small_one = k4(geo, dn_part.astype(BF), w_grads, split_dp(geo, jnp.stack([
        jnp.sum(dn_part * unit_full, axis=0),
        jnp.sum(normed_two_grad * unit_two, axis=0),
        jnp.sum(dn_part, axis=0),
        lax.dynamic_update_slice_in_dim(zeros, query_bias_grad, column, 0),
        lax.dynamic_update_slice_in_dim(zeros, value_bias_grad, column, 0),
        jnp.sum(attn_branch.astype(F32), axis=0),
        jnp.sum(normed_two_grad, axis=0),
        jnp.sum(branch.astype(F32), axis=0),
        up_bias_grad[0], up_bias_grad[1], up_bias_grad[2], up_bias_grad[3],
    ])))
    unit_one, scale_one = norm_stats(residual)
    input_grad = middle_grad + norm_back(dn_total, unit_one, scale_one, gains[0])
    return (
        output, input_grad, w_out[None, :3], w_out[3].T[None], mlp_grads[0][None], mlp_grads[1].T[None],
        small_one[None, :2], small_one[None, 2:12])


def split_dp(geo, rows):
    n, width = rows.shape
    pad = -n % 8
    rows = jnp.pad(rows, ((0, pad), (0, 0)))
    return rows.reshape(n + pad, geo.dp, width // geo.dp).transpose(1, 0, 2)


def solution(mesh):
    geo = Geometry(mesh.shape["dp"], mesh.shape["tensor"])
    return jax.shard_map(
        functools.partial(per_device, geo),
        mesh=mesh,
        in_specs=(
            P(("dp", "tensor"), None),
            P("dp"),
            P(None, None, "dp", "tensor"),
            P(None, "tensor", "dp"),
            P(None, "dp", "tensor"),
            P(None, "tensor", "dp"),
            P(None, None, "dp"),
            P(None, None, "dp"),
            P(("dp", "tensor"), None),
        ),
        out_specs=(
            P(("dp", "tensor"), None),
            P(("dp", "tensor"), None),
            P(None, None, "dp", "tensor"),
            P(None, "tensor", "dp"),
            P(None, "dp", "tensor"),
            P(None, "tensor", "dp"),
            P(None, None, "dp"),
            P(None, None, "dp"),
        ),
        check_vma=False,
    )
```

```python
import functools

import jax
import jax.numpy as jnp
from jax import lax
from jax.experimental import pallas as pl
from jax.experimental.pallas import tpu as pltpu
from jax.sharding import PartitionSpec as P

HD = 64
SEQ = 1024
EPSILON = 1e-05
MASKED = -1e30
MESH_ID = pl.DeviceIdType.MESH
BF = jnp.bfloat16
F32 = jnp.float32
ANY = pl.BlockSpec(memory_space=pl.ANY)
VM = pl.BlockSpec(memory_space=pltpu.VMEM)


def layer_norm(values, gain_row, shift_row):
    center = values - jnp.mean(values, axis=-1, keepdims=True)
    spread = jnp.mean(center * center, axis=-1, keepdims=True)
    return center * lax.rsqrt(spread + EPSILON) * gain_row + shift_row


def norm_stats(values):
    center = values - jnp.mean(values, axis=-1, keepdims=True)
    spread = jnp.mean(center * center, axis=-1, keepdims=True)
    scale = lax.rsqrt(spread + EPSILON)
    return center * scale, scale


def norm_back(grad, unit, scale, gain_row):
    u = grad * gain_row
    mean_u = jnp.mean(u, axis=-1, keepdims=True)
    mean_ux = jnp.mean(u * unit, axis=-1, keepdims=True)
    return scale * (u - mean_u - unit * mean_ux)


def gelu_tanh(values):
    return jax.nn.gelu(values, approximate=True)


class Geometry:
    def __init__(self, dp, tensor):
        self.dp, self.tensor = dp, tensor
        self.c_size = 2
        rest = dp // 2
        self.a_size = 1
        while self.a_size * self.a_size < rest:
            self.a_size *= 2
        self.b_size = rest // self.a_size
        assert self.a_size * self.b_size * 2 == dp

    def bind(self):
        spot = Spot()
        spot.geo = self
        spot.d = lax.axis_index("dp")
        spot.t = lax.axis_index("tensor")
        spot.c = lax.rem(spot.d, 2)
        half = lax.div(spot.d, 2)
        spot.a = lax.rem(half, self.a_size)
        spot.b = lax.div(half, self.a_size)
        return spot


class Spot:
    def rank(self, b, a, c):
        return (b * self.geo.a_size + a) * 2 + c

    def at_t(self, t):
        return (self.d, t)

    def at_d(self, d):
        return (d, self.t)


def ring_next(rank, step, size):
    return lax.rem(rank + step, size)


def ring_prev(rank, step, size):
    return lax.rem(rank + size - step, size)


class Wire:
    def __init__(self, send, recv):
        self.send_sems, self.recv_sems = send, recv
        self.count = 0
        self.pending = []

    def take(self, n):
        first = self.count
        self.count += n
        return first

    def copy(self, i, src, dst, device):
        return pltpu.make_async_remote_copy(
            src_ref=src, dst_ref=dst, send_sem=self.send_sems.at[i], recv_sem=self.recv_sems.at[i],
            device_id=device, device_id_type=MESH_ID)

    def start(self, i, src, dst, device, when=None):
        copy = self.copy(i, src, dst, device)
        if when is None:
            copy.start()
        else:
            pl.when(when)(copy.start)
        self.pending.append((copy, when))

    def landed(self, i, dst, device, when=None):
        copy = self.copy(i, dst, dst, device)
        if when is None:
            copy.wait_recv()
        else:
            pl.when(when)(copy.wait_recv)

    def drain(self):
        for copy, when in self.pending:
            if when is None:
                copy.wait_send()
            else:
                pl.when(when)(copy.wait_send)
        self.pending = []


def greet(spot, with_dp=True):
    geo = spot.geo
    barrier = pltpu.get_barrier_semaphore()
    total = 0
    for step in range(1, geo.tensor):
        pl.semaphore_signal(barrier, inc=1, device_id=spot.at_t(ring_next(spot.t, step, geo.tensor)), device_id_type=MESH_ID)
        total += 1
    for step in range(1, geo.dp):
        pl.semaphore_signal(barrier, inc=1, device_id=spot.at_d(ring_next(spot.d, step, geo.dp)), device_id_type=MESH_ID)
        total += 1
    pl.semaphore_wait(barrier, total)


class LineGather:
    def __init__(self, spot, wire, src, slot):
        self.spot, self.wire, self.src, self.slot = spot, wire, src, slot
        self.size = spot.geo.tensor
        self.line = self.size == 4
        self.first = wire.take(6 if self.line else self.size - 1)

    def start(self):
        spot, t = self.spot, self.spot.t
        if not self.line:
            for step in range(1, self.size):
                self.wire.start(self.first + step - 1, self.src, self.slot(t), spot.at_t(ring_next(t, step, self.size)))
            return
        for k, delta in enumerate((2, -2, 1, -1)):
            to = t + delta
            ok = (to >= 0) & (to < self.size)
            self.wire.start(self.first + k, self.src, self.slot(t), spot.at_t(to), when=ok)

    def forward(self):
        if not self.line:
            return
        spot, t = self.spot, self.spot.t
        self.wire.landed(self.first + 0, self.slot(t - 2), spot.at_t(t - 2), when=t == 2)
        self.wire.start(self.first + 4, self.slot(t - 2), self.slot(t - 2), spot.at_t(t + 1), when=t == 2)
        self.wire.landed(self.first + 1, self.slot(t + 2), spot.at_t(t + 2), when=t == 1)
        self.wire.start(self.first + 5, self.slot(t + 2), self.slot(t + 2), spot.at_t(t - 1), when=t == 1)

    def finish(self):
        spot, t = self.spot, self.spot.t
        if not self.line:
            for step in range(1, self.size):
                source = ring_prev(t, step, self.size)
                self.wire.landed(self.first + step - 1, self.slot(source), spot.at_t(source))
            return
        self.wire.landed(self.first + 0, self.slot(t - 2), spot.at_t(t - 2), when=t == 3)
        self.wire.landed(self.first + 1, self.slot(t + 2), spot.at_t(t + 2), when=t == 0)
        self.wire.landed(self.first + 2, self.slot(t - 1), spot.at_t(t - 1), when=t >= 1)
        self.wire.landed(self.first + 3, self.slot(t + 1), spot.at_t(t + 1), when=t <= 2)
        self.wire.landed(self.first + 4, self.slot(t - 3), spot.at_t(t - 1), when=t == 3)
        self.wire.landed(self.first + 5, self.slot(t + 3), spot.at_t(t + 1), when=t == 0)


class LineScatter:
    def __init__(self, spot, wire, part, land, add):
        self.spot, self.wire, self.part, self.land, self.add = spot, wire, part, land, add
        self.size = spot.geo.tensor
        self.line = self.size == 4
        self.first = wire.take(6 if self.line else self.size - 1)

    def start(self):
        spot, t = self.spot, self.spot.t
        if not self.line:
            for step in range(1, self.size):
                to = ring_next(t, step, self.size)
                self.wire.start(self.first + step - 1, self.part(to), self.land(step - 1), spot.at_t(to))
            return
        self.wire.start(self.first + 4, self.part(3), self.land(4), spot.at_t(1), when=t == 0)
        self.wire.start(self.first + 5, self.part(0), self.land(4), spot.at_t(2), when=t == 3)
        self.wire.start(self.first + 0, self.part(2), self.land(0), spot.at_t(2), when=t == 0)
        self.wire.start(self.first + 1, self.part(1), self.land(1), spot.at_t(1), when=t == 3)
        self.wire.start(self.first + 2, self.part(jnp.minimum(t + 1, 3)), self.land(2), spot.at_t(t + 1), when=t <= 2)
        self.wire.start(self.first + 3, self.part(jnp.maximum(t - 1, 0)), self.land(3), spot.at_t(t - 1), when=t >= 1)

    def start_block(self, i):
        spot, t = self.spot, self.spot.t
        if i == 3:
            self.wire.start(self.first + 4, self.part(3), self.land(4), spot.at_t(1), when=t == 0)
        if i == 0:
            self.wire.start(self.first + 5, self.part(0), self.land(4), spot.at_t(2), when=t == 3)
        if i == 2:
            self.wire.start(self.first + 0, self.part(2), self.land(0), spot.at_t(2), when=t == 0)
        if i == 1:
            self.wire.start(self.first + 1, self.part(1), self.land(1), spot.at_t(1), when=t == 3)
        if i >= 1:
            self.wire.start(self.first + 2, self.part(i), self.land(2), spot.at_t(i), when=t == i - 1)
        if i <= 2:
            self.wire.start(self.first + 3, self.part(i), self.land(3), spot.at_t(i), when=t == i + 1)

    def forward(self):
        if not self.line:
            return
        spot, t = self.spot, self.spot.t

        @pl.when(t == 1)
        def _():
            self.wire.landed(self.first + 4, self.land(4), spot.at_t(0))
            self.add(self.part(3), self.land(4))

        @pl.when(t == 2)
        def _():
            self.wire.landed(self.first + 5, self.land(4), spot.at_t(3))
            self.add(self.part(0), self.land(4))

        self.wire.start(self.first + 0, self.part(3), self.land(0), spot.at_t(3), when=t == 1)
        self.wire.start(self.first + 1, self.part(0), self.land(1), spot.at_t(0), when=t == 2)

    def finish(self, total):
        spot, t = self.spot, self.spot.t
        if not self.line:
            for step in range(1, self.size):
                self.wire.landed(self.first + step - 1, self.land(step - 1), spot.at_t(ring_prev(t, step, self.size)))
                total(self.land(step - 1))
            return
        for k, delta in enumerate((2, -2, 1, -1)):
            source = t - delta

            @pl.when((source >= 0) & (source < self.size))
            def _():
                self.wire.landed(self.first + k, self.land(k), spot.at_t(source))
                total(self.land(k))


def add_into(rows):
    def add(dst, src):
        dst[...] = (dst[...].astype(F32) + src[...].astype(F32)).astype(dst.dtype)

    return add


def add_tiled(dst, src, tile):
    count = dst.shape[0] // tile

    def step(i, carry):
        rows = pl.ds(pl.multiple_of(i * tile, tile), tile)
        dst[rows] = (dst[rows].astype(F32) + src[rows].astype(F32)).astype(dst.dtype)
        return carry

    lax.fori_loop(0, count, step, 0)


class WeightGather:
    def __init__(self, spot, wire, piece, full):
        geo = spot.geo
        self.spot, self.wire, self.piece, self.full = spot, wire, piece, full
        self.rows = piece.shape[0]
        self.line = LineGather(spot, wire, piece, lambda t: full.at[t, self.span(spot.d)])
        self.one_a = wire.take(geo.a_size - 1)
        self.one_b = wire.take(geo.b_size - 1)
        self.two_a = wire.take((geo.b_size - 1) * geo.a_size)
        self.two_b = wire.take((geo.a_size - 1) * geo.b_size)
        self.last = wire.take(geo.a_size * geo.b_size)
        self.half = geo.tensor // 2

    def span(self, d):
        return pl.ds(pl.multiple_of(d * self.rows, self.rows), self.rows)

    def low(self, d):
        return self.full.at[pl.ds(0, self.half), self.span(d)]

    def high(self, d):
        return self.full.at[pl.ds(self.half, self.spot.geo.tensor - self.half), self.span(d)]

    def both(self, d):
        return self.full.at[:, self.span(d)]

    def first(self):
        spot, geo = self.spot, self.spot.geo
        mine = spot.d
        for j in range(1, geo.a_size):
            to = spot.rank(spot.b, ring_next(spot.a, j, geo.a_size), spot.c)
            self.wire.start(self.one_a + j - 1, self.low(mine), self.low(mine), spot.at_d(to))
        for j in range(1, geo.b_size):
            to = spot.rank(ring_next(spot.b, j, geo.b_size), spot.a, spot.c)
            self.wire.start(self.one_b + j - 1, self.high(mine), self.high(mine), spot.at_d(to))
        sibling = spot.rank(spot.b, spot.a, 1 - spot.c)
        self.wire.start(self.last, self.both(mine), self.both(mine), spot.at_d(sibling))

    def second(self):
        spot, geo = self.spot, self.spot.geo
        for i in range(geo.a_size):
            held = spot.rank(spot.b, ring_prev(spot.a, i, geo.a_size), spot.c)
            if i:
                self.wire.landed(self.one_a + i - 1, self.low(held), spot.at_d(held))
            for j in range(1, geo.b_size):
                to = spot.rank(ring_next(spot.b, j, geo.b_size), spot.a, spot.c)
                self.wire.start(self.two_a + (j - 1) * geo.a_size + i, self.low(held), self.low(held), spot.at_d(to))
        for i in range(geo.b_size):
            held = spot.rank(ring_prev(spot.b, i, geo.b_size), spot.a, spot.c)
            if i:
                self.wire.landed(self.one_b + i - 1, self.high(held), spot.at_d(held))
            for j in range(1, geo.a_size):
                to = spot.rank(spot.b, ring_next(spot.a, j, geo.a_size), spot.c)
                self.wire.start(self.two_b + (j - 1) * geo.b_size + i, self.high(held), self.high(held), spot.at_d(to))

    def third(self):
        spot, geo = self.spot, self.spot.geo
        for j in range(1, geo.b_size):
            for i in range(geo.a_size):
                held = spot.rank(ring_prev(spot.b, j, geo.b_size), ring_prev(spot.a, i, geo.a_size), spot.c)
                source = spot.rank(ring_prev(spot.b, j, geo.b_size), spot.a, spot.c)
                self.wire.landed(self.two_a + (j - 1) * geo.a_size + i, self.low(held), spot.at_d(source))
        for j in range(1, geo.a_size):
            for i in range(geo.b_size):
                held = spot.rank(ring_prev(spot.b, i, geo.b_size), ring_prev(spot.a, j, geo.a_size), spot.c)
                source = spot.rank(spot.b, ring_prev(spot.a, j, geo.a_size), spot.c)
                self.wire.landed(self.two_b + (j - 1) * geo.b_size + i, self.high(held), spot.at_d(source))
        sibling = spot.rank(spot.b, spot.a, 1 - spot.c)
        for j in range(geo.b_size):
            for i in range(geo.a_size):
                if i or j:
                    held = spot.rank(ring_prev(spot.b, j, geo.b_size), ring_prev(spot.a, i, geo.a_size), spot.c)
                    self.wire.start(self.last + j * geo.a_size + i, self.both(held), self.both(held), spot.at_d(sibling))

    def fourth(self):
        spot, geo = self.spot, self.spot.geo
        sibling = spot.rank(spot.b, spot.a, 1 - spot.c)
        for j in range(geo.b_size):
            for i in range(geo.a_size):
                held = spot.rank(ring_prev(spot.b, j, geo.b_size), ring_prev(spot.a, i, geo.a_size), 1 - spot.c)
                self.wire.landed(self.last + j * geo.a_size + i, self.both(held), spot.at_d(sibling))


def gather_sems(geo):
    ab = geo.a_size * geo.b_size
    return 6 + geo.tensor + geo.a_size + geo.b_size + 3 * ab


class WeightScatter:
    def __init__(self, spot, wire, part, held, mine, one_a, one_b, two_a, two_b, land, sem):
        geo = spot.geo
        self.spot, self.wire, self.part, self.held, self.mine = spot, wire, part, held, mine
        self.one_a_buf, self.one_b_buf, self.two_a_buf, self.two_b_buf = one_a, one_b, two_a, two_b
        self.sem = sem
        self.rows = held.shape[3]
        self.half = geo.tensor // 2
        ab = geo.a_size * geo.b_size
        self.zero = wire.take(ab)
        self.one_a = wire.take(geo.a_size - 1)
        self.one_b = wire.take(geo.b_size - 1)
        self.two_a = wire.take(geo.b_size - 1)
        self.two_b = wire.take(geo.a_size - 1)
        here = held.at[spot.b, spot.a]
        self.line = LineScatter(spot, wire, lambda t: here.at[t], lambda k: land.at[k], lambda dst, src: add_tiled(dst, src, min(64, self.rows)))

    def span(self, d):
        return pl.ds(pl.multiple_of(d * self.rows, self.rows), self.rows)

    def start(self):
        spot, geo = self.spot, self.spot.geo
        sibling = spot.rank(spot.b, spot.a, 1 - spot.c)
        self.loads = []
        for b in range(geo.b_size):
            for a in range(geo.a_size):
                theirs = self.part.at[:, self.span(spot.rank(b, a, 1 - spot.c))]
                self.wire.start(self.zero + b * geo.a_size + a, theirs, self.held.at[b, a], spot.at_d(sibling))
                ours = self.part.at[:, self.span(spot.rank(b, a, spot.c))]
                load = pltpu.make_async_copy(ours, self.mine.at[b, a], self.sem.at[b * geo.a_size + a])
                load.start()
                self.loads.append(load)

    def add(self, dst, src):
        n = dst.shape[0]
        tile = min(64, self.rows)
        per = self.rows // tile

        def step(i, carry):
            rows = pl.ds(pl.multiple_of(lax.rem(i, per) * tile, tile), tile)
            j = lax.div(i, per)
            dst[j, rows] = (dst[j, rows].astype(F32) + src[j, rows].astype(F32)).astype(dst.dtype)
            return carry

        lax.fori_loop(0, n * per, step, 0)

    def first(self):
        spot, geo = self.spot, self.spot.geo
        sibling = spot.rank(spot.b, spot.a, 1 - spot.c)
        for b in range(geo.b_size):
            for a in range(geo.a_size):
                i = b * geo.a_size + a
                self.loads[i].wait()
                self.wire.landed(self.zero + i, self.held.at[b, a], spot.at_d(sibling))
                self.add(self.held.at[b, a], self.mine.at[b, a])
        for j in range(1, geo.a_size):
            a = ring_next(spot.a, j, geo.a_size)
            to = spot.rank(spot.b, a, spot.c)
            self.wire.start(self.one_a + j - 1, self.held.at[:, a, pl.ds(0, self.half)], self.one_a_buf.at[j - 1], spot.at_d(to))
        for j in range(1, geo.b_size):
            b = ring_next(spot.b, j, geo.b_size)
            to = spot.rank(b, spot.a, spot.c)
            self.wire.start(self.one_b + j - 1, self.held.at[b, :, pl.ds(self.half, self.half)], self.one_b_buf.at[j - 1], spot.at_d(to))

    def second(self):
        spot, geo = self.spot, self.spot.geo
        low, high = pl.ds(0, self.half), pl.ds(self.half, self.half)
        for j in range(1, geo.a_size):
            self.wire.landed(self.one_a + j - 1, self.one_a_buf.at[j - 1], spot.at_d(spot.rank(spot.b, ring_prev(spot.a, j, geo.a_size), spot.c)))
            for b in range(geo.b_size):
                self.add(self.held.at[b, spot.a, low], self.one_a_buf.at[j - 1, b])
        for j in range(1, geo.b_size):
            b = ring_next(spot.b, j, geo.b_size)
            self.wire.start(self.two_a + j - 1, self.held.at[b, spot.a, low], self.two_a_buf.at[j - 1], spot.at_d(spot.rank(b, spot.a, spot.c)))
        for j in range(1, geo.b_size):
            self.wire.landed(self.one_b + j - 1, self.one_b_buf.at[j - 1], spot.at_d(spot.rank(ring_prev(spot.b, j, geo.b_size), spot.a, spot.c)))
            for a in range(geo.a_size):
                self.add(self.held.at[spot.b, a, high], self.one_b_buf.at[j - 1, a])
        for j in range(1, geo.a_size):
            a = ring_next(spot.a, j, geo.a_size)
            self.wire.start(self.two_b + j - 1, self.held.at[spot.b, a, high], self.two_b_buf.at[j - 1], spot.at_d(spot.rank(spot.b, a, spot.c)))

    def third(self):
        spot, geo = self.spot, self.spot.geo
        low, high = pl.ds(0, self.half), pl.ds(self.half, self.half)
        for j in range(1, geo.b_size):
            self.wire.landed(self.two_a + j - 1, self.two_a_buf.at[j - 1], spot.at_d(spot.rank(ring_prev(spot.b, j, geo.b_size), spot.a, spot.c)))
            self.add(self.held.at[spot.b, spot.a, low], self.two_a_buf.at[j - 1])
        for j in range(1, geo.a_size):
            self.wire.landed(self.two_b + j - 1, self.two_b_buf.at[j - 1], spot.at_d(spot.rank(spot.b, ring_prev(spot.a, j, geo.a_size), spot.c)))
            self.add(self.held.at[spot.b, spot.a, high], self.two_b_buf.at[j - 1])
        self.line.start()

    def fourth(self, out):
        spot = self.spot
        self.line.forward()
        here = self.held.at[spot.b, spot.a, spot.t]
        tile = min(64, self.rows)

        def step(i, carry):
            rows = pl.ds(pl.multiple_of(i * tile, tile), tile)
            out[rows] = here[rows].astype(F32)
            return carry

        lax.fori_loop(0, self.rows // tile, step, 0)
        self.line.finish(lambda ref: add_tiled(out, ref, tile))


def k3_body(geo, ga_ref, g_ref, gaf, out, *rest):
    *bufs, send, recv, local, loads = rest
    spot = geo.bind()
    wire = Wire(send, recv)
    rows = ga_ref.shape[0]

    def slot(t):
        return gaf.at[pl.ds(pl.multiple_of(t * rows, rows), rows)]

    own = pltpu.make_async_copy(ga_ref, slot(spot.t), local.at[0])
    own.start()
    greet(spot)
    gather = LineGather(spot, wire, ga_ref, slot)
    scatters = [WeightScatter(spot, wire, g_ref.at[k], *(buf.at[k] for buf in bufs), loads.at[k]) for k in range(2)]
    scatters[1].start()
    scatters[0].start()
    gather.start()
    scatters[1].first()
    scatters[0].first()
    gather.forward()
    scatters[1].second()
    scatters[0].second()
    scatters[1].third()
    scatters[0].third()
    gather.finish()
    scatters[1].fourth(out.at[1])
    scatters[0].fourth(out.at[0])
    wire.drain()
    own.wait()


def k3(geo, ga, grads):
    rows = grads.shape[2] // geo.dp
    width = grads.shape[3]
    t, a, b = geo.tensor, geo.a_size, geo.b_size
    ab = a * b
    half = t // 2
    sems = 12 + 2 * t + 2 * (ab + 2 * a + 2 * b + 6)
    return pl.pallas_call(
        functools.partial(k3_body, geo),
        out_shape=(
            jax.ShapeDtypeStruct((t * ga.shape[0], ga.shape[1]), BF),
            jax.ShapeDtypeStruct((2, rows, width), F32),
        ),
        in_specs=[ANY, ANY],
        out_specs=(ANY, VM),
        scratch_shapes=[
            pltpu.VMEM((2, b, a, t, rows, width), BF),
            pltpu.VMEM((2, b, a, t, rows, width), BF),
            pltpu.VMEM((2, a - 1, b, half, rows, width), BF),
            pltpu.VMEM((2, b - 1, a, half, rows, width), BF),
            pltpu.VMEM((2, b - 1, half, rows, width), BF),
            pltpu.VMEM((2, a - 1, half, rows, width), BF),
            pltpu.VMEM((2, max(5, t - 1), rows, width), BF),
            pltpu.SemaphoreType.DMA((sems,)), pltpu.SemaphoreType.DMA((sems,)),
            pltpu.SemaphoreType.DMA((1,)), pltpu.SemaphoreType.DMA((2, ab))],
        compiler_params=pltpu.CompilerParams(collective_id=3, has_side_effects=True, vmem_limit_bytes=56 * 2**20),
        name="k3",
    )(ga, grads)


def k4_body(geo, part, w_ref, s_ref, total, wout, sout, land, wland, sland, stot, tland, send, recv):
    spot = geo.bind()
    wire = Wire(send, recv)
    rows = total.shape[0]
    wrows = wout.shape[1]
    greet(spot)

    def block(t):
        return part.at[pl.ds(pl.multiple_of(t * rows, rows), rows)]

    def wblock(d):
        return w_ref.at[:, pl.ds(pl.multiple_of(d * wrows, wrows), wrows)]

    small = wire.take(geo.dp - 1)
    big = wire.take(geo.dp - 1)
    last = wire.take(geo.tensor - 1)
    scatter = LineScatter(spot, wire, block, lambda k: land.at[k], lambda dst, src: add_tiled(dst, src, 64))
    scatter.start()
    for step in range(1, geo.dp):
        to = ring_next(spot.d, step, geo.dp)
        wire.start(small + step - 1, s_ref.at[to], sland.at[step - 1], spot.at_d(to))
    for step in range(1, geo.dp):
        to = ring_next(spot.d, step, geo.dp)
        wire.start(big + step - 1, wblock(to), wland.at[step - 1], spot.at_d(to))
    stot[...] = s_ref[spot.d]
    for step in range(1, geo.dp):
        wire.landed(small + step - 1, sland.at[step - 1], spot.at_d(ring_prev(spot.d, step, geo.dp)))
        stot[...] += sland[step - 1]
    for step in range(1, geo.tensor):
        wire.start(last + step - 1, stot, tland.at[step - 1], spot.at_t(ring_next(spot.t, step, geo.tensor)))
    scatter.forward()
    own = wblock(spot.d)
    for k in range(w_ref.shape[0]):
        wout[k] = own[k].astype(F32)
    for step in range(1, geo.dp):
        wire.landed(big + step - 1, wland.at[step - 1], spot.at_d(ring_prev(spot.d, step, geo.dp)))

        def add(k, carry):
            wout[k] += wland[step - 1, k].astype(F32)
            return carry

        lax.fori_loop(0, w_ref.shape[0], add, 0)
    sout[...] = stot[...]
    for step in range(1, geo.tensor):
        wire.landed(last + step - 1, tland.at[step - 1], spot.at_t(ring_prev(spot.t, step, geo.tensor)))
        sout[...] += tland[step - 1]
    mine = block(spot.t)

    def set_total(i, carry):
        span = pl.ds(pl.multiple_of(i * 64, 64), 64)
        total[span] = mine[span].astype(F32)
        return carry

    lax.fori_loop(0, rows // 64, set_total, 0)
    scatter.finish(lambda ref: add_tiled(total, ref, 64))
    wire.drain()


def k4(geo, part, wgrad, small):
    rows = part.shape[0] // geo.tensor
    width = part.shape[1]
    wshape = (wgrad.shape[0], wgrad.shape[1] // geo.dp, wgrad.shape[2])
    sshape = small.shape[1:]
    sems = 6 + 2 * geo.tensor + 2 * geo.dp
    return pl.pallas_call(
        functools.partial(k4_body, geo),
        out_shape=(
            jax.ShapeDtypeStruct((rows, width), F32),
            jax.ShapeDtypeStruct(wshape, F32),
            jax.ShapeDtypeStruct(sshape, F32),
        ),
        in_specs=[VM, VM, VM],
        out_specs=(VM, VM, VM),
        scratch_shapes=[
            pltpu.VMEM((max(5, geo.tensor - 1), rows, width), BF),
            pltpu.VMEM((geo.dp - 1,) + wshape, BF),
            pltpu.VMEM((geo.dp - 1,) + sshape, F32),
            pltpu.VMEM(sshape, F32),
            pltpu.VMEM((geo.tensor - 1,) + sshape, F32),
            pltpu.SemaphoreType.DMA((sems,)), pltpu.SemaphoreType.DMA((sems,))],
        compiler_params=pltpu.CompilerParams(collective_id=4, has_side_effects=True, vmem_limit_bytes=48 * 2**20),
        name="k4",
    )(part, wgrad, small)


PAIR = 2 * HD


def nt(x, w):
    return lax.dot_general(x, w, (((1,), (1,)), ((), ())), preferred_element_type=F32)


def nn(x, w):
    return lax.dot_general(x, w, (((1,), (0,)), ((), ())), preferred_element_type=F32)


def tn(x, w):
    return lax.dot_general(x, w, (((0,), (0,)), ((), ())), preferred_element_type=F32)


def block_bias(seg_col, seg_row, bias, start, rows, keys):
    query = seg_col[start:start + rows, :]
    for first in range(0, keys, rows):
        key = seg_row[:, first:first + rows]
        seen = query == key
        if first + rows > start:
            q_pos = start + lax.broadcasted_iota(jnp.int32, (rows, rows), 0)
            k_pos = first + lax.broadcasted_iota(jnp.int32, (rows, rows), 1)
            seen = seen & (k_pos <= q_pos)
        bias[:, first:first + rows] = jnp.where(seen, 0.0, MASKED).astype(F32)


def one_head(pair, head):
    lane = lax.broadcasted_iota(jnp.int32, pair.shape, 1)
    return jnp.where((lane < HD) if head == 0 else (lane >= HD), pair, jnp.zeros_like(pair))


def attend_block(qkv, bias, att, lse, start, rows):
    keys = start + rows
    width = qkv.shape[2]
    stat_lane = lax.broadcasted_iota(jnp.int32, (rows, 128), 1)
    stats = jnp.zeros((rows, 128), F32)
    for p in range(width // PAIR):
        lanes = slice(p * PAIR, (p + 1) * PAIR)
        query = qkv[0, start:keys, lanes]
        outs = []
        for head in range(2):
            s = nt(one_head(query, head), qkv[1, 0:keys, lanes]) + bias[:, 0:keys]
            top = jnp.max(s, axis=1, keepdims=True)
            e = jnp.exp(s - top)
            total = jnp.sum(e, axis=1, keepdims=True)
            prob = (e * (1.0 / total)).astype(BF)
            outs.append(nn(prob, qkv[2, 0:keys, lanes]))
            stats = jnp.where(stat_lane == 2 * p + head, top + jnp.log(total), stats)
        lane = lax.broadcasted_iota(jnp.int32, outs[0].shape, 1)
        att[start:keys, lanes] = jnp.where(lane < HD, outs[0], outs[1]).astype(BF)
    lse[start:keys, :] = stats


def attend_block_back(qkv, bias, lse, do, dq, dk, dv, start, rows):
    keys = start + rows
    width = qkv.shape[2]
    stat_lane = lax.broadcasted_iota(jnp.int32, (rows, 128), 1)
    stats = lse[start:keys, :]
    for p in range(width // PAIR):
        lanes = slice(p * PAIR, (p + 1) * PAIR)
        query = qkv[0, start:keys, lanes]
        grad = do[start:keys, lanes]
        dqs, dks, dvs = [], [], []
        for head in range(2):
            level = jnp.sum(jnp.where(stat_lane == 2 * p + head, stats, 0.0), axis=1, keepdims=True)
            s = nt(one_head(query, head), qkv[1, 0:keys, lanes]) + bias[:, 0:keys]
            prob = jnp.exp(s - level)
            d_prob = nt(one_head(grad, head), qkv[2, 0:keys, lanes])
            mixed = prob * d_prob
            ds = (mixed - prob * jnp.sum(mixed, axis=1, keepdims=True)).astype(BF)
            dqs.append(nn(ds, qkv[1, 0:keys, lanes]))
            dks.append(tn(ds, query))
            dvs.append(tn(prob.astype(BF), grad))
        lane = lax.broadcasted_iota(jnp.int32, dqs[0].shape, 1)
        dq[start:keys, lanes] = (jnp.where(lane < HD, dqs[0], dqs[1]) * (HD ** -0.5)).astype(dq.dtype)
        lane = lax.broadcasted_iota(jnp.int32, dks[0].shape, 1)
        dk[0:keys, lanes] += jnp.where(lane < HD, dks[0], dks[1])
        dv[0:keys, lanes] += jnp.where(lane < HD, dvs[0], dvs[1])


def attend_body(qkv, seg_col, seg_row, att, lse, bias):
    rows = 256
    for start in range(0, SEQ, rows):
        block_bias(seg_col, seg_row, bias, start, rows, start + rows)
        attend_block(qkv, bias, att, lse, start, rows)


def attend(qkv, seg_col, seg_row):
    return pl.pallas_call(
        attend_body,
        out_shape=(jax.ShapeDtypeStruct(qkv.shape[1:], BF), jax.ShapeDtypeStruct((qkv.shape[1], 128), F32)),
        in_specs=[VM] * 3, out_specs=(VM, VM),
        scratch_shapes=[pltpu.VMEM((256, SEQ), F32)],
        compiler_params=pltpu.CompilerParams(vmem_limit_bytes=40 * 2**20),
        name="attend",
    )(qkv, seg_col, seg_row)


def attend_back_body(qkv, seg_col, seg_row, lse, do, dqkv, bias, dk, dv):
    rows = 256
    dk[...] = jnp.zeros_like(dk)
    dv[...] = jnp.zeros_like(dv)
    for start in range(SEQ - rows, -1, -rows):
        block_bias(seg_col, seg_row, bias, start, rows, start + rows)
        attend_block_back(qkv, bias, lse, do, dqkv.at[0], dk, dv, start, rows)
        dqkv[1, start:start + rows, :] = dk[start:start + rows, :].astype(BF)
        dqkv[2, start:start + rows, :] = dv[start:start + rows, :].astype(BF)


def attend_back(qkv, seg_col, seg_row, lse, do):
    return pl.pallas_call(
        attend_back_body,
        out_shape=jax.ShapeDtypeStruct(qkv.shape, BF),
        in_specs=[VM] * 5, out_specs=VM,
        scratch_shapes=[pltpu.VMEM((256, SEQ), F32), pltpu.VMEM(qkv.shape[1:], F32), pltpu.VMEM(qkv.shape[1:], F32)],
        compiler_params=pltpu.CompilerParams(vmem_limit_bytes=40 * 2**20),
        name="attend_back",
    )(qkv, seg_col, seg_row, lse, do)


def loop_rows(count, tile, body):
    def step(i, carry):
        body(pl.ds(pl.multiple_of(i * tile, tile), tile))
        return carry

    lax.fori_loop(0, count // tile, step, 0)


def sub_rows(start, count, tile, body):
    def step(i, carry):
        body(pl.ds(pl.multiple_of(start + i * tile, tile), tile))
        return carry

    lax.fori_loop(0, count // tile, step, 0)


def mk1_body(geo, x_ref, aw_ref, ow_ref, up_ref, down_ref, gain_ref, bias_ref, seg_col, seg_row,
             n1, qkv, att, lse, wf, sf, total, xf, full,
             rows12, part, land, bias, wsend, dsend, ssend, send, recv, local):
    spot = geo.bind()
    wire = Wire(send, recv)
    size = geo.tensor
    rows = x_ref.shape[0]
    wrows = aw_ref.shape[1]
    mrows = up_ref.shape[0]
    heads = aw_ref.shape[2]

    def xslot(t):
        return xf.at[pl.ds(pl.multiple_of(t * rows, rows), rows)]

    def wslot(d):
        return wf.at[:, pl.ds(pl.multiple_of(d * wrows, wrows), wrows)]

    def block(i):
        return part.at[pl.ds(pl.multiple_of(i * rows, rows), rows)]

    gain_copy = pltpu.make_async_copy(x_ref, xslot(spot.t), local.at[0])
    gain_copy.start()
    span = pl.ds(pl.multiple_of(spot.d * mrows, mrows), mrows)
    up_copy = pltpu.make_async_copy(up_ref, full.at[0, spot.t, span], local.at[1])
    up_copy.start()
    ssend[0:2, :] = gain_ref[...].astype(F32)
    ssend[2:12, :] = bias_ref[...].astype(F32)
    wsend[0:3] = aw_ref[...]
    wsend[3] = ow_ref[...].T
    greet(spot)
    ups = WeightGather(spot, wire, up_ref, full.at[0])
    downs = WeightGather(spot, wire, dsend, full.at[1])
    xs = LineGather(spot, wire, x_ref, xslot)
    ups.line.start()
    small = wire.take(geo.dp - 1)
    big = wire.take(geo.dp - 1)
    for step in range(1, geo.dp):
        wire.start(small + step - 1, ssend, sf.at[spot.d], spot.at_d(ring_next(spot.d, step, geo.dp)))
    for step in range(1, geo.dp):
        wire.start(big + step - 1, wsend, wslot(spot.d), spot.at_d(ring_next(spot.d, step, geo.dp)))
    sf[spot.d] = ssend[...]
    wf[:, pl.ds(pl.multiple_of(spot.d * wrows, wrows), wrows)] = wsend[...]
    dsend[...] = down_ref[...].T
    down_copy = pltpu.make_async_copy(dsend, full.at[1, spot.t, span], local.at[2])
    down_copy.start()
    ups.line.forward()
    xs.start()
    up_copy.wait()
    ups.line.finish()
    ups.first()
    for step in range(1, geo.dp):
        source = ring_prev(spot.d, step, geo.dp)
        wire.landed(small + step - 1, sf.at[source], spot.at_d(source))
    piece = ssend.shape[1]
    for d in range(geo.dp):
        rows12[:, d * piece:(d + 1) * piece] = sf[d]
    for step in range(1, geo.dp):
        source = ring_prev(spot.d, step, geo.dp)
        wire.landed(big + step - 1, wslot(source), spot.at_d(source))
    gain_copy.wait()
    column = pl.ds(pl.multiple_of(spot.t * heads, 128), heads)

    def project(t):
        def norm(r):
            n1[r] = layer_norm(xf[r].astype(F32), rows12[0:1, :], rows12[2:3, :]).astype(BF)

        sub_rows(pl.multiple_of(t * rows, rows), rows, min(64, rows), norm)
        r = pl.ds(pl.multiple_of(t * rows, rows), rows)
        normed = n1[r]
        qkv[0, r] = ((nn(normed, wf[0]) + rows12[3:4, column]).astype(BF).astype(F32) * HD ** -0.5).astype(BF)
        qkv[1, r] = nn(normed, wf[1]).astype(BF)
        qkv[2, r] = (nn(normed, wf[2]) + rows12[4:5, column]).astype(BF)

    project(spot.t)
    ups.second()
    xs.forward()
    xs.finish()
    downs.line.start()

    def other(step, carry):
        project(ring_next(spot.t, step, size))
        return carry

    lax.fori_loop(1, size, other, 0)
    ups.third()
    scatter = LineScatter(spot, wire, block, lambda k: land.at[k], lambda dst, src: add_tiled(dst, src, 64))
    qrows = min(256, SEQ)
    for start in range(0, SEQ, qrows):
        block_bias(seg_col, seg_row, bias, start, qrows, start + qrows)
        attend_block(qkv, bias, att, lse, start, qrows)
        part[start:start + qrows, :] = nt(att[start:start + qrows, :], wf[3]).astype(BF)
        if scatter.line:
            scatter.start_block(start // rows)
        if start == 0:
            downs.line.forward()
    if not scatter.line:
        scatter.start()
    down_copy.wait()
    downs.line.finish()
    downs.first()
    scatter.forward()
    downs.second()
    mine = block(spot.t)

    def set_total(r):
        total[r] = mine[r].astype(F32)

    loop_rows(rows, min(64, rows), set_total)
    scatter.finish(lambda ref: add_tiled(total, ref, 64))
    ups.fourth()
    downs.third()
    downs.fourth()
    wire.drain()


def mk1(geo, x, aw, ow, up, down, gains, biases, seg_col, seg_row):
    rows, width = x.shape
    wrows, heads = aw.shape[1:]
    size = geo.tensor
    sems = 12 + 2 * size + 2 * geo.dp + 2 * gather_sems(geo)
    seq = size * rows
    return pl.pallas_call(
        functools.partial(mk1_body, geo),
        out_shape=(
            jax.ShapeDtypeStruct((seq, width), BF),
            jax.ShapeDtypeStruct((3, seq, heads), BF),
            jax.ShapeDtypeStruct((seq, heads), BF),
            jax.ShapeDtypeStruct((seq, 128), F32),
            jax.ShapeDtypeStruct((4, width, heads), BF),
            jax.ShapeDtypeStruct((geo.dp, 12, wrows), F32),
            jax.ShapeDtypeStruct((rows, width), F32),
            jax.ShapeDtypeStruct((seq, width), BF),
            jax.ShapeDtypeStruct((2, size, width, up.shape[1]), BF),
        ),
        in_specs=[ANY, VM, VM, ANY, VM, VM, VM, VM, VM],
        out_specs=(VM,) * 8 + (ANY,),
        scratch_shapes=[
            pltpu.VMEM((12, width), F32),
            pltpu.VMEM((seq, width), BF),
            pltpu.VMEM((max(5, size - 1), rows, width), BF),
            pltpu.VMEM((min(256, SEQ), SEQ), F32),
            pltpu.VMEM((4, wrows, heads), BF),
            pltpu.VMEM(up.shape, BF),
            pltpu.VMEM((12, wrows), F32),
            pltpu.SemaphoreType.DMA((sems,)), pltpu.SemaphoreType.DMA((sems,)), pltpu.SemaphoreType.DMA((3,))],
        compiler_params=pltpu.CompilerParams(collective_id=1, has_side_effects=True, vmem_limit_bytes=50 * 2**20),
        name="mk1",
    )(x, aw, ow, up, down, gains, biases, seg_col, seg_row)


def dot_nt(x, w):
    return lax.dot_general(x, w, (((1,), (1,)), ((), ())), preferred_element_type=F32)


def dot_tn(x, w):
    return lax.dot_general(x, w, (((0,), (0,)), ((), ())), preferred_element_type=F32)


def per_device(geo, activations, segments, attn_weight, out_weight, up_weight, down_weight, norm_gains, bias_rows, cotangent):
    tensor_rank = lax.axis_index("tensor")
    width = activations.shape[1]
    head_width = attn_weight.shape[3]
    seg_col, seg_row = segments[:, None], segments[None, :]
    normed_full, project, attended, log_total, w_full, small_full, attn_sum, x_full, m_full = mk1(
        geo, activations, attn_weight[0], out_weight[0], up_weight[0], down_weight[0], norm_gains[0], bias_rows[0], seg_col, seg_row)
    rows12 = small_full.transpose(1, 0, 2).reshape(12, width)
    gains, biases = rows12[:2], rows12[2:]
    column = tensor_rank * head_width

    residual = activations.astype(F32)
    middle = residual + (attn_sum + biases[3])
    unit_two, scale_two = norm_stats(middle)
    normed_two = (unit_two * gains[1] + biases[4]).astype(BF)
    up_full, down_full = m_full[0], m_full[1]
    tensor = up_full.shape[0]
    unit_width = up_full.shape[2]
    up_bias = biases[6:10].reshape(1, -1)
    hidden = jnp.concatenate([jnp.dot(normed_two, up_full[s], preferred_element_type=F32) for s in range(tensor)], axis=1) + up_bias
    active = gelu_tanh(hidden).astype(BF)
    branch = cotangent.astype(BF)
    ff = sum(dot_nt(active[:, s * unit_width:(s + 1) * unit_width], down_full[s]) for s in range(tensor))
    output = middle + (ff + biases[5])
    active_grad = jnp.concatenate([jnp.dot(branch, down_full[s], preferred_element_type=F32) for s in range(tensor)], axis=1)
    hidden_grad = jax.vjp(gelu_tanh, hidden)[1](active_grad)[0].astype(BF)
    up_bias_grad = jnp.sum(hidden_grad.astype(F32), axis=0).reshape(4, width)
    grads = jnp.stack([
        jnp.stack([dot_tn(normed_two, hidden_grad[:, s * unit_width:(s + 1) * unit_width]).astype(BF) for s in range(tensor)]),
        jnp.stack([dot_tn(branch, active[:, s * unit_width:(s + 1) * unit_width]).astype(BF) for s in range(tensor)]),
    ])
    normed_two_grad = sum(dot_nt(hidden_grad[:, s * unit_width:(s + 1) * unit_width], up_full[s]) for s in range(tensor))
    middle_grad = cotangent + norm_back(normed_two_grad, unit_two, scale_two, gains[1])
    attn_branch = middle_grad.astype(BF)
    ga_full, mlp_grads = k3(geo, attn_branch, grads)

    attended_grad = jnp.dot(ga_full, w_full[3], preferred_element_type=F32).astype(BF)
    project_grad = attend_back(project, seg_col, seg_row, log_total, attended_grad)
    dn_part = sum(dot_nt(project_grad[j], w_full[j]) for j in range(3))
    w_grads = jnp.stack([dot_tn(normed_full, project_grad[j]).astype(BF) for j in range(3)] + [dot_tn(ga_full, attended).astype(BF)])

    query_bias_grad = jnp.sum(project_grad[0].astype(F32), axis=0)
    value_bias_grad = jnp.sum(project_grad[2].astype(F32), axis=0)
    zeros = jnp.zeros((width,), F32)
    dn_total, w_out, small_one = k4(geo, dn_part.astype(BF), w_grads, split_dp(geo, jnp.stack([
        jnp.sum(dn_part * norm_stats(x_full.astype(F32))[0], axis=0),
        jnp.sum(normed_two_grad * unit_two, axis=0),
        jnp.sum(dn_part, axis=0),
        lax.dynamic_update_slice_in_dim(zeros, query_bias_grad, column, 0),
        lax.dynamic_update_slice_in_dim(zeros, value_bias_grad, column, 0),
        jnp.sum(attn_branch.astype(F32), axis=0),
        jnp.sum(normed_two_grad, axis=0),
        jnp.sum(branch.astype(F32), axis=0),
        up_bias_grad[0], up_bias_grad[1], up_bias_grad[2], up_bias_grad[3],
    ])))
    unit_one, scale_one = norm_stats(residual)
    input_grad = middle_grad + norm_back(dn_total, unit_one, scale_one, gains[0])
    return (
        output, input_grad, w_out[None, :3], w_out[3].T[None], mlp_grads[0][None], mlp_grads[1].T[None],
        small_one[None, :2], small_one[None, 2:12])


def split_dp(geo, rows):
    n, width = rows.shape
    pad = -n % 8
    rows = jnp.pad(rows, ((0, pad), (0, 0)))
    return rows.reshape(n + pad, geo.dp, width // geo.dp).transpose(1, 0, 2)


def solution(mesh):
    geo = Geometry(mesh.shape["dp"], mesh.shape["tensor"])
    return jax.shard_map(
        functools.partial(per_device, geo),
        mesh=mesh,
        in_specs=(
            P(("dp", "tensor"), None),
            P("dp"),
            P(None, None, "dp", "tensor"),
            P(None, "tensor", "dp"),
            P(None, "dp", "tensor"),
            P(None, "tensor", "dp"),
            P(None, None, "dp"),
            P(None, None, "dp"),
            P(("dp", "tensor"), None),
        ),
        out_specs=(
            P(("dp", "tensor"), None),
            P(("dp", "tensor"), None),
            P(None, None, "dp", "tensor"),
            P(None, "tensor", "dp"),
            P(None, "dp", "tensor"),
            P(None, "tensor", "dp"),
            P(None, None, "dp"),
            P(None, None, "dp"),
        ),
        check_vma=False,
    )
```

```python
import functools

import jax
import jax.numpy as jnp
from jax import lax
from jax.experimental import pallas as pl
from jax.experimental.pallas import tpu as pltpu
from jax.sharding import PartitionSpec as P

HD = 64
SEQ = 1024
EPSILON = 1e-05
MASKED = -1e30
MESH_ID = pl.DeviceIdType.MESH
BF = jnp.bfloat16
F32 = jnp.float32
ANY = pl.BlockSpec(memory_space=pl.ANY)
VM = pl.BlockSpec(memory_space=pltpu.VMEM)


def layer_norm(values, gain_row, shift_row):
    center = values - jnp.mean(values, axis=-1, keepdims=True)
    spread = jnp.mean(center * center, axis=-1, keepdims=True)
    return center * lax.rsqrt(spread + EPSILON) * gain_row + shift_row


def norm_stats(values):
    center = values - jnp.mean(values, axis=-1, keepdims=True)
    spread = jnp.mean(center * center, axis=-1, keepdims=True)
    scale = lax.rsqrt(spread + EPSILON)
    return center * scale, scale


def norm_back(grad, unit, scale, gain_row):
    u = grad * gain_row
    mean_u = jnp.mean(u, axis=-1, keepdims=True)
    mean_ux = jnp.mean(u * unit, axis=-1, keepdims=True)
    return scale * (u - mean_u - unit * mean_ux)


def gelu_tanh(values):
    return jax.nn.gelu(values, approximate=True)


class Geometry:
    def __init__(self, dp, tensor):
        self.dp, self.tensor = dp, tensor
        self.c_size = 2
        rest = dp // 2
        self.a_size = 1
        while self.a_size * self.a_size < rest:
            self.a_size *= 2
        self.b_size = rest // self.a_size
        assert self.a_size * self.b_size * 2 == dp

    def bind(self):
        spot = Spot()
        spot.geo = self
        spot.d = lax.axis_index("dp")
        spot.t = lax.axis_index("tensor")
        spot.c = lax.rem(spot.d, 2)
        half = lax.div(spot.d, 2)
        spot.a = lax.rem(half, self.a_size)
        spot.b = lax.div(half, self.a_size)
        return spot


class Spot:
    def rank(self, b, a, c):
        return (b * self.geo.a_size + a) * 2 + c

    def at_t(self, t):
        return (self.d, t)

    def at_d(self, d):
        return (d, self.t)


def ring_next(rank, step, size):
    return lax.rem(rank + step, size)


def ring_prev(rank, step, size):
    return lax.rem(rank + size - step, size)


class Wire:
    def __init__(self, send, recv):
        self.send_sems, self.recv_sems = send, recv
        self.count = 0
        self.pending = []

    def take(self, n):
        first = self.count
        self.count += n
        return first

    def copy(self, i, src, dst, device):
        return pltpu.make_async_remote_copy(
            src_ref=src, dst_ref=dst, send_sem=self.send_sems.at[i], recv_sem=self.recv_sems.at[i],
            device_id=device, device_id_type=MESH_ID)

    def plan(self, i, src, dst, device, when=None):
        return self.copy(i, src, dst, device), when

    def go(self, planned):
        copy, when = planned
        if when is None:
            copy.start()
        else:
            pl.when(when)(copy.start)
        self.pending.append(planned)

    def start(self, i, src, dst, device, when=None):
        self.go(self.plan(i, src, dst, device, when))

    def landed(self, i, dst, device, when=None):
        copy = self.copy(i, dst, dst, device)
        if when is None:
            copy.wait_recv()
        else:
            pl.when(when)(copy.wait_recv)

    def drain(self):
        for copy, when in self.pending:
            if when is None:
                copy.wait_send()
            else:
                pl.when(when)(copy.wait_send)
        self.pending = []


def greet(spot, with_dp=True):
    geo = spot.geo
    barrier = pltpu.get_barrier_semaphore()
    total = 0
    for step in range(1, geo.tensor):
        pl.semaphore_signal(barrier, inc=1, device_id=spot.at_t(ring_next(spot.t, step, geo.tensor)), device_id_type=MESH_ID)
        total += 1
    for step in range(1, geo.dp):
        pl.semaphore_signal(barrier, inc=1, device_id=spot.at_d(ring_next(spot.d, step, geo.dp)), device_id_type=MESH_ID)
        total += 1
    pl.semaphore_wait(barrier, total)


class LineGather:
    def __init__(self, spot, wire, src, slot):
        self.spot, self.wire, self.slot = spot, wire, slot
        self.size = spot.geo.tensor
        self.line = self.size == 4
        self.first = wire.take(6 if self.line else self.size - 1)
        t = spot.t
        self.sends, self.passes = [], []
        if not self.line:
            for step in range(1, self.size):
                self.sends.append(wire.plan(self.first + step - 1, src, slot(t), spot.at_t(ring_next(t, step, self.size))))
            return
        for k, delta in enumerate((2, -2, 1, -1)):
            to = t + delta
            self.sends.append(wire.plan(self.first + k, src, slot(t), spot.at_t(to), when=(to >= 0) & (to < self.size)))
        for k, delta in enumerate((-2, 2)):
            at_work = t == (2, 1)[k]
            piece = slot(t + delta)
            self.passes.append((at_work, t + delta, wire.plan(self.first + 4 + k, piece, piece, spot.at_t(t + (1, -1)[k]), when=at_work)))

    def start(self):
        for planned in self.sends:
            self.wire.go(planned)

    def forward(self):
        for k, (at_work, source, planned) in enumerate(self.passes):
            self.wire.landed(self.first + k, self.slot(source), self.spot.at_t(source), when=at_work)
            self.wire.go(planned)

    def finish(self):
        spot, t = self.spot, self.spot.t
        if not self.line:
            for step in range(1, self.size):
                source = ring_prev(t, step, self.size)
                self.wire.landed(self.first + step - 1, self.slot(source), spot.at_t(source))
            return
        self.wire.landed(self.first + 0, self.slot(t - 2), spot.at_t(t - 2), when=t == 3)
        self.wire.landed(self.first + 1, self.slot(t + 2), spot.at_t(t + 2), when=t == 0)
        self.wire.landed(self.first + 2, self.slot(t - 1), spot.at_t(t - 1), when=t >= 1)
        self.wire.landed(self.first + 3, self.slot(t + 1), spot.at_t(t + 1), when=t <= 2)
        self.wire.landed(self.first + 4, self.slot(t - 3), spot.at_t(t - 1), when=t == 3)
        self.wire.landed(self.first + 5, self.slot(t + 3), spot.at_t(t + 1), when=t == 0)


class LineScatter:
    def __init__(self, spot, wire, part, land, add):
        self.spot, self.wire, self.part, self.land, self.add = spot, wire, part, land, add
        self.size = spot.geo.tensor
        self.line = self.size == 4
        self.first = wire.take(6 if self.line else self.size - 1)

    def start(self):
        spot, t = self.spot, self.spot.t
        if not self.line:
            for step in range(1, self.size):
                to = ring_next(t, step, self.size)
                self.wire.start(self.first + step - 1, self.part(to), self.land(step - 1), spot.at_t(to))
            return
        self.wire.start(self.first + 4, self.part(3), self.land(4), spot.at_t(1), when=t == 0)
        self.wire.start(self.first + 5, self.part(0), self.land(4), spot.at_t(2), when=t == 3)
        self.wire.start(self.first + 0, self.part(2), self.land(0), spot.at_t(2), when=t == 0)
        self.wire.start(self.first + 1, self.part(1), self.land(1), spot.at_t(1), when=t == 3)
        self.wire.start(self.first + 2, self.part(jnp.minimum(t + 1, 3)), self.land(2), spot.at_t(t + 1), when=t <= 2)
        self.wire.start(self.first + 3, self.part(jnp.maximum(t - 1, 0)), self.land(3), spot.at_t(t - 1), when=t >= 1)

    def start_block(self, i):
        spot, t = self.spot, self.spot.t
        if i == 3:
            self.wire.start(self.first + 4, self.part(3), self.land(4), spot.at_t(1), when=t == 0)
        if i == 0:
            self.wire.start(self.first + 5, self.part(0), self.land(4), spot.at_t(2), when=t == 3)
        if i == 2:
            self.wire.start(self.first + 0, self.part(2), self.land(0), spot.at_t(2), when=t == 0)
        if i == 1:
            self.wire.start(self.first + 1, self.part(1), self.land(1), spot.at_t(1), when=t == 3)
        if i >= 1:
            self.wire.start(self.first + 2, self.part(i), self.land(2), spot.at_t(i), when=t == i - 1)
        if i <= 2:
            self.wire.start(self.first + 3, self.part(i), self.land(3), spot.at_t(i), when=t == i + 1)

    def forward(self):
        if not self.line:
            return
        spot, t = self.spot, self.spot.t

        @pl.when(t == 1)
        def _():
            self.wire.landed(self.first + 4, self.land(4), spot.at_t(0))
            self.add(self.part(3), self.land(4))

        @pl.when(t == 2)
        def _():
            self.wire.landed(self.first + 5, self.land(4), spot.at_t(3))
            self.add(self.part(0), self.land(4))

        self.wire.start(self.first + 0, self.part(3), self.land(0), spot.at_t(3), when=t == 1)
        self.wire.start(self.first + 1, self.part(0), self.land(1), spot.at_t(0), when=t == 2)

    def finish(self, total):
        spot, t = self.spot, self.spot.t
        if not self.line:
            for step in range(1, self.size):
                self.wire.landed(self.first + step - 1, self.land(step - 1), spot.at_t(ring_prev(t, step, self.size)))
                total(self.land(step - 1))
            return
        for k, delta in enumerate((2, -2, 1, -1)):
            source = t - delta

            @pl.when((source >= 0) & (source < self.size))
            def _():
                self.wire.landed(self.first + k, self.land(k), spot.at_t(source))
                total(self.land(k))


def add_tiled(dst, src, tile):
    count = dst.shape[0] // tile

    def step(i, carry):
        rows = pl.ds(pl.multiple_of(i * tile, tile), tile)
        dst[rows] = (dst[rows].astype(F32) + src[rows].astype(F32)).astype(dst.dtype)
        return carry

    lax.fori_loop(0, count, step, 0)


class WeightGather:
    def __init__(self, spot, wire, rows, full):
        geo = spot.geo
        self.spot, self.wire, self.full, self.rows = spot, wire, full, rows
        self.slots = full.shape[0]
        self.half = self.slots // 2
        self.one_a = wire.take(geo.a_size - 1)
        self.one_b = wire.take(geo.b_size - 1)
        self.two_a = wire.take((geo.b_size - 1) * geo.a_size)
        self.two_b = wire.take((geo.a_size - 1) * geo.b_size)
        self.last = wire.take(geo.a_size * geo.b_size)

    def span(self, d):
        return pl.ds(pl.multiple_of(d * self.rows, self.rows), self.rows)

    def low(self, d):
        return self.full.at[pl.ds(0, self.half), self.span(d)]

    def high(self, d):
        return self.full.at[pl.ds(self.half, self.slots - self.half), self.span(d)]

    def both(self, d):
        return self.full.at[:, self.span(d)]

    def first(self):
        spot, geo = self.spot, self.spot.geo
        mine = spot.d
        for j in range(1, geo.a_size):
            to = spot.rank(spot.b, ring_next(spot.a, j, geo.a_size), spot.c)
            self.wire.start(self.one_a + j - 1, self.low(mine), self.low(mine), spot.at_d(to))
        for j in range(1, geo.b_size):
            to = spot.rank(ring_next(spot.b, j, geo.b_size), spot.a, spot.c)
            self.wire.start(self.one_b + j - 1, self.high(mine), self.high(mine), spot.at_d(to))
        sibling = spot.rank(spot.b, spot.a, 1 - spot.c)
        self.wire.start(self.last, self.both(mine), self.both(mine), spot.at_d(sibling))

    def second(self):
        spot, geo = self.spot, self.spot.geo
        for i in range(geo.a_size):
            held = spot.rank(spot.b, ring_prev(spot.a, i, geo.a_size), spot.c)
            if i:
                self.wire.landed(self.one_a + i - 1, self.low(held), spot.at_d(held))
            for j in range(1, geo.b_size):
                to = spot.rank(ring_next(spot.b, j, geo.b_size), spot.a, spot.c)
                self.wire.start(self.two_a + (j - 1) * geo.a_size + i, self.low(held), self.low(held), spot.at_d(to))
        for i in range(geo.b_size):
            held = spot.rank(ring_prev(spot.b, i, geo.b_size), spot.a, spot.c)
            if i:
                self.wire.landed(self.one_b + i - 1, self.high(held), spot.at_d(held))
            for j in range(1, geo.a_size):
                to = spot.rank(spot.b, ring_next(spot.a, j, geo.a_size), spot.c)
                self.wire.start(self.two_b + (j - 1) * geo.b_size + i, self.high(held), self.high(held), spot.at_d(to))

    def third(self):
        spot, geo = self.spot, self.spot.geo
        for j in range(1, geo.b_size):
            for i in range(geo.a_size):
                held = spot.rank(ring_prev(spot.b, j, geo.b_size), ring_prev(spot.a, i, geo.a_size), spot.c)
                source = spot.rank(ring_prev(spot.b, j, geo.b_size), spot.a, spot.c)
                self.wire.landed(self.two_a + (j - 1) * geo.a_size + i, self.low(held), spot.at_d(source))
        for j in range(1, geo.a_size):
            for i in range(geo.b_size):
                held = spot.rank(ring_prev(spot.b, i, geo.b_size), ring_prev(spot.a, j, geo.a_size), spot.c)
                source = spot.rank(spot.b, ring_prev(spot.a, j, geo.a_size), spot.c)
                self.wire.landed(self.two_b + (j - 1) * geo.b_size + i, self.high(held), spot.at_d(source))
        sibling = spot.rank(spot.b, spot.a, 1 - spot.c)
        for j in range(geo.b_size):
            for i in range(geo.a_size):
                if i or j:
                    held = spot.rank(ring_prev(spot.b, j, geo.b_size), ring_prev(spot.a, i, geo.a_size), spot.c)
                    self.wire.start(self.last + j * geo.a_size + i, self.both(held), self.both(held), spot.at_d(sibling))

    def fourth(self):
        spot, geo = self.spot, self.spot.geo
        sibling = spot.rank(spot.b, spot.a, 1 - spot.c)
        for j in range(geo.b_size):
            for i in range(geo.a_size):
                held = spot.rank(ring_prev(spot.b, j, geo.b_size), ring_prev(spot.a, i, geo.a_size), 1 - spot.c)
                self.wire.landed(self.last + j * geo.a_size + i, self.both(held), spot.at_d(sibling))


def gather_sems(geo):
    return geo.a_size + geo.b_size + 3 * geo.a_size * geo.b_size


class WeightScatter:
    def __init__(self, spot, wire, held, one_a, one_b, two_a, two_b):
        geo = spot.geo
        self.spot, self.wire, self.held = spot, wire, held
        self.one_a_buf, self.one_b_buf, self.two_a_buf, self.two_b_buf = one_a, one_b, two_a, two_b
        self.slots, self.rows = held.shape[2], held.shape[3]
        self.half = self.slots // 2
        self.one_a = wire.take(geo.a_size - 1)
        self.one_b = wire.take(geo.b_size - 1)
        self.two_a = wire.take(geo.b_size - 1)
        self.two_b = wire.take(geo.a_size - 1)
        low, high = pl.ds(0, self.half), pl.ds(self.half, self.half)
        self.sends = []
        for j in range(1, geo.a_size):
            a = ring_next(spot.a, j, geo.a_size)
            self.sends.append(wire.plan(self.one_a + j - 1, held.at[:, a, low], one_a.at[j - 1], spot.at_d(spot.rank(spot.b, a, spot.c))))
        for j in range(1, geo.b_size):
            b = ring_next(spot.b, j, geo.b_size)
            self.sends.append(wire.plan(self.one_b + j - 1, held.at[b, :, high], one_b.at[j - 1], spot.at_d(spot.rank(b, spot.a, spot.c))))

    def add(self, dst, src):
        tile = min(64, self.rows)
        per = self.rows // tile

        def step(i, carry):
            rows = pl.ds(pl.multiple_of(lax.rem(i, per) * tile, tile), tile)
            j = lax.div(i, per)
            dst[j, rows] = (dst[j, rows].astype(F32) + src[j, rows].astype(F32)).astype(dst.dtype)
            return carry

        lax.fori_loop(0, dst.shape[0] * per, step, 0)

    def first(self):
        for planned in self.sends:
            self.wire.go(planned)

    def second(self):
        spot, geo = self.spot, self.spot.geo
        low, high = pl.ds(0, self.half), pl.ds(self.half, self.half)
        for j in range(1, geo.a_size):
            self.wire.landed(self.one_a + j - 1, self.one_a_buf.at[j - 1], spot.at_d(spot.rank(spot.b, ring_prev(spot.a, j, geo.a_size), spot.c)))
            for b in range(geo.b_size):
                self.add(self.held.at[b, spot.a, low], self.one_a_buf.at[j - 1, b])
        for j in range(1, geo.b_size):
            b = ring_next(spot.b, j, geo.b_size)
            self.wire.start(self.two_a + j - 1, self.held.at[b, spot.a, low], self.two_a_buf.at[j - 1], spot.at_d(spot.rank(b, spot.a, spot.c)))
        for j in range(1, geo.b_size):
            self.wire.landed(self.one_b + j - 1, self.one_b_buf.at[j - 1], spot.at_d(spot.rank(ring_prev(spot.b, j, geo.b_size), spot.a, spot.c)))
            for a in range(geo.a_size):
                self.add(self.held.at[spot.b, a, high], self.one_b_buf.at[j - 1, a])
        for j in range(1, geo.a_size):
            a = ring_next(spot.a, j, geo.a_size)
            self.wire.start(self.two_b + j - 1, self.held.at[spot.b, a, high], self.two_b_buf.at[j - 1], spot.at_d(spot.rank(spot.b, a, spot.c)))

    def third(self):
        spot, geo = self.spot, self.spot.geo
        low, high = pl.ds(0, self.half), pl.ds(self.half, self.half)
        for j in range(1, geo.b_size):
            self.wire.landed(self.two_a + j - 1, self.two_a_buf.at[j - 1], spot.at_d(spot.rank(ring_prev(spot.b, j, geo.b_size), spot.a, spot.c)))
            self.add(self.held.at[spot.b, spot.a, low], self.two_a_buf.at[j - 1])
        for j in range(1, geo.a_size):
            self.wire.landed(self.two_b + j - 1, self.two_b_buf.at[j - 1], spot.at_d(spot.rank(spot.b, ring_prev(spot.a, j, geo.a_size), spot.c)))
            self.add(self.held.at[spot.b, spot.a, high], self.two_b_buf.at[j - 1])


def scatter_sems(geo):
    return 2 * geo.a_size + 2 * geo.b_size


def scatter_bufs(geo, n, slots, rows, width):
    a, b, half = geo.a_size, geo.b_size, slots // 2
    return [
        pltpu.VMEM((n, b, a, slots, rows, width), BF),
        pltpu.VMEM((n, a - 1, b, half, rows, width), BF),
        pltpu.VMEM((n, b - 1, a, half, rows, width), BF),
        pltpu.VMEM((n, b - 1, half, rows, width), BF),
        pltpu.VMEM((n, a - 1, half, rows, width), BF),
    ]


def loop_rows(count, tile, body, start=0):
    def step(i, carry):
        body(pl.ds(pl.multiple_of(start + i * tile, tile), tile))
        return carry

    lax.fori_loop(0, count // tile, step, 0)


def fetch(copies):
    for copy in copies:
        copy.start()
    return copies


def settle(copies):
    for copy in copies:
        copy.wait()


PAIR = 2 * HD


def nt(x, w):
    return lax.dot_general(x, w, (((1,), (1,)), ((), ())), preferred_element_type=F32)


def nn(x, w):
    return lax.dot_general(x, w, (((1,), (0,)), ((), ())), preferred_element_type=F32)


def tn(x, w):
    return lax.dot_general(x, w, (((0,), (0,)), ((), ())), preferred_element_type=F32)


def block_bias(seg_col, seg_row, bias, start, rows, keys):
    query = seg_col[start:start + rows, 0:1]
    for first in range(0, keys, rows):
        key = seg_row[:, first:first + rows]
        seen = query == key
        if first + rows > start:
            q_pos = start + lax.broadcasted_iota(jnp.int32, (rows, rows), 0)
            k_pos = first + lax.broadcasted_iota(jnp.int32, (rows, rows), 1)
            seen = seen & (k_pos <= q_pos)
        bias[:, first:first + rows] = jnp.where(seen, 0.0, MASKED).astype(F32)


def one_head(pair, head):
    lane = lax.broadcasted_iota(jnp.int32, pair.shape, 1)
    return jnp.where((lane < HD) if head == 0 else (lane >= HD), pair, jnp.zeros_like(pair))


def attend_block(qkv, bias, att, lse, start, rows):
    keys = start + rows
    width = qkv.shape[2]
    stat_lane = lax.broadcasted_iota(jnp.int32, (rows, 128), 1)
    stats = jnp.zeros((rows, 128), F32)
    for p in range(width // PAIR):
        lanes = slice(p * PAIR, (p + 1) * PAIR)
        query = qkv[0, start:keys, lanes]
        outs = []
        for head in range(2):
            s = nt(one_head(query, head), qkv[1, 0:keys, lanes]) + bias[:, 0:keys]
            top = jnp.max(s, axis=1, keepdims=True)
            e = jnp.exp(s - top)
            total = jnp.sum(e, axis=1, keepdims=True)
            prob = (e * (1.0 / total)).astype(BF)
            outs.append(nn(prob, qkv[2, 0:keys, lanes]))
            stats = jnp.where(stat_lane == 2 * p + head, top + jnp.log(total), stats)
        lane = lax.broadcasted_iota(jnp.int32, outs[0].shape, 1)
        att[start:keys, lanes] = jnp.where(lane < HD, outs[0], outs[1]).astype(BF)
    lse[start:keys, :] = stats


def attend_block_back(qkv, bias, lse, do, dq, dk, dv, start, rows):
    keys = start + rows
    width = qkv.shape[2]
    stat_lane = lax.broadcasted_iota(jnp.int32, (rows, 128), 1)
    stats = lse[start:keys, :]
    for p in range(width // PAIR):
        lanes = slice(p * PAIR, (p + 1) * PAIR)
        query = qkv[0, start:keys, lanes]
        grad = do[start:keys, lanes]
        dqs, dks, dvs = [], [], []
        for head in range(2):
            level = jnp.sum(jnp.where(stat_lane == 2 * p + head, stats, 0.0), axis=1, keepdims=True)
            s = nt(one_head(query, head), qkv[1, 0:keys, lanes]) + bias[:, 0:keys]
            prob = jnp.exp(s - level)
            d_prob = nt(one_head(grad, head), qkv[2, 0:keys, lanes])
            mixed = prob * d_prob
            ds = (mixed - prob * jnp.sum(mixed, axis=1, keepdims=True)).astype(BF)
            dqs.append(nn(ds, qkv[1, 0:keys, lanes]))
            dks.append(tn(ds, query))
            dvs.append(tn(prob.astype(BF), grad))
        lane = lax.broadcasted_iota(jnp.int32, dqs[0].shape, 1)
        dq[start:keys, lanes] = (jnp.where(lane < HD, dqs[0], dqs[1]) * (HD ** -0.5)).astype(dq.dtype)
        lane = lax.broadcasted_iota(jnp.int32, dks[0].shape, 1)
        dk[0:keys, lanes] += jnp.where(lane < HD, dks[0], dks[1])
        dv[0:keys, lanes] += jnp.where(lane < HD, dvs[0], dvs[1])


def mk1_body(geo, x_ref, aw_ref, ow_ref, up_ref, down_ref, gain_ref, bias_ref, seg_ref,
             n1t, qkv, att, lse, wf, rows12, total, xf, seg_col, full,
             sf, n1, part, land, bias, wsend, ow_in, down_in, dsend, gain_in, bias_in, seg_row, ssend, send, recv, local):
    spot = geo.bind()
    wire = Wire(send, recv)
    size = geo.tensor
    rows = x_ref.shape[0]
    wrows = aw_ref.shape[1]
    mrows = up_ref.shape[0]
    heads = aw_ref.shape[2]

    def xslot(t):
        return xf.at[pl.ds(pl.multiple_of(t * rows, rows), rows)]

    def block(i):
        return part.at[pl.ds(pl.multiple_of(i * rows, rows), rows)]

    wspan = pl.ds(pl.multiple_of(spot.d * wrows, wrows), wrows)
    span = pl.ds(pl.multiple_of(spot.d * mrows, mrows), mrows)
    pairs = [
        (gain_ref, gain_in), (bias_ref, bias_in), (aw_ref, wsend.at[pl.ds(0, 3)]), (ow_ref, ow_in), (up_ref, full.at[0, spot.t, span]),
        (x_ref, xslot(spot.t)), (down_ref, down_in), (seg_ref, seg_row)]
    loads = fetch([pltpu.make_async_copy(src, dst, local.at[i]) for i, (src, dst) in enumerate(pairs)])
    greet(spot)
    weights = WeightGather(spot, wire, wrows, wf)
    lines = [LineGather(spot, wire, src, lambda t, k=k: full.at[k, t, span]) for k, src in enumerate((up_ref, dsend))]
    ups, downs = [WeightGather(spot, wire, mrows, full.at[k]) for k in range(2)]
    xs = LineGather(spot, wire, x_ref, xslot)
    small = wire.take(geo.dp - 1)
    lines[0].start()
    settle(loads[0:4])
    ssend[0:2, :] = gain_in[...].astype(F32)
    ssend[2:12, :] = bias_in[...].astype(F32)
    for step in range(1, geo.dp):
        wire.start(small + step - 1, ssend, sf.at[spot.d], spot.at_d(ring_next(spot.d, step, geo.dp)))
    wsend[3] = ow_in[...].T
    wf[:, wspan] = wsend[...]
    weights.first()
    sf[spot.d] = ssend[...]
    loads[6].wait()
    dsend[...] = down_in[...].T
    down_copy = pltpu.make_async_copy(dsend, full.at[1, spot.t, span], local.at[8])
    down_copy.start()
    weights.second()
    lines[0].forward()
    xs.start()
    weights.third()
    loads[4].wait()
    lines[0].finish()
    ups.first()
    for step in range(1, geo.dp):
        source = ring_prev(spot.d, step, geo.dp)
        wire.landed(small + step - 1, sf.at[source], spot.at_d(source))
    piece = ssend.shape[1]
    for d in range(geo.dp):
        rows12[:, d * piece:(d + 1) * piece] = sf[d]
    loads[7].wait()
    seg_col[...] = jnp.broadcast_to(seg_row[...], (128, seg_row.shape[1])).T
    weights.fourth()
    loads[5].wait()
    column = pl.ds(pl.multiple_of(spot.t * heads, 128), heads)

    def project(t):
        def norm(r):
            n1[r] = layer_norm(xf[r].astype(F32), rows12[0:1, :], rows12[2:3, :]).astype(BF)

        first = pl.multiple_of(t * rows, rows)
        loop_rows(rows, min(64, rows), norm, first)
        r = pl.ds(first, rows)
        normed = n1[r]
        qkv[0, r] = ((nn(normed, wf[0]) + rows12[3:4, column]).astype(BF).astype(F32) * HD ** -0.5).astype(BF)
        qkv[1, r] = nn(normed, wf[1]).astype(BF)
        qkv[2, r] = (nn(normed, wf[2]) + rows12[4:5, column]).astype(BF)

    project(spot.t)
    ups.second()
    xs.forward()
    xs.finish()
    lines[1].start()

    def other(step, carry):
        project(ring_next(spot.t, step, size))
        return carry

    lax.fori_loop(1, size, other, 0)
    ups.third()
    scatter = LineScatter(spot, wire, block, lambda k: land.at[k], lambda dst, src: add_tiled(dst, src, 64))
    qrows = min(256, SEQ)
    for start in range(0, SEQ, qrows):
        block_bias(seg_col, seg_row, bias, start, qrows, start + qrows)
        attend_block(qkv, bias, att, lse, start, qrows)
        part[start:start + qrows, :] = nt(att[start:start + qrows, :], wf[3]).astype(BF)
        if scatter.line:
            scatter.start_block(start // rows)
        if start == 0:
            lines[1].forward()
    if not scatter.line:
        scatter.start()
    down_copy.wait()
    lines[1].finish()
    downs.first()
    for start in range(0, SEQ, qrows):
        n1t[:, start:start + qrows] = n1[start:start + qrows, :].T
    scatter.forward()
    downs.second()
    mine = block(spot.t)

    def set_total(r):
        total[r] = mine[r].astype(F32)

    loop_rows(rows, min(64, rows), set_total)
    scatter.finish(lambda ref: add_tiled(total, ref, 64))
    ups.fourth()
    downs.third()
    downs.fourth()
    wire.drain()


def mk1(geo, x, aw, ow, up, down, gains, biases, seg_row):
    rows, width = x.shape
    wrows, heads = aw.shape[1:]
    size = geo.tensor
    sems = 24 + 4 * size + geo.dp + 3 * gather_sems(geo)
    seq = size * rows
    return pl.pallas_call(
        functools.partial(mk1_body, geo),
        out_shape=(
            jax.ShapeDtypeStruct((width, seq), BF),
            jax.ShapeDtypeStruct((3, seq, heads), BF),
            jax.ShapeDtypeStruct((seq, heads), BF),
            jax.ShapeDtypeStruct((seq, 128), F32),
            jax.ShapeDtypeStruct((4, width, heads), BF),
            jax.ShapeDtypeStruct((12, width), F32),
            jax.ShapeDtypeStruct((rows, width), F32),
            jax.ShapeDtypeStruct((seq, width), BF),
            jax.ShapeDtypeStruct((seq, 128), jnp.int32),
            jax.ShapeDtypeStruct((2, size, width, up.shape[1]), BF),
        ),
        in_specs=[ANY] * 8,
        out_specs=(VM,) * 9 + (ANY,),
        scratch_shapes=[
            pltpu.VMEM((geo.dp, 12, wrows), F32),
            pltpu.VMEM((seq, width), BF),
            pltpu.VMEM((seq, width), BF),
            pltpu.VMEM((max(5, size - 1), rows, width), BF),
            pltpu.VMEM((min(256, SEQ), SEQ), F32),
            pltpu.VMEM((4, wrows, heads), BF),
            pltpu.VMEM(ow.shape, BF),
            pltpu.VMEM(down.shape, BF),
            pltpu.VMEM(up.shape, BF),
            pltpu.VMEM(gains.shape, BF),
            pltpu.VMEM(biases.shape, BF),
            pltpu.VMEM(seg_row.shape, jnp.int32),
            pltpu.VMEM((12, wrows), F32),
            pltpu.SemaphoreType.DMA((sems,)), pltpu.SemaphoreType.DMA((sems,)), pltpu.SemaphoreType.DMA((9,))],
        compiler_params=pltpu.CompilerParams(collective_id=1, has_side_effects=True, vmem_limit_bytes=56 * 2**20),
        name="mk1",
    )(x, aw, ow, up, down, gains, biases, seg_row)


GELU_C = 0.7978845608028654


def gelu_parts(a):
    square = a * a
    tanh = jnp.tanh(GELU_C * a * (1.0 + 0.044715 * square))
    half = 0.5 * (1.0 + tanh)
    slope = half + 0.5 * a * (1.0 - tanh * tanh) * (GELU_C * (1.0 + 3 * 0.044715 * square))
    return a * half, slope


def column_sum(values):
    return jnp.sum(values, axis=0, keepdims=True)


def mk2_body(geo, m_ref, cot_ref, n1t_ref, qkv_ref, att_ref, lse_ref, wf_ref, rows_ref, sum_ref, xf_ref, segc_ref, segr_ref,
             out, igrad, awg, owg, upg, downg, gaing, biasg,
             mid, cot, rows12, n1t, qkv, att, lse, wf, xf, seg_col, seg_row, gaf, sums, spart, sland, stot, tland,
             held, one_a, one_b, two_a, two_b, wheld, wone_a, wone_b, wtwo_a, wtwo_b, mland, land, gtot,
             send, recv, local, msem):
    spot = geo.bind()
    wire = Wire(send, recv)
    size = geo.tensor
    rows, width = out.shape
    seq = size * rows
    heads = att.shape[1]
    unit = m_ref.shape[3]
    mrows = upg.shape[0]
    wrows = awg.shape[1]
    a_size, b_size = geo.a_size, geo.b_size
    ab = a_size * b_size
    chunk = min(512, unit)
    per = unit // chunk
    count = size * per
    tail = min(64, rows)
    tile = min(64, mrows)
    sibling = spot.at_d(spot.rank(spot.b, spot.a, 1 - spot.c))
    pairs = [
        (sum_ref, mid), (xf_ref, xf), (rows_ref, rows12), (cot_ref, cot), (wf_ref, wf), (qkv_ref, qkv), (att_ref, att), (lse_ref, lse),
        (n1t_ref, n1t), (segc_ref, seg_col), (segr_ref, seg_row)]
    loads = fetch([pltpu.make_async_copy(src, dst, local.at[i]) for i, (src, dst) in enumerate(pairs)])
    greet(spot)

    def slot(t):
        return gaf.at[pl.ds(pl.multiple_of(t * rows, rows), rows)]

    def own_rows(r, n):
        return pl.ds(pl.multiple_of(spot.t * rows + r.start, n), n)

    gather = LineGather(spot, wire, slot(spot.t), slot)
    zero = [wire.take(size) for _ in range(2)]
    wzero = wire.take(ab)
    scatters = [WeightScatter(spot, wire, *(buf.at[k] for buf in (held, one_a, one_b, two_a, two_b))) for k in range(2)]
    wscatter = WeightScatter(spot, wire, *(buf.at[0] for buf in (wheld, wone_a, wone_b, wtwo_a, wtwo_b)))

    def line_of(k):
        here = held.at[k, spot.b, spot.a]
        return LineScatter(spot, wire, lambda t: here.at[t], lambda j: mland.at[k, j], lambda dst, src: add_tiled(dst, src, tile))

    lines = [line_of(k) for k in range(2)]
    small = wire.take(geo.dp - 1)
    last = wire.take(size - 1)
    sums[...] = jnp.zeros_like(sums)

    def mlp(mbuf, hmid, da, n2, gm, turned, n2t, gmt, snd, dn2):
        def mload(j, s):
            return pltpu.make_async_copy(
                m_ref.at[:, lax.div(j, per), :, pl.ds(pl.multiple_of(lax.rem(j, per) * chunk, chunk), chunk)], mbuf.at[s], msem.at[s])

        mload(0, 0).start()
        settle(loads[0:4])

        def norm(r):
            value = xf[own_rows(r, tail)].astype(F32) + (mid[r] + rows12[5:6, :])
            mid[r] = value
            n2[r] = layer_norm(value, rows12[1:2, :], rows12[6:7, :]).astype(BF)
            branch = cot[r].astype(BF)
            gm[r] = branch
            sums[7:8, :] += column_sum(branch.astype(F32))

        loop_rows(rows, tail, norm)

        def turn(value, dst):
            turned[...] = value[...].T
            for i in range(ab):
                for other in range(2):
                    core = lax.rem(spot.c + other, 2)
                    dst[other, i * mrows:(i + 1) * mrows, :] = turned[pl.ds(pl.multiple_of((i * 2 + core) * mrows, mrows), mrows), :]

        turn(gm, gmt)
        dn2[...] = jnp.zeros_like(dn2)
        out[...] = jnp.zeros_like(out)

        def cols_of(j):
            return pl.ds(pl.multiple_of(j * chunk, chunk), chunk)

        def sub_of(j):
            return pl.ds(pl.multiple_of(lax.rem(j, per) * chunk, chunk), chunk)

        def sending(k, t):
            return wire.copy(zero[k] + t, snd.at[:, :, t], held.at[k, :, :, t], sibling)

        def give(k, j, left, right):
            product = nn(left[1], right).astype(BF)
            t = lax.div(j, per)
            for i in range(ab):
                snd[i // a_size, i % a_size, t, :, sub_of(j)] = product[i * mrows:(i + 1) * mrows, :]

            @pl.when(lax.rem(j, per) == per - 1)
            def _():
                sending(k, t).start()

        def keep(k, j, left, right):
            t = lax.div(j, per)

            @pl.when(lax.rem(j, per) == 0)
            def _():
                sending(k, t).wait_recv()

            product = nn(left[0], right)
            for i in range(ab):
                b, a = i // a_size, i % a_size
                held[k, b, a, t, :, sub_of(j)] = (
                    held[k, b, a, t, :, sub_of(j)].astype(F32) + product[i * mrows:(i + 1) * mrows, :]).astype(BF)

        def one(j, carry):
            s = lax.rem(j, 2)
            mload(j, s).wait()

            @pl.when(j + 1 < count)
            def _():
                mload(j + 1, 1 - s).start()

            cols = cols_of(j)
            row = pl.ds(8 + lax.div(j * chunk, width), 1)
            bcols = pl.ds(pl.multiple_of(lax.rem(j * chunk, width), chunk), chunk)
            a = nn(n2[...], mbuf[s, 0]) + rows12[row, bcols]
            value, slope = gelu_parts(a)
            active = value.astype(BF)
            hmid[:, cols] = active
            grad = (nn(gm[...], mbuf[s, 1]) * slope).astype(BF)
            da[:, cols] = grad
            sums[row, bcols] = column_sum(grad.astype(F32))
            give(1, j, gmt, active)
            dn2[...] += nt(grad, mbuf[s, 0])
            out[...] += nt(active, mbuf[s, 1])
            return carry

        lax.fori_loop(0, count, one, 0)

        def back(r):
            value = mid[r]
            unit_two, scale_two = norm_stats(value)
            grad = dn2[r]
            total = cot[r] + norm_back(grad, unit_two, scale_two, rows12[1:2, :])
            cot[r] = total
            branch = total.astype(BF)
            gaf[own_rows(r, tail)] = branch
            sums[1:2, :] += column_sum(grad * unit_two)
            sums[6:7, :] += column_sum(grad)
            sums[5:6, :] += column_sum(branch.astype(F32))
            out[r] = value + (out[r] + rows12[7:8, :])

        loop_rows(rows, tail, back)
        gather.start()

        def keep_down(j, carry):
            keep(1, j, gmt, hmid[:, cols_of(j)])
            return carry

        lax.fori_loop(0, count, keep_down, 0)
        scatters[1].first()
        turn(n2, n2t)
        for t in range(size):
            sending(1, t).wait_send()

        def give_up(j, carry):
            give(0, j, n2t, da[:, cols_of(j)])
            return carry

        lax.fori_loop(0, count, give_up, 0)
        gather.forward()

        def keep_up(j, carry):
            keep(0, j, n2t, da[:, cols_of(j)])
            return carry

        lax.fori_loop(0, count, keep_up, 0)
        scatters[0].first()
        for t in range(size):
            sending(0, t).wait_send()

    ff = size * unit
    pl.run_scoped(
        mlp,
        pltpu.VMEM((2, 2, width, chunk), BF),
        pltpu.VMEM((rows, ff), BF),
        pltpu.VMEM((rows, ff), BF),
        pltpu.VMEM((rows, width), BF),
        pltpu.VMEM((rows, width), BF),
        pltpu.VMEM((width, rows), BF),
        pltpu.VMEM((2, ab * mrows, rows), BF),
        pltpu.VMEM((2, ab * mrows, rows), BF),
        pltpu.VMEM((b_size, a_size, size, mrows, unit), BF),
        pltpu.VMEM((rows, width), F32),
    )
    settle(loads[4:])
    scatters[1].second()
    gather.finish()

    def attention(gat, do, dqkv, dk, dv, bias, wg, part):
        def block(i):
            return part.at[pl.ds(pl.multiple_of(i * rows, rows), rows)]

        scatter = LineScatter(spot, wire, block, lambda k: land.at[k], lambda dst, src: add_tiled(dst, src, tail))
        column = pl.ds(pl.multiple_of(spot.t * heads, 128), heads)
        dk[...] = jnp.zeros_like(dk)
        dv[...] = jnp.zeros_like(dv)
        qrows = min(256, SEQ)
        half = width // 2
        for start in range(SEQ - qrows, -1, -qrows):
            end = start + qrows
            do[start:end, :] = nn(gaf[start:end, :], wf[3]).astype(BF)
            block_bias(seg_col, seg_row, bias, start, qrows, end)
            attend_block_back(qkv, bias, lse, do, dqkv.at[0], dk, dv, start, qrows)
            dqkv[1, start:end, :] = dk[start:end, :].astype(BF)
            dqkv[2, start:end, :] = dv[start:end, :].astype(BF)
            for j in (0, 2):
                sums[3 + j // 2:4 + j // 2, column] += column_sum(dqkv[j, start:end, :].astype(F32))
            x = xf[start:end, :].astype(F32)
            center = x - jnp.mean(x, axis=-1, keepdims=True)
            unit_one = center * lax.rsqrt(jnp.mean(center * center, axis=-1, keepdims=True) + EPSILON)
            for first in range(0, width, half):
                cols = slice(first, first + half)
                term = sum(nt(dqkv[j, start:end, :], wf[j, cols, :]) for j in range(3))
                sums[0:1, cols] += column_sum(term * unit_one[:, cols])
                sums[2:3, cols] += column_sum(term)
                part[start:end, cols] = term.astype(BF)
            if scatter.line:
                scatter.start_block(start // rows)
            gat[:, start:end] = gaf[start:end, :].T
            if start == SEQ - 2 * qrows:
                scatters[1].third()
                lines[1].start()
        if not scatter.line:
            scatter.start()
        piece = spart.shape[2]
        for d in range(geo.dp):
            spart[d] = sums[:, d * piece:(d + 1) * piece]
        for step in range(1, geo.dp):
            to = ring_next(spot.d, step, geo.dp)
            wire.start(small + step - 1, spart.at[to], sland.at[step - 1], spot.at_d(to))
        stot[...] = spart[spot.d]
        scatter.forward()

        def wgrad(r):
            for j in range(3):
                wg[j, r] = nn(n1t[r], dqkv[j]).astype(BF)
            wg[3, r] = nn(gat[r], att[...]).astype(BF)

        loop_rows(width, min(256, width), wgrad)

        def wspan(i, core):
            return pl.ds(pl.multiple_of((i * 2 + core) * wrows, wrows), wrows)

        for i in range(ab):
            wire.start(wzero + i, wg.at[:, wspan(i, 1 - spot.c)], wheld.at[0, i // a_size, i % a_size], sibling)
        scatters[0].second()
        for i in range(ab):
            here = wheld.at[0, i // a_size, i % a_size]
            wire.landed(wzero + i, here, sibling)
            wscatter.add(here, wg.at[:, wspan(i, spot.c)])
        wscatter.first()
        lines[1].forward()
        for step in range(1, geo.dp):
            wire.landed(small + step - 1, sland.at[step - 1], spot.at_d(ring_prev(spot.d, step, geo.dp)))
            stot[...] += sland[step - 1]
        for step in range(1, size):
            wire.start(last + step - 1, stot, tland.at[step - 1], spot.at_t(ring_next(spot.t, step, size)))
        scatters[0].third()
        lines[0].start()
        wscatter.second()
        mine = block(spot.t)

        def set_total(r):
            igrad[r] = mine[r].astype(F32)

        loop_rows(rows, tail, set_total)
        scatter.finish(lambda ref: add_tiled(igrad, ref, tail))

        def back(r):
            unit_one, scale_one = norm_stats(xf[own_rows(r, tail)].astype(F32))
            igrad[r] = cot[r] + norm_back(igrad[r], unit_one, scale_one, rows12[0:1, :])

        loop_rows(rows, tail, back)

        def line_end(k, total):
            here = held.at[k, spot.b, spot.a, spot.t]

            def set_row(r):
                total[r] = here[r].astype(F32)

            loop_rows(mrows, tile, set_row)
            lines[k].finish(lambda ref: add_tiled(total, ref, tile))

        line_end(1, gtot)
        downg[...] = gtot[...].T
        lines[0].forward()
        wscatter.third()
        sums_w = wheld.at[0, spot.b, spot.a]
        for j in range(3):
            awg[j] = sums_w[j].astype(F32)
        owg[...] = sums_w[3].astype(F32).T
        for step in range(1, size):
            wire.landed(last + step - 1, tland.at[step - 1], spot.at_t(ring_prev(spot.t, step, size)))
        total = stot[...]
        for step in range(1, size):
            total = total + tland[step - 1]
        gaing[...] = total[0:2, :]
        biasg[...] = total[2:12, :]
        line_end(0, upg)
        wire.drain()

    pl.run_scoped(
        attention,
        pltpu.VMEM((width, seq), BF),
        pltpu.VMEM((seq, heads), BF),
        pltpu.VMEM((3, seq, heads), BF),
        pltpu.VMEM((seq, heads), F32),
        pltpu.VMEM((seq, heads), F32),
        pltpu.VMEM((min(256, SEQ), SEQ), F32),
        pltpu.VMEM((4, width, heads), BF),
        pltpu.VMEM((seq, width), BF),
    )


def mk2(geo, m_full, cot, n1t, qkv, att, lse, wf, rows12, attn_sum, xf, seg_col, seg_row):
    rows, width = cot.shape
    seq, heads = att.shape
    size = geo.tensor
    unit = m_full.shape[3]
    mrows = width // geo.dp
    wrows = width // geo.dp
    sems = 30 + 8 * size + geo.a_size * geo.b_size + 3 * scatter_sems(geo) + geo.dp
    like = lambda x: pltpu.VMEM(x.shape, x.dtype)
    return pl.pallas_call(
        functools.partial(mk2_body, geo),
        out_shape=(
            jax.ShapeDtypeStruct((rows, width), F32),
            jax.ShapeDtypeStruct((rows, width), F32),
            jax.ShapeDtypeStruct((3, wrows, heads), F32),
            jax.ShapeDtypeStruct((heads, wrows), F32),
            jax.ShapeDtypeStruct((mrows, unit), F32),
            jax.ShapeDtypeStruct((unit, mrows), F32),
            jax.ShapeDtypeStruct((2, wrows), F32),
            jax.ShapeDtypeStruct((10, wrows), F32),
        ),
        in_specs=[ANY] * 12,
        out_specs=(VM,) * 8,
        scratch_shapes=[
            like(attn_sum), like(cot), like(rows12), like(n1t), like(qkv), like(att), like(lse), like(wf), like(xf), like(seg_col),
            like(seg_row),
            pltpu.VMEM((seq, width), BF),
            pltpu.VMEM((12, width), F32),
            pltpu.VMEM((geo.dp, 12, wrows), F32),
            pltpu.VMEM((geo.dp - 1, 12, wrows), F32),
            pltpu.VMEM((12, wrows), F32),
            pltpu.VMEM((size - 1, 12, wrows), F32),
            *scatter_bufs(geo, 2, size, mrows, unit),
            *scatter_bufs(geo, 1, 4, wrows, heads),
            pltpu.VMEM((2, max(5, size - 1), mrows, unit), BF),
            pltpu.VMEM((max(5, size - 1), rows, width), BF),
            pltpu.VMEM((mrows, unit), F32),
            pltpu.SemaphoreType.DMA((sems,)), pltpu.SemaphoreType.DMA((sems,)), pltpu.SemaphoreType.DMA((11,)),
            pltpu.SemaphoreType.DMA((2,))],
        compiler_params=pltpu.CompilerParams(collective_id=2, has_side_effects=True, vmem_limit_bytes=60 * 2**20),
        name="mk2",
    )(m_full, cot, n1t, qkv, att, lse, wf, rows12, attn_sum, xf, seg_col, seg_row)


def per_device(geo, activations, segments, attn_weight, out_weight, up_weight, down_weight, norm_gains, bias_rows, cotangent):
    normed_t, project, attended, log_total, w_full, rows12, attn_sum, x_full, seg_col, m_full = mk1(
        geo, activations, attn_weight[0], out_weight[0], up_weight[0], down_weight[0], norm_gains[0], bias_rows[0], segments[None, :])
    outs = mk2(
        geo, m_full, cotangent, normed_t, project, attended, log_total, w_full, rows12, attn_sum, x_full, seg_col, segments[None, :])
    return outs[:2] + tuple(part[None] for part in outs[2:])


def solution(mesh):
    geo = Geometry(mesh.shape["dp"], mesh.shape["tensor"])
    return jax.shard_map(
        functools.partial(per_device, geo),
        mesh=mesh,
        in_specs=(
            P(("dp", "tensor"), None),
            P("dp"),
            P(None, None, "dp", "tensor"),
            P(None, "tensor", "dp"),
            P(None, "dp", "tensor"),
            P(None, "tensor", "dp"),
            P(None, None, "dp"),
            P(None, None, "dp"),
            P(("dp", "tensor"), None),
        ),
        out_specs=(
            P(("dp", "tensor"), None),
            P(("dp", "tensor"), None),
            P(None, None, "dp", "tensor"),
            P(None, "tensor", "dp"),
            P(None, "dp", "tensor"),
            P(None, "tensor", "dp"),
            P(None, None, "dp"),
            P(None, None, "dp"),
        ),
        check_vma=False,
    )
```

```python
import functools

import jax
import jax.numpy as jnp
from jax import lax
from jax.experimental import pallas as pl
from jax.experimental.pallas import tpu as pltpu
from jax.sharding import PartitionSpec as P

HD = 64
EPSILON = 1e-05
MASKED = -1e30
MESH_ID = pl.DeviceIdType.MESH
BF = jnp.bfloat16
F32 = jnp.float32
ANY = pl.BlockSpec(memory_space=pl.ANY)
VM = pl.BlockSpec(memory_space=pltpu.VMEM)


def layer_norm(values, gain_row, shift_row):
    center = values - jnp.mean(values, axis=-1, keepdims=True)
    spread = jnp.mean(center * center, axis=-1, keepdims=True)
    return center * lax.rsqrt(spread + EPSILON) * gain_row + shift_row


def norm_stats(values):
    center = values - jnp.mean(values, axis=-1, keepdims=True)
    spread = jnp.mean(center * center, axis=-1, keepdims=True)
    scale = lax.rsqrt(spread + EPSILON)
    return center * scale, scale


def norm_back(grad, unit, scale, gain_row):
    u = grad * gain_row
    mean_u = jnp.mean(u, axis=-1, keepdims=True)
    mean_ux = jnp.mean(u * unit, axis=-1, keepdims=True)
    return scale * (u - mean_u - unit * mean_ux)


def gelu_tanh(values):
    return jax.nn.gelu(values, approximate=True)


class Geometry:
    def __init__(self, dp, tensor):
        self.dp, self.tensor = dp, tensor
        self.c_size = 2
        rest = dp // 2
        self.a_size = 1
        while self.a_size * self.a_size < rest:
            self.a_size *= 2
        self.b_size = rest // self.a_size
        assert self.a_size * self.b_size * 2 == dp

    def bind(self):
        spot = Spot()
        spot.geo = self
        spot.d = lax.axis_index("dp")
        spot.t = lax.axis_index("tensor")
        spot.c = lax.rem(spot.d, 2)
        half = lax.div(spot.d, 2)
        spot.a = lax.rem(half, self.a_size)
        spot.b = lax.div(half, self.a_size)
        return spot


class Spot:
    def rank(self, b, a, c):
        return (b * self.geo.a_size + a) * 2 + c

    def at_t(self, t):
        return (self.d, t)

    def at_d(self, d):
        return (d, self.t)


def ring_next(rank, step, size):
    return lax.rem(rank + step, size)


def ring_prev(rank, step, size):
    return lax.rem(rank + size - step, size)


class Wire:
    def __init__(self, send, recv):
        self.send_sems, self.recv_sems = send, recv
        self.count = 0
        self.pending = []

    def take(self, n):
        first = self.count
        self.count += n
        return first

    def copy(self, i, src, dst, device):
        return pltpu.make_async_remote_copy(
            src_ref=src, dst_ref=dst, send_sem=self.send_sems.at[i], recv_sem=self.recv_sems.at[i],
            device_id=device, device_id_type=MESH_ID)

    def plan(self, i, src, dst, device, when=None):
        return self.copy(i, src, dst, device), when

    def go(self, planned):
        copy, when = planned
        if when is None:
            copy.start()
        else:
            pl.when(when)(copy.start)
        if not any(other is planned for other in self.pending):
            self.pending.append(planned)

    def start(self, i, src, dst, device, when=None):
        self.go(self.plan(i, src, dst, device, when))

    def landed(self, i, dst, device, when=None):
        copy = self.copy(i, dst, dst, device)
        if when is None:
            copy.wait_recv()
        else:
            pl.when(when)(copy.wait_recv)

    def sent(self, plans):
        for planned in plans:
            copy, when = planned
            self.pending = [other for other in self.pending if other is not planned]
            if when is None:
                copy.wait_send()
            else:
                pl.when(when)(copy.wait_send)

    def drain(self):
        for copy, when in self.pending:
            if when is None:
                copy.wait_send()
            else:
                pl.when(when)(copy.wait_send)
        self.pending = []


def greet(spot):
    geo = spot.geo
    barrier = pltpu.get_barrier_semaphore()
    total = 0
    for step in range(1, geo.tensor):
        pl.semaphore_signal(barrier, inc=1, device_id=spot.at_t(ring_next(spot.t, step, geo.tensor)), device_id_type=MESH_ID)
        total += 1
    for step in range(1, geo.dp):
        pl.semaphore_signal(barrier, inc=1, device_id=spot.at_d(ring_next(spot.d, step, geo.dp)), device_id_type=MESH_ID)
        total += 1
    return lambda: pl.semaphore_wait(barrier, total)


def halves(ref, count, part):
    rows = ref.shape[-2] // count
    return ref.at[(slice(None),) * (len(ref.shape) - 2) + (pl.ds(part * rows, rows),)]


class LineGather:
    def __init__(self, spot, wire, src, slot, parts=2):
        self.spot, self.wire, self.src, self.slot, self.parts = spot, wire, src, slot, parts
        self.size = size = spot.geo.tensor
        self.base = [wire.take((size - 1) * parts) for _ in range(2)]
        t = spot.t
        self.sends = {}
        for k in range(size - 1):
            for part in range(parts):
                for side in range(2):
                    self.sends[k, part, side] = self.plan(k, part, side)

    def place(self, k, side):
        t = self.spot.t
        origin = t - k if side == 0 else t + k
        there = (origin >= 0) & (origin < self.size)
        onward = t + 1 if side == 0 else t - 1
        return origin, there, t - 1 if side == 0 else t + 1, onward, there & (onward >= 0) & (onward < self.size)

    def plan(self, k, part, side):
        origin, _, _, onward, going = self.place(k, side)
        piece = halves(self.slot(origin), self.parts, part)
        first = isinstance(k, int) and k == 0
        src = halves(self.src, self.parts, part) if first else piece
        return self.wire.plan(self.base[side] + k * self.parts + part, src, piece, self.spot.at_t(onward), when=going)

    def start(self):
        for part in range(self.parts):
            for side in range(2):
                self.wire.go(self.sends[0, part, side])

    def step(self, k):
        for part in range(self.parts):
            for side in range(2):
                origin, there, near, _, _ = self.place(k, side)
                piece = halves(self.slot(origin), self.parts, part)
                self.wire.landed(self.base[side] + (k - 1) * self.parts + part, piece, self.spot.at_t(near), when=there)
                if not isinstance(k, int):
                    copy, going = self.plan(k, part, side)
                    pl.when(going & (k < self.size - 1))(copy.start)
                elif k < self.size - 1:
                    self.wire.go(self.sends[k, part, side])

    def owe(self):
        for (k, part, side), planned in self.sends.items():
            if k > 0:
                self.wire.pending.append(planned)


class LineScatter:
    def __init__(self, spot, wire, part, land, add, rising=False, parts=2):
        self.spot, self.wire, self.part, self.land, self.add, self.parts = spot, wire, part, land, add, parts
        self.size = spot.geo.tensor
        base = [wire.take(self.size * parts) for _ in range(2)]
        t, end = spot.t, self.size - 1
        self.starts, self.hops = {}, {}
        for h in range(parts):
            for j in range(self.size):
                if j > 0:
                    self.starts[0, j, h] = wire.plan(
                        base[0] + j * parts + h, halves(part(j), parts, h), halves(land(0, j), parts, h), spot.at_t(1), when=t == 0)
                if j < end:
                    self.starts[1, j, h] = wire.plan(
                        base[1] + j * parts + h, halves(part(j), parts, h), halves(land(1, j), parts, h), spot.at_t(end - 1), when=t == end)
        self.events = []
        if rising:
            for e in range(1, 2 * end):
                self.events.append((10 * e, 0, e + 1 - t, (t >= 1) & (e + 1 - t >= t) & (e + 1 - t <= end)))
        for s in range(1, self.size):
            if not rising:
                self.events.append((10 * s, 0, end - s + t, (t >= 1) & (s >= t)))
            self.events.append((10 * s + (15 if rising else 0), 1, s - (end - t), (end - t >= 1) & (s >= end - t)))
        self.events.sort(key=lambda event: event[0])
        self.hops = []
        for _, side, j, here in self.events:
            near = spot.at_t(t - 1 if side == 0 else t + 1)
            away = spot.at_t(t + 1 if side == 0 else t - 1)
            for h in range(parts):
                held = halves(land(side, j), parts, h)
                i = base[side] + j * parts + h
                self.hops.append((here & (j == t), here & (j != t), j, h, held, wire.copy(i, held, held, near),
                                  wire.plan(i, held, held, away, when=here & (j != t))))

    def start_block(self, j):
        for side in range(2):
            for h in range(self.parts):
                if (side, j, h) in self.starts:
                    self.wire.go(self.starts[side, j, h])

    def start(self):
        for n in range(self.size):
            for side, j in ((0, self.size - 1 - n), (1, n)):
                for h in range(self.parts):
                    if (side, j, h) in self.starts:
                        self.wire.go(self.starts[side, j, h])

    def count(self):
        return len(self.hops)

    def step(self, first, last, total):
        for final, passing, j, h, held, landing, onward in self.hops[first:last]:
            @pl.when(final)
            def _():
                landing.wait_recv()
                total(held, h)

            @pl.when(passing)
            def _():
                landing.wait_recv()
                self.add(held, halves(self.part(j), self.parts, h))

            self.wire.go(onward)

    def plans(self):
        return list(self.starts.values()) + [hop[-1] for hop in self.hops]


def add_tiled(dst, src, tile):
    def step(i, carry):
        rows = pl.ds(pl.multiple_of(i * tile, tile), tile)
        dst[rows] = (dst[rows].astype(F32) + src[rows].astype(F32)).astype(dst.dtype)
        return carry

    lax.fori_loop(0, dst.shape[0] // tile, step, 0)


class WeightGather:
    def __init__(self, spot, wire, rows, full):
        geo = spot.geo
        self.spot, self.wire, self.full, self.rows = spot, wire, full, rows
        self.slots = full.shape[0]
        self.half = self.slots // 2
        self.one_a = wire.take(geo.a_size - 1)
        self.one_b = wire.take(geo.b_size - 1)
        self.two_a = wire.take((geo.b_size - 1) * geo.a_size)
        self.two_b = wire.take((geo.a_size - 1) * geo.b_size)
        self.last = wire.take(2 * geo.a_size * geo.b_size)
        self.plan_shares()
        self.plan_hops()

    def span(self, d):
        return pl.ds(pl.multiple_of(d * self.rows, self.rows), self.rows)

    def low(self, d):
        return self.full.at[pl.ds(0, self.half), self.span(d)]

    def high(self, d):
        return self.full.at[pl.ds(self.half, self.slots - self.half), self.span(d)]

    def plan_shares(self):
        spot, geo = self.spot, self.spot.geo
        self.shares = {}
        for j in range(geo.b_size):
            for i in range(geo.a_size):
                held = spot.rank(ring_prev(spot.b, j, geo.b_size), ring_prev(spot.a, i, geo.a_size), spot.c)
                sibling = spot.rank(spot.b, spot.a, 1 - spot.c)
                for part in range(2):
                    half = (self.low, self.high)[part](held)
                    self.shares[part, j, i] = self.wire.plan(
                        self.last + 2 * (j * geo.a_size + i) + part, half, half, spot.at_d(sibling))

    def share(self, part, j, i):
        self.wire.go(self.shares[part, j, i])

    def plan_hops(self):
        spot, geo, wire = self.spot, self.spot.geo, self.wire
        self.ones, self.twos_a, self.twos_b = [], {}, {}
        mine = spot.d
        for j in range(1, geo.a_size):
            to = spot.rank(spot.b, ring_next(spot.a, j, geo.a_size), spot.c)
            self.ones.append(wire.plan(self.one_a + j - 1, self.low(mine), self.low(mine), spot.at_d(to)))
        for j in range(1, geo.b_size):
            to = spot.rank(ring_next(spot.b, j, geo.b_size), spot.a, spot.c)
            self.ones.append(wire.plan(self.one_b + j - 1, self.high(mine), self.high(mine), spot.at_d(to)))
        for i in range(geo.a_size):
            held = spot.rank(spot.b, ring_prev(spot.a, i, geo.a_size), spot.c)
            for j in range(1, geo.b_size):
                to = spot.rank(ring_next(spot.b, j, geo.b_size), spot.a, spot.c)
                self.twos_a[i, j] = wire.plan(self.two_a + (j - 1) * geo.a_size + i, self.low(held), self.low(held), spot.at_d(to))
        for i in range(geo.b_size):
            held = spot.rank(ring_prev(spot.b, i, geo.b_size), spot.a, spot.c)
            for j in range(1, geo.a_size):
                to = spot.rank(spot.b, ring_next(spot.a, j, geo.a_size), spot.c)
                self.twos_b[i, j] = wire.plan(self.two_b + (j - 1) * geo.b_size + i, self.high(held), self.high(held), spot.at_d(to))

    def first(self):
        for planned in self.ones:
            self.wire.go(planned)
        self.share(0, 0, 0)
        self.share(1, 0, 0)

    def second(self):
        spot, geo = self.spot, self.spot.geo
        for i in range(geo.a_size):
            held = spot.rank(spot.b, ring_prev(spot.a, i, geo.a_size), spot.c)
            if i:
                self.wire.landed(self.one_a + i - 1, self.low(held), spot.at_d(held))
                self.share(0, 0, i)
            for j in range(1, geo.b_size):
                self.wire.go(self.twos_a[i, j])
        for i in range(geo.b_size):
            held = spot.rank(ring_prev(spot.b, i, geo.b_size), spot.a, spot.c)
            if i:
                self.wire.landed(self.one_b + i - 1, self.high(held), spot.at_d(held))
                self.share(1, i, 0)
            for j in range(1, geo.a_size):
                self.wire.go(self.twos_b[i, j])

    def third(self):
        spot, geo = self.spot, self.spot.geo
        for j in range(1, geo.b_size):
            for i in range(geo.a_size):
                held = spot.rank(ring_prev(spot.b, j, geo.b_size), ring_prev(spot.a, i, geo.a_size), spot.c)
                source = spot.rank(ring_prev(spot.b, j, geo.b_size), spot.a, spot.c)
                self.wire.landed(self.two_a + (j - 1) * geo.a_size + i, self.low(held), spot.at_d(source))
                self.share(0, j, i)
        for j in range(1, geo.a_size):
            for i in range(geo.b_size):
                held = spot.rank(ring_prev(spot.b, i, geo.b_size), ring_prev(spot.a, j, geo.a_size), spot.c)
                source = spot.rank(spot.b, ring_prev(spot.a, j, geo.a_size), spot.c)
                self.wire.landed(self.two_b + (j - 1) * geo.b_size + i, self.high(held), spot.at_d(source))
                self.share(1, i, j)

    def fourth(self):
        spot, geo = self.spot, self.spot.geo
        sibling = spot.rank(spot.b, spot.a, 1 - spot.c)
        for j in range(geo.b_size):
            for i in range(geo.a_size):
                held = spot.rank(ring_prev(spot.b, j, geo.b_size), ring_prev(spot.a, i, geo.a_size), 1 - spot.c)
                for part in range(2):
                    half = (self.low, self.high)[part](held)
                    self.wire.landed(self.last + 2 * (j * geo.a_size + i) + part, half, spot.at_d(sibling))


def gather_sems(geo):
    return geo.a_size + geo.b_size + 4 * geo.a_size * geo.b_size


class WeightScatter:
    def __init__(self, spot, wire, held, one_a, one_b, two_a, two_b):
        geo = spot.geo
        self.spot, self.wire, self.held = spot, wire, held
        self.one_a_buf, self.one_b_buf, self.two_a_buf, self.two_b_buf = one_a, one_b, two_a, two_b
        self.slots, self.rows = held.shape[2], held.shape[3]
        self.half = self.slots // 2
        self.one_a = wire.take(geo.a_size - 1)
        self.one_b = wire.take(geo.b_size - 1)
        self.two_a = wire.take(geo.b_size - 1)
        self.two_b = wire.take(geo.a_size - 1)
        low, high = pl.ds(0, self.half), pl.ds(self.half, self.half)
        self.sends = []
        for j in range(1, geo.a_size):
            a = ring_next(spot.a, j, geo.a_size)
            self.sends.append(wire.plan(self.one_a + j - 1, held.at[:, a, low], one_a.at[j - 1], spot.at_d(spot.rank(spot.b, a, spot.c))))
        for j in range(1, geo.b_size):
            b = ring_next(spot.b, j, geo.b_size)
            self.sends.append(wire.plan(self.one_b + j - 1, held.at[b, :, high], one_b.at[j - 1], spot.at_d(spot.rank(b, spot.a, spot.c))))
        self.later = []
        for j in range(1, geo.b_size):
            b = ring_next(spot.b, j, geo.b_size)
            self.later.append(wire.plan(self.two_a + j - 1, held.at[b, spot.a, low], two_a.at[j - 1], spot.at_d(spot.rank(b, spot.a, spot.c))))
        for j in range(1, geo.a_size):
            a = ring_next(spot.a, j, geo.a_size)
            self.later.append(wire.plan(self.two_b + j - 1, held.at[spot.b, a, high], two_b.at[j - 1], spot.at_d(spot.rank(spot.b, a, spot.c))))

    def add(self, dst, src):
        tile = min(64, self.rows)
        per = self.rows // tile

        def step(i, carry):
            rows = pl.ds(pl.multiple_of(lax.rem(i, per) * tile, tile), tile)
            j = lax.div(i, per)
            dst[j, rows] = (dst[j, rows].astype(F32) + src[j, rows].astype(F32)).astype(dst.dtype)
            return carry

        lax.fori_loop(0, dst.shape[0] * per, step, 0)

    def first(self):
        for planned in self.sends:
            self.wire.go(planned)

    def second(self):
        spot, geo = self.spot, self.spot.geo
        low, high = pl.ds(0, self.half), pl.ds(self.half, self.half)
        for j in range(1, geo.a_size):
            self.wire.landed(self.one_a + j - 1, self.one_a_buf.at[j - 1], spot.at_d(spot.rank(spot.b, ring_prev(spot.a, j, geo.a_size), spot.c)))
            for b in range(geo.b_size):
                self.add(self.held.at[b, spot.a, low], self.one_a_buf.at[j - 1, b])
        for j in range(1, geo.b_size):
            self.wire.landed(self.one_b + j - 1, self.one_b_buf.at[j - 1], spot.at_d(spot.rank(ring_prev(spot.b, j, geo.b_size), spot.a, spot.c)))
            for a in range(geo.a_size):
                self.add(self.held.at[spot.b, a, high], self.one_b_buf.at[j - 1, a])
        for planned in self.later:
            self.wire.go(planned)

    def third(self):
        spot, geo = self.spot, self.spot.geo
        low, high = pl.ds(0, self.half), pl.ds(self.half, self.half)
        for j in range(1, geo.b_size):
            self.wire.landed(self.two_a + j - 1, self.two_a_buf.at[j - 1], spot.at_d(spot.rank(ring_prev(spot.b, j, geo.b_size), spot.a, spot.c)))
            self.add(self.held.at[spot.b, spot.a, low], self.two_a_buf.at[j - 1])
        for j in range(1, geo.a_size):
            self.wire.landed(self.two_b + j - 1, self.two_b_buf.at[j - 1], spot.at_d(spot.rank(spot.b, ring_prev(spot.a, j, geo.a_size), spot.c)))
            self.add(self.held.at[spot.b, spot.a, high], self.two_b_buf.at[j - 1])


def scatter_sems(geo):
    return 2 * geo.a_size + 2 * geo.b_size


def scatter_bufs(geo, n, slots, rows, width):
    a, b, half = geo.a_size, geo.b_size, slots // 2
    return [
        pltpu.VMEM((n, b, a, slots, rows, width), BF),
        pltpu.VMEM((a - 1, b, half, rows, width), BF),
        pltpu.VMEM((b - 1, a, half, rows, width), BF),
        pltpu.VMEM((b - 1, half, rows, width), BF),
        pltpu.VMEM((a - 1, half, rows, width), BF),
    ]


def loop_rows(count, tile, body, start=0):
    def step(i, carry):
        body(pl.ds(pl.multiple_of(start + i * tile, tile), tile))
        return carry

    lax.fori_loop(0, count // tile, step, 0)


def fetch(copies):
    for copy in copies:
        copy.start()
    return copies


def settle(copies):
    for copy in copies:
        copy.wait()


PAIR = 2 * HD


def nt(x, w):
    return lax.dot_general(x, w, (((1,), (1,)), ((), ())), preferred_element_type=F32)


def nn(x, w):
    return lax.dot_general(x, w, (((1,), (0,)), ((), ())), preferred_element_type=F32)


def tn(x, w):
    return lax.dot_general(x, w, (((0,), (0,)), ((), ())), preferred_element_type=F32)


def block_bias(seg_col, seg_row, bias, start, rows, keys):
    query = seg_col[start:start + rows, 0:1]
    for first in range(0, keys, rows):
        key = seg_row[:, first:first + rows]
        seen = query == key
        if first + rows > start:
            q_pos = start + lax.broadcasted_iota(jnp.int32, (rows, rows), 0)
            k_pos = first + lax.broadcasted_iota(jnp.int32, (rows, rows), 1)
            seen = seen & (k_pos <= q_pos)
        bias[:, first:first + rows] = jnp.where(seen, 0.0, MASKED).astype(F32)


def one_head(pair, head):
    lane = lax.broadcasted_iota(jnp.int32, pair.shape, 1)
    return jnp.where((lane < HD) if head == 0 else (lane >= HD), pair, jnp.zeros_like(pair))


def attend_block(qkv, bias, att, lse, start, rows):
    keys = start + rows
    width = qkv.shape[2]
    stat_lane = lax.broadcasted_iota(jnp.int32, (rows, 128), 1)
    stats = jnp.zeros((rows, 128), F32)
    for p in range(width // PAIR):
        lanes = slice(p * PAIR, (p + 1) * PAIR)
        query = qkv[0, start:keys, lanes]
        outs = []
        for head in range(2):
            s = nt(one_head(query, head), qkv[1, 0:keys, lanes]) + bias[:, 0:keys]
            top = jnp.max(s, axis=1, keepdims=True)
            e = jnp.exp(s - top)
            total = jnp.sum(e, axis=1, keepdims=True)
            prob = (e * (1.0 / total)).astype(BF)
            outs.append(nn(prob, qkv[2, 0:keys, lanes]))
            stats = jnp.where(stat_lane == 2 * p + head, top + jnp.log(total), stats)
        lane = lax.broadcasted_iota(jnp.int32, outs[0].shape, 1)
        att[start:keys, lanes] = jnp.where(lane < HD, outs[0], outs[1]).astype(BF)
    lse[start:keys, :] = stats


def attend_block_back(qkv, bias, lse, do, dq, dk, dv, start, rows):
    keys = start + rows
    width = qkv.shape[2]
    stat_lane = lax.broadcasted_iota(jnp.int32, (rows, 128), 1)
    stats = lse[start:keys, :]
    for p in range(width // PAIR):
        lanes = slice(p * PAIR, (p + 1) * PAIR)
        query = qkv[0, start:keys, lanes]
        grad = do[start:keys, lanes]
        dqs, dks, dvs = [], [], []
        for head in range(2):
            level = jnp.sum(jnp.where(stat_lane == 2 * p + head, stats, 0.0), axis=1, keepdims=True)
            s = nt(one_head(query, head), qkv[1, 0:keys, lanes]) + bias[:, 0:keys]
            prob = jnp.exp(s - level)
            d_prob = nt(one_head(grad, head), qkv[2, 0:keys, lanes])
            mixed = prob * d_prob
            ds = (mixed - prob * jnp.sum(mixed, axis=1, keepdims=True)).astype(BF)
            dqs.append(nn(ds, qkv[1, 0:keys, lanes]))
            dks.append(tn(ds, query))
            dvs.append(tn(prob.astype(BF), grad))
        lane = lax.broadcasted_iota(jnp.int32, dqs[0].shape, 1)
        dq[start:keys, lanes] = (jnp.where(lane < HD, dqs[0], dqs[1]) * (HD ** -0.5)).astype(dq.dtype)
        lane = lax.broadcasted_iota(jnp.int32, dks[0].shape, 1)
        dk[0:keys, lanes] += jnp.where(lane < HD, dks[0], dks[1])
        dv[0:keys, lanes] += jnp.where(lane < HD, dvs[0], dvs[1])


GELU_C = 0.7978845608028654


def gelu_parts(a):
    square = a * a
    tanh = jnp.tanh(GELU_C * a * (1.0 + 0.044715 * square))
    half = 0.5 * (1.0 + tanh)
    slope = half + 0.5 * a * (1.0 - tanh * tanh) * (GELU_C * (1.0 + 3 * 0.044715 * square))
    return a * half, slope


def column_sum(values):
    return jnp.sum(values, axis=0, keepdims=True)


def block_body(geo, x_ref, aw_ref, ow_ref, up_ref, down_ref, gain_ref, bias_ref, seg_ref, cot_ref,
               full, out_ref, igrad_ref, awg_ref, owg_ref, upg_ref, downg_ref, gaing_ref, biasg_ref,
               xf, n1, n1t, qkv, att, lse, wf, part, land, bias, mid, cot, gaf, rows12, seg_col, seg_row,
               sf, wsend, ow_in, down_in, msend, gain_in, bias_in, ssend,
               sums, spart, sland, stot, tland,
               held, one_a, one_b, two_a, two_b, wheld, wone_a, wone_b, wtwo_a, wtwo_b, mland,
               gtot, downg, awg, owg, gaing, biasg,
               send, recv, local, msem, osem):
    spot = geo.bind()
    wire = Wire(send, recv)
    size = geo.tensor
    rows, width = x_ref.shape
    seq = size * rows
    wrows, heads = aw_ref.shape[1:]
    mrows, unit = up_ref.shape
    a_size, b_size = geo.a_size, geo.b_size
    ab = a_size * b_size
    chunk = min(512, unit)
    per = unit // chunk
    pieces = msem.shape[1]
    count = size * per
    tail = min(64, rows)
    tile = min(64, mrows)
    end = size - 1
    sibling = spot.at_d(spot.rank(spot.b, spot.a, 1 - spot.c))
    wspan = pl.ds(pl.multiple_of(spot.d * wrows, wrows), wrows)
    mspan = pl.ds(pl.multiple_of(spot.d * mrows, mrows), mrows)
    column = pl.ds(pl.multiple_of(spot.t * heads, 128), heads)

    def block_of(ref, t):
        return ref.at[pl.ds(pl.multiple_of(t * rows, rows), rows)]

    def own_rows(r, n):
        return pl.ds(pl.multiple_of(spot.t * rows + r.start, n), n)

    weights = WeightGather(spot, wire, wrows, wf)
    wlines = [LineGather(spot, wire, msend.at[k], lambda t, k=k: full.at[k, pl.ds(t * per, per), mspan]) for k in range(2)]
    ups, downs = [WeightGather(spot, wire, mrows, full.at[k]) for k in range(2)]
    xs = LineGather(spot, wire, x_ref, lambda t: block_of(xf, t))
    gas = LineGather(spot, wire, block_of(gaf, spot.t), lambda t: block_of(gaf, t))
    blocks = [
        LineScatter(spot, wire, lambda t: block_of(part, t), lambda side, j: land.at[side, j - 1 + side],
                    lambda dst, src: add_tiled(dst, src, tail), rising=k == 0) for k in range(2)]
    scatters = [WeightScatter(spot, wire, held.at[k], one_a, one_b, two_a, two_b) for k in range(2)]
    wscatter = WeightScatter(spot, wire, wheld.at[0], wone_a, wone_b, wtwo_a, wtwo_b)

    def line_of(k):
        here = held.at[k, spot.b, spot.a]
        return LineScatter(spot, wire, lambda t: here.at[t], lambda side, j: mland.at[k, side, j - 1 + side],
                           lambda dst, src: add_tiled(dst, src, min(64, mrows // 2)))

    lines = [line_of(k) for k in range(2)]
    zero = [wire.take(size) for _ in range(2)]
    wzero = wire.take(ab)
    gains_in = wire.take(geo.dp - 1)
    small = wire.take(geo.dp - 1)
    last = wire.take(size - 1)

    pairs = [
        (gain_ref, gain_in), (bias_ref, bias_in), (aw_ref, wsend.at[pl.ds(0, 3)]), (ow_ref, ow_in),
        (x_ref, block_of(xf, spot.t)), (down_ref, down_in), (seg_ref, seg_row), (cot_ref, cot)]
    pairs += [(up_ref.at[:, pl.ds(i * chunk, chunk)], msend.at[0, i]) for i in range(per)]
    loads = fetch([pltpu.make_async_copy(src, dst, local.at[i]) for i, (src, dst) in enumerate(pairs)])
    met = greet(spot)
    sums[...] = jnp.zeros_like(sums)
    settle(loads[0:4])
    ssend[0:2, :] = gain_in[...].astype(F32)
    ssend[2:12, :] = bias_in[...].astype(F32)
    sf[spot.d] = ssend[...]
    wsend[3] = ow_in[...].T
    wf[:, wspan] = wsend[...]
    settle(loads[8:])

    def store(k):
        return pltpu.make_async_copy(msend.at[k], full.at[k, pl.ds(spot.t * per, per), mspan], osem.at[k])

    store(0).start()
    met()
    wlines[0].start()
    for step in range(1, geo.dp):
        wire.start(gains_in + step - 1, ssend, sf.at[spot.d], spot.at_d(ring_next(spot.d, step, geo.dp)))
    weights.first()
    loads[5].wait()
    for i in range(per):
        msend[1, i] = down_in[i * chunk:(i + 1) * chunk, :].T
    store(1).start()
    wlines[0].step(1)
    weights.second()
    for k in range(2, size - 1):
        wlines[0].step(k)
    xs.start()
    weights.third()
    store(0).wait()
    wlines[0].step(end)
    ups.first()
    for step in range(1, geo.dp):
        source = ring_prev(spot.d, step, geo.dp)
        wire.landed(gains_in + step - 1, sf.at[source], spot.at_d(source))
    piece = ssend.shape[1]
    for d in range(geo.dp):
        rows12[:, d * piece:(d + 1) * piece] = sf[d]
    loads[6].wait()
    seg_col[...] = jnp.broadcast_to(seg_row[...], (128, seq)).T
    weights.fourth()
    loads[4].wait()

    def project(t):
        def norm(r):
            n1[r] = layer_norm(xf[r].astype(F32), rows12[0:1, :], rows12[2:3, :]).astype(BF)

        first = pl.multiple_of(t * rows, rows)
        loop_rows(rows, tail, norm, first)
        r = pl.ds(first, rows)
        normed = n1[r]
        qkv[0, r] = ((nn(normed, wf[0]) + rows12[3:4, column]).astype(BF).astype(F32) * HD ** -0.5).astype(BF)
        qkv[1, r] = nn(normed, wf[1]).astype(BF)
        qkv[2, r] = (nn(normed, wf[2]) + rows12[4:5, column]).astype(BF)

    def arrive(k, carry):
        @pl.when(k >= 1)
        def _():
            xs.step(k)

        @pl.when(k == end - 1)
        def _():
            wlines[1].start()

        def side(i, inner):
            t = spot.t + (2 * i - 1) * k

            @pl.when((t >= 0) & (t < size) & ((i == 0) | (k >= 1)))
            def _():
                project(t)

            return inner

        lax.fori_loop(0, 2, side, 0)

        @pl.when(k == 1)
        def _():
            ups.second()

        @pl.when(k == end)
        def _():
            wlines[1].step(1)
            ups.third()

        for i in range(size):
            start = i * rows

            @pl.when(jnp.maximum(spot.t, i - spot.t) == k)
            def _():
                block_bias(seg_col, seg_row, bias, start, rows, start + rows)
                attend_block(qkv, bias, att, lse, start, rows)
                part[start:start + rows, :] = nt(att[start:start + rows, :], wf[3]).astype(BF)
                blocks[0].start_block(i)

            if i == 1:
                @pl.when(k == end)
                def _():
                    wlines[1].step(2)

        return carry

    lax.fori_loop(0, size, arrive, 0)
    xs.owe()
    for k in range(3, size):
        wlines[1].step(k)
    store(1).wait()
    downs.first()
    for i in range(size):
        n1t[:, i * rows:(i + 1) * rows] = n1[i * rows:(i + 1) * rows, :].T

    def set_total(r):
        mid[r] = part[own_rows(r, tail)].astype(F32)

    loop_rows(rows, tail, set_total)

    def mid_total(ref, h):
        n = ref.shape[0]
        add_tiled(mid.at[pl.ds(h * n, n)], ref, tail)

    events = blocks[0].count()
    blocks[0].step(0, events // 2, mid_total)
    ups.fourth()
    downs.second()
    blocks[0].step(events // 2, events, mid_total)

    def mlp(mbuf, hmid, da, n2, gm, turned, n2t, gmt, snd, dn2, outv):
        def cols_of(j):
            return pl.ds(pl.multiple_of(j * chunk, chunk), chunk)

        def sub_of(j):
            return pl.ds(pl.multiple_of(lax.rem(j, per) * chunk, chunk), chunk)

        def mload(k, j, s):
            n = width // pieces
            return [
                pltpu.make_async_copy(
                    full.at[k, j, pl.ds(i * n, n)], mbuf.at[s, pl.ds(i * n, n)], msem.at[s, i])
                for i in range(pieces)]

        def depth(which):
            return mbuf.shape[0] // len(which)

        def ahead(which):
            for j in range(min(depth(which) - 1, count)):
                for n, k in enumerate(which):
                    fetch(mload(k, j, j * len(which) + n))

        def streamed(which, body):
            deep = depth(which)

            def one(j, carry):
                slots = [lax.rem(j, deep) * len(which) + n for n in range(len(which))]
                for n, k in enumerate(which):
                    settle(mload(k, j, slots[n]))

                @pl.when(j + deep - 1 < count)
                def _():
                    for n, k in enumerate(which):
                        fetch(mload(k, j + deep - 1, lax.rem(j + deep - 1, deep) * len(which) + n))

                body(j, *slots)
                return carry

            lax.fori_loop(0, count, one, 0)

        ahead((0,))
        loads[7].wait()

        def norm(r):
            value = xf[own_rows(r, tail)].astype(F32) + (mid[r] + rows12[5:6, :])
            mid[r] = value
            n2[r] = layer_norm(value, rows12[1:2, :], rows12[6:7, :]).astype(BF)
            branch = cot[r].astype(BF)
            gm[r] = branch
            sums[7:8, :] += column_sum(branch.astype(F32))

        loop_rows(rows, tail, norm)

        def turn(value, dst):
            turned[...] = value[...].T
            for i in range(ab):
                for other in range(2):
                    core = lax.rem(spot.c + other, 2)
                    dst[other, i * mrows:(i + 1) * mrows, :] = turned[pl.ds(pl.multiple_of((i * 2 + core) * mrows, mrows), mrows), :]

        downs.third()
        turn(gm, gmt)

        def sending(k, t):
            return wire.copy(zero[k] + t, snd.at[:, :, t], held.at[k, :, :, t], sibling)

        def give(k, j, left, right):
            product = nn(left[1], right).astype(BF)
            t = lax.div(j, per)
            for i in range(ab):
                snd[i // a_size, i % a_size, t, :, sub_of(j)] = product[i * mrows:(i + 1) * mrows, :]

            @pl.when(lax.rem(j, per) == per - 1)
            def _():
                sending(k, t).start()

        def keep(k, j, left, right):
            t = lax.div(j, per)

            @pl.when(lax.rem(j, per) == 0)
            def _():
                sending(k, t).wait_recv()

            product = nn(left[0], right)
            for i in range(ab):
                b, a = i // a_size, i % a_size
                held[k, b, a, t, :, sub_of(j)] = (
                    held[k, b, a, t, :, sub_of(j)].astype(F32) + product[i * mrows:(i + 1) * mrows, :]).astype(BF)

        def hidden(j, s):
            cols = cols_of(j)
            row = pl.ds(8 + lax.div(j * chunk, width), 1)
            bcols = pl.ds(pl.multiple_of(lax.rem(j * chunk, width), chunk), chunk)
            value, slope = gelu_parts(nn(n2[...], mbuf[s]) + rows12[row, bcols])
            active = value.astype(BF)
            hmid[:, cols] = active
            da[:, cols] = slope.astype(BF)
            give(1, j, gmt, active)

        streamed((0,), hidden)
        downs.fourth()
        ahead((0, 1))

        def keep_down(j, carry):
            keep(1, j, gmt, hmid[:, cols_of(j)])
            return carry

        lax.fori_loop(0, count, keep_down, 0)
        scatters[1].first()
        dn2[...] = jnp.zeros_like(dn2)
        outv[...] = jnp.zeros_like(outv)

        def hidden_back(j, s, s_down):
            cols = cols_of(j)
            row = pl.ds(8 + lax.div(j * chunk, width), 1)
            bcols = pl.ds(pl.multiple_of(lax.rem(j * chunk, width), chunk), chunk)
            grad = (nn(gm[...], mbuf[s_down]) * da[:, cols].astype(F32)).astype(BF)
            da[:, cols] = grad
            sums[row, bcols] = column_sum(grad.astype(F32))
            dn2[...] += nt(grad, mbuf[s])

        streamed((0, 1), hidden_back)

        def back(r):
            value = mid[r]
            unit_two, scale_two = norm_stats(value)
            grad = dn2[r]
            total = cot[r] + norm_back(grad, unit_two, scale_two, rows12[1:2, :])
            cot[r] = total
            branch = total.astype(BF)
            gaf[own_rows(r, tail)] = branch
            sums[1:2, :] += column_sum(grad * unit_two)
            sums[6:7, :] += column_sum(grad)
            sums[5:6, :] += column_sum(branch.astype(F32))

        loop_rows(rows, tail, back)
        wire.sent(blocks[0].plans())
        gas.start()
        turn(n2, n2t)
        for t in range(size):
            sending(1, t).wait_send()

        def give_up(j, carry):
            give(0, j, n2t, da[:, cols_of(j)])
            return carry

        lax.fori_loop(0, count, give_up, 0)

        def keep_up(j, carry):
            keep(0, j, n2t, da[:, cols_of(j)])
            return carry

        lax.fori_loop(0, count, keep_up, 0)
        ahead((1,))
        scatters[1].second()

        def output(j, s):
            outv[...] += nt(hmid[:, cols_of(j)], mbuf[s])

        streamed((1,), output)

        def set_out(r):
            outv[r] = mid[r] + (outv[r] + rows12[7:8, :])

        loop_rows(rows, tail, set_out)
        out_copy = pltpu.make_async_copy(outv, out_ref, osem.at[0])
        out_copy.start()
        for t in range(size):
            sending(0, t).wait_send()
        out_copy.wait()

    ff = size * unit
    pl.run_scoped(
        mlp,
        pltpu.VMEM((6, width, chunk), BF),
        pltpu.VMEM((rows, ff), BF),
        pltpu.VMEM((rows, ff), BF),
        pltpu.VMEM((rows, width), BF),
        pltpu.VMEM((rows, width), BF),
        pltpu.VMEM((width, rows), BF),
        pltpu.VMEM((2, ab * mrows, rows), BF),
        pltpu.VMEM((2, ab * mrows, rows), BF),
        pltpu.VMEM((b_size, a_size, size, mrows, unit), BF),
        pltpu.VMEM((rows, width), F32),
        pltpu.VMEM((rows, width), F32),
    )

    def attention(gat, do, dqkv, dk, dv, wg):
        def own_line(k, total):
            here = held.at[k, spot.b, spot.a, spot.t]

            def set_row(r):
                total[r] = here[r].astype(F32)

            loop_rows(mrows, tile, set_row)

        def down_total(ref, h):
            n = ref.shape[0]
            add_tiled(gtot.at[pl.ds(h * n, n)], ref, min(tile, n))

        def arrived(t):
            r = pl.ds(pl.multiple_of(t * rows, rows), rows)
            value = gaf[r]
            do[r] = nn(value, wf[3]).astype(BF)
            gat[:, r] = value.T

        dk[...] = jnp.zeros_like(dk)
        dv[...] = jnp.zeros_like(dv)

        def arrive_back(k, carry):
            @pl.when(k >= 1)
            def _():
                gas.step(k)

            @pl.when(k == 1)
            def _():
                scatters[1].third()
                lines[1].start()
                scatters[0].first()

            def side(i, inner):
                t = spot.t + (2 * i - 1) * k

                @pl.when((t >= 0) & (t < size) & ((i == 0) | (k >= 1)))
                def _():
                    arrived(t)

                return inner

            lax.fori_loop(0, 2, side, 0)
            for i in range(size):
                @pl.when((i == spot.t - k) | (i == spot.t + k))
                def _():
                    start, stop = i * rows, (i + 1) * rows
                    block_bias(seg_col, seg_row, bias, start, rows, stop)
                    attend_block_back(qkv, bias, lse, do, dqkv.at[0], dk, dv, start, rows)

            @pl.when(k == end - 1)
            def _():
                lines[1].step(0, lines[1].count() // 3, down_total)

            return carry

        lax.fori_loop(0, size, arrive_back, 0)
        gas.owe()
        own_line(1, gtot)
        half = width // 2
        dqkv[1] = dk[...].astype(BF)
        dqkv[2] = dv[...].astype(BF)
        order = []
        for i in range(size // 2):
            order += [end - i, i]
        for i in order:
            start, stop = i * rows, (i + 1) * rows
            for first in range(0, width, half):
                cols = slice(first, first + half)
                part[start:stop, cols] = sum(nt(dqkv[j, start:stop, :], wf[j, cols, :]) for j in range(3)).astype(BF)
            blocks[1].start_block(i)
        scatters[0].second()
        third = lines[1].count() // 3
        lines[1].step(third, 2 * third, down_total)
        loop_rows(rows, tail, lambda r: set_total(r))
        third = blocks[1].count() // 3
        blocks[1].step(0, third, mid_total)
        lines[1].step(2 * (lines[1].count() // 3), lines[1].count(), down_total)
        downg[...] = gtot[...].T
        def first_norm(r):
            unit_one, _ = norm_stats(xf[r].astype(F32))
            term = part[r].astype(F32)
            sums[0:1, :] += column_sum(term * unit_one)
            sums[2:3, :] += column_sum(term)

        loop_rows(seq, tail, first_norm)
        sums[3:4, column] = column_sum(dqkv[0].astype(F32))
        sums[4:5, column] = column_sum(dqkv[2].astype(F32))
        for d in range(geo.dp):
            spart[d] = sums[:, d * piece:(d + 1) * piece]
        for step in range(1, geo.dp):
            to = ring_next(spot.d, step, geo.dp)
            wire.start(small + step - 1, spart.at[to], sland.at[step - 1], spot.at_d(to))
        stot[...] = spart[spot.d]
        def wgrad(r):
            for j in range(3):
                wg[j, r] = nn(n1t[r], dqkv[j]).astype(BF)
            wg[3, r] = nn(gat[r], att[...]).astype(BF)

        loop_rows(width, min(256, width), wgrad)

        def wrows_of(i, core):
            return pl.ds(pl.multiple_of((i * 2 + core) * wrows, wrows), wrows)

        for i in range(ab):
            wire.start(wzero + i, wg.at[:, wrows_of(i, 1 - spot.c)], wheld.at[0, i // a_size, i % a_size], sibling)
        for i in range(ab):
            here = wheld.at[0, i // a_size, i % a_size]
            wire.landed(wzero + i, here, sibling)
            wscatter.add(here, wg.at[:, wrows_of(i, spot.c)])
        wscatter.first()
        blocks[1].step(third, 2 * third, mid_total)
        for step in range(1, geo.dp):
            wire.landed(small + step - 1, sland.at[step - 1], spot.at_d(ring_prev(spot.d, step, geo.dp)))
            stot[...] += sland[step - 1]
        for step in range(1, size):
            wire.start(last + step - 1, stot, tland.at[step - 1], spot.at_t(ring_next(spot.t, step, size)))
        scatters[0].third()
        lines[0].start()
        stores = fetch([pltpu.make_async_copy(downg, downg_ref, osem.at[1])])
        own_line(0, gtot)
        wscatter.second()
        blocks[1].step(2 * third, blocks[1].count(), mid_total)

        def back(r):
            unit_one, scale_one = norm_stats(xf[own_rows(r, tail)].astype(F32))
            cot[r] = cot[r] + norm_back(mid[r], unit_one, scale_one, rows12[0:1, :])

        loop_rows(rows, tail, back)
        stores += fetch([pltpu.make_async_copy(cot, igrad_ref, osem.at[0])])
        events = lines[0].count()
        lines[0].step(0, events // 3, down_total)
        wscatter.third()
        lines[0].step(events // 3, 2 * events // 3, down_total)
        sums_w = wheld.at[0, spot.b, spot.a]
        for j in range(3):
            awg[j] = sums_w[j].astype(F32)
        owg[...] = sums_w[3].astype(F32).T
        for step in range(1, size):
            wire.landed(last + step - 1, tland.at[step - 1], spot.at_t(ring_prev(spot.t, step, size)))
        total = stot[...]
        for step in range(1, size):
            total = total + tland[step - 1]
        gaing[...] = total[0:2, :]
        for i in range(biasg.shape[0]):
            biasg[i] = total[2 + i:3 + i, :]
        stores += fetch([
            pltpu.make_async_copy(awg, awg_ref, osem.at[2]),
            pltpu.make_async_copy(owg, owg_ref, osem.at[3]),
            pltpu.make_async_copy(gaing, gaing_ref, osem.at[4]),
            pltpu.make_async_copy(biasg, biasg_ref, osem.at[5])])
        lines[0].step(2 * events // 3, events, down_total)
        stores += fetch([pltpu.make_async_copy(gtot, upg_ref, osem.at[6])])
        wire.drain()
        settle(stores)

    pl.run_scoped(
        attention,
        pltpu.VMEM((width, seq), BF),
        pltpu.VMEM((seq, heads), BF),
        pltpu.VMEM((3, seq, heads), BF),
        pltpu.VMEM((seq, heads), F32),
        pltpu.VMEM((seq, heads), F32),
        pltpu.VMEM((4, width, heads), BF),
    )


def block_kernel(geo, x, aw, ow, up, down, gains, biases, seg_row, cot):
    rows, width = x.shape
    wrows, heads = aw.shape[1:]
    mrows, unit = up.shape
    size = geo.tensor
    seq = size * rows
    chunk = min(512, unit)
    sems = 3 * gather_sems(geo) + 48 * size + 3 * scatter_sems(geo) + geo.a_size * geo.b_size + 2 * geo.dp
    like = lambda x: pltpu.VMEM(x.shape, x.dtype)
    return pl.pallas_call(
        functools.partial(block_body, geo),
        out_shape=(
            jax.ShapeDtypeStruct((2, size * (unit // chunk), width, chunk), BF),
            jax.ShapeDtypeStruct((rows, width), F32),
            jax.ShapeDtypeStruct((rows, width), F32),
            jax.ShapeDtypeStruct((3, wrows, heads), F32),
            jax.ShapeDtypeStruct((heads, wrows), F32),
            jax.ShapeDtypeStruct((mrows, unit), F32),
            jax.ShapeDtypeStruct((unit, mrows), F32),
            jax.ShapeDtypeStruct((2, wrows), F32),
            jax.ShapeDtypeStruct((10, 1, wrows), F32),
        ),
        in_specs=[ANY] * 9,
        out_specs=(ANY,) * 9,
        scratch_shapes=[
            pltpu.VMEM((seq, width), BF),
            pltpu.VMEM((seq, width), BF),
            pltpu.VMEM((width, seq), BF),
            pltpu.VMEM((3, seq, heads), BF),
            pltpu.VMEM((seq, heads), BF),
            pltpu.VMEM((seq, 128), F32),
            pltpu.VMEM((4, width, heads), BF),
            pltpu.VMEM((seq, width), BF),
            pltpu.VMEM((2, size - 1, rows, width), BF),
            pltpu.VMEM((rows, seq), F32),
            pltpu.VMEM((rows, width), F32),
            pltpu.VMEM((rows, width), F32),
            pltpu.VMEM((seq, width), BF),
            pltpu.VMEM((12, width), F32),
            pltpu.VMEM((seq, 128), jnp.int32),
            like(seg_row),
            pltpu.VMEM((geo.dp, 12, wrows), F32),
            pltpu.VMEM((4, wrows, heads), BF),
            like(ow), like(down), pltpu.VMEM((2, unit // chunk, mrows, chunk), BF), like(gains), like(biases),
            pltpu.VMEM((12, wrows), F32),
            pltpu.VMEM((12, width), F32),
            pltpu.VMEM((geo.dp, 12, wrows), F32),
            pltpu.VMEM((geo.dp - 1, 12, wrows), F32),
            pltpu.VMEM((12, wrows), F32),
            pltpu.VMEM((size - 1, 12, wrows), F32),
            *scatter_bufs(geo, 2, size, mrows, unit),
            *scatter_bufs(geo, 1, 4, wrows, heads),
            pltpu.VMEM((2, 2, size - 1, mrows, unit), BF),
            pltpu.VMEM((mrows, unit), F32),
            pltpu.VMEM((unit, mrows), F32),
            pltpu.VMEM((3, wrows, heads), F32),
            pltpu.VMEM((heads, wrows), F32),
            pltpu.VMEM((2, wrows), F32),
            pltpu.VMEM((10, 1, wrows), F32),
            pltpu.SemaphoreType.DMA((sems,)), pltpu.SemaphoreType.DMA((sems,)), pltpu.SemaphoreType.DMA((8 + unit // chunk,)),
            pltpu.SemaphoreType.DMA((6, 2)), pltpu.SemaphoreType.DMA((7,))],
        compiler_params=pltpu.CompilerParams(collective_id=1, has_side_effects=True, vmem_limit_bytes=61 * 2**20),
        name="block",
    )(x, aw, ow, up, down, gains, biases, seg_row, cot)


def hand_over_body(*refs):
    *refs, loads, stores = refs
    count = len(refs) // 3
    ins, outs, bufs = refs[:count], refs[count:2 * count], refs[2 * count:]
    coming = fetch([pltpu.make_async_copy(ins[i], bufs[i], loads.at[i]) for i in range(count)])
    going = []
    for i in range(count):
        coming[i].wait()
        going += fetch([pltpu.make_async_copy(bufs[i], outs[i], stores.at[i])])
    settle(going)


def hand_over(parts):
    return pl.pallas_call(
        hand_over_body,
        out_shape=tuple(jax.ShapeDtypeStruct(part.shape, part.dtype) for part in parts),
        in_specs=[ANY] * len(parts),
        out_specs=(ANY,) * len(parts),
        scratch_shapes=[pltpu.VMEM(part.shape, part.dtype) for part in parts] + [pltpu.SemaphoreType.DMA((len(parts),))] * 2,
        name="hand_over",
    )(*parts)


def per_device(geo, activations, segments, attn_weight, out_weight, up_weight, down_weight, norm_gains, bias_rows, cotangent):
    outs = block_kernel(
        geo, activations, attn_weight[0], out_weight[0], up_weight[0], down_weight[0], norm_gains[0], bias_rows[0], segments[None, :],
        cotangent)
    outs = hand_over(outs[1:])
    return outs[:2] + tuple(part[None] for part in outs[2:7]) + (outs[7].reshape(1, 10, -1),)


def solution(mesh):
    geo = Geometry(mesh.shape["dp"], mesh.shape["tensor"])
    return jax.shard_map(
        functools.partial(per_device, geo),
        mesh=mesh,
        in_specs=(
            P(("dp", "tensor"), None),
            P("dp"),
            P(None, None, "dp", "tensor"),
            P(None, "tensor", "dp"),
            P(None, "dp", "tensor"),
            P(None, "tensor", "dp"),
            P(None, None, "dp"),
            P(None, None, "dp"),
            P(("dp", "tensor"), None),
        ),
        out_specs=(
            P(("dp", "tensor"), None),
            P(("dp", "tensor"), None),
            P(None, None, "dp", "tensor"),
            P(None, "tensor", "dp"),
            P(None, "dp", "tensor"),
            P(None, "tensor", "dp"),
            P(None, None, "dp"),
            P(None, None, "dp"),
        ),
        check_vma=False,
    )
```

```python
import functools

import jax
import jax.numpy as jnp
from jax import lax
from jax.experimental import pallas as pl
from jax.experimental.pallas import tpu as pltpu
from jax.sharding import PartitionSpec as P

HD = 64
EPSILON = 1e-05
MASKED = -1e30
MESH_ID = pl.DeviceIdType.MESH
BF = jnp.bfloat16
F32 = jnp.float32
ANY = pl.BlockSpec(memory_space=pl.ANY)
VM = pl.BlockSpec(memory_space=pltpu.VMEM)


def layer_norm(values, gain_row, shift_row):
    center = values - jnp.mean(values, axis=-1, keepdims=True)
    spread = jnp.mean(center * center, axis=-1, keepdims=True)
    return center * lax.rsqrt(spread + EPSILON) * gain_row + shift_row


def norm_stats(values):
    center = values - jnp.mean(values, axis=-1, keepdims=True)
    spread = jnp.mean(center * center, axis=-1, keepdims=True)
    scale = lax.rsqrt(spread + EPSILON)
    return center * scale, scale


def norm_back(grad, unit, scale, gain_row):
    u = grad * gain_row
    mean_u = jnp.mean(u, axis=-1, keepdims=True)
    mean_ux = jnp.mean(u * unit, axis=-1, keepdims=True)
    return scale * (u - mean_u - unit * mean_ux)


def gelu_tanh(values):
    return jax.nn.gelu(values, approximate=True)


class Geometry:
    def __init__(self, dp, tensor):
        self.dp, self.tensor = dp, tensor
        self.c_size = 2
        rest = dp // 2
        self.a_size = 1
        while self.a_size * self.a_size < rest:
            self.a_size *= 2
        self.b_size = rest // self.a_size
        assert self.a_size * self.b_size * 2 == dp

    def bind(self):
        spot = Spot()
        spot.geo = self
        spot.d = lax.axis_index("dp")
        spot.t = lax.axis_index("tensor")
        spot.c = lax.rem(spot.d, 2)
        half = lax.div(spot.d, 2)
        spot.a = lax.rem(half, self.a_size)
        spot.b = lax.div(half, self.a_size)
        return spot


class Spot:
    def rank(self, b, a, c):
        return (b * self.geo.a_size + a) * 2 + c

    def at_t(self, t):
        return (self.d, t)

    def at_d(self, d):
        return (d, self.t)


def ring_next(rank, step, size):
    return lax.rem(rank + step, size)


def ring_prev(rank, step, size):
    return lax.rem(rank + size - step, size)


class Wire:
    def __init__(self, send, recv):
        self.send_sems, self.recv_sems = send, recv
        self.count = 0
        self.pending = []

    def take(self, n):
        first = self.count
        self.count += n
        return first

    def copy(self, i, src, dst, device):
        return pltpu.make_async_remote_copy(
            src_ref=src, dst_ref=dst, send_sem=self.send_sems.at[i], recv_sem=self.recv_sems.at[i],
            device_id=device, device_id_type=MESH_ID)

    def plan(self, i, src, dst, device, when=None):
        return self.copy(i, src, dst, device), when

    def go(self, planned):
        copy, when = planned
        if when is None:
            copy.start()
        else:
            pl.when(when)(copy.start)
        self.owe(planned)

    def owe(self, planned):
        if not any(other is planned for other in self.pending):
            self.pending.append(planned)

    def start(self, i, src, dst, device, when=None):
        self.go(self.plan(i, src, dst, device, when))

    def landed(self, i, dst, device, when=None):
        copy = self.copy(i, dst, dst, device)
        if when is None:
            copy.wait_recv()
        else:
            pl.when(when)(copy.wait_recv)

    def sent(self, plans):
        for planned in plans:
            copy, when = planned
            self.pending = [other for other in self.pending if other is not planned]
            if when is None:
                copy.wait_send()
            else:
                pl.when(when)(copy.wait_send)

    def drain(self):
        for copy, when in self.pending:
            if when is None:
                copy.wait_send()
            else:
                pl.when(when)(copy.wait_send)
        self.pending = []


def greet(spot):
    geo = spot.geo
    barrier = pltpu.get_barrier_semaphore()
    total = 0
    for step in range(1, geo.tensor):
        pl.semaphore_signal(barrier, inc=1, device_id=spot.at_t(ring_next(spot.t, step, geo.tensor)), device_id_type=MESH_ID)
        total += 1
    for step in range(1, geo.dp):
        pl.semaphore_signal(barrier, inc=1, device_id=spot.at_d(ring_next(spot.d, step, geo.dp)), device_id_type=MESH_ID)
        total += 1
    return lambda: pl.semaphore_wait(barrier, total)


def halves(ref, count, part):
    rows = ref.shape[-2] // count
    return ref.at[(slice(None),) * (len(ref.shape) - 2) + (pl.ds(part * rows, rows),)]


class LineGather:
    def __init__(self, spot, wire, src, slot, parts=2):
        self.spot, self.wire, self.src, self.slot, self.parts = spot, wire, src, slot, parts
        self.size = size = spot.geo.tensor
        self.base = [wire.take((size - 1) * parts) for _ in range(2)]
        t = spot.t
        self.sends = {}
        for k in range(size - 1):
            for part in range(parts):
                for side in range(2):
                    self.sends[k, part, side] = self.plan(k, part, side)

    def place(self, k, side):
        t = self.spot.t
        origin = t - k if side == 0 else t + k
        there = (origin >= 0) & (origin < self.size)
        onward = t + 1 if side == 0 else t - 1
        return origin, there, t - 1 if side == 0 else t + 1, onward, there & (onward >= 0) & (onward < self.size)

    def plan(self, k, part, side):
        origin, _, _, onward, going = self.place(k, side)
        piece = halves(self.slot(origin), self.parts, part)
        first = isinstance(k, int) and k == 0
        src = halves(self.src, self.parts, part) if first else piece
        return self.wire.plan(self.base[side] + k * self.parts + part, src, piece, self.spot.at_t(onward), when=going)

    def start(self):
        for part in range(self.parts):
            for side in range(2):
                self.wire.go(self.sends[0, part, side])

    def step(self, k):
        for part in range(self.parts):
            for side in range(2):
                origin, there, near, _, _ = self.place(k, side)
                piece = halves(self.slot(origin), self.parts, part)
                self.wire.landed(self.base[side] + (k - 1) * self.parts + part, piece, self.spot.at_t(near), when=there)
                if not isinstance(k, int):
                    copy, going = self.plan(k, part, side)
                    pl.when(going & (k < self.size - 1))(copy.start)
                elif k < self.size - 1:
                    self.wire.go(self.sends[k, part, side])

    def owe(self):
        for (k, part, side), planned in self.sends.items():
            if k > 0:
                self.wire.owe(planned)


class LineScatter:
    def __init__(self, spot, wire, part, land, add, rising=None, parts=2):
        self.spot, self.wire, self.part, self.land, self.add, self.parts = spot, wire, part, land, add, parts
        self.size = spot.geo.tensor
        base = self.base = [wire.take((self.size - 1) * parts) for _ in range(2)]
        t, end = spot.t, self.size - 1
        self.starts, self.hops = {}, {}
        for h in range(parts):
            for j in range(self.size):
                if j > 0:
                    self.starts[0, j, h] = wire.plan(
                        base[0] + (j - 1) * parts + h, halves(part(j), parts, h), halves(land(0, j), parts, h), spot.at_t(1), when=t == 0)
                if j < end:
                    self.starts[1, j, h] = wire.plan(
                        base[1] + j * parts + h, halves(part(j), parts, h), halves(land(1, j), parts, h), spot.at_t(end - 1), when=t == end)
        self.events = []
        for side in range(2):
            place = t if side == 0 else end - t
            if side == rising:
                for e in range(1, 2 * end):
                    far = e + 1 - place
                    self.events.append((10 * e, side, far if side == 0 else end - far, (place >= 1) & (far >= place) & (far <= end)))
            else:
                for s in range(1, self.size):
                    far = end - s + place
                    at = 10 * s + (0 if rising is None else 15)
                    self.events.append((at, side, far if side == 0 else end - far, (place >= 1) & (s >= place)))
        self.events.sort(key=lambda event: event[0])
        self.hops = []
        for _, side, j, here in self.events:
            near = spot.at_t(t - 1 if side == 0 else t + 1)
            away = spot.at_t(t + 1 if side == 0 else t - 1)
            for h in range(parts):
                held = halves(land(side, j), parts, h)
                i = base[side] + (j - 1 + side) * parts + h
                self.hops.append((here & (j == t), here & (j != t), j, h, held, wire.copy(i, held, held, near),
                                  wire.plan(i, held, held, away, when=here & (j != t))))

    def start_block(self, j):
        for side in range(2):
            for h in range(self.parts):
                if (side, j, h) in self.starts:
                    self.wire.go(self.starts[side, j, h])

    def start_traced(self, j):
        spot, t, end = self.spot, self.spot.t, self.size - 1
        for side in range(2):
            first, to = (0, 1) if side == 0 else (end, end - 1)
            for h in range(self.parts):
                copy, when = self.wire.plan(
                    self.base[side] + (j - 1 + side) * self.parts + h, halves(self.part(j), self.parts, h),
                    halves(self.land(side, j), self.parts, h), spot.at_t(to), when=(t == first) & (j != first))
                pl.when(when)(copy.start)

    def owe_starts(self):
        for planned in self.starts.values():
            self.wire.owe(planned)

    def start(self):
        for n in range(self.size):
            for side, j in ((0, self.size - 1 - n), (1, n)):
                for h in range(self.parts):
                    if (side, j, h) in self.starts:
                        self.wire.go(self.starts[side, j, h])

    def count(self):
        return len(self.hops)

    def step(self, first, last, total):
        for final, passing, j, h, held, landing, onward in self.hops[first:last]:
            @pl.when(final)
            def _():
                landing.wait_recv()
                total(held, h)

            @pl.when(passing)
            def _():
                landing.wait_recv()
                self.add(held, halves(self.part(j), self.parts, h))

            self.wire.go(onward)

    def plans(self):
        return list(self.starts.values()) + [hop[-1] for hop in self.hops]


def add_tiled(dst, src, tile):
    def step(i, carry):
        rows = pl.ds(pl.multiple_of(i * tile, tile), tile)
        dst[rows] = (dst[rows].astype(F32) + src[rows].astype(F32)).astype(dst.dtype)
        return carry

    lax.fori_loop(0, dst.shape[0] // tile, step, 0)


class WeightGather:
    def __init__(self, spot, wire, rows, full):
        geo = spot.geo
        self.spot, self.wire, self.full, self.rows = spot, wire, full, rows
        self.slots = full.shape[0]
        self.half = self.slots // 2
        self.one_a = wire.take(geo.a_size - 1)
        self.one_b = wire.take(geo.b_size - 1)
        self.two_a = wire.take((geo.b_size - 1) * geo.a_size)
        self.two_b = wire.take((geo.a_size - 1) * geo.b_size)
        self.last = wire.take(2 * geo.a_size * geo.b_size)
        self.plan_shares()
        self.plan_hops()

    def span(self, d):
        return pl.ds(pl.multiple_of(d * self.rows, self.rows), self.rows)

    def low(self, d):
        return self.full.at[pl.ds(0, self.half), self.span(d)]

    def high(self, d):
        return self.full.at[pl.ds(self.half, self.slots - self.half), self.span(d)]

    def plan_shares(self):
        spot, geo = self.spot, self.spot.geo
        self.shares = {}
        for j in range(geo.b_size):
            for i in range(geo.a_size):
                held = spot.rank(ring_prev(spot.b, j, geo.b_size), ring_prev(spot.a, i, geo.a_size), spot.c)
                sibling = spot.rank(spot.b, spot.a, 1 - spot.c)
                for part in range(2):
                    half = (self.low, self.high)[part](held)
                    self.shares[part, j, i] = self.wire.plan(
                        self.last + 2 * (j * geo.a_size + i) + part, half, half, spot.at_d(sibling))

    def share(self, part, j, i):
        self.wire.go(self.shares[part, j, i])

    def plan_hops(self):
        spot, geo, wire = self.spot, self.spot.geo, self.wire
        self.ones, self.twos_a, self.twos_b = [], {}, {}
        mine = spot.d
        for j in range(1, geo.a_size):
            to = spot.rank(spot.b, ring_next(spot.a, j, geo.a_size), spot.c)
            self.ones.append(wire.plan(self.one_a + j - 1, self.low(mine), self.low(mine), spot.at_d(to)))
        for j in range(1, geo.b_size):
            to = spot.rank(ring_next(spot.b, j, geo.b_size), spot.a, spot.c)
            self.ones.append(wire.plan(self.one_b + j - 1, self.high(mine), self.high(mine), spot.at_d(to)))
        for i in range(geo.a_size):
            held = spot.rank(spot.b, ring_prev(spot.a, i, geo.a_size), spot.c)
            for j in range(1, geo.b_size):
                to = spot.rank(ring_next(spot.b, j, geo.b_size), spot.a, spot.c)
                self.twos_a[i, j] = wire.plan(self.two_a + (j - 1) * geo.a_size + i, self.low(held), self.low(held), spot.at_d(to))
        for i in range(geo.b_size):
            held = spot.rank(ring_prev(spot.b, i, geo.b_size), spot.a, spot.c)
            for j in range(1, geo.a_size):
                to = spot.rank(spot.b, ring_next(spot.a, j, geo.a_size), spot.c)
                self.twos_b[i, j] = wire.plan(self.two_b + (j - 1) * geo.b_size + i, self.high(held), self.high(held), spot.at_d(to))

    def first(self):
        for planned in self.ones:
            self.wire.go(planned)
        self.share(0, 0, 0)
        self.share(1, 0, 0)

    def second(self):
        spot, geo = self.spot, self.spot.geo
        for i in range(geo.a_size):
            held = spot.rank(spot.b, ring_prev(spot.a, i, geo.a_size), spot.c)
            if i:
                self.wire.landed(self.one_a + i - 1, self.low(held), spot.at_d(held))
                self.share(0, 0, i)
            for j in range(1, geo.b_size):
                self.wire.go(self.twos_a[i, j])
        for i in range(geo.b_size):
            held = spot.rank(ring_prev(spot.b, i, geo.b_size), spot.a, spot.c)
            if i:
                self.wire.landed(self.one_b + i - 1, self.high(held), spot.at_d(held))
                self.share(1, i, 0)
            for j in range(1, geo.a_size):
                self.wire.go(self.twos_b[i, j])

    def third(self):
        spot, geo = self.spot, self.spot.geo
        for j in range(1, geo.b_size):
            for i in range(geo.a_size):
                held = spot.rank(ring_prev(spot.b, j, geo.b_size), ring_prev(spot.a, i, geo.a_size), spot.c)
                source = spot.rank(ring_prev(spot.b, j, geo.b_size), spot.a, spot.c)
                self.wire.landed(self.two_a + (j - 1) * geo.a_size + i, self.low(held), spot.at_d(source))
                self.share(0, j, i)
        for j in range(1, geo.a_size):
            for i in range(geo.b_size):
                held = spot.rank(ring_prev(spot.b, i, geo.b_size), ring_prev(spot.a, j, geo.a_size), spot.c)
                source = spot.rank(spot.b, ring_prev(spot.a, j, geo.a_size), spot.c)
                self.wire.landed(self.two_b + (j - 1) * geo.b_size + i, self.high(held), spot.at_d(source))
                self.share(1, i, j)

    def fourth(self):
        spot, geo = self.spot, self.spot.geo
        sibling = spot.rank(spot.b, spot.a, 1 - spot.c)
        for j in range(geo.b_size):
            for i in range(geo.a_size):
                held = spot.rank(ring_prev(spot.b, j, geo.b_size), ring_prev(spot.a, i, geo.a_size), 1 - spot.c)
                for part in range(2):
                    half = (self.low, self.high)[part](held)
                    self.wire.landed(self.last + 2 * (j * geo.a_size + i) + part, half, spot.at_d(sibling))


def gather_sems(geo):
    return geo.a_size + geo.b_size - 2 + (geo.b_size - 1) * geo.a_size + (geo.a_size - 1) * geo.b_size + 2 * geo.a_size * geo.b_size


class WeightScatter:
    def __init__(self, spot, wire, held, one_a, one_b, two_a, two_b):
        geo = spot.geo
        self.spot, self.wire, self.held = spot, wire, held
        self.one_a_buf, self.one_b_buf, self.two_a_buf, self.two_b_buf = one_a, one_b, two_a, two_b
        self.slots, self.rows = held.shape[2], held.shape[3]
        self.half = self.slots // 2
        self.one_a = wire.take(geo.a_size - 1)
        self.one_b = wire.take(geo.b_size - 1)
        self.two_a = wire.take(geo.b_size - 1)
        self.two_b = wire.take(geo.a_size - 1)
        low, high = pl.ds(0, self.half), pl.ds(self.half, self.half)
        self.sends = []
        for j in range(1, geo.a_size):
            a = ring_next(spot.a, j, geo.a_size)
            self.sends.append(wire.plan(self.one_a + j - 1, held.at[:, a, low], one_a.at[j - 1], spot.at_d(spot.rank(spot.b, a, spot.c))))
        for j in range(1, geo.b_size):
            b = ring_next(spot.b, j, geo.b_size)
            self.sends.append(wire.plan(self.one_b + j - 1, held.at[b, :, high], one_b.at[j - 1], spot.at_d(spot.rank(b, spot.a, spot.c))))
        self.later = []
        for j in range(1, geo.b_size):
            b = ring_next(spot.b, j, geo.b_size)
            self.later.append(wire.plan(self.two_a + j - 1, held.at[b, spot.a, low], two_a.at[j - 1], spot.at_d(spot.rank(b, spot.a, spot.c))))
        for j in range(1, geo.a_size):
            a = ring_next(spot.a, j, geo.a_size)
            self.later.append(wire.plan(self.two_b + j - 1, held.at[spot.b, a, high], two_b.at[j - 1], spot.at_d(spot.rank(spot.b, a, spot.c))))

    def add(self, dst, src):
        tile = min(64, self.rows)
        per = self.rows // tile

        def step(i, carry):
            rows = pl.ds(pl.multiple_of(lax.rem(i, per) * tile, tile), tile)
            j = lax.div(i, per)
            dst[j, rows] = (dst[j, rows].astype(F32) + src[j, rows].astype(F32)).astype(dst.dtype)
            return carry

        lax.fori_loop(0, dst.shape[0] * per, step, 0)

    def first(self):
        for planned in self.sends:
            self.wire.go(planned)

    def second(self):
        spot, geo = self.spot, self.spot.geo
        low, high = pl.ds(0, self.half), pl.ds(self.half, self.half)
        for j in range(1, geo.a_size):
            self.wire.landed(self.one_a + j - 1, self.one_a_buf.at[j - 1], spot.at_d(spot.rank(spot.b, ring_prev(spot.a, j, geo.a_size), spot.c)))
            for b in range(geo.b_size):
                self.add(self.held.at[b, spot.a, low], self.one_a_buf.at[j - 1, b])
        for j in range(1, geo.b_size):
            self.wire.landed(self.one_b + j - 1, self.one_b_buf.at[j - 1], spot.at_d(spot.rank(ring_prev(spot.b, j, geo.b_size), spot.a, spot.c)))
            for a in range(geo.a_size):
                self.add(self.held.at[spot.b, a, high], self.one_b_buf.at[j - 1, a])
        for planned in self.later:
            self.wire.go(planned)

    def third(self):
        spot, geo = self.spot, self.spot.geo
        low, high = pl.ds(0, self.half), pl.ds(self.half, self.half)
        for j in range(1, geo.b_size):
            self.wire.landed(self.two_a + j - 1, self.two_a_buf.at[j - 1], spot.at_d(spot.rank(ring_prev(spot.b, j, geo.b_size), spot.a, spot.c)))
            self.add(self.held.at[spot.b, spot.a, low], self.two_a_buf.at[j - 1])
        for j in range(1, geo.a_size):
            self.wire.landed(self.two_b + j - 1, self.two_b_buf.at[j - 1], spot.at_d(spot.rank(spot.b, ring_prev(spot.a, j, geo.a_size), spot.c)))
            self.add(self.held.at[spot.b, spot.a, high], self.two_b_buf.at[j - 1])


def scatter_sems(geo):
    return 2 * (geo.a_size + geo.b_size - 2)


def scatter_bufs(geo, n, sets, slots, rows, width):
    a, b, half = geo.a_size, geo.b_size, slots // 2
    return [
        pltpu.VMEM((n, b, a, slots, rows, width), BF),
        pltpu.VMEM((sets, a - 1, b, half, rows, width), BF),
        pltpu.VMEM((sets, b - 1, a, half, rows, width), BF),
        pltpu.VMEM((sets, b - 1, half, rows, width), BF),
        pltpu.VMEM((sets, a - 1, half, rows, width), BF),
    ]


def loop_rows(count, tile, body, start=0):
    def step(i, carry):
        body(pl.ds(pl.multiple_of(start + i * tile, tile), tile))
        return carry

    lax.fori_loop(0, count // tile, step, 0)


def fetch(copies):
    for copy in copies:
        copy.start()
    return copies


def settle(copies):
    for copy in copies:
        copy.wait()


PAIR = 2 * HD


def nt(x, w):
    return lax.dot_general(x, w, (((1,), (1,)), ((), ())), preferred_element_type=F32)


def nn(x, w):
    return lax.dot_general(x, w, (((1,), (0,)), ((), ())), preferred_element_type=F32)


def tn(x, w):
    return lax.dot_general(x, w, (((0,), (0,)), ((), ())), preferred_element_type=F32)


def block_bias(seg_col, seg_row, bias, start, rows, keys):
    query = seg_col[start:start + rows, 0:1]
    for first in range(0, keys, rows):
        key = seg_row[:, first:first + rows]
        seen = query == key
        if first + rows > start:
            q_pos = start + lax.broadcasted_iota(jnp.int32, (rows, rows), 0)
            k_pos = first + lax.broadcasted_iota(jnp.int32, (rows, rows), 1)
            seen = seen & (k_pos <= q_pos)
        bias[:, first:first + rows] = jnp.where(seen, 0.0, MASKED).astype(F32)


def one_head(pair, head):
    lane = lax.broadcasted_iota(jnp.int32, pair.shape, 1)
    return jnp.where((lane < HD) if head == 0 else (lane >= HD), pair, jnp.zeros_like(pair))


def attend_block(qkv, bias, att, lse, start, rows):
    keys = start + rows
    width = qkv.shape[2]
    stat_lane = lax.broadcasted_iota(jnp.int32, (rows, 128), 1)
    stats = jnp.zeros((rows, 128), F32)
    for p in range(width // PAIR):
        lanes = slice(p * PAIR, (p + 1) * PAIR)
        query = qkv[0, start:keys, lanes]
        outs = []
        for head in range(2):
            s = nt(one_head(query, head), qkv[1, 0:keys, lanes]) + bias[:, 0:keys]
            top = jnp.max(s, axis=1, keepdims=True)
            e = jnp.exp(s - top)
            total = jnp.sum(e, axis=1, keepdims=True)
            prob = (e * (1.0 / total)).astype(BF)
            outs.append(nn(prob, qkv[2, 0:keys, lanes]))
            stats = jnp.where(stat_lane == 2 * p + head, top + jnp.log(total), stats)
        lane = lax.broadcasted_iota(jnp.int32, outs[0].shape, 1)
        att[start:keys, lanes] = jnp.where(lane < HD, outs[0], outs[1]).astype(BF)
    lse[start:keys, :] = stats


def attend_block_back(qkv, bias, lse, do, dq, dk, dv, start, rows):
    keys = start + rows
    width = qkv.shape[2]
    stat_lane = lax.broadcasted_iota(jnp.int32, (rows, 128), 1)
    stats = lse[start:keys, :]
    for p in range(width // PAIR):
        lanes = slice(p * PAIR, (p + 1) * PAIR)
        query = qkv[0, start:keys, lanes]
        grad = do[start:keys, lanes]
        dqs, dks, dvs = [], [], []
        for head in range(2):
            level = jnp.sum(jnp.where(stat_lane == 2 * p + head, stats, 0.0), axis=1, keepdims=True)
            s = nt(one_head(query, head), qkv[1, 0:keys, lanes]) + bias[:, 0:keys]
            prob = jnp.exp(s - level)
            d_prob = nt(one_head(grad, head), qkv[2, 0:keys, lanes])
            mixed = prob * d_prob
            ds = (mixed - prob * jnp.sum(mixed, axis=1, keepdims=True)).astype(BF)
            dqs.append(nn(ds, qkv[1, 0:keys, lanes]))
            dks.append(tn(ds, query))
            dvs.append(tn(prob.astype(BF), grad))
        lane = lax.broadcasted_iota(jnp.int32, dqs[0].shape, 1)
        dq[start:keys, lanes] = (jnp.where(lane < HD, dqs[0], dqs[1]) * (HD ** -0.5)).astype(dq.dtype)
        lane = lax.broadcasted_iota(jnp.int32, dks[0].shape, 1)
        dk[0:keys, lanes] += jnp.where(lane < HD, dks[0], dks[1])
        dv[0:keys, lanes] += jnp.where(lane < HD, dvs[0], dvs[1])


GELU_C = 0.7978845608028654


def gelu_parts(a):
    square = a * a
    tanh = jnp.tanh(GELU_C * a * (1.0 + 0.044715 * square))
    half = 0.5 * (1.0 + tanh)
    slope = half + 0.5 * a * (1.0 - tanh * tanh) * (GELU_C * (1.0 + 3 * 0.044715 * square))
    return a * half, slope


def column_sum(values):
    return jnp.sum(values, axis=0, keepdims=True)


def block_body(geo, x_ref, aw_ref, ow_ref, up_ref, down_ref, gain_ref, bias_ref, seg_ref, cot_ref,
               full, out_ref, igrad_ref, awg_ref, owg_ref, upg_ref, downg_ref, gaing_ref, biasg_ref,
               xf, n1, n1t, qkv, att, lse, wf, part, land, bias, mid, cot, gaf, rows12, seg_col, seg_row,
               sf, wsend, ow_in, down_in, msend, gain_in, bias_in, ssend,
               sums, spart, sland, stot, tland,
               held, one_a, one_b, two_a, two_b, wheld, wone_a, wone_b, wtwo_a, wtwo_b, mland,
               gtot, downg, awg, owg, gaing, biasg,
               send, recv, local, msem, osem):
    spot = geo.bind()
    wire = Wire(send, recv)
    size = geo.tensor
    rows, width = x_ref.shape
    seq = size * rows
    wrows, heads = aw_ref.shape[1:]
    mrows, unit = up_ref.shape
    a_size, b_size = geo.a_size, geo.b_size
    ab = a_size * b_size
    chunk = min(512, unit)
    per = unit // chunk
    pieces = msem.shape[1]
    count = size * per
    tail = min(64, rows)
    tile = min(64, mrows)
    end = size - 1
    sibling = spot.at_d(spot.rank(spot.b, spot.a, 1 - spot.c))
    wspan = pl.ds(pl.multiple_of(spot.d * wrows, wrows), wrows)
    mspan = pl.ds(pl.multiple_of(spot.d * mrows, mrows), mrows)
    column = pl.ds(pl.multiple_of(spot.t * heads, 128), heads)

    def block_of(ref, t):
        return ref.at[pl.ds(pl.multiple_of(t * rows, rows), rows)]

    def own_rows(r, n):
        return pl.ds(pl.multiple_of(spot.t * rows + r.start, n), n)

    weights = WeightGather(spot, wire, wrows, wf)
    halved = [(k, p) for k in range(2) for p in range(per)]
    wlines, gathers = {}, {}
    for k, p in halved:
        wlines[k, p] = LineGather(spot, wire, msend.at[k, p], lambda t, k=k, p=p: full.at[k, p, t, mspan], parts=1)
        gathers[k, p] = WeightGather(spot, wire, mrows, full.at[k, p])
    xs = LineGather(spot, wire, x_ref, lambda t: block_of(xf, t))
    gas = LineGather(spot, wire, block_of(gaf, spot.t), lambda t: block_of(gaf, t))
    blocks = [
        LineScatter(spot, wire, lambda t: block_of(part, t), lambda side, j: land.at[side, j - 1 + side],
                    lambda dst, src: add_tiled(dst, src, tail), rising=k) for k in range(2)]
    scatters, lines = {}, {}

    def line_of(k, p):
        here = held.at[k * per + p, spot.b, spot.a]
        return LineScatter(spot, wire, lambda t: here.at[t], lambda side, j: mland.at[k * per + p, side, j - 1 + side],
                           lambda dst, src: add_tiled(dst, src, tile), parts=1)

    for k, p in halved:
        scatters[k, p] = WeightScatter(spot, wire, held.at[k * per + p], *(buf.at[k * per + p] for buf in (one_a, one_b, two_a, two_b)))
        lines[k, p] = line_of(k, p)
    wscatter = WeightScatter(spot, wire, wheld.at[0], wone_a.at[0], wone_b.at[0], wtwo_a.at[0], wtwo_b.at[0])
    zero = [wire.take(count) for _ in range(2)]
    wzero = wire.take(ab)
    gains_in = wire.take(geo.dp - 1)
    small = wire.take(geo.dp - 1)
    last = wire.take(size - 1)
    assert wire.count == send.shape[0]

    pairs = [
        (gain_ref, gain_in), (bias_ref, bias_in), (aw_ref, wsend.at[pl.ds(0, 3)]), (ow_ref, ow_in),
        (x_ref, block_of(xf, spot.t)), (down_ref, down_in), (seg_ref, seg_row), (cot_ref, cot)]
    pairs += [(up_ref.at[:, pl.ds(i * chunk, chunk)], msend.at[0, i]) for i in range(per)]
    loads = fetch([pltpu.make_async_copy(src, dst, local.at[i]) for i, (src, dst) in enumerate(pairs)])
    met = greet(spot)
    sums[...] = jnp.zeros_like(sums)
    settle(loads[0:4])
    ssend[0:2, :] = gain_in[...].astype(F32)
    ssend[2:12, :] = bias_in[...].astype(F32)
    sf[spot.d] = ssend[...]
    wsend[3] = ow_in[...].T
    wf[:, wspan] = wsend[...]
    settle(loads[8:])

    def store(k):
        return pltpu.make_async_copy(msend.at[k], full.at[k, :, spot.t, mspan], osem.at[k])

    store(0).start()
    met()
    for p in range(per):
        wlines[0, p].start()
    for step in range(1, geo.dp):
        wire.start(gains_in + step - 1, ssend, sf.at[spot.d], spot.at_d(ring_next(spot.d, step, geo.dp)))
    weights.first()
    loads[5].wait()
    for i in range(per):
        msend[1, i] = down_in[i * chunk:(i + 1) * chunk, :].T
    store(1).start()
    for k in range(1, end):
        for p in range(per):
            wlines[0, p].step(k)
        if k == 1:
            weights.second()
    xs.start()
    weights.third()
    store(0).wait()
    for p in range(per):
        wlines[0, p].step(end)
        gathers[0, p].first()
    for step in range(1, geo.dp):
        source = ring_prev(spot.d, step, geo.dp)
        wire.landed(gains_in + step - 1, sf.at[source], spot.at_d(source))
    piece = ssend.shape[1]
    for d in range(geo.dp):
        rows12[:, d * piece:(d + 1) * piece] = sf[d]
    loads[6].wait()
    seg_col[...] = jnp.broadcast_to(seg_row[...], (128, seq)).T
    weights.fourth()
    loads[4].wait()

    def project(t):
        def norm(r):
            source = pl.ds(pl.multiple_of(t * rows + r.start, tail), tail)
            n1[r] = layer_norm(xf[source].astype(F32), rows12[0:1, :], rows12[2:3, :]).astype(BF)

        loop_rows(rows, tail, norm)
        r = pl.ds(pl.multiple_of(t * rows, rows), rows)
        normed = n1[...]
        n1t[:, r] = normed.T
        qkv[0, r] = ((nn(normed, wf[0]) + rows12[3:4, column]).astype(BF).astype(F32) * HD ** -0.5).astype(BF)
        qkv[1, r] = nn(normed, wf[1]).astype(BF)
        qkv[2, r] = (nn(normed, wf[2]) + rows12[4:5, column]).astype(BF)

    def arrive(k, carry):
        @pl.when(k >= 1)
        def _():
            xs.step(k)

        @pl.when(k == end - 1)
        def _():
            for p in range(per):
                wlines[1, p].start()

        def side(i, inner):
            t = spot.t + (2 * i - 1) * k

            @pl.when((t >= 0) & (t < size) & ((i == 0) | (k >= 1)))
            def _():
                project(t)

            return inner

        lax.fori_loop(0, 2, side, 0)

        @pl.when(k == 1)
        def _():
            for p in range(per):
                gathers[0, p].second()

        for i in range(size):
            start = i * rows

            @pl.when(jnp.maximum(spot.t, i - spot.t) == k)
            def _():
                block_bias(seg_col, seg_row, bias, start, rows, start + rows)
                attend_block(qkv, bias, att, lse, start, rows)
                part[start:start + rows, :] = nt(att[start:start + rows, :], wf[3]).astype(BF)
                blocks[0].start_block(i)

        return carry

    lax.fori_loop(0, size, arrive, 0)
    xs.owe()
    for k in range(1, end):
        for p in range(per):
            wlines[1, p].step(k)
        if k == 1:
            for p in range(per):
                gathers[0, p].third()
    store(1).wait()
    for p in range(per):
        wlines[1, p].step(end)
        gathers[1, p].first()
    def set_total(r):
        mid[r] = part[own_rows(r, tail)].astype(F32)

    loop_rows(rows, tail, set_total)

    def mid_total(ref, h):
        n = ref.shape[0]
        add_tiled(mid.at[pl.ds(h * n, n)], ref, tail)

    events = blocks[0].count()
    blocks[0].step(0, 3 * events // 8, mid_total)
    gathers[1, 0].second()
    blocks[0].step(3 * events // 8, 5 * events // 8, mid_total)
    for p in range(per):
        gathers[0, p].fourth()
    for p in range(1, per):
        gathers[1, p].second()
    blocks[0].step(5 * events // 8, events, mid_total)

    def mlp(mbuf, hmid, da, n2, gm, turned, left, snd, dn2):
        def cols_of(j):
            return pl.ds(pl.multiple_of(unit_of(j) * chunk, chunk), chunk)

        def unit_of(j):
            return lax.rem(j, size) * per + lax.div(j, size)

        def mload(k, j, s):
            n = width // pieces
            return [
                pltpu.make_async_copy(
                    full.at[k, lax.div(j, size), lax.rem(j, size), pl.ds(i * n, n)], mbuf.at[s, pl.ds(i * n, n)], msem.at[s, i])
                for i in range(pieces)]

        def depth(which):
            return mbuf.shape[0] // len(which)

        def ahead(which):
            for j in range(min(depth(which) - 1, count)):
                for n, k in enumerate(which):
                    fetch(mload(k, j, j * len(which) + n))

        def streamed(which, body, first=0, stop=count):
            deep = depth(which)

            def one(j, carry):
                slots = [lax.rem(j, deep) * len(which) + n for n in range(len(which))]
                for n, k in enumerate(which):
                    settle(mload(k, j, slots[n]))

                @pl.when(j + deep - 1 < count)
                def _():
                    for n, k in enumerate(which):
                        fetch(mload(k, j + deep - 1, lax.rem(j + deep - 1, deep) * len(which) + n))

                body(j, *slots)
                return carry

            lax.fori_loop(first, stop, one, 0)

        ahead((0,))
        loads[7].wait()

        def norm(r):
            value = xf[own_rows(r, tail)].astype(F32) + (mid[r] + rows12[5:6, :])
            mid[r] = value
            n2[r] = layer_norm(value, rows12[1:2, :], rows12[6:7, :]).astype(BF)
            branch = cot[r].astype(BF)
            gm[r] = branch
            sums[7:8, :] += column_sum(branch.astype(F32))

        loop_rows(rows, tail, norm)

        def turn(value):
            turned[...] = value[...].T
            for i in range(ab):
                for other in range(2):
                    core = lax.rem(spot.c + other, 2)
                    left[other, i * mrows:(i + 1) * mrows, :] = turned[pl.ds(pl.multiple_of((i * 2 + core) * mrows, mrows), mrows), :]

        turn(gm)

        def sending(k, j):
            p, t = lax.div(j, size), lax.rem(j, size)
            return wire.copy(zero[k] + j, snd.at[p, :, :, t], held.at[k * per + p, :, :, t], sibling)

        def give(k, j, right):
            product = nn(left[1], right).astype(BF)
            p, t = lax.div(j, size), lax.rem(j, size)
            for i in range(ab):
                snd[p, i // a_size, i % a_size, t] = product[i * mrows:(i + 1) * mrows, :]
            sending(k, j).start()

        def keep(k, j, right):
            p, t = lax.div(j, size), lax.rem(j, size)
            product = nn(left[0], right)
            sending(k, j).wait_recv()
            for i in range(ab):
                b, a = i // a_size, i % a_size
                held[k * per + p, b, a, t] = (
                    held[k * per + p, b, a, t].astype(F32) + product[i * mrows:(i + 1) * mrows, :]).astype(BF)

        def hidden(j, s):
            cols = cols_of(j)
            row = pl.ds(8 + lax.div(unit_of(j) * chunk, width), 1)
            bcols = pl.ds(pl.multiple_of(lax.rem(unit_of(j) * chunk, width), chunk), chunk)
            value, slope = gelu_parts(nn(n2[...], mbuf[s]) + rows12[row, bcols])
            active = value.astype(BF)
            hmid[:, cols] = active
            da[:, cols] = slope.astype(BF)
            give(1, j, active)

        def keep_down(j, carry):
            keep(1, j, hmid[:, cols_of(j)])
            return carry

        for p in range(per):
            streamed((0,), hidden, p * size, (p + 1) * size)
            gathers[1, p].third()
            lax.fori_loop(p * size, (p + 1) * size, keep_down, 0)
            scatters[1, p].first()
        for p in range(per):
            gathers[1, p].fourth()
        ahead((0, 1))
        dn2[...] = jnp.zeros_like(dn2)

        def hidden_back(j, s, s_down):
            cols = cols_of(j)
            row = pl.ds(8 + lax.div(unit_of(j) * chunk, width), 1)
            bcols = pl.ds(pl.multiple_of(lax.rem(unit_of(j) * chunk, width), chunk), chunk)
            grad = (nn(gm[...], mbuf[s_down]) * da[:, cols].astype(F32)).astype(BF)
            da[:, cols] = grad
            sums[row, bcols] = column_sum(grad.astype(F32))
            dn2[...] += nt(grad, mbuf[s])

        streamed((0, 1), hidden_back)

        def back(r):
            value = mid[r]
            unit_two, scale_two = norm_stats(value)
            grad = dn2[r]
            total = cot[r] + norm_back(grad, unit_two, scale_two, rows12[1:2, :])
            cot[r] = total
            branch = total.astype(BF)
            gaf[own_rows(r, tail)] = branch
            sums[1:2, :] += column_sum(grad * unit_two)
            sums[6:7, :] += column_sum(grad)
            sums[5:6, :] += column_sum(branch.astype(F32))

        loop_rows(rows, tail, back)
        wire.sent(blocks[0].plans())
        gas.start()
        turn(n2)
        def give_up(j, carry):
            sending(1, j).wait_send()
            give(0, j, da[:, cols_of(j)])
            return carry

        lax.fori_loop(0, count, give_up, 0)
        scatters[1, 0].second()

        def keep_up(j, carry):
            keep(0, j, da[:, cols_of(j)])
            return carry

        for p in range(per):
            lax.fori_loop(p * size, (p + 1) * size, keep_up, 0)
            if p:
                scatters[1, p].second()
        ahead((1,))
        gas.step(1)
        scatters[1, 0].third()
        lines[1, 0].start()
        scatters[0, 0].first()
        dn2[...] = jnp.zeros_like(dn2)

        def output(j, s):
            dn2[...] += nt(hmid[:, cols_of(j)], mbuf[s])

        streamed((1,), output)

        def set_out(r):
            dn2[r] = mid[r] + (dn2[r] + rows12[7:8, :])

        loop_rows(rows, tail, set_out)
        out_copy = pltpu.make_async_copy(dn2, out_ref, osem.at[0])
        out_copy.start()
        for p in range(1, per):
            scatters[1, p].third()
            lines[1, p].start()
        for j in range(count):
            sending(0, j).wait_send()
        out_copy.wait()

    ff = size * unit
    pl.run_scoped(
        mlp,
        pltpu.VMEM((6, width, chunk), BF),
        pltpu.VMEM((rows, ff), BF),
        pltpu.VMEM((rows, ff), BF),
        pltpu.VMEM((rows, width), BF),
        pltpu.VMEM((rows, width), BF),
        pltpu.VMEM((width, rows), BF),
        pltpu.VMEM((2, ab * mrows, rows), BF),
        pltpu.VMEM((per, b_size, a_size, size, mrows, chunk), BF),
        pltpu.VMEM((rows, width), F32),
    )

    def attention(gat, do, dqkv, dk, dv, wg):
        def own_line(k):
            for p in range(per):
                here = held.at[k * per + p, spot.b, spot.a, spot.t]

                def set_row(r):
                    gtot[r, p * chunk:(p + 1) * chunk] = here[r].astype(F32)

                loop_rows(mrows, tile, set_row)

        def line_total(p):
            return lambda ref, h: add_tiled(gtot.at[:, pl.ds(p * chunk, chunk)], ref, tile)

        def line_step(k, p, s):
            third = lines[k, p].count() // 3
            lines[k, p].step(s * third, (s + 1) * third, line_total(p))

        def arrived(t):
            r = pl.ds(pl.multiple_of(t * rows, rows), rows)
            value = gaf[r]
            do[r] = nn(value, wf[3]).astype(BF)
            gat[:, r] = value.T

        dk[...] = jnp.zeros_like(dk)
        dv[...] = jnp.zeros_like(dv)

        half = width // 2

        def norm_grad(i):
            r = pl.ds(pl.multiple_of(i * rows, rows), rows)
            dqkv[1, r] = dk[r].astype(BF)
            dqkv[2, r] = dv[r].astype(BF)
            for first in range(0, width, half):
                cols = slice(first, first + half)
                part[r, cols] = sum(nt(dqkv[j, r], wf[j, cols, :]) for j in range(3)).astype(BF)
            blocks[1].start_traced(i)

        plan = {(1, p, n): n + 1 + p for p in range(per) for n in range(end - 1)}
        plan = {key: at for key, at in plan.items() if at < size}

        def arrive_back(k, carry):
            for n in range(1, size):
                @pl.when(k == n)
                def _():
                    if n == 1 and size > 2:
                        gas.step(2)
                    for key, at in plan.items():
                        if at == n:
                            line_step(*key)
                    if n == end:
                        scatters[0, 0].second()
                        for p in range(1, per):
                            scatters[0, p].first()

            @pl.when(k >= 3)
            def _():
                gas.step(k)

            def side(i, inner):
                t = spot.t + (2 * i - 1) * k

                @pl.when((t >= 0) & (t < size) & ((i == 0) | (k >= 1)))
                def _():
                    arrived(t)

                return inner

            lax.fori_loop(0, 2, side, 0)
            for i in range(size):
                @pl.when((i == spot.t - k) | (i == spot.t + k))
                def _():
                    start, stop = i * rows, (i + 1) * rows
                    block_bias(seg_col, seg_row, bias, start, rows, stop)
                    attend_block_back(qkv, bias, lse, do, dqkv.at[0], dk, dv, start, rows)

            def ready(n, inner):
                i = jnp.where(lax.rem(n, 2) == 0, end - lax.div(n, 2), lax.div(n, 2))

                @pl.when(jnp.maximum(end - spot.t, spot.t - i) == k)
                def _():
                    norm_grad(i)

                return inner

            lax.fori_loop(0, size, ready, 0)
            return carry

        lax.fori_loop(0, size, arrive_back, 0)
        gas.owe()
        blocks[1].owe_starts()
        loop_rows(rows, tail, lambda r: set_total(r))
        own_line(1)
        for p in range(per):
            for n in range(end):
                if (1, p, n) not in plan:
                    line_step(1, p, n)
        downg[...] = gtot[...].T
        stores = fetch([pltpu.make_async_copy(downg, downg_ref, osem.at[1])])
        events = blocks[1].count()
        scatters[0, 0].third()
        lines[0, 0].start()

        def first_norm(r):
            unit_one, _ = norm_stats(xf[r].astype(F32))
            term = part[r].astype(F32)
            sums[0:1, :] += column_sum(term * unit_one)
            sums[2:3, :] += column_sum(term)

        loop_rows(seq, tail, first_norm)
        sums[3:4, column] = column_sum(dqkv[0].astype(F32))
        sums[4:5, column] = column_sum(dqkv[2].astype(F32))
        for d in range(geo.dp):
            spart[d] = sums[:, d * piece:(d + 1) * piece]
        for step in range(1, geo.dp):
            to = ring_next(spot.d, step, geo.dp)
            wire.start(small + step - 1, spart.at[to], sland.at[step - 1], spot.at_d(to))
        stot[...] = spart[spot.d]
        blocks[1].step(0, 4 * events // 8, mid_total)
        for p in range(1, per):
            scatters[0, p].second()

        def wgrad(r):
            for j in range(3):
                wg[j, r] = nn(n1t[r], dqkv[j]).astype(BF)
            wg[3, r] = nn(gat[r], att[...]).astype(BF)

        loop_rows(width, min(256, width), wgrad)

        def wrows_of(i, core):
            return pl.ds(pl.multiple_of((i * 2 + core) * wrows, wrows), wrows)

        for i in range(ab):
            wire.start(wzero + i, wg.at[:, wrows_of(i, 1 - spot.c)], wheld.at[0, i // a_size, i % a_size], sibling)
        blocks[1].step(4 * events // 8, 6 * events // 8, mid_total)
        for p in range(1, per):
            scatters[0, p].third()
            lines[0, p].start()
        own_line(0)
        for i in range(ab):
            here = wheld.at[0, i // a_size, i % a_size]
            wire.landed(wzero + i, here, sibling)
            wscatter.add(here, wg.at[:, wrows_of(i, spot.c)])
        wscatter.first()
        for step in range(1, geo.dp):
            wire.landed(small + step - 1, sland.at[step - 1], spot.at_d(ring_prev(spot.d, step, geo.dp)))
            stot[...] += sland[step - 1]
        for step in range(1, size):
            wire.start(last + step - 1, stot, tland.at[step - 1], spot.at_t(ring_next(spot.t, step, size)))
        blocks[1].step(6 * events // 8, events, mid_total)

        def back(r):
            unit_one, scale_one = norm_stats(xf[own_rows(r, tail)].astype(F32))
            cot[r] = cot[r] + norm_back(mid[r], unit_one, scale_one, rows12[0:1, :])

        loop_rows(rows, tail, back)
        stores += fetch([pltpu.make_async_copy(cot, igrad_ref, osem.at[0])])
        wscatter.second()
        ends = sorted((2 * p + n, p, n) for p in range(per) for n in range(end))
        for _, p, n in ends[:2]:
            line_step(0, p, n)
        wscatter.third()
        sums_w = wheld.at[0, spot.b, spot.a]
        for j in range(3):
            awg[j] = sums_w[j].astype(F32)
        owg[...] = sums_w[3].astype(F32).T
        stores += fetch([
            pltpu.make_async_copy(awg, awg_ref, osem.at[2]),
            pltpu.make_async_copy(owg, owg_ref, osem.at[3])])
        for _, p, n in ends[2:]:
            line_step(0, p, n)
        stores += fetch([pltpu.make_async_copy(gtot, upg_ref, osem.at[6])])
        for step in range(1, size):
            wire.landed(last + step - 1, tland.at[step - 1], spot.at_t(ring_prev(spot.t, step, size)))
        total = stot[...]
        for step in range(1, size):
            total = total + tland[step - 1]
        gaing[...] = total[0:2, :]
        for i in range(biasg.shape[0]):
            biasg[i] = total[2 + i:3 + i, :]
        stores += fetch([
            pltpu.make_async_copy(gaing, gaing_ref, osem.at[4]),
            pltpu.make_async_copy(biasg, biasg_ref, osem.at[5])])
        wire.drain()
        settle(stores)

    pl.run_scoped(
        attention,
        pltpu.VMEM((width, seq), BF),
        pltpu.VMEM((seq, heads), BF),
        pltpu.VMEM((3, seq, heads), BF),
        pltpu.VMEM((seq, heads), F32),
        pltpu.VMEM((seq, heads), F32),
        pltpu.VMEM((4, width, heads), BF),
    )


def block_kernel(geo, x, aw, ow, up, down, gains, biases, seg_row, cot):
    rows, width = x.shape
    wrows, heads = aw.shape[1:]
    mrows, unit = up.shape
    size = geo.tensor
    seq = size * rows
    chunk = min(512, unit)
    per = unit // chunk
    sems = ((2 * per + 1) * (gather_sems(geo) + scatter_sems(geo)) + (size - 1) * (2 * 4 + 2 * 4 + 4 * per * 2 + 1) + 2 * per * size
            + geo.a_size * geo.b_size + 2 * (geo.dp - 1))
    like = lambda x: pltpu.VMEM(x.shape, x.dtype)
    return pl.pallas_call(
        functools.partial(block_body, geo),
        out_shape=(
            jax.ShapeDtypeStruct((2, unit // chunk, size, width, chunk), BF),
            jax.ShapeDtypeStruct((rows, width), F32),
            jax.ShapeDtypeStruct((rows, width), F32),
            jax.ShapeDtypeStruct((3, wrows, heads), F32),
            jax.ShapeDtypeStruct((heads, wrows), F32),
            jax.ShapeDtypeStruct((mrows, unit), F32),
            jax.ShapeDtypeStruct((unit, mrows), F32),
            jax.ShapeDtypeStruct((2, wrows), F32),
            jax.ShapeDtypeStruct((10, 1, wrows), F32),
        ),
        in_specs=[ANY] * 9,
        out_specs=(ANY,) * 9,
        scratch_shapes=[
            pltpu.VMEM((seq, width), BF),
            pltpu.VMEM((rows, width), BF),
            pltpu.VMEM((width, seq), BF),
            pltpu.VMEM((3, seq, heads), BF),
            pltpu.VMEM((seq, heads), BF),
            pltpu.VMEM((seq, 128), F32),
            pltpu.VMEM((4, width, heads), BF),
            pltpu.VMEM((seq, width), BF),
            pltpu.VMEM((2, size - 1, rows, width), BF),
            pltpu.VMEM((rows, seq), F32),
            pltpu.VMEM((rows, width), F32),
            pltpu.VMEM((rows, width), F32),
            pltpu.VMEM((seq, width), BF),
            pltpu.VMEM((12, width), F32),
            pltpu.VMEM((seq, 128), jnp.int32),
            like(seg_row),
            pltpu.VMEM((geo.dp, 12, wrows), F32),
            pltpu.VMEM((4, wrows, heads), BF),
            like(ow), like(down), pltpu.VMEM((2, unit // chunk, mrows, chunk), BF), like(gains), like(biases),
            pltpu.VMEM((12, wrows), F32),
            pltpu.VMEM((12, width), F32),
            pltpu.VMEM((geo.dp, 12, wrows), F32),
            pltpu.VMEM((geo.dp - 1, 12, wrows), F32),
            pltpu.VMEM((12, wrows), F32),
            pltpu.VMEM((size - 1, 12, wrows), F32),
            *scatter_bufs(geo, 2 * (unit // chunk), 2 * (unit // chunk), size, mrows, chunk),
            *scatter_bufs(geo, 1, 1, 4, wrows, heads),
            pltpu.VMEM((2 * (unit // chunk), 2, size - 1, mrows, chunk), BF),
            pltpu.VMEM((mrows, unit), F32),
            pltpu.VMEM((unit, mrows), F32),
            pltpu.VMEM((3, wrows, heads), F32),
            pltpu.VMEM((heads, wrows), F32),
            pltpu.VMEM((2, wrows), F32),
            pltpu.VMEM((10, 1, wrows), F32),
            pltpu.SemaphoreType.DMA((sems,)), pltpu.SemaphoreType.DMA((sems,)), pltpu.SemaphoreType.DMA((8 + unit // chunk,)),
            pltpu.SemaphoreType.DMA((6, 2)), pltpu.SemaphoreType.DMA((7,))],
        compiler_params=pltpu.CompilerParams(collective_id=1, has_side_effects=True, vmem_limit_bytes=62 * 2**20),
        name="block",
    )(x, aw, ow, up, down, gains, biases, seg_row, cot)


def hand_over_body(*refs):
    *refs, loads, stores = refs
    count = len(refs) // 3
    ins, outs, bufs = refs[:count], refs[count:2 * count], refs[2 * count:]
    coming = fetch([pltpu.make_async_copy(ins[i], bufs[i], loads.at[i]) for i in range(count)])
    going = []
    for i in range(count):
        coming[i].wait()
        going += fetch([pltpu.make_async_copy(bufs[i], outs[i], stores.at[i])])
    settle(going)


def hand_over(parts):
    return pl.pallas_call(
        hand_over_body,
        out_shape=tuple(jax.ShapeDtypeStruct(part.shape, part.dtype) for part in parts),
        in_specs=[ANY] * len(parts),
        out_specs=(ANY,) * len(parts),
        scratch_shapes=[pltpu.VMEM(part.shape, part.dtype) for part in parts] + [pltpu.SemaphoreType.DMA((len(parts),))] * 2,
        name="hand_over",
    )(*parts)


def per_device(geo, activations, segments, attn_weight, out_weight, up_weight, down_weight, norm_gains, bias_rows, cotangent):
    outs = block_kernel(
        geo, activations, attn_weight[0], out_weight[0], up_weight[0], down_weight[0], norm_gains[0], bias_rows[0], segments[None, :],
        cotangent)
    outs = hand_over(outs[1:])
    return outs[:2] + tuple(part[None] for part in outs[2:7]) + (outs[7].reshape(1, 10, -1),)


def solution(mesh):
    geo = Geometry(mesh.shape["dp"], mesh.shape["tensor"])
    return jax.shard_map(
        functools.partial(per_device, geo),
        mesh=mesh,
        in_specs=(
            P(("dp", "tensor"), None),
            P("dp"),
            P(None, None, "dp", "tensor"),
            P(None, "tensor", "dp"),
            P(None, "dp", "tensor"),
            P(None, "tensor", "dp"),
            P(None, None, "dp"),
            P(None, None, "dp"),
            P(("dp", "tensor"), None),
        ),
        out_specs=(
            P(("dp", "tensor"), None),
            P(("dp", "tensor"), None),
            P(None, None, "dp", "tensor"),
            P(None, "tensor", "dp"),
            P(None, "dp", "tensor"),
            P(None, "tensor", "dp"),
            P(None, None, "dp"),
            P(None, None, "dp"),
        ),
        check_vma=False,
    )
```

```python
import functools

import jax
import jax.numpy as jnp
from jax import lax
from jax.experimental import pallas as pl
from jax.experimental.pallas import tpu as pltpu
from jax.sharding import PartitionSpec as P

HD = 64
EPSILON = 1e-05
MASKED = -1e30
MESH_ID = pl.DeviceIdType.MESH
BF = jnp.bfloat16
F32 = jnp.float32
ANY = pl.BlockSpec(memory_space=pl.ANY)
VM = pl.BlockSpec(memory_space=pltpu.VMEM)


def layer_norm(values, gain_row, shift_row):
    center = values - jnp.mean(values, axis=-1, keepdims=True)
    spread = jnp.mean(center * center, axis=-1, keepdims=True)
    return center * lax.rsqrt(spread + EPSILON) * gain_row + shift_row


def norm_stats(values):
    center = values - jnp.mean(values, axis=-1, keepdims=True)
    spread = jnp.mean(center * center, axis=-1, keepdims=True)
    scale = lax.rsqrt(spread + EPSILON)
    return center * scale, scale


def norm_back(grad, unit, scale, gain_row):
    u = grad * gain_row
    mean_u = jnp.mean(u, axis=-1, keepdims=True)
    mean_ux = jnp.mean(u * unit, axis=-1, keepdims=True)
    return scale * (u - mean_u - unit * mean_ux)


def gelu_tanh(values):
    return jax.nn.gelu(values, approximate=True)


class Geometry:
    def __init__(self, dp, tensor):
        self.dp, self.tensor = dp, tensor
        self.c_size = 2
        rest = dp // 2
        self.a_size = 1
        while self.a_size * self.a_size < rest:
            self.a_size *= 2
        self.b_size = rest // self.a_size
        assert self.a_size * self.b_size * 2 == dp

    def bind(self):
        spot = Spot()
        spot.geo = self
        spot.d = lax.axis_index("dp")
        spot.t = lax.axis_index("tensor")
        spot.c = lax.rem(spot.d, 2)
        half = lax.div(spot.d, 2)
        spot.a = lax.rem(half, self.a_size)
        spot.b = lax.div(half, self.a_size)
        return spot


class Spot:
    def rank(self, b, a, c):
        return (b * self.geo.a_size + a) * 2 + c

    def at_t(self, t):
        return (self.d, t)

    def at_d(self, d):
        return (d, self.t)


def ring_next(rank, step, size):
    return lax.rem(rank + step, size)


def ring_prev(rank, step, size):
    return lax.rem(rank + size - step, size)


class Wire:
    def __init__(self, send, recv):
        self.send_sems, self.recv_sems = send, recv
        self.count = 0
        self.pending = []

    def take(self, n):
        first = self.count
        self.count += n
        return first

    def copy(self, i, src, dst, device):
        return pltpu.make_async_remote_copy(
            src_ref=src, dst_ref=dst, send_sem=self.send_sems.at[i], recv_sem=self.recv_sems.at[i],
            device_id=device, device_id_type=MESH_ID)

    def plan(self, i, src, dst, device, when=None):
        return self.copy(i, src, dst, device), when

    def go(self, planned):
        copy, when = planned
        if when is None:
            copy.start()
        else:
            pl.when(when)(copy.start)
        self.owe(planned)

    def owe(self, planned):
        if not any(other is planned for other in self.pending):
            self.pending.append(planned)

    def start(self, i, src, dst, device, when=None):
        self.go(self.plan(i, src, dst, device, when))

    def landed(self, i, dst, device, when=None):
        copy = self.copy(i, dst, dst, device)
        if when is None:
            copy.wait_recv()
        else:
            pl.when(when)(copy.wait_recv)

    def sent(self, plans):
        for planned in plans:
            copy, when = planned
            self.pending = [other for other in self.pending if other is not planned]
            if when is None:
                copy.wait_send()
            else:
                pl.when(when)(copy.wait_send)

    def drain(self):
        for copy, when in self.pending:
            if when is None:
                copy.wait_send()
            else:
                pl.when(when)(copy.wait_send)
        self.pending = []


def greet(spot):
    geo = spot.geo
    barrier = pltpu.get_barrier_semaphore()
    total = 0
    for step in range(1, geo.tensor):
        pl.semaphore_signal(barrier, inc=1, device_id=spot.at_t(ring_next(spot.t, step, geo.tensor)), device_id_type=MESH_ID)
        total += 1
    for step in range(1, geo.dp):
        pl.semaphore_signal(barrier, inc=1, device_id=spot.at_d(ring_next(spot.d, step, geo.dp)), device_id_type=MESH_ID)
        total += 1
    return lambda: pl.semaphore_wait(barrier, total)


def halves(ref, count, part):
    rows = ref.shape[-2] // count
    return ref.at[(slice(None),) * (len(ref.shape) - 2) + (pl.ds(part * rows, rows),)]


class LineGather:
    def __init__(self, spot, wire, src, slot, parts=2):
        self.spot, self.wire, self.src, self.slot, self.parts = spot, wire, src, slot, parts
        self.size = size = spot.geo.tensor
        self.base = [wire.take((size - 1) * parts) for _ in range(2)]
        t = spot.t
        self.sends = {}
        for k in range(size - 1):
            for part in range(parts):
                for side in range(2):
                    self.sends[k, part, side] = self.plan(k, part, side)

    def place(self, k, side):
        t = self.spot.t
        origin = t - k if side == 0 else t + k
        there = (origin >= 0) & (origin < self.size)
        onward = t + 1 if side == 0 else t - 1
        return origin, there, t - 1 if side == 0 else t + 1, onward, there & (onward >= 0) & (onward < self.size)

    def plan(self, k, part, side):
        origin, _, _, onward, going = self.place(k, side)
        piece = halves(self.slot(origin), self.parts, part)
        first = isinstance(k, int) and k == 0
        src = halves(self.src, self.parts, part) if first else piece
        return self.wire.plan(self.base[side] + k * self.parts + part, src, piece, self.spot.at_t(onward), when=going)

    def start(self):
        for part in range(self.parts):
            for side in range(2):
                self.wire.go(self.sends[0, part, side])

    def step(self, k):
        for part in range(self.parts):
            for side in range(2):
                origin, there, near, _, _ = self.place(k, side)
                piece = halves(self.slot(origin), self.parts, part)
                self.wire.landed(self.base[side] + (k - 1) * self.parts + part, piece, self.spot.at_t(near), when=there)
                if not isinstance(k, int):
                    copy, going = self.plan(k, part, side)
                    pl.when(going & (k < self.size - 1))(copy.start)
                elif k < self.size - 1:
                    self.wire.go(self.sends[k, part, side])

    def owe(self):
        for (k, part, side), planned in self.sends.items():
            if k > 0:
                self.wire.owe(planned)


class LineScatter:
    def __init__(self, spot, wire, part, land, add, rising=None, parts=2):
        self.spot, self.wire, self.part, self.land, self.add, self.parts = spot, wire, part, land, add, parts
        self.size = spot.geo.tensor
        base = self.base = [wire.take((self.size - 1) * parts) for _ in range(2)]
        t, end = spot.t, self.size - 1
        self.starts, self.hops = {}, {}
        for h in range(parts):
            for j in range(self.size):
                if j > 0:
                    self.starts[0, j, h] = wire.plan(
                        base[0] + (j - 1) * parts + h, halves(part(j), parts, h), halves(land(0, j), parts, h), spot.at_t(1), when=t == 0)
                if j < end:
                    self.starts[1, j, h] = wire.plan(
                        base[1] + j * parts + h, halves(part(j), parts, h), halves(land(1, j), parts, h), spot.at_t(end - 1), when=t == end)
        self.events = []
        for side in range(2):
            place = t if side == 0 else end - t
            if side == rising:
                for e in range(1, 2 * end):
                    far = e + 1 - place
                    self.events.append((10 * e, side, far if side == 0 else end - far, (place >= 1) & (far >= place) & (far <= end)))
            else:
                for s in range(1, self.size):
                    far = end - s + place
                    at = 10 * s + (0 if rising is None else 15)
                    self.events.append((at, side, far if side == 0 else end - far, (place >= 1) & (s >= place)))
        self.events.sort(key=lambda event: event[0])
        self.hops = []
        for _, side, j, here in self.events:
            near = spot.at_t(t - 1 if side == 0 else t + 1)
            away = spot.at_t(t + 1 if side == 0 else t - 1)
            for h in range(parts):
                held = halves(land(side, j), parts, h)
                i = base[side] + (j - 1 + side) * parts + h
                self.hops.append((here & (j == t), here & (j != t), j, h, held, wire.copy(i, held, held, near),
                                  wire.plan(i, held, held, away, when=here & (j != t))))

    def start_block(self, j):
        for side in range(2):
            for h in range(self.parts):
                if (side, j, h) in self.starts:
                    self.wire.go(self.starts[side, j, h])

    def start_traced(self, j):
        spot, t, end = self.spot, self.spot.t, self.size - 1
        for side in range(2):
            first, to = (0, 1) if side == 0 else (end, end - 1)
            for h in range(self.parts):
                copy, when = self.wire.plan(
                    self.base[side] + (j - 1 + side) * self.parts + h, halves(self.part(j), self.parts, h),
                    halves(self.land(side, j), self.parts, h), spot.at_t(to), when=(t == first) & (j != first) & (j != 1 if side == 0 else True))
                pl.when(when)(copy.start)

    def start_near(self):
        for h in range(self.parts):
            self.wire.go(self.starts[0, 1, h])

    def owe_starts(self):
        for planned in self.starts.values():
            self.wire.owe(planned)

    def start(self):
        for n in range(self.size):
            for side, j in ((0, self.size - 1 - n), (1, n)):
                for h in range(self.parts):
                    if (side, j, h) in self.starts:
                        self.wire.go(self.starts[side, j, h])

    def count(self):
        return len(self.hops)

    def step(self, first, last, total):
        for final, passing, j, h, held, landing, onward in self.hops[first:last]:
            @pl.when(final)
            def _():
                landing.wait_recv()
                total(held, h)

            @pl.when(passing)
            def _():
                landing.wait_recv()
                self.add(held, halves(self.part(j), self.parts, h))

            self.wire.go(onward)

    def plans(self):
        return list(self.starts.values()) + [hop[-1] for hop in self.hops]


def add_tiled(dst, src, tile):
    def step(i, carry):
        rows = pl.ds(pl.multiple_of(i * tile, tile), tile)
        dst[rows] = (dst[rows].astype(F32) + src[rows].astype(F32)).astype(dst.dtype)
        return carry

    lax.fori_loop(0, dst.shape[0] // tile, step, 0)


class WeightGather:
    def __init__(self, spot, wire, rows, full):
        geo = spot.geo
        self.spot, self.wire, self.full, self.rows = spot, wire, full, rows
        self.slots = full.shape[0]
        self.half = self.slots // 2
        self.one_a = wire.take(geo.a_size - 1)
        self.one_b = wire.take(geo.b_size - 1)
        self.two_a = wire.take((geo.b_size - 1) * geo.a_size)
        self.two_b = wire.take((geo.a_size - 1) * geo.b_size)
        self.last = wire.take(2 * geo.a_size * geo.b_size)
        self.plan_shares()
        self.plan_hops()

    def span(self, d):
        return pl.ds(pl.multiple_of(d * self.rows, self.rows), self.rows)

    def low(self, d):
        return self.full.at[pl.ds(0, self.half), self.span(d)]

    def high(self, d):
        return self.full.at[pl.ds(self.half, self.slots - self.half), self.span(d)]

    def plan_shares(self):
        spot, geo = self.spot, self.spot.geo
        self.shares = {}
        for j in range(geo.b_size):
            for i in range(geo.a_size):
                held = spot.rank(ring_prev(spot.b, j, geo.b_size), ring_prev(spot.a, i, geo.a_size), spot.c)
                sibling = spot.rank(spot.b, spot.a, 1 - spot.c)
                for part in range(2):
                    half = (self.low, self.high)[part](held)
                    self.shares[part, j, i] = self.wire.plan(
                        self.last + 2 * (j * geo.a_size + i) + part, half, half, spot.at_d(sibling))

    def share(self, part, j, i):
        self.wire.go(self.shares[part, j, i])

    def plan_hops(self):
        spot, geo, wire = self.spot, self.spot.geo, self.wire
        self.ones, self.twos_a, self.twos_b = [], {}, {}
        mine = spot.d
        for j in range(1, geo.a_size):
            to = spot.rank(spot.b, ring_next(spot.a, j, geo.a_size), spot.c)
            self.ones.append(wire.plan(self.one_a + j - 1, self.low(mine), self.low(mine), spot.at_d(to)))
        for j in range(1, geo.b_size):
            to = spot.rank(ring_next(spot.b, j, geo.b_size), spot.a, spot.c)
            self.ones.append(wire.plan(self.one_b + j - 1, self.high(mine), self.high(mine), spot.at_d(to)))
        for i in range(geo.a_size):
            held = spot.rank(spot.b, ring_prev(spot.a, i, geo.a_size), spot.c)
            for j in range(1, geo.b_size):
                to = spot.rank(ring_next(spot.b, j, geo.b_size), spot.a, spot.c)
                self.twos_a[i, j] = wire.plan(self.two_a + (j - 1) * geo.a_size + i, self.low(held), self.low(held), spot.at_d(to))
        for i in range(geo.b_size):
            held = spot.rank(ring_prev(spot.b, i, geo.b_size), spot.a, spot.c)
            for j in range(1, geo.a_size):
                to = spot.rank(spot.b, ring_next(spot.a, j, geo.a_size), spot.c)
                self.twos_b[i, j] = wire.plan(self.two_b + (j - 1) * geo.b_size + i, self.high(held), self.high(held), spot.at_d(to))

    def first(self):
        for planned in self.ones:
            self.wire.go(planned)
        self.share(0, 0, 0)
        self.share(1, 0, 0)

    def second(self):
        spot, geo = self.spot, self.spot.geo
        for i in range(geo.a_size):
            held = spot.rank(spot.b, ring_prev(spot.a, i, geo.a_size), spot.c)
            if i:
                self.wire.landed(self.one_a + i - 1, self.low(held), spot.at_d(held))
                self.share(0, 0, i)
            for j in range(1, geo.b_size):
                self.wire.go(self.twos_a[i, j])
        for i in range(geo.b_size):
            held = spot.rank(ring_prev(spot.b, i, geo.b_size), spot.a, spot.c)
            if i:
                self.wire.landed(self.one_b + i - 1, self.high(held), spot.at_d(held))
                self.share(1, i, 0)
            for j in range(1, geo.a_size):
                self.wire.go(self.twos_b[i, j])

    def third(self):
        spot, geo = self.spot, self.spot.geo
        for j in range(1, geo.b_size):
            for i in range(geo.a_size):
                held = spot.rank(ring_prev(spot.b, j, geo.b_size), ring_prev(spot.a, i, geo.a_size), spot.c)
                source = spot.rank(ring_prev(spot.b, j, geo.b_size), spot.a, spot.c)
                self.wire.landed(self.two_a + (j - 1) * geo.a_size + i, self.low(held), spot.at_d(source))
                self.share(0, j, i)
        for j in range(1, geo.a_size):
            for i in range(geo.b_size):
                held = spot.rank(ring_prev(spot.b, i, geo.b_size), ring_prev(spot.a, j, geo.a_size), spot.c)
                source = spot.rank(spot.b, ring_prev(spot.a, j, geo.a_size), spot.c)
                self.wire.landed(self.two_b + (j - 1) * geo.b_size + i, self.high(held), spot.at_d(source))
                self.share(1, i, j)

    def fourth(self):
        spot, geo = self.spot, self.spot.geo
        sibling = spot.rank(spot.b, spot.a, 1 - spot.c)
        for j in range(geo.b_size):
            for i in range(geo.a_size):
                held = spot.rank(ring_prev(spot.b, j, geo.b_size), ring_prev(spot.a, i, geo.a_size), 1 - spot.c)
                for part in range(2):
                    half = (self.low, self.high)[part](held)
                    self.wire.landed(self.last + 2 * (j * geo.a_size + i) + part, half, spot.at_d(sibling))


def gather_sems(geo):
    return geo.a_size + geo.b_size - 2 + (geo.b_size - 1) * geo.a_size + (geo.a_size - 1) * geo.b_size + 2 * geo.a_size * geo.b_size


class WeightScatter:
    def __init__(self, spot, wire, held, one_a, one_b, two_a, two_b):
        geo = spot.geo
        self.spot, self.wire, self.held = spot, wire, held
        self.one_a_buf, self.one_b_buf, self.two_a_buf, self.two_b_buf = one_a, one_b, two_a, two_b
        self.slots, self.rows = held.shape[2], held.shape[3]
        self.half = self.slots // 2
        self.one_a = wire.take(geo.a_size - 1)
        self.one_b = wire.take(geo.b_size - 1)
        self.two_a = wire.take(geo.b_size - 1)
        self.two_b = wire.take(geo.a_size - 1)
        low, high = pl.ds(0, self.half), pl.ds(self.half, self.half)
        self.sends = []
        for j in range(1, geo.a_size):
            a = ring_next(spot.a, j, geo.a_size)
            self.sends.append(wire.plan(self.one_a + j - 1, held.at[:, a, low], one_a.at[j - 1], spot.at_d(spot.rank(spot.b, a, spot.c))))
        for j in range(1, geo.b_size):
            b = ring_next(spot.b, j, geo.b_size)
            self.sends.append(wire.plan(self.one_b + j - 1, held.at[b, :, high], one_b.at[j - 1], spot.at_d(spot.rank(b, spot.a, spot.c))))
        self.later = []
        for j in range(1, geo.b_size):
            b = ring_next(spot.b, j, geo.b_size)
            self.later.append(wire.plan(self.two_a + j - 1, held.at[b, spot.a, low], two_a.at[j - 1], spot.at_d(spot.rank(b, spot.a, spot.c))))
        for j in range(1, geo.a_size):
            a = ring_next(spot.a, j, geo.a_size)
            self.later.append(wire.plan(self.two_b + j - 1, held.at[spot.b, a, high], two_b.at[j - 1], spot.at_d(spot.rank(spot.b, a, spot.c))))

    def add(self, dst, src):
        tile = min(64, self.rows)
        per = self.rows // tile

        def step(i, carry):
            rows = pl.ds(pl.multiple_of(lax.rem(i, per) * tile, tile), tile)
            j = lax.div(i, per)
            dst[j, rows] = (dst[j, rows].astype(F32) + src[j, rows].astype(F32)).astype(dst.dtype)
            return carry

        lax.fori_loop(0, dst.shape[0] * per, step, 0)

    def first(self):
        for planned in self.sends:
            self.wire.go(planned)

    def second(self):
        spot, geo = self.spot, self.spot.geo
        low, high = pl.ds(0, self.half), pl.ds(self.half, self.half)
        for j in range(1, geo.a_size):
            self.wire.landed(self.one_a + j - 1, self.one_a_buf.at[j - 1], spot.at_d(spot.rank(spot.b, ring_prev(spot.a, j, geo.a_size), spot.c)))
            for b in range(geo.b_size):
                self.add(self.held.at[b, spot.a, low], self.one_a_buf.at[j - 1, b])
        for j in range(1, geo.b_size):
            self.wire.landed(self.one_b + j - 1, self.one_b_buf.at[j - 1], spot.at_d(spot.rank(ring_prev(spot.b, j, geo.b_size), spot.a, spot.c)))
            for a in range(geo.a_size):
                self.add(self.held.at[spot.b, a, high], self.one_b_buf.at[j - 1, a])
        for planned in self.later:
            self.wire.go(planned)

    def third(self):
        spot, geo = self.spot, self.spot.geo
        low, high = pl.ds(0, self.half), pl.ds(self.half, self.half)
        for j in range(1, geo.b_size):
            self.wire.landed(self.two_a + j - 1, self.two_a_buf.at[j - 1], spot.at_d(spot.rank(ring_prev(spot.b, j, geo.b_size), spot.a, spot.c)))
            self.add(self.held.at[spot.b, spot.a, low], self.two_a_buf.at[j - 1])
        for j in range(1, geo.a_size):
            self.wire.landed(self.two_b + j - 1, self.two_b_buf.at[j - 1], spot.at_d(spot.rank(spot.b, ring_prev(spot.a, j, geo.a_size), spot.c)))
            self.add(self.held.at[spot.b, spot.a, high], self.two_b_buf.at[j - 1])


def scatter_sems(geo):
    return 2 * (geo.a_size + geo.b_size - 2)


def scatter_bufs(geo, n, sets, slots, rows, width):
    a, b, half = geo.a_size, geo.b_size, slots // 2
    return [
        pltpu.VMEM((n, b, a, slots, rows, width), BF),
        pltpu.VMEM((sets, a - 1, b, half, rows, width), BF),
        pltpu.VMEM((sets, b - 1, a, half, rows, width), BF),
        pltpu.VMEM((sets, b - 1, half, rows, width), BF),
        pltpu.VMEM((sets, a - 1, half, rows, width), BF),
    ]


def loop_rows(count, tile, body, start=0):
    def step(i, carry):
        body(pl.ds(pl.multiple_of(start + i * tile, tile), tile))
        return carry

    lax.fori_loop(0, count // tile, step, 0)


def fetch(copies):
    for copy in copies:
        copy.start()
    return copies


def settle(copies):
    for copy in copies:
        copy.wait()


PAIR = 2 * HD


def nt(x, w):
    return lax.dot_general(x, w, (((1,), (1,)), ((), ())), preferred_element_type=F32)


def nn(x, w):
    return lax.dot_general(x, w, (((1,), (0,)), ((), ())), preferred_element_type=F32)


def tn(x, w):
    return lax.dot_general(x, w, (((0,), (0,)), ((), ())), preferred_element_type=F32)


def block_bias(seg_col, seg_row, bias, start, rows, keys):
    query = seg_col[start:start + rows, 0:1]
    for first in range(0, keys, rows):
        key = seg_row[:, first:first + rows]
        seen = query == key
        if first + rows > start:
            q_pos = start + lax.broadcasted_iota(jnp.int32, (rows, rows), 0)
            k_pos = first + lax.broadcasted_iota(jnp.int32, (rows, rows), 1)
            seen = seen & (k_pos <= q_pos)
        bias[:, first:first + rows] = jnp.where(seen, 0.0, MASKED).astype(F32)


def one_head(pair, head):
    lane = lax.broadcasted_iota(jnp.int32, pair.shape, 1)
    return jnp.where((lane < HD) if head == 0 else (lane >= HD), pair, jnp.zeros_like(pair))


def attend_block(qkv, bias, att, lse, start, rows):
    keys = start + rows
    width = qkv.shape[2]
    stat_lane = lax.broadcasted_iota(jnp.int32, (rows, 128), 1)
    stats = jnp.zeros((rows, 128), F32)
    for p in range(width // PAIR):
        lanes = slice(p * PAIR, (p + 1) * PAIR)
        query = qkv[0, start:keys, lanes]
        outs = []
        for head in range(2):
            s = nt(one_head(query, head), qkv[1, 0:keys, lanes]) + bias[:, 0:keys]
            top = jnp.max(s, axis=1, keepdims=True)
            e = jnp.exp(s - top)
            total = jnp.sum(e, axis=1, keepdims=True)
            prob = (e * (1.0 / total)).astype(BF)
            outs.append(nn(prob, qkv[2, 0:keys, lanes]))
            stats = jnp.where(stat_lane == 2 * p + head, top + jnp.log(total), stats)
        lane = lax.broadcasted_iota(jnp.int32, outs[0].shape, 1)
        att[start:keys, lanes] = jnp.where(lane < HD, outs[0], outs[1]).astype(BF)
    lse[start:keys, :] = stats


def attend_block_back(qkv, bias, lse, do, dq, dk, dv, start, rows):
    keys = start + rows
    width = qkv.shape[2]
    stat_lane = lax.broadcasted_iota(jnp.int32, (rows, 128), 1)
    stats = lse[start:keys, :]
    for p in range(width // PAIR):
        lanes = slice(p * PAIR, (p + 1) * PAIR)
        query = qkv[0, start:keys, lanes]
        grad = do[start:keys, lanes]
        dqs, dks, dvs = [], [], []
        for head in range(2):
            level = jnp.sum(jnp.where(stat_lane == 2 * p + head, stats, 0.0), axis=1, keepdims=True)
            s = nt(one_head(query, head), qkv[1, 0:keys, lanes]) + bias[:, 0:keys]
            prob = jnp.exp(s - level)
            d_prob = nt(one_head(grad, head), qkv[2, 0:keys, lanes])
            mixed = prob * d_prob
            ds = (mixed - prob * jnp.sum(mixed, axis=1, keepdims=True)).astype(BF)
            dqs.append(nn(ds, qkv[1, 0:keys, lanes]))
            dks.append(tn(ds, query))
            dvs.append(tn(prob.astype(BF), grad))
        lane = lax.broadcasted_iota(jnp.int32, dqs[0].shape, 1)
        dq[start:keys, lanes] = (jnp.where(lane < HD, dqs[0], dqs[1]) * (HD ** -0.5)).astype(dq.dtype)
        lane = lax.broadcasted_iota(jnp.int32, dks[0].shape, 1)
        dk[0:keys, lanes] += jnp.where(lane < HD, dks[0], dks[1])
        dv[0:keys, lanes] += jnp.where(lane < HD, dvs[0], dvs[1])


GELU_C = 0.7978845608028654


def gelu_parts(a):
    square = a * a
    tanh = jnp.tanh(GELU_C * a * (1.0 + 0.044715 * square))
    half = 0.5 * (1.0 + tanh)
    slope = half + 0.5 * a * (1.0 - tanh * tanh) * (GELU_C * (1.0 + 3 * 0.044715 * square))
    return a * half, slope


def column_sum(values):
    return jnp.sum(values, axis=0, keepdims=True)


def block_body(geo, x_ref, aw_ref, ow_ref, up_ref, down_ref, gain_ref, bias_ref, seg_ref, cot_ref,
               full, out_ref, igrad_ref, awg_ref, owg_ref, upg_ref, downg_ref, gaing_ref, biasg_ref,
               xf, n1, n1t, qkv, att, lse, wf, part, land, bias, mid, cot, gaf, rows12, seg_col, seg_row,
               sf, wsend, ow_in, down_in, msend, gain_in, bias_in, ssend,
               sums, spart, sland, stot, tland,
               held, one_a, one_b, two_a, two_b, wheld, wone_a, wone_b, wtwo_a, wtwo_b, mland,
               gtot, downg, awg, owg, gaing, biasg,
               send, recv, local, msem, osem):
    spot = geo.bind()
    wire = Wire(send, recv)
    size = geo.tensor
    rows, width = x_ref.shape
    seq = size * rows
    wrows, heads = aw_ref.shape[1:]
    mrows, unit = up_ref.shape
    a_size, b_size = geo.a_size, geo.b_size
    ab = a_size * b_size
    chunk = min(512, unit)
    per = unit // chunk
    pieces = msem.shape[1]
    count = size * per
    tail = min(64, rows)
    tile = min(64, mrows)
    end = size - 1
    sibling = spot.at_d(spot.rank(spot.b, spot.a, 1 - spot.c))
    wspan = pl.ds(pl.multiple_of(spot.d * wrows, wrows), wrows)
    mspan = pl.ds(pl.multiple_of(spot.d * mrows, mrows), mrows)
    column = pl.ds(pl.multiple_of(spot.t * heads, 128), heads)

    def block_of(ref, t):
        return ref.at[pl.ds(pl.multiple_of(t * rows, rows), rows)]

    def own_rows(r, n):
        return pl.ds(pl.multiple_of(spot.t * rows + r.start, n), n)

    weights = WeightGather(spot, wire, wrows, wf)
    halved = [(k, p) for k in range(2) for p in range(per)]
    wlines, gathers = {}, {}
    for k, p in halved:
        wlines[k, p] = LineGather(spot, wire, msend.at[k, p], lambda t, k=k, p=p: full.at[k, p, t, mspan], parts=1)
        gathers[k, p] = WeightGather(spot, wire, mrows, full.at[k, p])
    xs = LineGather(spot, wire, x_ref, lambda t: block_of(xf, t))
    gas = LineGather(spot, wire, block_of(gaf, spot.t), lambda t: block_of(gaf, t))
    blocks = [
        LineScatter(spot, wire, lambda t: block_of(part, t), lambda side, j: land.at[side, j - 1 + side],
                    lambda dst, src: add_tiled(dst, src, tail), rising=k) for k in range(2)]
    scatters, lines = {}, {}

    def line_of(k, p):
        here = held.at[k * per + p, spot.b, spot.a]
        return LineScatter(spot, wire, lambda t: here.at[t], lambda side, j: mland.at[k * per + p, side, j - 1 + side],
                           lambda dst, src: add_tiled(dst, src, tile), parts=1)

    for k, p in halved:
        scatters[k, p] = WeightScatter(spot, wire, held.at[k * per + p], *(buf.at[k * per + p] for buf in (one_a, one_b, two_a, two_b)))
        lines[k, p] = line_of(k, p)
    wscatter = WeightScatter(spot, wire, wheld.at[0], wone_a.at[0], wone_b.at[0], wtwo_a.at[0], wtwo_b.at[0])
    zero = [wire.take(count) for _ in range(2)]
    wzero = wire.take(ab)
    gains_in = wire.take(geo.dp - 1)
    small = wire.take(geo.dp - 1)
    last = wire.take(size - 1)
    assert wire.count == send.shape[0]

    pairs = [
        (gain_ref, gain_in), (bias_ref, bias_in), (aw_ref, wsend.at[pl.ds(0, 3)]), (ow_ref, ow_in),
        (x_ref, block_of(xf, spot.t)), (down_ref, down_in), (seg_ref, seg_row), (cot_ref, cot)]
    pairs += [(up_ref.at[:, pl.ds(i * chunk, chunk)], msend.at[0, i]) for i in range(per)]
    loads = fetch([pltpu.make_async_copy(src, dst, local.at[i]) for i, (src, dst) in enumerate(pairs)])
    met = greet(spot)
    sums[...] = jnp.zeros_like(sums)
    settle(loads[0:4])
    ssend[0:2, :] = gain_in[...].astype(F32)
    ssend[2:12, :] = bias_in[...].astype(F32)
    sf[spot.d] = ssend[...]
    wsend[3] = ow_in[...].T
    wf[:, wspan] = wsend[...]
    settle(loads[8:])

    def store(k):
        return pltpu.make_async_copy(msend.at[k], full.at[k, :, spot.t, mspan], osem.at[k])

    store(0).start()
    met()
    for p in range(per):
        wlines[0, p].start()
    for step in range(1, geo.dp):
        wire.start(gains_in + step - 1, ssend, sf.at[spot.d], spot.at_d(ring_next(spot.d, step, geo.dp)))
    weights.first()
    loads[5].wait()
    for i in range(per):
        msend[1, i] = down_in[i * chunk:(i + 1) * chunk, :].T
    store(1).start()
    for k in range(1, end):
        for p in range(per):
            wlines[0, p].step(k)
        if k == 1:
            weights.second()
    xs.start()
    weights.third()
    store(0).wait()
    for p in range(per):
        wlines[0, p].step(end)
        gathers[0, p].first()
    for step in range(1, geo.dp):
        source = ring_prev(spot.d, step, geo.dp)
        wire.landed(gains_in + step - 1, sf.at[source], spot.at_d(source))
    piece = ssend.shape[1]
    for d in range(geo.dp):
        rows12[:, d * piece:(d + 1) * piece] = sf[d]
    loads[6].wait()
    seg_col[...] = jnp.broadcast_to(seg_row[...], (128, seq)).T
    weights.fourth()
    loads[4].wait()

    def project(t):
        def norm(r):
            source = pl.ds(pl.multiple_of(t * rows + r.start, tail), tail)
            n1[r] = layer_norm(xf[source].astype(F32), rows12[0:1, :], rows12[2:3, :]).astype(BF)

        loop_rows(rows, tail, norm)
        r = pl.ds(pl.multiple_of(t * rows, rows), rows)
        normed = n1[...]
        n1t[:, r] = normed.T
        qkv[0, r] = ((nn(normed, wf[0]) + rows12[3:4, column]).astype(BF).astype(F32) * HD ** -0.5).astype(BF)
        qkv[1, r] = nn(normed, wf[1]).astype(BF)
        qkv[2, r] = (nn(normed, wf[2]) + rows12[4:5, column]).astype(BF)

    def arrive(k, carry):
        @pl.when(k >= 1)
        def _():
            xs.step(k)

        @pl.when(k == end - 1)
        def _():
            for p in range(per):
                wlines[1, p].start()

        def side(i, inner):
            t = spot.t + (2 * i - 1) * k

            @pl.when((t >= 0) & (t < size) & ((i == 0) | (k >= 1)))
            def _():
                project(t)

            return inner

        lax.fori_loop(0, 2, side, 0)

        @pl.when(k == 1)
        def _():
            for p in range(per):
                gathers[0, p].second()

        for i in range(size):
            start = i * rows

            @pl.when(jnp.maximum(spot.t, i - spot.t) == k)
            def _():
                block_bias(seg_col, seg_row, bias, start, rows, start + rows)
                attend_block(qkv, bias, att, lse, start, rows)
                part[start:start + rows, :] = nt(att[start:start + rows, :], wf[3]).astype(BF)
                blocks[0].start_block(i)

        return carry

    lax.fori_loop(0, size, arrive, 0)
    xs.owe()
    for k in range(1, end):
        for p in range(per):
            wlines[1, p].step(k)
        if k == 1:
            for p in range(per):
                gathers[0, p].third()
    store(1).wait()
    for p in range(per):
        wlines[1, p].step(end)
        gathers[1, p].first()
    def set_total(r):
        mid[r] = part[own_rows(r, tail)].astype(F32)

    loop_rows(rows, tail, set_total)

    def mid_total(ref, h):
        n = ref.shape[0]
        add_tiled(mid.at[pl.ds(h * n, n)], ref, tail)

    events = blocks[0].count()
    blocks[0].step(0, 3 * events // 8, mid_total)
    gathers[1, 0].second()
    blocks[0].step(3 * events // 8, 5 * events // 8, mid_total)
    for p in range(per):
        gathers[0, p].fourth()
    for p in range(1, per):
        gathers[1, p].second()
    blocks[0].step(5 * events // 8, events, mid_total)

    def mlp(mbuf, hmid, da, n2, gm, turned, left, snd, dn2):
        def cols_of(j):
            return pl.ds(pl.multiple_of(unit_of(j) * chunk, chunk), chunk)

        def unit_of(j):
            return lax.rem(j, size) * per + lax.div(j, size)

        def mload(k, j, s):
            n = width // pieces
            return [
                pltpu.make_async_copy(
                    full.at[k, lax.div(j, size), lax.rem(j, size), pl.ds(i * n, n)], mbuf.at[s, pl.ds(i * n, n)], msem.at[s, i])
                for i in range(pieces)]

        def depth(which):
            return mbuf.shape[0] // len(which)

        def ahead(which):
            for j in range(min(depth(which) - 1, count)):
                for n, k in enumerate(which):
                    fetch(mload(k, j, j * len(which) + n))

        def streamed(which, body, first=0, stop=count):
            deep = depth(which)

            def one(j, carry):
                slots = [lax.rem(j, deep) * len(which) + n for n in range(len(which))]
                for n, k in enumerate(which):
                    settle(mload(k, j, slots[n]))

                @pl.when(j + deep - 1 < count)
                def _():
                    for n, k in enumerate(which):
                        fetch(mload(k, j + deep - 1, lax.rem(j + deep - 1, deep) * len(which) + n))

                body(j, *slots)
                return carry

            lax.fori_loop(first, stop, one, 0)

        ahead((0,))
        loads[7].wait()

        def norm(r):
            value = xf[own_rows(r, tail)].astype(F32) + (mid[r] + rows12[5:6, :])
            mid[r] = value
            n2[r] = layer_norm(value, rows12[1:2, :], rows12[6:7, :]).astype(BF)
            branch = cot[r].astype(BF)
            gm[r] = branch
            sums[7:8, :] += column_sum(branch.astype(F32))

        loop_rows(rows, tail, norm)

        def turn(value):
            turned[...] = value[...].T
            for i in range(ab):
                for other in range(2):
                    core = lax.rem(spot.c + other, 2)
                    left[other, i * mrows:(i + 1) * mrows, :] = turned[pl.ds(pl.multiple_of((i * 2 + core) * mrows, mrows), mrows), :]

        turn(gm)

        def sending(k, j):
            p, t = lax.div(j, size), lax.rem(j, size)
            return wire.copy(zero[k] + j, snd.at[p, :, :, t], held.at[k * per + p, :, :, t], sibling)

        def give(k, j, right):
            product = nn(left[1], right).astype(BF)
            p, t = lax.div(j, size), lax.rem(j, size)
            for i in range(ab):
                snd[p, i // a_size, i % a_size, t] = product[i * mrows:(i + 1) * mrows, :]
            sending(k, j).start()

        def keep(k, j, right):
            p, t = lax.div(j, size), lax.rem(j, size)
            product = nn(left[0], right)
            sending(k, j).wait_recv()
            for i in range(ab):
                b, a = i // a_size, i % a_size
                held[k * per + p, b, a, t] = (
                    held[k * per + p, b, a, t].astype(F32) + product[i * mrows:(i + 1) * mrows, :]).astype(BF)

        def hidden(j, s):
            cols = cols_of(j)
            row = pl.ds(8 + lax.div(unit_of(j) * chunk, width), 1)
            bcols = pl.ds(pl.multiple_of(lax.rem(unit_of(j) * chunk, width), chunk), chunk)
            value, slope = gelu_parts(nn(n2[...], mbuf[s]) + rows12[row, bcols])
            active = value.astype(BF)
            hmid[:, cols] = active
            da[:, cols] = slope.astype(BF)
            give(1, j, active)

        def keep_down(j, carry):
            keep(1, j, hmid[:, cols_of(j)])
            return carry

        for p in range(per):
            streamed((0,), hidden, p * size, (p + 1) * size)
            gathers[1, p].third()
            lax.fori_loop(p * size, (p + 1) * size, keep_down, 0)
            scatters[1, p].first()
        for p in range(per):
            gathers[1, p].fourth()
        ahead((0, 1))
        dn2[...] = jnp.zeros_like(dn2)

        def hidden_back(j, s, s_down):
            cols = cols_of(j)
            row = pl.ds(8 + lax.div(unit_of(j) * chunk, width), 1)
            bcols = pl.ds(pl.multiple_of(lax.rem(unit_of(j) * chunk, width), chunk), chunk)
            grad = (nn(gm[...], mbuf[s_down]) * da[:, cols].astype(F32)).astype(BF)
            da[:, cols] = grad
            sums[row, bcols] = column_sum(grad.astype(F32))
            dn2[...] += nt(grad, mbuf[s])

        streamed((0, 1), hidden_back)

        def back(r):
            value = mid[r]
            unit_two, scale_two = norm_stats(value)
            grad = dn2[r]
            total = cot[r] + norm_back(grad, unit_two, scale_two, rows12[1:2, :])
            cot[r] = total
            branch = total.astype(BF)
            gaf[own_rows(r, tail)] = branch
            sums[1:2, :] += column_sum(grad * unit_two)
            sums[6:7, :] += column_sum(grad)
            sums[5:6, :] += column_sum(branch.astype(F32))

        loop_rows(rows, tail, back)
        wire.sent(blocks[0].plans())
        gas.start()
        turn(n2)
        def give_up(j, carry):
            sending(1, j).wait_send()
            give(0, j, da[:, cols_of(j)])
            return carry

        lax.fori_loop(0, count, give_up, 0)
        scatters[1, 0].second()

        def keep_up(j, carry):
            keep(0, j, da[:, cols_of(j)])
            return carry

        for p in range(per):
            lax.fori_loop(p * size, (p + 1) * size, keep_up, 0)
            if p:
                scatters[1, p].second()
        ahead((1,))
        gas.step(1)
        scatters[1, 0].third()
        lines[1, 0].start()
        scatters[0, 0].first()
        dn2[...] = jnp.zeros_like(dn2)

        def output(j, s):
            dn2[...] += nt(hmid[:, cols_of(j)], mbuf[s])

        streamed((1,), output)

        def set_out(r):
            dn2[r] = mid[r] + (dn2[r] + rows12[7:8, :])

        loop_rows(rows, tail, set_out)
        out_copy = pltpu.make_async_copy(dn2, out_ref, osem.at[0])
        out_copy.start()
        for p in range(1, per):
            scatters[1, p].third()
            lines[1, p].start()
        for j in range(count):
            sending(0, j).wait_send()
        out_copy.wait()

    ff = size * unit
    pl.run_scoped(
        mlp,
        pltpu.VMEM((6, width, chunk), BF),
        pltpu.VMEM((rows, ff), BF),
        pltpu.VMEM((rows, ff), BF),
        pltpu.VMEM((rows, width), BF),
        pltpu.VMEM((rows, width), BF),
        pltpu.VMEM((width, rows), BF),
        pltpu.VMEM((2, ab * mrows, rows), BF),
        pltpu.VMEM((per, b_size, a_size, size, mrows, chunk), BF),
        pltpu.VMEM((rows, width), F32),
    )

    def attention(gat, do, dqkv, dk, dv, wg):
        def own_line(k):
            for p in range(per):
                here = held.at[k * per + p, spot.b, spot.a, spot.t]

                def set_row(r):
                    gtot[r, p * chunk:(p + 1) * chunk] = here[r].astype(F32)

                loop_rows(mrows, tile, set_row)

        def line_total(p):
            return lambda ref, h: add_tiled(gtot.at[:, pl.ds(p * chunk, chunk)], ref, tile)

        def line_step(k, p, s):
            third = lines[k, p].count() // 3
            lines[k, p].step(s * third, (s + 1) * third, line_total(p))

        def arrived(t):
            r = pl.ds(pl.multiple_of(t * rows, rows), rows)
            value = gaf[r]
            do[r] = nn(value, wf[3]).astype(BF)
            gat[:, r] = value.T

        dk[...] = jnp.zeros_like(dk)
        dv[...] = jnp.zeros_like(dv)

        half = width // 2

        def norm_grad(i):
            r = pl.ds(pl.multiple_of(i * rows, rows), rows)
            dqkv[1, r] = dk[r].astype(BF)
            dqkv[2, r] = dv[r].astype(BF)
            for first in range(0, width, half):
                cols = slice(first, first + half)
                part[r, cols] = sum(nt(dqkv[j, r], wf[j, cols, :]) for j in range(3)).astype(BF)
            blocks[1].start_traced(i)

        plan = {(1, p, n): n + 1 + p for p in range(per) for n in range(end - 1)}
        plan = {key: at for key, at in plan.items() if at < size}

        def arrive_back(k, carry):
            for n in range(1, size):
                @pl.when(k == n)
                def _():
                    if n == 1 and size > 2:
                        gas.step(2)
                    for key, at in plan.items():
                        if at == n:
                            line_step(*key)
                    if n == end:
                        scatters[0, 0].second()
                        for p in range(1, per):
                            scatters[0, p].first()

            @pl.when(k >= 3)
            def _():
                gas.step(k)

            def side(i, inner):
                t = spot.t + (2 * i - 1) * k

                @pl.when((t >= 0) & (t < size) & ((i == 0) | (k >= 1)))
                def _():
                    arrived(t)

                return inner

            lax.fori_loop(0, 2, side, 0)
            for i in range(size):
                @pl.when((i == spot.t - k) | (i == spot.t + k))
                def _():
                    start, stop = i * rows, (i + 1) * rows
                    block_bias(seg_col, seg_row, bias, start, rows, stop)
                    attend_block_back(qkv, bias, lse, do, dqkv.at[0], dk, dv, start, rows)

            @pl.when((k == end) & (spot.t == 0))
            def _():
                scatters[0, 0].third()
                lines[0, 0].start()

            def ready(n, inner):
                i = jnp.where(lax.rem(n, 2) == 0, end - lax.div(n, 2), lax.div(n, 2))

                @pl.when(jnp.maximum(end - spot.t, spot.t - i) == k)
                def _():
                    norm_grad(i)

                return inner

            lax.fori_loop(0, size, ready, 0)
            return carry

        lax.fori_loop(0, size, arrive_back, 0)
        gas.owe()
        blocks[1].owe_starts()
        loop_rows(rows, tail, lambda r: set_total(r))
        own_line(1)
        for p in range(per):
            for n in range(end):
                if (1, p, n) not in plan:
                    line_step(1, p, n)
        downg[...] = gtot[...].T
        stores = fetch([pltpu.make_async_copy(downg, downg_ref, osem.at[1])])
        events = blocks[1].count()

        @pl.when(spot.t != 0)
        def _():
            scatters[0, 0].third()
            lines[0, 0].start()

        def first_norm(r):
            unit_one, _ = norm_stats(xf[r].astype(F32))
            term = part[r].astype(F32)
            sums[0:1, :] += column_sum(term * unit_one)
            sums[2:3, :] += column_sum(term)

        loop_rows(seq, tail, first_norm)
        sums[3:4, column] = column_sum(dqkv[0].astype(F32))
        sums[4:5, column] = column_sum(dqkv[2].astype(F32))
        for d in range(geo.dp):
            spart[d] = sums[:, d * piece:(d + 1) * piece]
        for step in range(1, geo.dp):
            to = ring_next(spot.d, step, geo.dp)
            wire.start(small + step - 1, spart.at[to], sland.at[step - 1], spot.at_d(to))
        stot[...] = spart[spot.d]
        blocks[1].step(0, 4 * events // 8, mid_total)
        for p in range(1, per):
            scatters[0, p].second()
        if end > 1:
            line_step(0, 0, 0)

        def wgrad(r):
            for j in range(3):
                wg[j, r] = nn(n1t[r], dqkv[j]).astype(BF)
            wg[3, r] = nn(gat[r], att[...]).astype(BF)

        loop_rows(width, min(256, width), wgrad)

        def wrows_of(i, core):
            return pl.ds(pl.multiple_of((i * 2 + core) * wrows, wrows), wrows)

        for i in range(ab):
            wire.start(wzero + i, wg.at[:, wrows_of(i, 1 - spot.c)], wheld.at[0, i // a_size, i % a_size], sibling)
        for n in range(1, end - 1):
            line_step(0, 0, n)
        blocks[1].step(4 * events // 8, 6 * events // 8, mid_total)
        for p in range(1, per):
            scatters[0, p].third()
            lines[0, p].start()
        blocks[1].start_near()
        own_line(0)
        for i in range(ab):
            here = wheld.at[0, i // a_size, i % a_size]
            wire.landed(wzero + i, here, sibling)
            wscatter.add(here, wg.at[:, wrows_of(i, spot.c)])
        wscatter.first()
        for step in range(1, geo.dp):
            wire.landed(small + step - 1, sland.at[step - 1], spot.at_d(ring_prev(spot.d, step, geo.dp)))
            stot[...] += sland[step - 1]
        for step in range(1, size):
            wire.start(last + step - 1, stot, tland.at[step - 1], spot.at_t(ring_next(spot.t, step, size)))
        for p in range(1, per):
            for n in range(end - 1):
                line_step(0, p, n)
        wscatter.second()
        blocks[1].step(6 * events // 8, events, mid_total)

        def back(r):
            unit_one, scale_one = norm_stats(xf[own_rows(r, tail)].astype(F32))
            cot[r] = cot[r] + norm_back(mid[r], unit_one, scale_one, rows12[0:1, :])

        loop_rows(rows, tail, back)
        stores += fetch([pltpu.make_async_copy(cot, igrad_ref, osem.at[0])])
        wscatter.third()
        sums_w = wheld.at[0, spot.b, spot.a]
        for j in range(3):
            awg[j] = sums_w[j].astype(F32)
        owg[...] = sums_w[3].astype(F32).T
        stores += fetch([
            pltpu.make_async_copy(awg, awg_ref, osem.at[2]),
            pltpu.make_async_copy(owg, owg_ref, osem.at[3])])
        for p in range(per):
            line_step(0, p, end - 1)
        stores += fetch([pltpu.make_async_copy(gtot, upg_ref, osem.at[6])])
        for step in range(1, size):
            wire.landed(last + step - 1, tland.at[step - 1], spot.at_t(ring_prev(spot.t, step, size)))
        total = stot[...]
        for step in range(1, size):
            total = total + tland[step - 1]
        gaing[...] = total[0:2, :]
        for i in range(biasg.shape[0]):
            biasg[i] = total[2 + i:3 + i, :]
        stores += fetch([
            pltpu.make_async_copy(gaing, gaing_ref, osem.at[4]),
            pltpu.make_async_copy(biasg, biasg_ref, osem.at[5])])
        wire.drain()
        settle(stores)

    pl.run_scoped(
        attention,
        pltpu.VMEM((width, seq), BF),
        pltpu.VMEM((seq, heads), BF),
        pltpu.VMEM((3, seq, heads), BF),
        pltpu.VMEM((seq, heads), F32),
        pltpu.VMEM((seq, heads), F32),
        pltpu.VMEM((4, width, heads), BF),
    )


def block_kernel(geo, x, aw, ow, up, down, gains, biases, seg_row, cot):
    rows, width = x.shape
    wrows, heads = aw.shape[1:]
    mrows, unit = up.shape
    size = geo.tensor
    seq = size * rows
    chunk = min(512, unit)
    per = unit // chunk
    sems = ((2 * per + 1) * (gather_sems(geo) + scatter_sems(geo)) + (size - 1) * (2 * 4 + 2 * 4 + 4 * per * 2 + 1) + 2 * per * size
            + geo.a_size * geo.b_size + 2 * (geo.dp - 1))
    like = lambda x: pltpu.VMEM(x.shape, x.dtype)
    return pl.pallas_call(
        functools.partial(block_body, geo),
        out_shape=(
            jax.ShapeDtypeStruct((2, unit // chunk, size, width, chunk), BF),
            jax.ShapeDtypeStruct((rows, width), F32),
            jax.ShapeDtypeStruct((rows, width), F32),
            jax.ShapeDtypeStruct((3, wrows, heads), F32),
            jax.ShapeDtypeStruct((heads, wrows), F32),
            jax.ShapeDtypeStruct((mrows, unit), F32),
            jax.ShapeDtypeStruct((unit, mrows), F32),
            jax.ShapeDtypeStruct((2, wrows), F32),
            jax.ShapeDtypeStruct((10, 1, wrows), F32),
        ),
        in_specs=[ANY] * 9,
        out_specs=(ANY,) * 9,
        scratch_shapes=[
            pltpu.VMEM((seq, width), BF),
            pltpu.VMEM((rows, width), BF),
            pltpu.VMEM((width, seq), BF),
            pltpu.VMEM((3, seq, heads), BF),
            pltpu.VMEM((seq, heads), BF),
            pltpu.VMEM((seq, 128), F32),
            pltpu.VMEM((4, width, heads), BF),
            pltpu.VMEM((seq, width), BF),
            pltpu.VMEM((2, size - 1, rows, width), BF),
            pltpu.VMEM((rows, seq), F32),
            pltpu.VMEM((rows, width), F32),
            pltpu.VMEM((rows, width), F32),
            pltpu.VMEM((seq, width), BF),
            pltpu.VMEM((12, width), F32),
            pltpu.VMEM((seq, 128), jnp.int32),
            like(seg_row),
            pltpu.VMEM((geo.dp, 12, wrows), F32),
            pltpu.VMEM((4, wrows, heads), BF),
            like(ow), like(down), pltpu.VMEM((2, unit // chunk, mrows, chunk), BF), like(gains), like(biases),
            pltpu.VMEM((12, wrows), F32),
            pltpu.VMEM((12, width), F32),
            pltpu.VMEM((geo.dp, 12, wrows), F32),
            pltpu.VMEM((geo.dp - 1, 12, wrows), F32),
            pltpu.VMEM((12, wrows), F32),
            pltpu.VMEM((size - 1, 12, wrows), F32),
            *scatter_bufs(geo, 2 * (unit // chunk), 2 * (unit // chunk), size, mrows, chunk),
            *scatter_bufs(geo, 1, 1, 4, wrows, heads),
            pltpu.VMEM((2 * (unit // chunk), 2, size - 1, mrows, chunk), BF),
            pltpu.VMEM((mrows, unit), F32),
            pltpu.VMEM((unit, mrows), F32),
            pltpu.VMEM((3, wrows, heads), F32),
            pltpu.VMEM((heads, wrows), F32),
            pltpu.VMEM((2, wrows), F32),
            pltpu.VMEM((10, 1, wrows), F32),
            pltpu.SemaphoreType.DMA((sems,)), pltpu.SemaphoreType.DMA((sems,)), pltpu.SemaphoreType.DMA((8 + unit // chunk,)),
            pltpu.SemaphoreType.DMA((6, 2)), pltpu.SemaphoreType.DMA((7,))],
        compiler_params=pltpu.CompilerParams(collective_id=1, has_side_effects=True, vmem_limit_bytes=62 * 2**20),
        name="block",
    )(x, aw, ow, up, down, gains, biases, seg_row, cot)


def hand_over_body(*refs):
    *refs, loads, stores = refs
    count = len(refs) // 3
    ins, outs, bufs = refs[:count], refs[count:2 * count], refs[2 * count:]
    coming = fetch([pltpu.make_async_copy(ins[i], bufs[i], loads.at[i]) for i in range(count)])
    going = []
    for i in range(count):
        coming[i].wait()
        going += fetch([pltpu.make_async_copy(bufs[i], outs[i], stores.at[i])])
    settle(going)


def hand_over(parts):
    return pl.pallas_call(
        hand_over_body,
        out_shape=tuple(jax.ShapeDtypeStruct(part.shape, part.dtype) for part in parts),
        in_specs=[ANY] * len(parts),
        out_specs=(ANY,) * len(parts),
        scratch_shapes=[pltpu.VMEM(part.shape, part.dtype) for part in parts] + [pltpu.SemaphoreType.DMA((len(parts),))] * 2,
        name="hand_over",
    )(*parts)


def per_device(geo, activations, segments, attn_weight, out_weight, up_weight, down_weight, norm_gains, bias_rows, cotangent):
    outs = block_kernel(
        geo, activations, attn_weight[0], out_weight[0], up_weight[0], down_weight[0], norm_gains[0], bias_rows[0], segments[None, :],
        cotangent)
    outs = hand_over(outs[1:])
    return outs[:2] + tuple(part[None] for part in outs[2:7]) + (outs[7].reshape(1, 10, -1),)


def solution(mesh):
    geo = Geometry(mesh.shape["dp"], mesh.shape["tensor"])
    return jax.shard_map(
        functools.partial(per_device, geo),
        mesh=mesh,
        in_specs=(
            P(("dp", "tensor"), None),
            P("dp"),
            P(None, None, "dp", "tensor"),
            P(None, "tensor", "dp"),
            P(None, "dp", "tensor"),
            P(None, "tensor", "dp"),
            P(None, None, "dp"),
            P(None, None, "dp"),
            P(("dp", "tensor"), None),
        ),
        out_specs=(
            P(("dp", "tensor"), None),
            P(("dp", "tensor"), None),
            P(None, None, "dp", "tensor"),
            P(None, "tensor", "dp"),
            P(None, "dp", "tensor"),
            P(None, "tensor", "dp"),
            P(None, None, "dp"),
            P(None, None, "dp"),
        ),
        check_vma=False,
    )
```

```python
import functools

import jax
import jax.numpy as jnp
from jax import lax
from jax.experimental import pallas as pl
from jax.experimental.pallas import tpu as pltpu
from jax.sharding import PartitionSpec as P

HD = 64
EPSILON = 1e-05
MASKED = -1e30
MESH_ID = pl.DeviceIdType.MESH
BF = jnp.bfloat16
F32 = jnp.float32
ANY = pl.BlockSpec(memory_space=pl.ANY)
VM = pl.BlockSpec(memory_space=pltpu.VMEM)


def layer_norm(values, gain_row, shift_row):
    center = values - jnp.mean(values, axis=-1, keepdims=True)
    spread = jnp.mean(center * center, axis=-1, keepdims=True)
    return center * lax.rsqrt(spread + EPSILON) * gain_row + shift_row


def norm_stats(values):
    center = values - jnp.mean(values, axis=-1, keepdims=True)
    spread = jnp.mean(center * center, axis=-1, keepdims=True)
    scale = lax.rsqrt(spread + EPSILON)
    return center * scale, scale


def norm_back(grad, unit, scale, gain_row):
    u = grad * gain_row
    mean_u = jnp.mean(u, axis=-1, keepdims=True)
    mean_ux = jnp.mean(u * unit, axis=-1, keepdims=True)
    return scale * (u - mean_u - unit * mean_ux)


def gelu_tanh(values):
    return jax.nn.gelu(values, approximate=True)


class Geometry:
    def __init__(self, dp, tensor):
        self.dp, self.tensor = dp, tensor
        self.c_size = 2
        rest = dp // 2
        self.a_size = 1
        while self.a_size * self.a_size < rest:
            self.a_size *= 2
        self.b_size = rest // self.a_size
        assert self.a_size * self.b_size * 2 == dp

    def bind(self):
        spot = Spot()
        spot.geo = self
        spot.d = lax.axis_index("dp")
        spot.t = lax.axis_index("tensor")
        spot.c = lax.rem(spot.d, 2)
        half = lax.div(spot.d, 2)
        spot.a = lax.rem(half, self.a_size)
        spot.b = lax.div(half, self.a_size)
        return spot


class Spot:
    def rank(self, b, a, c):
        return (b * self.geo.a_size + a) * 2 + c

    def at_t(self, t):
        return (self.d, t)

    def at_d(self, d):
        return (d, self.t)


def ring_next(rank, step, size):
    return lax.rem(rank + step, size)


def ring_prev(rank, step, size):
    return lax.rem(rank + size - step, size)


class Wire:
    def __init__(self, send, recv):
        self.send_sems, self.recv_sems = send, recv
        self.count = 0
        self.pending = []

    def take(self, n):
        first = self.count
        self.count += n
        return first

    def copy(self, i, src, dst, device):
        return pltpu.make_async_remote_copy(
            src_ref=src, dst_ref=dst, send_sem=self.send_sems.at[i], recv_sem=self.recv_sems.at[i],
            device_id=device, device_id_type=MESH_ID)

    def plan(self, i, src, dst, device, when=None):
        return self.copy(i, src, dst, device), when

    def go(self, planned):
        copy, when = planned
        if when is None:
            copy.start()
        else:
            pl.when(when)(copy.start)
        self.owe(planned)

    def owe(self, planned):
        if not any(other is planned for other in self.pending):
            self.pending.append(planned)

    def start(self, i, src, dst, device, when=None):
        self.go(self.plan(i, src, dst, device, when))

    def landed(self, i, dst, device, when=None):
        copy = self.copy(i, dst, dst, device)
        if when is None:
            copy.wait_recv()
        else:
            pl.when(when)(copy.wait_recv)

    def sent(self, plans):
        for planned in plans:
            copy, when = planned
            self.pending = [other for other in self.pending if other is not planned]
            if when is None:
                copy.wait_send()
            else:
                pl.when(when)(copy.wait_send)

    def drain(self):
        for copy, when in self.pending:
            if when is None:
                copy.wait_send()
            else:
                pl.when(when)(copy.wait_send)
        self.pending = []


def greet(spot):
    geo = spot.geo
    barrier = pltpu.get_barrier_semaphore()
    total = 0
    for step in range(1, geo.tensor):
        pl.semaphore_signal(barrier, inc=1, device_id=spot.at_t(ring_next(spot.t, step, geo.tensor)), device_id_type=MESH_ID)
        total += 1
    for step in range(1, geo.dp):
        pl.semaphore_signal(barrier, inc=1, device_id=spot.at_d(ring_next(spot.d, step, geo.dp)), device_id_type=MESH_ID)
        total += 1
    return lambda: pl.semaphore_wait(barrier, total)


def halves(ref, count, part):
    rows = ref.shape[-2] // count
    return ref.at[(slice(None),) * (len(ref.shape) - 2) + (pl.ds(part * rows, rows),)]


class LineGather:
    def __init__(self, spot, wire, src, slot, parts=2):
        self.spot, self.wire, self.src, self.slot, self.parts = spot, wire, src, slot, parts
        self.size = size = spot.geo.tensor
        self.base = [wire.take((size - 1) * parts) for _ in range(2)]
        t = spot.t
        self.sends = {}
        for k in range(size - 1):
            for part in range(parts):
                for side in range(2):
                    self.sends[k, part, side] = self.plan(k, part, side)

    def place(self, k, side):
        t = self.spot.t
        origin = t - k if side == 0 else t + k
        there = (origin >= 0) & (origin < self.size)
        onward = t + 1 if side == 0 else t - 1
        return origin, there, t - 1 if side == 0 else t + 1, onward, there & (onward >= 0) & (onward < self.size)

    def plan(self, k, part, side):
        origin, _, _, onward, going = self.place(k, side)
        piece = halves(self.slot(origin), self.parts, part)
        first = isinstance(k, int) and k == 0
        src = halves(self.src, self.parts, part) if first else piece
        return self.wire.plan(self.base[side] + k * self.parts + part, src, piece, self.spot.at_t(onward), when=going)

    def start(self, where=None):
        for part in range(self.parts):
            for side in range(2):
                planned = self.sends[0, part, side]
                if where is None:
                    self.wire.go(planned)
                else:
                    copy, when = planned
                    pl.when(when & self.inner(where))(copy.start)
                    self.wire.owe(planned)

    def inner(self, where):
        inner = (self.spot.t >= 1) & (self.spot.t < self.size - 1)
        return inner if where else jnp.logical_not(inner)

    def step(self, k, where=None):
        for part in range(self.parts):
            for side in range(2):
                origin, there, near, _, _ = self.place(k, side)
                if where is not None:
                    there = there & self.inner(where)
                piece = halves(self.slot(origin), self.parts, part)
                self.wire.landed(self.base[side] + (k - 1) * self.parts + part, piece, self.spot.at_t(near), when=there)
                if not isinstance(k, int):
                    copy, going = self.plan(k, part, side)
                    pl.when(going & (k < self.size - 1))(copy.start)
                elif k < self.size - 1 and where is not False:
                    self.wire.go(self.sends[k, part, side])

    def owe(self):
        for (k, part, side), planned in self.sends.items():
            if k > 0:
                self.wire.owe(planned)


class LineScatter:
    def __init__(self, spot, wire, part, land, add, rising=None, parts=2):
        self.spot, self.wire, self.part, self.land, self.add, self.parts = spot, wire, part, land, add, parts
        self.size = spot.geo.tensor
        base = self.base = [wire.take((self.size - 1) * parts) for _ in range(2)]
        t, end = spot.t, self.size - 1
        self.starts, self.hops = {}, {}
        for h in range(parts):
            for j in range(self.size):
                if j > 0:
                    self.starts[0, j, h] = wire.plan(
                        base[0] + (j - 1) * parts + h, halves(part(j), parts, h), halves(land(0, j), parts, h), spot.at_t(1), when=t == 0)
                if j < end:
                    self.starts[1, j, h] = wire.plan(
                        base[1] + j * parts + h, halves(part(j), parts, h), halves(land(1, j), parts, h), spot.at_t(end - 1), when=t == end)
        self.events = []
        for side in range(2):
            place = t if side == 0 else end - t
            if side == rising:
                for e in range(1, 2 * end):
                    far = e + 1 - place
                    self.events.append((10 * e, side, far if side == 0 else end - far, (place >= 1) & (far >= place) & (far <= end)))
            else:
                for s in range(1, self.size):
                    far = end - s + place
                    at = 10 * s + (0 if rising is None else 15)
                    self.events.append((at, side, far if side == 0 else end - far, (place >= 1) & (s >= place)))
        self.events.sort(key=lambda event: event[0])
        self.hops = []
        for _, side, j, here in self.events:
            near = spot.at_t(t - 1 if side == 0 else t + 1)
            away = spot.at_t(t + 1 if side == 0 else t - 1)
            for h in range(parts):
                held = halves(land(side, j), parts, h)
                i = base[side] + (j - 1 + side) * parts + h
                self.hops.append((here & (j == t), here & (j != t), j, h, held, wire.copy(i, held, held, near),
                                  wire.plan(i, held, held, away, when=here & (j != t))))

    def start_block(self, j):
        for side in range(2):
            for h in range(self.parts):
                if (side, j, h) in self.starts:
                    self.wire.go(self.starts[side, j, h])

    def start_traced(self, j):
        spot, t, end = self.spot, self.spot.t, self.size - 1
        for side in range(2):
            first, to = (0, 1) if side == 0 else (end, end - 1)
            for h in range(self.parts):
                copy, when = self.wire.plan(
                    self.base[side] + (j - 1 + side) * self.parts + h, halves(self.part(j), self.parts, h),
                    halves(self.land(side, j), self.parts, h), spot.at_t(to), when=(t == first) & (j != first) & (j != 1 if side == 0 else (j == 0) | (j == end - 1)))
                pl.when(when)(copy.start)

    def start_middle(self):
        for j in range(1, self.size - 2):
            for h in range(self.parts):
                self.wire.go(self.starts[1, j, h])

    def start_near(self):
        for h in range(self.parts):
            self.wire.go(self.starts[0, 1, h])

    def owe_starts(self):
        for planned in self.starts.values():
            self.wire.owe(planned)

    def start(self):
        for n in range(self.size):
            for side, j in ((0, self.size - 1 - n), (1, n)):
                for h in range(self.parts):
                    if (side, j, h) in self.starts:
                        self.wire.go(self.starts[side, j, h])

    def count(self):
        return len(self.hops)

    def step(self, first, last, total):
        for final, passing, j, h, held, landing, onward in self.hops[first:last]:
            @pl.when(final)
            def _():
                landing.wait_recv()
                total(held, h)

            @pl.when(passing)
            def _():
                landing.wait_recv()
                self.add(held, halves(self.part(j), self.parts, h))

            self.wire.go(onward)

    def plans(self):
        return list(self.starts.values()) + [hop[-1] for hop in self.hops]


def add_tiled(dst, src, tile):
    def step(i, carry):
        rows = pl.ds(pl.multiple_of(i * tile, tile), tile)
        dst[rows] = (dst[rows].astype(F32) + src[rows].astype(F32)).astype(dst.dtype)
        return carry

    lax.fori_loop(0, dst.shape[0] // tile, step, 0)


class WeightGather:
    def __init__(self, spot, wire, rows, full):
        geo = spot.geo
        self.spot, self.wire, self.full, self.rows = spot, wire, full, rows
        self.slots = full.shape[0]
        self.half = self.slots // 2
        self.one_a = wire.take(geo.a_size - 1)
        self.one_b = wire.take(geo.b_size - 1)
        self.two_a = wire.take((geo.b_size - 1) * geo.a_size)
        self.two_b = wire.take((geo.a_size - 1) * geo.b_size)
        self.last = wire.take(2 * geo.a_size * geo.b_size)
        self.plan_shares()
        self.plan_hops()

    def span(self, d):
        return pl.ds(pl.multiple_of(d * self.rows, self.rows), self.rows)

    def low(self, d):
        return self.full.at[pl.ds(0, self.half), self.span(d)]

    def high(self, d):
        return self.full.at[pl.ds(self.half, self.slots - self.half), self.span(d)]

    def plan_shares(self):
        spot, geo = self.spot, self.spot.geo
        self.shares = {}
        for j in range(geo.b_size):
            for i in range(geo.a_size):
                held = spot.rank(ring_prev(spot.b, j, geo.b_size), ring_prev(spot.a, i, geo.a_size), spot.c)
                sibling = spot.rank(spot.b, spot.a, 1 - spot.c)
                for part in range(2):
                    half = (self.low, self.high)[part](held)
                    self.shares[part, j, i] = self.wire.plan(
                        self.last + 2 * (j * geo.a_size + i) + part, half, half, spot.at_d(sibling))

    def share(self, part, j, i):
        self.wire.go(self.shares[part, j, i])

    def plan_hops(self):
        spot, geo, wire = self.spot, self.spot.geo, self.wire
        self.ones, self.twos_a, self.twos_b = [], {}, {}
        mine = spot.d
        for j in range(1, geo.a_size):
            to = spot.rank(spot.b, ring_next(spot.a, j, geo.a_size), spot.c)
            self.ones.append(wire.plan(self.one_a + j - 1, self.low(mine), self.low(mine), spot.at_d(to)))
        for j in range(1, geo.b_size):
            to = spot.rank(ring_next(spot.b, j, geo.b_size), spot.a, spot.c)
            self.ones.append(wire.plan(self.one_b + j - 1, self.high(mine), self.high(mine), spot.at_d(to)))
        for i in range(geo.a_size):
            held = spot.rank(spot.b, ring_prev(spot.a, i, geo.a_size), spot.c)
            for j in range(1, geo.b_size):
                to = spot.rank(ring_next(spot.b, j, geo.b_size), spot.a, spot.c)
                self.twos_a[i, j] = wire.plan(self.two_a + (j - 1) * geo.a_size + i, self.low(held), self.low(held), spot.at_d(to))
        for i in range(geo.b_size):
            held = spot.rank(ring_prev(spot.b, i, geo.b_size), spot.a, spot.c)
            for j in range(1, geo.a_size):
                to = spot.rank(spot.b, ring_next(spot.a, j, geo.a_size), spot.c)
                self.twos_b[i, j] = wire.plan(self.two_b + (j - 1) * geo.b_size + i, self.high(held), self.high(held), spot.at_d(to))

    def first(self):
        for planned in self.ones:
            self.wire.go(planned)
        self.share(0, 0, 0)
        self.share(1, 0, 0)

    def second(self):
        spot, geo = self.spot, self.spot.geo
        for i in range(geo.a_size):
            held = spot.rank(spot.b, ring_prev(spot.a, i, geo.a_size), spot.c)
            if i:
                self.wire.landed(self.one_a + i - 1, self.low(held), spot.at_d(held))
                self.share(0, 0, i)
            for j in range(1, geo.b_size):
                self.wire.go(self.twos_a[i, j])
        for i in range(geo.b_size):
            held = spot.rank(ring_prev(spot.b, i, geo.b_size), spot.a, spot.c)
            if i:
                self.wire.landed(self.one_b + i - 1, self.high(held), spot.at_d(held))
                self.share(1, i, 0)
            for j in range(1, geo.a_size):
                self.wire.go(self.twos_b[i, j])

    def third(self):
        spot, geo = self.spot, self.spot.geo
        for j in range(1, geo.b_size):
            for i in range(geo.a_size):
                held = spot.rank(ring_prev(spot.b, j, geo.b_size), ring_prev(spot.a, i, geo.a_size), spot.c)
                source = spot.rank(ring_prev(spot.b, j, geo.b_size), spot.a, spot.c)
                self.wire.landed(self.two_a + (j - 1) * geo.a_size + i, self.low(held), spot.at_d(source))
                self.share(0, j, i)
        for j in range(1, geo.a_size):
            for i in range(geo.b_size):
                held = spot.rank(ring_prev(spot.b, i, geo.b_size), ring_prev(spot.a, j, geo.a_size), spot.c)
                source = spot.rank(spot.b, ring_prev(spot.a, j, geo.a_size), spot.c)
                self.wire.landed(self.two_b + (j - 1) * geo.b_size + i, self.high(held), spot.at_d(source))
                self.share(1, i, j)

    def fourth(self):
        spot, geo = self.spot, self.spot.geo
        sibling = spot.rank(spot.b, spot.a, 1 - spot.c)
        for j in range(geo.b_size):
            for i in range(geo.a_size):
                held = spot.rank(ring_prev(spot.b, j, geo.b_size), ring_prev(spot.a, i, geo.a_size), 1 - spot.c)
                for part in range(2):
                    half = (self.low, self.high)[part](held)
                    self.wire.landed(self.last + 2 * (j * geo.a_size + i) + part, half, spot.at_d(sibling))


def gather_sems(geo):
    return geo.a_size + geo.b_size - 2 + (geo.b_size - 1) * geo.a_size + (geo.a_size - 1) * geo.b_size + 2 * geo.a_size * geo.b_size


class WeightScatter:
    def __init__(self, spot, wire, held, one_a, one_b, two_a, two_b):
        geo = spot.geo
        self.spot, self.wire, self.held = spot, wire, held
        self.one_a_buf, self.one_b_buf, self.two_a_buf, self.two_b_buf = one_a, one_b, two_a, two_b
        self.slots, self.rows = held.shape[2], held.shape[3]
        self.half = self.slots // 2
        self.one_a = wire.take(geo.a_size - 1)
        self.one_b = wire.take(geo.b_size - 1)
        self.two_a = wire.take(geo.b_size - 1)
        self.two_b = wire.take(geo.a_size - 1)
        low, high = pl.ds(0, self.half), pl.ds(self.half, self.half)
        self.sends = []
        for j in range(1, geo.a_size):
            a = ring_next(spot.a, j, geo.a_size)
            self.sends.append(wire.plan(self.one_a + j - 1, held.at[:, a, low], one_a.at[j - 1], spot.at_d(spot.rank(spot.b, a, spot.c))))
        for j in range(1, geo.b_size):
            b = ring_next(spot.b, j, geo.b_size)
            self.sends.append(wire.plan(self.one_b + j - 1, held.at[b, :, high], one_b.at[j - 1], spot.at_d(spot.rank(b, spot.a, spot.c))))
        self.later = []
        for j in range(1, geo.b_size):
            b = ring_next(spot.b, j, geo.b_size)
            self.later.append(wire.plan(self.two_a + j - 1, held.at[b, spot.a, low], two_a.at[j - 1], spot.at_d(spot.rank(b, spot.a, spot.c))))
        for j in range(1, geo.a_size):
            a = ring_next(spot.a, j, geo.a_size)
            self.later.append(wire.plan(self.two_b + j - 1, held.at[spot.b, a, high], two_b.at[j - 1], spot.at_d(spot.rank(spot.b, a, spot.c))))

    def add(self, dst, src):
        tile = min(64, self.rows)
        per = self.rows // tile

        def step(i, carry):
            rows = pl.ds(pl.multiple_of(lax.rem(i, per) * tile, tile), tile)
            j = lax.div(i, per)
            dst[j, rows] = (dst[j, rows].astype(F32) + src[j, rows].astype(F32)).astype(dst.dtype)
            return carry

        lax.fori_loop(0, dst.shape[0] * per, step, 0)

    def first(self):
        for planned in self.sends:
            self.wire.go(planned)

    def second(self):
        spot, geo = self.spot, self.spot.geo
        low, high = pl.ds(0, self.half), pl.ds(self.half, self.half)
        for j in range(1, geo.a_size):
            self.wire.landed(self.one_a + j - 1, self.one_a_buf.at[j - 1], spot.at_d(spot.rank(spot.b, ring_prev(spot.a, j, geo.a_size), spot.c)))
            for b in range(geo.b_size):
                self.add(self.held.at[b, spot.a, low], self.one_a_buf.at[j - 1, b])
        for j in range(1, geo.b_size):
            self.wire.landed(self.one_b + j - 1, self.one_b_buf.at[j - 1], spot.at_d(spot.rank(ring_prev(spot.b, j, geo.b_size), spot.a, spot.c)))
            for a in range(geo.a_size):
                self.add(self.held.at[spot.b, a, high], self.one_b_buf.at[j - 1, a])
        for planned in self.later:
            self.wire.go(planned)

    def third(self):
        spot, geo = self.spot, self.spot.geo
        low, high = pl.ds(0, self.half), pl.ds(self.half, self.half)
        for j in range(1, geo.b_size):
            self.wire.landed(self.two_a + j - 1, self.two_a_buf.at[j - 1], spot.at_d(spot.rank(ring_prev(spot.b, j, geo.b_size), spot.a, spot.c)))
            self.add(self.held.at[spot.b, spot.a, low], self.two_a_buf.at[j - 1])
        for j in range(1, geo.a_size):
            self.wire.landed(self.two_b + j - 1, self.two_b_buf.at[j - 1], spot.at_d(spot.rank(spot.b, ring_prev(spot.a, j, geo.a_size), spot.c)))
            self.add(self.held.at[spot.b, spot.a, high], self.two_b_buf.at[j - 1])


def scatter_sems(geo):
    return 2 * (geo.a_size + geo.b_size - 2)


def scatter_bufs(geo, n, sets, slots, rows, width):
    a, b, half = geo.a_size, geo.b_size, slots // 2
    return [
        pltpu.VMEM((n, b, a, slots, rows, width), BF),
        pltpu.VMEM((sets, a - 1, b, half, rows, width), BF),
        pltpu.VMEM((sets, b - 1, a, half, rows, width), BF),
        pltpu.VMEM((sets, b - 1, half, rows, width), BF),
        pltpu.VMEM((sets, a - 1, half, rows, width), BF),
    ]


def loop_rows(count, tile, body, start=0):
    def step(i, carry):
        body(pl.ds(pl.multiple_of(start + i * tile, tile), tile))
        return carry

    lax.fori_loop(0, count // tile, step, 0)


def fetch(copies):
    for copy in copies:
        copy.start()
    return copies


def settle(copies):
    for copy in copies:
        copy.wait()


PAIR = 2 * HD


def nt(x, w):
    return lax.dot_general(x, w, (((1,), (1,)), ((), ())), preferred_element_type=F32)


def nn(x, w):
    return lax.dot_general(x, w, (((1,), (0,)), ((), ())), preferred_element_type=F32)


def tn(x, w):
    return lax.dot_general(x, w, (((0,), (0,)), ((), ())), preferred_element_type=F32)


def block_bias(seg_col, seg_row, bias, start, rows, keys):
    query = seg_col[start:start + rows, 0:1]
    for first in range(0, keys, rows):
        key = seg_row[:, first:first + rows]
        seen = query == key
        if first + rows > start:
            q_pos = start + lax.broadcasted_iota(jnp.int32, (rows, rows), 0)
            k_pos = first + lax.broadcasted_iota(jnp.int32, (rows, rows), 1)
            seen = seen & (k_pos <= q_pos)
        bias[:, first:first + rows] = jnp.where(seen, 0.0, MASKED).astype(F32)


def one_head(pair, head):
    lane = lax.broadcasted_iota(jnp.int32, pair.shape, 1)
    return jnp.where((lane < HD) if head == 0 else (lane >= HD), pair, jnp.zeros_like(pair))


def attend_block(qkv, bias, att, lse, start, rows):
    keys = start + rows
    width = qkv.shape[2]
    stat_lane = lax.broadcasted_iota(jnp.int32, (rows, 128), 1)
    stats = jnp.zeros((rows, 128), F32)
    for p in range(width // PAIR):
        lanes = slice(p * PAIR, (p + 1) * PAIR)
        query = qkv[0, start:keys, lanes]
        outs = []
        for head in range(2):
            s = nt(one_head(query, head), qkv[1, 0:keys, lanes]) + bias[:, 0:keys]
            top = jnp.max(s, axis=1, keepdims=True)
            e = jnp.exp(s - top)
            total = jnp.sum(e, axis=1, keepdims=True)
            prob = (e * (1.0 / total)).astype(BF)
            outs.append(nn(prob, qkv[2, 0:keys, lanes]))
            stats = jnp.where(stat_lane == 2 * p + head, top + jnp.log(total), stats)
        lane = lax.broadcasted_iota(jnp.int32, outs[0].shape, 1)
        att[start:keys, lanes] = jnp.where(lane < HD, outs[0], outs[1]).astype(BF)
    lse[start:keys, :] = stats


def attend_block_back(qkv, bias, lse, do, dq, dk, dv, start, rows):
    keys = start + rows
    width = qkv.shape[2]
    stat_lane = lax.broadcasted_iota(jnp.int32, (rows, 128), 1)
    stats = lse[start:keys, :]
    for p in range(width // PAIR):
        lanes = slice(p * PAIR, (p + 1) * PAIR)
        query = qkv[0, start:keys, lanes]
        grad = do[start:keys, lanes]
        dqs, dks, dvs = [], [], []
        for head in range(2):
            level = jnp.sum(jnp.where(stat_lane == 2 * p + head, stats, 0.0), axis=1, keepdims=True)
            s = nt(one_head(query, head), qkv[1, 0:keys, lanes]) + bias[:, 0:keys]
            prob = jnp.exp(s - level)
            d_prob = nt(one_head(grad, head), qkv[2, 0:keys, lanes])
            mixed = prob * d_prob
            ds = (mixed - prob * jnp.sum(mixed, axis=1, keepdims=True)).astype(BF)
            dqs.append(nn(ds, qkv[1, 0:keys, lanes]))
            dks.append(tn(ds, query))
            dvs.append(tn(prob.astype(BF), grad))
        lane = lax.broadcasted_iota(jnp.int32, dqs[0].shape, 1)
        dq[start:keys, lanes] = (jnp.where(lane < HD, dqs[0], dqs[1]) * (HD ** -0.5)).astype(dq.dtype)
        lane = lax.broadcasted_iota(jnp.int32, dks[0].shape, 1)
        dk[0:keys, lanes] += jnp.where(lane < HD, dks[0], dks[1])
        dv[0:keys, lanes] += jnp.where(lane < HD, dvs[0], dvs[1])


GELU_C = 0.7978845608028654


def gelu_parts(a):
    square = a * a
    tanh = jnp.tanh(GELU_C * a * (1.0 + 0.044715 * square))
    half = 0.5 * (1.0 + tanh)
    slope = half + 0.5 * a * (1.0 - tanh * tanh) * (GELU_C * (1.0 + 3 * 0.044715 * square))
    return a * half, slope


def column_sum(values):
    return jnp.sum(values, axis=0, keepdims=True)


def block_body(geo, x_ref, aw_ref, ow_ref, up_ref, down_ref, gain_ref, bias_ref, seg_ref, cot_ref,
               full, out_ref, igrad_ref, awg_ref, owg_ref, upg_ref, downg_ref, gaing_ref, biasg_ref,
               xf, n1, n1t, qkv, att, lse, wf, part, land, bias, mid, cot, gaf, rows12, seg_col, seg_row,
               sf, wsend, ow_in, down_in, msend, gain_in, bias_in, ssend,
               sums, spart, sland, stot, tland,
               held, one_a, one_b, two_a, two_b, wheld, wone_a, wone_b, wtwo_a, wtwo_b, mland,
               gtot, downg, awg, owg, gaing, biasg,
               send, recv, local, msem, osem):
    spot = geo.bind()
    wire = Wire(send, recv)
    size = geo.tensor
    rows, width = x_ref.shape
    seq = size * rows
    wrows, heads = aw_ref.shape[1:]
    mrows, unit = up_ref.shape
    a_size, b_size = geo.a_size, geo.b_size
    ab = a_size * b_size
    chunk = min(512, unit)
    per = unit // chunk
    pieces = msem.shape[1]
    count = size * per
    tail = min(64, rows)
    tile = min(64, mrows)
    end = size - 1
    sibling = spot.at_d(spot.rank(spot.b, spot.a, 1 - spot.c))
    wspan = pl.ds(pl.multiple_of(spot.d * wrows, wrows), wrows)
    mspan = pl.ds(pl.multiple_of(spot.d * mrows, mrows), mrows)
    column = pl.ds(pl.multiple_of(spot.t * heads, 128), heads)

    def block_of(ref, t):
        return ref.at[pl.ds(pl.multiple_of(t * rows, rows), rows)]

    def own_rows(r, n):
        return pl.ds(pl.multiple_of(spot.t * rows + r.start, n), n)

    weights = WeightGather(spot, wire, wrows, wf)
    halved = [(k, p) for k in range(2) for p in range(per)]
    wlines, gathers = {}, {}
    for k, p in halved:
        wlines[k, p] = LineGather(spot, wire, msend.at[k, p], lambda t, k=k, p=p: full.at[k, p, t, mspan], parts=1)
        gathers[k, p] = WeightGather(spot, wire, mrows, full.at[k, p])
    xs = LineGather(spot, wire, x_ref, lambda t: block_of(xf, t))
    gas = LineGather(spot, wire, block_of(gaf, spot.t), lambda t: block_of(gaf, t))
    blocks = [
        LineScatter(spot, wire, lambda t: block_of(part, t), lambda side, j: land.at[side, j - 1 + side],
                    lambda dst, src: add_tiled(dst, src, tail), rising=(0, None)[k]) for k in range(2)]
    scatters, lines = {}, {}

    def line_of(k, p):
        here = held.at[k * per + p, spot.b, spot.a]
        return LineScatter(spot, wire, lambda t: here.at[t], lambda side, j: mland.at[k * per + p, side, j - 1 + side],
                           lambda dst, src: add_tiled(dst, src, tile), parts=1)

    for k, p in halved:
        scatters[k, p] = WeightScatter(spot, wire, held.at[k * per + p], *(buf.at[k * per + p] for buf in (one_a, one_b, two_a, two_b)))
        lines[k, p] = line_of(k, p)
    wscatter = WeightScatter(spot, wire, wheld.at[0], wone_a.at[0], wone_b.at[0], wtwo_a.at[0], wtwo_b.at[0])
    zero = [wire.take(count) for _ in range(2)]
    wzero = wire.take(ab)
    gains_in = wire.take(geo.dp - 1)
    small = wire.take(geo.dp - 1)
    last = wire.take(size - 1)
    assert wire.count == send.shape[0]

    pairs = [
        (gain_ref, gain_in), (bias_ref, bias_in), (aw_ref, wsend.at[pl.ds(0, 3)]), (ow_ref, ow_in),
        (x_ref, block_of(xf, spot.t)), (down_ref, down_in), (seg_ref, seg_row), (cot_ref, cot)]
    pairs += [(up_ref.at[:, pl.ds(i * chunk, chunk)], msend.at[0, i]) for i in range(per)]
    loads = fetch([pltpu.make_async_copy(src, dst, local.at[i]) for i, (src, dst) in enumerate(pairs)])
    met = greet(spot)
    sums[...] = jnp.zeros_like(sums)
    settle(loads[0:4])
    ssend[0:2, :] = gain_in[...].astype(F32)
    ssend[2:12, :] = bias_in[...].astype(F32)
    sf[spot.d] = ssend[...]
    wsend[3] = ow_in[...].T
    wf[:, wspan] = wsend[...]
    settle(loads[8:])

    def store(k):
        return pltpu.make_async_copy(msend.at[k], full.at[k, :, spot.t, mspan], osem.at[k])

    store(0).start()
    met()
    for p in range(per):
        wlines[0, p].start()
    for step in range(1, geo.dp):
        wire.start(gains_in + step - 1, ssend, sf.at[spot.d], spot.at_d(ring_next(spot.d, step, geo.dp)))
    weights.first()
    loads[5].wait()
    for i in range(per):
        msend[1, i] = down_in[i * chunk:(i + 1) * chunk, :].T
    store(1).start()
    for k in range(1, end):
        for p in range(per):
            wlines[0, p].step(k)
        if k == 1:
            weights.second()
    xs.start()
    weights.third()
    store(0).wait()
    for p in range(per):
        wlines[0, p].step(end)
        gathers[0, p].first()
    for step in range(1, geo.dp):
        source = ring_prev(spot.d, step, geo.dp)
        wire.landed(gains_in + step - 1, sf.at[source], spot.at_d(source))
    piece = ssend.shape[1]
    for d in range(geo.dp):
        rows12[:, d * piece:(d + 1) * piece] = sf[d]
    loads[6].wait()
    seg_col[...] = jnp.broadcast_to(seg_row[...], (128, seq)).T
    weights.fourth()
    loads[4].wait()

    def project(t):
        def norm(r):
            source = pl.ds(pl.multiple_of(t * rows + r.start, tail), tail)
            n1[r] = layer_norm(xf[source].astype(F32), rows12[0:1, :], rows12[2:3, :]).astype(BF)

        loop_rows(rows, tail, norm)
        r = pl.ds(pl.multiple_of(t * rows, rows), rows)
        normed = n1[...]
        n1t[:, r] = normed.T
        qkv[0, r] = ((nn(normed, wf[0]) + rows12[3:4, column]).astype(BF).astype(F32) * HD ** -0.5).astype(BF)
        qkv[1, r] = nn(normed, wf[1]).astype(BF)
        qkv[2, r] = (nn(normed, wf[2]) + rows12[4:5, column]).astype(BF)

    def arrive(k, carry):
        @pl.when(k >= 1)
        def _():
            xs.step(k)

        @pl.when(k == end - 1)
        def _():
            wlines[1, 0].start()
            for p in range(1, per):
                wlines[1, p].start(False)

        def side(i, inner):
            t = spot.t + (2 * i - 1) * k

            @pl.when((t >= 0) & (t < size) & ((i == 0) | (k >= 1)))
            def _():
                project(t)

            return inner

        lax.fori_loop(0, 2, side, 0)

        @pl.when(k == 1)
        def _():
            for p in range(per):
                gathers[0, p].second()

        for i in range(size):
            start = i * rows

            @pl.when(jnp.maximum(spot.t, i - spot.t) == k)
            def _():
                block_bias(seg_col, seg_row, bias, start, rows, start + rows)
                attend_block(qkv, bias, att, lse, start, rows)
                part[start:start + rows, :] = nt(att[start:start + rows, :], wf[3]).astype(BF)
                blocks[0].start_block(i)

        return carry

    lax.fori_loop(0, size, arrive, 0)
    xs.owe()
    for k in range(1, end):
        wlines[1, 0].step(k)
        if k == max(1, end - 1):
            for p in range(1, per):
                wlines[1, p].start(True)
        if k == 1:
            for p in range(per):
                gathers[0, p].third()
    store(1).wait()
    wlines[1, 0].step(end)
    gathers[1, 0].first()
    for p in range(1, per):
        for k in range(1, size):
            wlines[1, p].step(k)
        gathers[1, p].first()

    def set_total(r):
        mid[r] = part[own_rows(r, tail)].astype(F32)

    loop_rows(rows, tail, set_total)

    def mid_total(ref, h):
        n = ref.shape[0]
        add_tiled(mid.at[pl.ds(h * n, n)], ref, tail)

    events = blocks[0].count()
    blocks[0].step(0, 3 * events // 8, mid_total)
    gathers[1, 0].second()
    blocks[0].step(3 * events // 8, 5 * events // 8, mid_total)
    for p in range(per):
        gathers[0, p].fourth()
    for p in range(1, per):
        gathers[1, p].second()
    blocks[0].step(5 * events // 8, events, mid_total)

    def mlp(mbuf, hmid, da, n2, gm, turned, left, snd, dn2):
        def cols_of(j):
            return pl.ds(pl.multiple_of(unit_of(j) * chunk, chunk), chunk)

        def unit_of(j):
            return lax.rem(j, size) * per + lax.div(j, size)

        def mload(k, j, s):
            n = width // pieces
            return [
                pltpu.make_async_copy(
                    full.at[k, lax.div(j, size), lax.rem(j, size), pl.ds(i * n, n)], mbuf.at[s, pl.ds(i * n, n)], msem.at[s, i])
                for i in range(pieces)]

        def depth(which):
            return mbuf.shape[0] // len(which)

        def ahead(which):
            for j in range(min(depth(which) - 1, count)):
                for n, k in enumerate(which):
                    fetch(mload(k, j, j * len(which) + n))

        def streamed(which, body, first=0, stop=count):
            deep = depth(which)

            def one(j, carry):
                slots = [lax.rem(j, deep) * len(which) + n for n in range(len(which))]
                for n, k in enumerate(which):
                    settle(mload(k, j, slots[n]))

                @pl.when(j + deep - 1 < count)
                def _():
                    for n, k in enumerate(which):
                        fetch(mload(k, j + deep - 1, lax.rem(j + deep - 1, deep) * len(which) + n))

                body(j, *slots)
                return carry

            lax.fori_loop(first, stop, one, 0)

        ahead((0,))
        loads[7].wait()

        def norm(r):
            value = xf[own_rows(r, tail)].astype(F32) + (mid[r] + rows12[5:6, :])
            mid[r] = value
            n2[r] = layer_norm(value, rows12[1:2, :], rows12[6:7, :]).astype(BF)
            branch = cot[r].astype(BF)
            gm[r] = branch
            sums[7:8, :] += column_sum(branch.astype(F32))

        loop_rows(rows, tail, norm)

        def turn(value):
            turned[...] = value[...].T
            for i in range(ab):
                for other in range(2):
                    core = lax.rem(spot.c + other, 2)
                    left[other, i * mrows:(i + 1) * mrows, :] = turned[pl.ds(pl.multiple_of((i * 2 + core) * mrows, mrows), mrows), :]

        turn(gm)

        def sending(k, j):
            p, t = lax.div(j, size), lax.rem(j, size)
            return wire.copy(zero[k] + j, snd.at[p, :, :, t], held.at[k * per + p, :, :, t], sibling)

        def give(k, j, right):
            product = nn(left[1], right).astype(BF)
            p, t = lax.div(j, size), lax.rem(j, size)
            for i in range(ab):
                snd[p, i // a_size, i % a_size, t] = product[i * mrows:(i + 1) * mrows, :]
            sending(k, j).start()

        def keep(k, j, right):
            p, t = lax.div(j, size), lax.rem(j, size)
            product = nn(left[0], right)
            sending(k, j).wait_recv()
            for i in range(ab):
                b, a = i // a_size, i % a_size
                held[k * per + p, b, a, t] = (
                    held[k * per + p, b, a, t].astype(F32) + product[i * mrows:(i + 1) * mrows, :]).astype(BF)

        def hidden(j, s):
            cols = cols_of(j)
            row = pl.ds(8 + lax.div(unit_of(j) * chunk, width), 1)
            bcols = pl.ds(pl.multiple_of(lax.rem(unit_of(j) * chunk, width), chunk), chunk)
            value, slope = gelu_parts(nn(n2[...], mbuf[s]) + rows12[row, bcols])
            active = value.astype(BF)
            hmid[:, cols] = active
            da[:, cols] = slope.astype(BF)
            give(1, j, active)

        def keep_down(j, carry):
            keep(1, j, hmid[:, cols_of(j)])
            return carry

        for p in range(per):
            streamed((0,), hidden, p * size, (p + 1) * size)
            gathers[1, p].third()
            lax.fori_loop(p * size, (p + 1) * size, keep_down, 0)
            scatters[1, p].first()
        for p in range(per):
            gathers[1, p].fourth()
        ahead((0, 1))
        dn2[...] = jnp.zeros_like(dn2)

        def hidden_back(j, s, s_down):
            cols = cols_of(j)
            row = pl.ds(8 + lax.div(unit_of(j) * chunk, width), 1)
            bcols = pl.ds(pl.multiple_of(lax.rem(unit_of(j) * chunk, width), chunk), chunk)
            grad = (nn(gm[...], mbuf[s_down]) * da[:, cols].astype(F32)).astype(BF)
            da[:, cols] = grad
            sums[row, bcols] = column_sum(grad.astype(F32))
            dn2[...] += nt(grad, mbuf[s])

        streamed((0, 1), hidden_back)

        def back(r):
            value = mid[r]
            unit_two, scale_two = norm_stats(value)
            grad = dn2[r]
            total = cot[r] + norm_back(grad, unit_two, scale_two, rows12[1:2, :])
            cot[r] = total
            branch = total.astype(BF)
            gaf[own_rows(r, tail)] = branch
            sums[1:2, :] += column_sum(grad * unit_two)
            sums[6:7, :] += column_sum(grad)
            sums[5:6, :] += column_sum(branch.astype(F32))

        loop_rows(rows, tail, back)
        wire.sent(blocks[0].plans())
        gas.start()
        turn(n2)
        def give_up(j, carry):
            sending(1, j).wait_send()
            give(0, j, da[:, cols_of(j)])
            return carry

        lax.fori_loop(0, count, give_up, 0)
        scatters[1, 0].second()

        def keep_up(j, carry):
            keep(0, j, da[:, cols_of(j)])
            return carry

        for p in range(per):
            lax.fori_loop(p * size, (p + 1) * size, keep_up, 0)
            if p:
                scatters[1, p].second()
        scatters[0, 0].first()
        ahead((1,))
        gas.step(1)
        scatters[1, 0].third()
        lines[1, 0].start()
        dn2[...] = jnp.zeros_like(dn2)

        def output(j, s):
            dn2[...] += nt(hmid[:, cols_of(j)], mbuf[s])

        streamed((1,), output)

        def set_out(r):
            dn2[r] = mid[r] + (dn2[r] + rows12[7:8, :])

        loop_rows(rows, tail, set_out)
        out_copy = pltpu.make_async_copy(dn2, out_ref, osem.at[0])
        out_copy.start()
        for p in range(1, per):
            scatters[1, p].third()
            lines[1, p].start()
        for j in range(count):
            sending(0, j).wait_send()
        out_copy.wait()

    ff = size * unit
    pl.run_scoped(
        mlp,
        pltpu.VMEM((6, width, chunk), BF),
        pltpu.VMEM((rows, ff), BF),
        pltpu.VMEM((rows, ff), BF),
        pltpu.VMEM((rows, width), BF),
        pltpu.VMEM((rows, width), BF),
        pltpu.VMEM((width, rows), BF),
        pltpu.VMEM((2, ab * mrows, rows), BF),
        pltpu.VMEM((per, b_size, a_size, size, mrows, chunk), BF),
        pltpu.VMEM((rows, width), F32),
    )

    def attention(gat, do, dqkv, dk, dv, wg):
        def own_line(k):
            for p in range(per):
                here = held.at[k * per + p, spot.b, spot.a, spot.t]

                def set_row(r):
                    gtot[r, p * chunk:(p + 1) * chunk] = here[r].astype(F32)

                loop_rows(mrows, tile, set_row)

        def line_total(p):
            return lambda ref, h: add_tiled(gtot.at[:, pl.ds(p * chunk, chunk)], ref, tile)

        def line_step(k, p, s):
            third = lines[k, p].count() // 3
            lines[k, p].step(s * third, (s + 1) * third, line_total(p))

        def arrived(t):
            r = pl.ds(pl.multiple_of(t * rows, rows), rows)
            value = gaf[r]
            do[r] = nn(value, wf[3]).astype(BF)
            gat[:, r] = value.T

        dk[...] = jnp.zeros_like(dk)
        dv[...] = jnp.zeros_like(dv)

        half = width // 2

        def norm_grad(i):
            r = pl.ds(pl.multiple_of(i * rows, rows), rows)
            dqkv[1, r] = dk[r].astype(BF)
            dqkv[2, r] = dv[r].astype(BF)
            for first in range(0, width, half):
                cols = slice(first, first + half)
                part[r, cols] = sum(nt(dqkv[j, r], wf[j, cols, :]) for j in range(3)).astype(BF)
            blocks[1].start_traced(i)

        plan = {(1, p, n): n + 1 + p for p in range(per) for n in range(end - 1)}
        plan = {key: at for key, at in plan.items() if at < size}

        def arrive_back(k, carry):
            for n in range(1, size):
                @pl.when(k == n)
                def _():
                    if n == 1 and size > 2:
                        gas.step(2)
                    for key, at in plan.items():
                        if at == n:
                            line_step(*key)
                    if n == max(1, end - 1):
                        scatters[0, 0].second()
                        for p in range(1, per):
                            scatters[0, p].first()

            @pl.when((k == end) & (spot.t == 0))
            def _():
                scatters[0, 0].third()
                lines[0, 0].start()

            @pl.when(k >= 3)
            def _():
                gas.step(k)

            def side(i, inner):
                t = spot.t + (2 * i - 1) * k

                @pl.when((t >= 0) & (t < size) & ((i == 0) | (k >= 1)))
                def _():
                    arrived(t)

                return inner

            lax.fori_loop(0, 2, side, 0)
            for i in range(size):
                @pl.when((i == spot.t - k) | (i == spot.t + k))
                def _():
                    start, stop = i * rows, (i + 1) * rows
                    block_bias(seg_col, seg_row, bias, start, rows, stop)
                    attend_block_back(qkv, bias, lse, do, dqkv.at[0], dk, dv, start, rows)

            def ready(n, inner):
                i = jnp.where(lax.rem(n, 2) == 0, end - lax.div(n, 2), lax.div(n, 2))

                @pl.when(jnp.maximum(end - spot.t, spot.t - i) == k)
                def _():
                    norm_grad(i)

                return inner

            lax.fori_loop(0, size, ready, 0)
            return carry

        lax.fori_loop(0, size, arrive_back, 0)
        gas.owe()
        blocks[1].owe_starts()
        blocks[1].start_middle()
        loop_rows(rows, tail, lambda r: set_total(r))
        own_line(1)
        for p in range(per):
            for n in range(end):
                if (1, p, n) not in plan:
                    line_step(1, p, n)
        downg[...] = gtot[...].T
        stores = fetch([pltpu.make_async_copy(downg, downg_ref, osem.at[1])])
        events = blocks[1].count()

        @pl.when(spot.t != 0)
        def _():
            scatters[0, 0].third()
            lines[0, 0].start()

        def first_norm(r):
            unit_one, _ = norm_stats(xf[r].astype(F32))
            term = part[r].astype(F32)
            sums[0:1, :] += column_sum(term * unit_one)
            sums[2:3, :] += column_sum(term)

        loop_rows(seq, tail, first_norm)
        sums[3:4, column] = column_sum(dqkv[0].astype(F32))
        sums[4:5, column] = column_sum(dqkv[2].astype(F32))
        for d in range(geo.dp):
            spart[d] = sums[:, d * piece:(d + 1) * piece]
        for step in range(1, geo.dp):
            to = ring_next(spot.d, step, geo.dp)
            wire.start(small + step - 1, spart.at[to], sland.at[step - 1], spot.at_d(to))
        stot[...] = spart[spot.d]
        blocks[1].step(0, events // 3, mid_total)
        for p in range(1, per):
            scatters[0, p].second()
        def wgrad(r):
            for j in range(3):
                wg[j, r] = nn(n1t[r], dqkv[j]).astype(BF)
            wg[3, r] = nn(gat[r], att[...]).astype(BF)

        loop_rows(width, min(256, width), wgrad)

        def wrows_of(i, core):
            return pl.ds(pl.multiple_of((i * 2 + core) * wrows, wrows), wrows)

        for i in range(ab):
            wire.start(wzero + i, wg.at[:, wrows_of(i, 1 - spot.c)], wheld.at[0, i // a_size, i % a_size], sibling)
        for p in range(1, per):
            scatters[0, p].third()
            lines[0, p].start()
        blocks[1].start_near()
        own_line(0)
        blocks[1].step(events // 3, 2 * events // 3, mid_total)
        for i in range(ab):
            here = wheld.at[0, i // a_size, i % a_size]
            wire.landed(wzero + i, here, sibling)
            wscatter.add(here, wg.at[:, wrows_of(i, spot.c)])
        wscatter.first()
        for step in range(1, geo.dp):
            wire.landed(small + step - 1, sland.at[step - 1], spot.at_d(ring_prev(spot.d, step, geo.dp)))
            stot[...] += sland[step - 1]
        for step in range(1, size):
            wire.start(last + step - 1, stot, tland.at[step - 1], spot.at_t(ring_next(spot.t, step, size)))
        if end > 1:
            line_step(0, 0, 0)
        wscatter.second()
        for n in range(1, end - 1):
            line_step(0, 0, n)
        for p in range(1, per):
            for n in range(end - 1):
                line_step(0, p, n)
        blocks[1].step(2 * events // 3, events, mid_total)

        def back(r):
            unit_one, scale_one = norm_stats(xf[own_rows(r, tail)].astype(F32))
            cot[r] = cot[r] + norm_back(mid[r], unit_one, scale_one, rows12[0:1, :])

        loop_rows(rows, tail, back)
        stores += fetch([pltpu.make_async_copy(cot, igrad_ref, osem.at[0])])
        wscatter.third()
        sums_w = wheld.at[0, spot.b, spot.a]
        for j in range(3):
            awg[j] = sums_w[j].astype(F32)
        owg[...] = sums_w[3].astype(F32).T
        stores += fetch([
            pltpu.make_async_copy(awg, awg_ref, osem.at[2]),
            pltpu.make_async_copy(owg, owg_ref, osem.at[3])])
        for p in range(per):
            line_step(0, p, end - 1)
        stores += fetch([pltpu.make_async_copy(gtot, upg_ref, osem.at[6])])
        for step in range(1, size):
            wire.landed(last + step - 1, tland.at[step - 1], spot.at_t(ring_prev(spot.t, step, size)))
        total = stot[...]
        for step in range(1, size):
            total = total + tland[step - 1]
        gaing[...] = total[0:2, :]
        for i in range(biasg.shape[0]):
            biasg[i] = total[2 + i:3 + i, :]
        stores += fetch([
            pltpu.make_async_copy(gaing, gaing_ref, osem.at[4]),
            pltpu.make_async_copy(biasg, biasg_ref, osem.at[5])])
        wire.drain()
        settle(stores)

    pl.run_scoped(
        attention,
        pltpu.VMEM((width, seq), BF),
        pltpu.VMEM((seq, heads), BF),
        pltpu.VMEM((3, seq, heads), BF),
        pltpu.VMEM((seq, heads), F32),
        pltpu.VMEM((seq, heads), F32),
        pltpu.VMEM((4, width, heads), BF),
    )


def block_kernel(geo, x, aw, ow, up, down, gains, biases, seg_row, cot):
    rows, width = x.shape
    wrows, heads = aw.shape[1:]
    mrows, unit = up.shape
    size = geo.tensor
    seq = size * rows
    chunk = min(512, unit)
    per = unit // chunk
    sems = ((2 * per + 1) * (gather_sems(geo) + scatter_sems(geo)) + (size - 1) * (2 * 4 + 2 * 4 + 4 * per * 2 + 1) + 2 * per * size
            + geo.a_size * geo.b_size + 2 * (geo.dp - 1))
    like = lambda x: pltpu.VMEM(x.shape, x.dtype)
    return pl.pallas_call(
        functools.partial(block_body, geo),
        out_shape=(
            jax.ShapeDtypeStruct((2, unit // chunk, size, width, chunk), BF),
            jax.ShapeDtypeStruct((rows, width), F32),
            jax.ShapeDtypeStruct((rows, width), F32),
            jax.ShapeDtypeStruct((3, wrows, heads), F32),
            jax.ShapeDtypeStruct((heads, wrows), F32),
            jax.ShapeDtypeStruct((mrows, unit), F32),
            jax.ShapeDtypeStruct((unit, mrows), F32),
            jax.ShapeDtypeStruct((2, wrows), F32),
            jax.ShapeDtypeStruct((10, 1, wrows), F32),
        ),
        in_specs=[ANY] * 9,
        out_specs=(ANY,) * 9,
        scratch_shapes=[
            pltpu.VMEM((seq, width), BF),
            pltpu.VMEM((rows, width), BF),
            pltpu.VMEM((width, seq), BF),
            pltpu.VMEM((3, seq, heads), BF),
            pltpu.VMEM((seq, heads), BF),
            pltpu.VMEM((seq, 128), F32),
            pltpu.VMEM((4, width, heads), BF),
            pltpu.VMEM((seq, width), BF),
            pltpu.VMEM((2, size - 1, rows, width), BF),
            pltpu.VMEM((rows, seq), F32),
            pltpu.VMEM((rows, width), F32),
            pltpu.VMEM((rows, width), F32),
            pltpu.VMEM((seq, width), BF),
            pltpu.VMEM((12, width), F32),
            pltpu.VMEM((seq, 128), jnp.int32),
            like(seg_row),
            pltpu.VMEM((geo.dp, 12, wrows), F32),
            pltpu.VMEM((4, wrows, heads), BF),
            like(ow), like(down), pltpu.VMEM((2, unit // chunk, mrows, chunk), BF), like(gains), like(biases),
            pltpu.VMEM((12, wrows), F32),
            pltpu.VMEM((12, width), F32),
            pltpu.VMEM((geo.dp, 12, wrows), F32),
            pltpu.VMEM((geo.dp - 1, 12, wrows), F32),
            pltpu.VMEM((12, wrows), F32),
            pltpu.VMEM((size - 1, 12, wrows), F32),
            *scatter_bufs(geo, 2 * (unit // chunk), 2 * (unit // chunk), size, mrows, chunk),
            *scatter_bufs(geo, 1, 1, 4, wrows, heads),
            pltpu.VMEM((2 * (unit // chunk), 2, size - 1, mrows, chunk), BF),
            pltpu.VMEM((mrows, unit), F32),
            pltpu.VMEM((unit, mrows), F32),
            pltpu.VMEM((3, wrows, heads), F32),
            pltpu.VMEM((heads, wrows), F32),
            pltpu.VMEM((2, wrows), F32),
            pltpu.VMEM((10, 1, wrows), F32),
            pltpu.SemaphoreType.DMA((sems,)), pltpu.SemaphoreType.DMA((sems,)), pltpu.SemaphoreType.DMA((8 + unit // chunk,)),
            pltpu.SemaphoreType.DMA((6, 2)), pltpu.SemaphoreType.DMA((7,))],
        compiler_params=pltpu.CompilerParams(collective_id=1, has_side_effects=True, vmem_limit_bytes=62 * 2**20),
        name="block",
    )(x, aw, ow, up, down, gains, biases, seg_row, cot)


def hand_over_body(*refs):
    *refs, loads, stores = refs
    count = len(refs) // 3
    ins, outs, bufs = refs[:count], refs[count:2 * count], refs[2 * count:]
    coming = fetch([pltpu.make_async_copy(ins[i], bufs[i], loads.at[i]) for i in range(count)])
    going = []
    for i in range(count):
        coming[i].wait()
        going += fetch([pltpu.make_async_copy(bufs[i], outs[i], stores.at[i])])
    settle(going)


def hand_over(parts):
    return pl.pallas_call(
        hand_over_body,
        out_shape=tuple(jax.ShapeDtypeStruct(part.shape, part.dtype) for part in parts),
        in_specs=[ANY] * len(parts),
        out_specs=(ANY,) * len(parts),
        scratch_shapes=[pltpu.VMEM(part.shape, part.dtype) for part in parts] + [pltpu.SemaphoreType.DMA((len(parts),))] * 2,
        name="hand_over",
    )(*parts)


def per_device(geo, activations, segments, attn_weight, out_weight, up_weight, down_weight, norm_gains, bias_rows, cotangent):
    outs = block_kernel(
        geo, activations, attn_weight[0], out_weight[0], up_weight[0], down_weight[0], norm_gains[0], bias_rows[0], segments[None, :],
        cotangent)
    outs = hand_over(outs[1:])
    return outs[:2] + tuple(part[None] for part in outs[2:7]) + (outs[7].reshape(1, 10, -1),)


def solution(mesh):
    geo = Geometry(mesh.shape["dp"], mesh.shape["tensor"])
    return jax.shard_map(
        functools.partial(per_device, geo),
        mesh=mesh,
        in_specs=(
            P(("dp", "tensor"), None),
            P("dp"),
            P(None, None, "dp", "tensor"),
            P(None, "tensor", "dp"),
            P(None, "dp", "tensor"),
            P(None, "tensor", "dp"),
            P(None, None, "dp"),
            P(None, None, "dp"),
            P(("dp", "tensor"), None),
        ),
        out_specs=(
            P(("dp", "tensor"), None),
            P(("dp", "tensor"), None),
            P(None, None, "dp", "tensor"),
            P(None, "tensor", "dp"),
            P(None, "dp", "tensor"),
            P(None, "tensor", "dp"),
            P(None, None, "dp"),
            P(None, None, "dp"),
        ),
        check_vma=False,
    )
```

```python
import functools

import jax
import jax.numpy as jnp
from jax import lax
from jax.experimental import pallas as pl
from jax.experimental.pallas import tpu as pltpu
from jax.sharding import PartitionSpec as P

HD = 64
EPSILON = 1e-05
MASKED = -1e30
MESH_ID = pl.DeviceIdType.MESH
BF = jnp.bfloat16
F32 = jnp.float32
ANY = pl.BlockSpec(memory_space=pl.ANY)
VM = pl.BlockSpec(memory_space=pltpu.VMEM)


def layer_norm(values, gain_row, shift_row):
    center = values - jnp.mean(values, axis=-1, keepdims=True)
    spread = jnp.mean(center * center, axis=-1, keepdims=True)
    return center * lax.rsqrt(spread + EPSILON) * gain_row + shift_row


def norm_stats(values):
    center = values - jnp.mean(values, axis=-1, keepdims=True)
    spread = jnp.mean(center * center, axis=-1, keepdims=True)
    scale = lax.rsqrt(spread + EPSILON)
    return center * scale, scale


def norm_back(grad, unit, scale, gain_row):
    u = grad * gain_row
    mean_u = jnp.mean(u, axis=-1, keepdims=True)
    mean_ux = jnp.mean(u * unit, axis=-1, keepdims=True)
    return scale * (u - mean_u - unit * mean_ux)


def gelu_tanh(values):
    return jax.nn.gelu(values, approximate=True)


class Geometry:
    def __init__(self, dp, tensor):
        self.dp, self.tensor = dp, tensor
        self.c_size = 2
        rest = dp // 2
        self.a_size = 1
        while self.a_size * self.a_size < rest:
            self.a_size *= 2
        self.b_size = rest // self.a_size
        assert self.a_size * self.b_size * 2 == dp

    def bind(self):
        spot = Spot()
        spot.geo = self
        spot.d = lax.axis_index("dp")
        spot.t = lax.axis_index("tensor")
        spot.c = lax.rem(spot.d, 2)
        half = lax.div(spot.d, 2)
        spot.a = lax.rem(half, self.a_size)
        spot.b = lax.div(half, self.a_size)
        return spot


class Spot:
    def rank(self, b, a, c):
        return (b * self.geo.a_size + a) * 2 + c

    def at_t(self, t):
        return (self.d, t)

    def at_d(self, d):
        return (d, self.t)


def ring_next(rank, step, size):
    return lax.rem(rank + step, size)


def ring_prev(rank, step, size):
    return lax.rem(rank + size - step, size)


class Wire:
    def __init__(self, send, recv, base):
        self.send_sems, self.recv_sems, self.base = send, recv, base
        self.count = self.grouped = 0
        self.pending, self.quiet, self.totals, self.group_of = [], [], [], {}

    def take_group(self, n, whole, device):
        first = self.base + self.grouped
        self.grouped += n
        group = self.base + len(self.totals)
        self.group_of.update((i, group) for i in range(first, first + n))
        self.totals.append((group, whole, device))
        return first

    def take(self, n):
        first = self.count
        self.count += n
        return first

    def copy(self, i, src, dst, device):
        return pltpu.make_async_remote_copy(
            src_ref=src, dst_ref=dst, send_sem=self.send_sems.at[self.group_of.get(i, i) if isinstance(i, int) else i], recv_sem=self.recv_sems.at[i],
            device_id=device, device_id_type=MESH_ID)

    def plan(self, i, src, dst, device, when=None):
        planned = self.copy(i, src, dst, device), when
        if isinstance(i, int) and i in self.group_of:
            self.quiet.append(planned)
        return planned

    def go(self, planned):
        copy, when = planned
        if when is None:
            copy.start()
        else:
            pl.when(when)(copy.start)
        self.owe(planned)

    def owe(self, planned):
        if not any(other is planned for other in self.pending + self.quiet):
            self.pending.append(planned)

    def start(self, i, src, dst, device, when=None):
        self.go(self.plan(i, src, dst, device, when))

    def landed(self, i, dst, device, when=None):
        copy = self.copy(i, dst, dst, device)
        if when is None:
            copy.wait_recv()
        else:
            pl.when(when)(copy.wait_recv)

    def sent(self, plans):
        for planned in plans:
            copy, when = planned
            self.pending = [other for other in self.pending if other is not planned]
            if when is None:
                copy.wait_send()
            else:
                pl.when(when)(copy.wait_send)

    def drain(self):
        for copy, when in self.pending:
            if when is None:
                copy.wait_send()
            else:
                pl.when(when)(copy.wait_send)
        for group, whole, device in self.totals:
            pltpu.make_async_remote_copy(
                src_ref=whole, dst_ref=whole, send_sem=self.send_sems.at[group], recv_sem=self.recv_sems.at[group],
                device_id=device, device_id_type=MESH_ID).wait_send()
        self.pending = []


def greet(spot):
    geo = spot.geo
    barrier = pltpu.get_barrier_semaphore()
    total = 0
    for step in range(1, geo.tensor):
        pl.semaphore_signal(barrier, inc=1, device_id=spot.at_t(ring_next(spot.t, step, geo.tensor)), device_id_type=MESH_ID)
        total += 1
    for step in range(1, geo.dp):
        pl.semaphore_signal(barrier, inc=1, device_id=spot.at_d(ring_next(spot.d, step, geo.dp)), device_id_type=MESH_ID)
        total += 1
    return lambda: pl.semaphore_wait(barrier, total)


def halves(ref, count, part):
    rows = ref.shape[-2] // count
    return ref.at[(slice(None),) * (len(ref.shape) - 2) + (pl.ds(part * rows, rows),)]


class LineGather:
    def __init__(self, spot, wire, src, slot, parts=2):
        self.spot, self.wire, self.src, self.slot, self.parts = spot, wire, src, slot, parts
        self.size = size = spot.geo.tensor
        self.base = [wire.take((size - 1) * parts) for _ in range(2)]
        t = spot.t
        self.sends = {}
        for k in range(size - 1):
            for part in range(parts):
                for side in range(2):
                    self.sends[k, part, side] = self.plan(k, part, side)

    def place(self, k, side):
        t = self.spot.t
        origin = t - k if side == 0 else t + k
        there = (origin >= 0) & (origin < self.size)
        onward = t + 1 if side == 0 else t - 1
        return origin, there, t - 1 if side == 0 else t + 1, onward, there & (onward >= 0) & (onward < self.size)

    def plan(self, k, part, side):
        origin, _, _, onward, going = self.place(k, side)
        piece = halves(self.slot(origin), self.parts, part)
        first = isinstance(k, int) and k == 0
        src = halves(self.src, self.parts, part) if first else piece
        return self.wire.plan(self.base[side] + k * self.parts + part, src, piece, self.spot.at_t(onward), when=going)

    def start(self, where=None):
        for part in range(self.parts):
            for side in range(2):
                planned = self.sends[0, part, side]
                if where is None:
                    self.wire.go(planned)
                else:
                    copy, when = planned
                    pl.when(when & self.inner(where))(copy.start)
                    self.wire.owe(planned)

    def inner(self, where):
        inner = (self.spot.t >= 1) & (self.spot.t < self.size - 1)
        return inner if where else jnp.logical_not(inner)

    def step(self, k, where=None):
        for part in range(self.parts):
            for side in range(2):
                origin, there, near, _, _ = self.place(k, side)
                if where is not None:
                    there = there & self.inner(where)
                piece = halves(self.slot(origin), self.parts, part)
                self.wire.landed(self.base[side] + (k - 1) * self.parts + part, piece, self.spot.at_t(near), when=there)
                if not isinstance(k, int):
                    copy, going = self.plan(k, part, side)
                    pl.when(going & (k < self.size - 1))(copy.start)
                elif k < self.size - 1 and where is not False:
                    self.wire.go(self.sends[k, part, side])

    def owe(self):
        for (k, part, side), planned in self.sends.items():
            if k > 0:
                self.wire.owe(planned)


class LineScatter:
    def __init__(self, spot, wire, part, land, add, rising=None, parts=2):
        self.spot, self.wire, self.part, self.land, self.add, self.parts = spot, wire, part, land, add, parts
        self.size = spot.geo.tensor
        base = self.base = [wire.take((self.size - 1) * parts) for _ in range(2)]
        t, end = spot.t, self.size - 1
        self.starts, self.hops = {}, {}
        for h in range(parts):
            for j in range(self.size):
                if j > 0:
                    self.starts[0, j, h] = wire.plan(
                        base[0] + (j - 1) * parts + h, halves(part(j), parts, h), halves(land(0, j), parts, h), spot.at_t(1), when=t == 0)
                if j < end:
                    self.starts[1, j, h] = wire.plan(
                        base[1] + j * parts + h, halves(part(j), parts, h), halves(land(1, j), parts, h), spot.at_t(end - 1), when=t == end)
        self.events = []
        for side in range(2):
            place = t if side == 0 else end - t
            if side == rising:
                for e in range(1, 2 * end):
                    far = e + 1 - place
                    self.events.append((10 * e, side, far if side == 0 else end - far, (place >= 1) & (far >= place) & (far <= end)))
            else:
                for s in range(1, self.size):
                    far = end - s + place
                    at = 10 * s + (0 if rising is None else 15)
                    self.events.append((at, side, far if side == 0 else end - far, (place >= 1) & (s >= place)))
        self.events.sort(key=lambda event: event[0])
        self.hops = []
        for _, side, j, here in self.events:
            near = spot.at_t(t - 1 if side == 0 else t + 1)
            away = spot.at_t(t + 1 if side == 0 else t - 1)
            for h in range(parts):
                held = halves(land(side, j), parts, h)
                i = base[side] + (j - 1 + side) * parts + h
                self.hops.append((here & (j == t), here & (j != t), j, h, held, wire.copy(i, held, held, near),
                                  wire.plan(i, held, held, away, when=here & (j != t))))

    def start_block(self, j):
        for side in range(2):
            for h in range(self.parts):
                if (side, j, h) in self.starts:
                    self.wire.go(self.starts[side, j, h])

    def start_traced(self, j):
        spot, t, end = self.spot, self.spot.t, self.size - 1
        for side in range(2):
            first, to = (0, 1) if side == 0 else (end, end - 1)
            for h in range(self.parts):
                copy, when = self.wire.plan(
                    self.base[side] + (j - 1 + side) * self.parts + h, halves(self.part(j), self.parts, h),
                    halves(self.land(side, j), self.parts, h), spot.at_t(to), when=(t == first) & (j != first) & (j != 1 if side == 0 else (j == 0) | (j == end - 1)))
                pl.when(when)(copy.start)

    def start_middle(self):
        for j in range(1, self.size - 2):
            for h in range(self.parts):
                self.wire.go(self.starts[1, j, h])

    def start_near(self):
        for h in range(self.parts):
            self.wire.go(self.starts[0, 1, h])

    def owe_starts(self):
        for planned in self.starts.values():
            self.wire.owe(planned)

    def start(self):
        for n in range(self.size):
            for side, j in ((0, self.size - 1 - n), (1, n)):
                for h in range(self.parts):
                    if (side, j, h) in self.starts:
                        self.wire.go(self.starts[side, j, h])

    def count(self):
        return len(self.hops)

    def step(self, first, last, total):
        for final, passing, j, h, held, landing, onward in self.hops[first:last]:
            @pl.when(final)
            def _():
                landing.wait_recv()
                total(held, h)

            @pl.when(passing)
            def _():
                landing.wait_recv()
                self.add(held, halves(self.part(j), self.parts, h))

            self.wire.go(onward)

    def plans(self):
        return list(self.starts.values()) + [hop[-1] for hop in self.hops]


def add_tiled(dst, src, tile):
    def step(i, carry):
        rows = pl.ds(pl.multiple_of(i * tile, tile), tile)
        dst[rows] = (dst[rows].astype(F32) + src[rows].astype(F32)).astype(dst.dtype)
        return carry

    lax.fori_loop(0, dst.shape[0] // tile, step, 0)


class WeightGather:
    def __init__(self, spot, wire, rows, full):
        geo = spot.geo
        self.spot, self.wire, self.full, self.rows = spot, wire, full, rows
        self.slots = full.shape[0]
        self.half = self.slots // 2
        a, b = geo.a_size, geo.b_size
        counts = [a - 1, b - 1, (b - 1) * a, (a - 1) * b, 2 * a * b]
        whole = full.at[:, pl.ds(0, sum(counts) // 2 * rows)]
        firsts = [wire.take_group(sum(counts), whole, spot.at_d(spot.rank(spot.b, spot.a, 1 - spot.c)))]
        for n in counts[:-1]:
            firsts.append(firsts[-1] + n)
        self.one_a, self.one_b, self.two_a, self.two_b, self.last = firsts
        self.plan_shares()
        self.plan_hops()

    def span(self, d):
        return pl.ds(pl.multiple_of(d * self.rows, self.rows), self.rows)

    def low(self, d):
        return self.full.at[pl.ds(0, self.half), self.span(d)]

    def high(self, d):
        return self.full.at[pl.ds(self.half, self.slots - self.half), self.span(d)]

    def plan_shares(self):
        spot, geo = self.spot, self.spot.geo
        self.shares = {}
        for j in range(geo.b_size):
            for i in range(geo.a_size):
                held = spot.rank(ring_prev(spot.b, j, geo.b_size), ring_prev(spot.a, i, geo.a_size), spot.c)
                sibling = spot.rank(spot.b, spot.a, 1 - spot.c)
                for part in range(2):
                    half = (self.low, self.high)[part](held)
                    self.shares[part, j, i] = self.wire.plan(
                        self.last + 2 * (j * geo.a_size + i) + part, half, half, spot.at_d(sibling))

    def share(self, part, j, i):
        self.wire.go(self.shares[part, j, i])

    def plan_hops(self):
        spot, geo, wire = self.spot, self.spot.geo, self.wire
        self.ones, self.twos_a, self.twos_b = [], {}, {}
        mine = spot.d
        for j in range(1, geo.a_size):
            to = spot.rank(spot.b, ring_next(spot.a, j, geo.a_size), spot.c)
            self.ones.append(wire.plan(self.one_a + j - 1, self.low(mine), self.low(mine), spot.at_d(to)))
        for j in range(1, geo.b_size):
            to = spot.rank(ring_next(spot.b, j, geo.b_size), spot.a, spot.c)
            self.ones.append(wire.plan(self.one_b + j - 1, self.high(mine), self.high(mine), spot.at_d(to)))
        for i in range(geo.a_size):
            held = spot.rank(spot.b, ring_prev(spot.a, i, geo.a_size), spot.c)
            for j in range(1, geo.b_size):
                to = spot.rank(ring_next(spot.b, j, geo.b_size), spot.a, spot.c)
                self.twos_a[i, j] = wire.plan(self.two_a + (j - 1) * geo.a_size + i, self.low(held), self.low(held), spot.at_d(to))
        for i in range(geo.b_size):
            held = spot.rank(ring_prev(spot.b, i, geo.b_size), spot.a, spot.c)
            for j in range(1, geo.a_size):
                to = spot.rank(spot.b, ring_next(spot.a, j, geo.a_size), spot.c)
                self.twos_b[i, j] = wire.plan(self.two_b + (j - 1) * geo.b_size + i, self.high(held), self.high(held), spot.at_d(to))

    def first(self):
        for planned in self.ones:
            self.wire.go(planned)
        self.share(0, 0, 0)
        self.share(1, 0, 0)

    def second(self):
        spot, geo = self.spot, self.spot.geo
        for i in range(geo.a_size):
            held = spot.rank(spot.b, ring_prev(spot.a, i, geo.a_size), spot.c)
            if i:
                self.wire.landed(self.one_a + i - 1, self.low(held), spot.at_d(held))
                self.share(0, 0, i)
            for j in range(1, geo.b_size):
                self.wire.go(self.twos_a[i, j])
        for i in range(geo.b_size):
            held = spot.rank(ring_prev(spot.b, i, geo.b_size), spot.a, spot.c)
            if i:
                self.wire.landed(self.one_b + i - 1, self.high(held), spot.at_d(held))
                self.share(1, i, 0)
            for j in range(1, geo.a_size):
                self.wire.go(self.twos_b[i, j])

    def third(self):
        spot, geo = self.spot, self.spot.geo
        for j in range(1, geo.b_size):
            for i in range(geo.a_size):
                held = spot.rank(ring_prev(spot.b, j, geo.b_size), ring_prev(spot.a, i, geo.a_size), spot.c)
                source = spot.rank(ring_prev(spot.b, j, geo.b_size), spot.a, spot.c)
                self.wire.landed(self.two_a + (j - 1) * geo.a_size + i, self.low(held), spot.at_d(source))
                self.share(0, j, i)
        for j in range(1, geo.a_size):
            for i in range(geo.b_size):
                held = spot.rank(ring_prev(spot.b, i, geo.b_size), ring_prev(spot.a, j, geo.a_size), spot.c)
                source = spot.rank(spot.b, ring_prev(spot.a, j, geo.a_size), spot.c)
                self.wire.landed(self.two_b + (j - 1) * geo.b_size + i, self.high(held), spot.at_d(source))
                self.share(1, i, j)

    def fourth(self):
        spot, geo = self.spot, self.spot.geo
        sibling = spot.rank(spot.b, spot.a, 1 - spot.c)
        for j in range(geo.b_size):
            for i in range(geo.a_size):
                held = spot.rank(ring_prev(spot.b, j, geo.b_size), ring_prev(spot.a, i, geo.a_size), 1 - spot.c)
                for part in range(2):
                    half = (self.low, self.high)[part](held)
                    self.wire.landed(self.last + 2 * (j * geo.a_size + i) + part, half, spot.at_d(sibling))


def gather_sems(geo):
    return geo.a_size + geo.b_size - 2 + (geo.b_size - 1) * geo.a_size + (geo.a_size - 1) * geo.b_size + 2 * geo.a_size * geo.b_size


class WeightScatter:
    def __init__(self, spot, wire, held, one_a, one_b, two_a, two_b):
        geo = spot.geo
        self.spot, self.wire, self.held = spot, wire, held
        self.one_a_buf, self.one_b_buf, self.two_a_buf, self.two_b_buf = one_a, one_b, two_a, two_b
        self.slots, self.rows = held.shape[2], held.shape[3]
        self.half = self.slots // 2
        self.one_a = wire.take(geo.a_size - 1)
        self.one_b = wire.take(geo.b_size - 1)
        self.two_a = wire.take(geo.b_size - 1)
        self.two_b = wire.take(geo.a_size - 1)
        low, high = pl.ds(0, self.half), pl.ds(self.half, self.half)
        self.sends = []
        for j in range(1, geo.a_size):
            a = ring_next(spot.a, j, geo.a_size)
            self.sends.append(wire.plan(self.one_a + j - 1, held.at[:, a, low], one_a.at[j - 1], spot.at_d(spot.rank(spot.b, a, spot.c))))
        for j in range(1, geo.b_size):
            b = ring_next(spot.b, j, geo.b_size)
            self.sends.append(wire.plan(self.one_b + j - 1, held.at[b, :, high], one_b.at[j - 1], spot.at_d(spot.rank(b, spot.a, spot.c))))
        self.later = []
        for j in range(1, geo.b_size):
            b = ring_next(spot.b, j, geo.b_size)
            self.later.append(wire.plan(self.two_a + j - 1, held.at[b, spot.a, low], two_a.at[j - 1], spot.at_d(spot.rank(b, spot.a, spot.c))))
        for j in range(1, geo.a_size):
            a = ring_next(spot.a, j, geo.a_size)
            self.later.append(wire.plan(self.two_b + j - 1, held.at[spot.b, a, high], two_b.at[j - 1], spot.at_d(spot.rank(spot.b, a, spot.c))))

    def add(self, dst, src):
        tile = min(64, self.rows)
        per = self.rows // tile

        def step(i, carry):
            rows = pl.ds(pl.multiple_of(lax.rem(i, per) * tile, tile), tile)
            j = lax.div(i, per)
            dst[j, rows] = (dst[j, rows].astype(F32) + src[j, rows].astype(F32)).astype(dst.dtype)
            return carry

        lax.fori_loop(0, dst.shape[0] * per, step, 0)

    def first(self):
        for planned in self.sends:
            self.wire.go(planned)

    def second(self):
        spot, geo = self.spot, self.spot.geo
        low, high = pl.ds(0, self.half), pl.ds(self.half, self.half)
        for j in range(1, geo.a_size):
            self.wire.landed(self.one_a + j - 1, self.one_a_buf.at[j - 1], spot.at_d(spot.rank(spot.b, ring_prev(spot.a, j, geo.a_size), spot.c)))
            for b in range(geo.b_size):
                self.add(self.held.at[b, spot.a, low], self.one_a_buf.at[j - 1, b])
        for j in range(1, geo.b_size):
            self.wire.landed(self.one_b + j - 1, self.one_b_buf.at[j - 1], spot.at_d(spot.rank(ring_prev(spot.b, j, geo.b_size), spot.a, spot.c)))
            for a in range(geo.a_size):
                self.add(self.held.at[spot.b, a, high], self.one_b_buf.at[j - 1, a])
        for planned in self.later:
            self.wire.go(planned)

    def third(self):
        spot, geo = self.spot, self.spot.geo
        low, high = pl.ds(0, self.half), pl.ds(self.half, self.half)
        for j in range(1, geo.b_size):
            self.wire.landed(self.two_a + j - 1, self.two_a_buf.at[j - 1], spot.at_d(spot.rank(ring_prev(spot.b, j, geo.b_size), spot.a, spot.c)))
            self.add(self.held.at[spot.b, spot.a, low], self.two_a_buf.at[j - 1])
        for j in range(1, geo.a_size):
            self.wire.landed(self.two_b + j - 1, self.two_b_buf.at[j - 1], spot.at_d(spot.rank(spot.b, ring_prev(spot.a, j, geo.a_size), spot.c)))
            self.add(self.held.at[spot.b, spot.a, high], self.two_b_buf.at[j - 1])


def scatter_sems(geo):
    return 2 * (geo.a_size + geo.b_size - 2)


def scatter_bufs(geo, n, sets, slots, rows, width):
    a, b, half = geo.a_size, geo.b_size, slots // 2
    return [
        pltpu.VMEM((n, b, a, slots, rows, width), BF),
        pltpu.VMEM((sets, a - 1, b, half, rows, width), BF),
        pltpu.VMEM((sets, b - 1, a, half, rows, width), BF),
        pltpu.VMEM((sets, b - 1, half, rows, width), BF),
        pltpu.VMEM((sets, a - 1, half, rows, width), BF),
    ]


def loop_rows(count, tile, body, start=0):
    def step(i, carry):
        body(pl.ds(pl.multiple_of(start + i * tile, tile), tile))
        return carry

    lax.fori_loop(0, count // tile, step, 0)


def fetch(copies):
    for copy in copies:
        copy.start()
    return copies


def settle(copies):
    for copy in copies:
        copy.wait()


PAIR = 2 * HD


def nt(x, w):
    return lax.dot_general(x, w, (((1,), (1,)), ((), ())), preferred_element_type=F32)


def nn(x, w):
    return lax.dot_general(x, w, (((1,), (0,)), ((), ())), preferred_element_type=F32)


def tn(x, w):
    return lax.dot_general(x, w, (((0,), (0,)), ((), ())), preferred_element_type=F32)


def block_bias(seg_col, seg_row, bias, start, rows, keys):
    query = seg_col[start:start + rows, 0:1]
    for first in range(0, keys, rows):
        key = seg_row[:, first:first + rows]
        seen = query == key
        if first + rows > start:
            q_pos = start + lax.broadcasted_iota(jnp.int32, (rows, rows), 0)
            k_pos = first + lax.broadcasted_iota(jnp.int32, (rows, rows), 1)
            seen = seen & (k_pos <= q_pos)
        bias[:, first:first + rows] = jnp.where(seen, 0.0, MASKED).astype(F32)


def one_head(pair, head):
    lane = lax.broadcasted_iota(jnp.int32, pair.shape, 1)
    return jnp.where((lane < HD) if head == 0 else (lane >= HD), pair, jnp.zeros_like(pair))


def attend_block(qkv, bias, att, lse, start, rows):
    keys = start + rows
    width = qkv.shape[2]
    stat_lane = lax.broadcasted_iota(jnp.int32, (rows, 128), 1)
    stats = jnp.zeros((rows, 128), F32)
    for p in range(width // PAIR):
        lanes = slice(p * PAIR, (p + 1) * PAIR)
        query = qkv[0, start:keys, lanes]
        outs = []
        for head in range(2):
            s = nt(one_head(query, head), qkv[1, 0:keys, lanes]) + bias[:, 0:keys]
            top = jnp.max(s, axis=1, keepdims=True)
            e = jnp.exp(s - top)
            total = jnp.sum(e, axis=1, keepdims=True)
            prob = (e * (1.0 / total)).astype(BF)
            outs.append(nn(prob, qkv[2, 0:keys, lanes]))
            stats = jnp.where(stat_lane == 2 * p + head, top + jnp.log(total), stats)
        lane = lax.broadcasted_iota(jnp.int32, outs[0].shape, 1)
        att[start:keys, lanes] = jnp.where(lane < HD, outs[0], outs[1]).astype(BF)
    lse[start:keys, :] = stats


def attend_block_back(qkv, bias, lse, do, dq, dk, dv, start, rows):
    keys = start + rows
    width = qkv.shape[2]
    stat_lane = lax.broadcasted_iota(jnp.int32, (rows, 128), 1)
    stats = lse[start:keys, :]
    for p in range(width // PAIR):
        lanes = slice(p * PAIR, (p + 1) * PAIR)
        query = qkv[0, start:keys, lanes]
        grad = do[start:keys, lanes]
        dqs, dks, dvs = [], [], []
        for head in range(2):
            level = jnp.sum(jnp.where(stat_lane == 2 * p + head, stats, 0.0), axis=1, keepdims=True)
            s = nt(one_head(query, head), qkv[1, 0:keys, lanes]) + bias[:, 0:keys]
            prob = jnp.exp(s - level)
            d_prob = nt(one_head(grad, head), qkv[2, 0:keys, lanes])
            mixed = prob * d_prob
            ds = (mixed - prob * jnp.sum(mixed, axis=1, keepdims=True)).astype(BF)
            dqs.append(nn(ds, qkv[1, 0:keys, lanes]))
            dks.append(tn(ds, query))
            dvs.append(tn(prob.astype(BF), grad))
        lane = lax.broadcasted_iota(jnp.int32, dqs[0].shape, 1)
        dq[start:keys, lanes] = (jnp.where(lane < HD, dqs[0], dqs[1]) * (HD ** -0.5)).astype(dq.dtype)
        lane = lax.broadcasted_iota(jnp.int32, dks[0].shape, 1)
        dk[0:keys, lanes] += jnp.where(lane < HD, dks[0], dks[1])
        dv[0:keys, lanes] += jnp.where(lane < HD, dvs[0], dvs[1])


GELU_C = 0.7978845608028654


def gelu_parts(a):
    square = a * a
    tanh = jnp.tanh(GELU_C * a * (1.0 + 0.044715 * square))
    half = 0.5 * (1.0 + tanh)
    slope = half + 0.5 * a * (1.0 - tanh * tanh) * (GELU_C * (1.0 + 3 * 0.044715 * square))
    return a * half, slope


def column_sum(values):
    return jnp.sum(values, axis=0, keepdims=True)


def block_body(geo, x_ref, aw_ref, ow_ref, up_ref, down_ref, gain_ref, bias_ref, seg_ref, cot_ref,
               full, out_ref, igrad_ref, awg_ref, owg_ref, upg_ref, downg_ref, gaing_ref, biasg_ref,
               xf, n1, n1t, qkv, att, lse, wf, part, land, bias, mid, cot, gaf, rows12, seg_col, seg_row,
               sf, wsend, ow_in, down_in, msend, gain_in, bias_in, ssend,
               sums, spart, sland, stot, tland,
               held, one_a, one_b, two_a, two_b, wheld, wone_a, wone_b, wtwo_a, wtwo_b, mland,
               gtot, downg, awg, owg, gaing, biasg,
               send, recv, local, msem, osem):
    spot = geo.bind()
    groups = 2 * (up_ref.shape[1] // min(512, up_ref.shape[1])) + 1
    wire = Wire(send, recv, send.shape[0] - groups)
    size = geo.tensor
    rows, width = x_ref.shape
    seq = size * rows
    wrows, heads = aw_ref.shape[1:]
    mrows, unit = up_ref.shape
    a_size, b_size = geo.a_size, geo.b_size
    ab = a_size * b_size
    chunk = min(512, unit)
    per = unit // chunk
    pieces = msem.shape[1]
    count = size * per
    tail = min(64, rows)
    tile = min(64, mrows)
    end = size - 1
    sibling = spot.at_d(spot.rank(spot.b, spot.a, 1 - spot.c))
    wspan = pl.ds(pl.multiple_of(spot.d * wrows, wrows), wrows)
    mspan = pl.ds(pl.multiple_of(spot.d * mrows, mrows), mrows)
    column = pl.ds(pl.multiple_of(spot.t * heads, 128), heads)

    def block_of(ref, t):
        return ref.at[pl.ds(pl.multiple_of(t * rows, rows), rows)]

    def own_rows(r, n):
        return pl.ds(pl.multiple_of(spot.t * rows + r.start, n), n)

    weights = WeightGather(spot, wire, wrows, wf)
    halved = [(k, p) for k in range(2) for p in range(per)]
    wlines, gathers = {}, {}
    for k, p in halved:
        wlines[k, p] = LineGather(spot, wire, msend.at[k, p], lambda t, k=k, p=p: full.at[k, p, t, mspan], parts=1)
        gathers[k, p] = WeightGather(spot, wire, mrows, full.at[k, p])
    xs = LineGather(spot, wire, x_ref, lambda t: block_of(xf, t))
    gas = LineGather(spot, wire, block_of(gaf, spot.t), lambda t: block_of(gaf, t))
    blocks = [
        LineScatter(spot, wire, lambda t: block_of(part, t), lambda side, j: land.at[side, j - 1 + side],
                    lambda dst, src: add_tiled(dst, src, tail), rising=(0, None)[k]) for k in range(2)]
    scatters, lines = {}, {}

    def line_of(k, p):
        here = held.at[k * per + p, spot.b, spot.a]
        return LineScatter(spot, wire, lambda t: here.at[t], lambda side, j: mland.at[k * per + p, side, j - 1 + side],
                           lambda dst, src: add_tiled(dst, src, tile), parts=1)

    for k, p in halved:
        scatters[k, p] = WeightScatter(spot, wire, held.at[k * per + p], *(buf.at[k * per + p] for buf in (one_a, one_b, two_a, two_b)))
        lines[k, p] = line_of(k, p)
    wscatter = WeightScatter(spot, wire, wheld.at[0], wone_a.at[0], wone_b.at[0], wtwo_a.at[0], wtwo_b.at[0])
    zero = [wire.take(count) for _ in range(2)]
    wzero = wire.take(ab)
    gains_in = wire.take(geo.dp - 1)
    small = wire.take(geo.dp - 1)
    last = wire.take(size - 1)
    assert wire.count == wire.base and recv.shape[0] == wire.base + wire.grouped

    pairs = [
        (gain_ref, gain_in), (bias_ref, bias_in), (aw_ref, wsend.at[pl.ds(0, 3)]), (ow_ref, ow_in),
        (x_ref, block_of(xf, spot.t)), (down_ref, down_in), (seg_ref, seg_row), (cot_ref, cot)]
    pairs += [(up_ref.at[:, pl.ds(i * chunk, chunk)], msend.at[0, i]) for i in range(per)]
    loads = fetch([pltpu.make_async_copy(src, dst, local.at[i]) for i, (src, dst) in enumerate(pairs)])
    met = greet(spot)
    sums[...] = jnp.zeros_like(sums)
    settle(loads[0:4])
    ssend[0:2, :] = gain_in[...].astype(F32)
    ssend[2:12, :] = bias_in[...].astype(F32)
    sf[spot.d] = ssend[...]
    wsend[3] = ow_in[...].T
    wf[:, wspan] = wsend[...]
    settle(loads[8:])

    def store(k):
        return pltpu.make_async_copy(msend.at[k], full.at[k, :, spot.t, mspan], osem.at[k])

    store(0).start()
    met()
    for p in range(per):
        wlines[0, p].start()
    for step in range(1, geo.dp):
        wire.start(gains_in + step - 1, ssend, sf.at[spot.d], spot.at_d(ring_next(spot.d, step, geo.dp)))
    weights.first()
    loads[5].wait()
    for i in range(per):
        msend[1, i] = down_in[i * chunk:(i + 1) * chunk, :].T
    store(1).start()
    for k in range(1, end):
        for p in range(per):
            wlines[0, p].step(k)
        if k == 1:
            weights.second()
    xs.start()
    weights.third()
    store(0).wait()
    for p in range(per):
        wlines[0, p].step(end)
        gathers[0, p].first()
    for step in range(1, geo.dp):
        source = ring_prev(spot.d, step, geo.dp)
        wire.landed(gains_in + step - 1, sf.at[source], spot.at_d(source))
    piece = ssend.shape[1]
    for d in range(geo.dp):
        rows12[:, d * piece:(d + 1) * piece] = sf[d]
    loads[6].wait()
    seg_col[...] = jnp.broadcast_to(seg_row[...], (128, seq)).T
    weights.fourth()
    loads[4].wait()

    def project(t):
        def norm(r):
            source = pl.ds(pl.multiple_of(t * rows + r.start, tail), tail)
            n1[r] = layer_norm(xf[source].astype(F32), rows12[0:1, :], rows12[2:3, :]).astype(BF)

        loop_rows(rows, tail, norm)
        r = pl.ds(pl.multiple_of(t * rows, rows), rows)
        normed = n1[...]
        n1t[:, r] = normed.T
        qkv[0, r] = ((nn(normed, wf[0]) + rows12[3:4, column]).astype(BF).astype(F32) * HD ** -0.5).astype(BF)
        qkv[1, r] = nn(normed, wf[1]).astype(BF)
        qkv[2, r] = (nn(normed, wf[2]) + rows12[4:5, column]).astype(BF)

    def arrive(k, carry):
        @pl.when(k >= 1)
        def _():
            xs.step(k)

        @pl.when(k == end - 1)
        def _():
            wlines[1, 0].start()
            for p in range(1, per):
                wlines[1, p].start(False)

        def side(i, inner):
            t = spot.t + (2 * i - 1) * k

            @pl.when((t >= 0) & (t < size) & ((i == 0) | (k >= 1)))
            def _():
                project(t)

            return inner

        lax.fori_loop(0, 2, side, 0)

        @pl.when(k == 1)
        def _():
            for p in range(per):
                gathers[0, p].second()

        for i in range(size):
            start = i * rows

            @pl.when(jnp.maximum(spot.t, i - spot.t) == k)
            def _():
                block_bias(seg_col, seg_row, bias, start, rows, start + rows)
                attend_block(qkv, bias, att, lse, start, rows)
                part[start:start + rows, :] = nt(att[start:start + rows, :], wf[3]).astype(BF)
                blocks[0].start_block(i)

        return carry

    lax.fori_loop(0, size, arrive, 0)
    xs.owe()
    for k in range(1, end):
        wlines[1, 0].step(k)
        if k == max(1, end - 1):
            for p in range(1, per):
                wlines[1, p].start(True)
        if k == 1:
            for p in range(per):
                gathers[0, p].third()
    store(1).wait()
    wlines[1, 0].step(end)
    gathers[1, 0].first()
    for p in range(1, per):
        for k in range(1, size):
            wlines[1, p].step(k)
        gathers[1, p].first()

    def set_total(r):
        mid[r] = part[own_rows(r, tail)].astype(F32)

    loop_rows(rows, tail, set_total)

    def mid_total(ref, h):
        n = ref.shape[0]
        add_tiled(mid.at[pl.ds(h * n, n)], ref, tail)

    events = blocks[0].count()
    blocks[0].step(0, 3 * events // 8, mid_total)
    gathers[1, 0].second()
    blocks[0].step(3 * events // 8, 5 * events // 8, mid_total)
    for p in range(per):
        gathers[0, p].fourth()
    for p in range(1, per):
        gathers[1, p].second()
    blocks[0].step(5 * events // 8, events, mid_total)

    def mlp(mbuf, hmid, da, n2, gm, turned, left, snd, dn2):
        def cols_of(j):
            return pl.ds(pl.multiple_of(unit_of(j) * chunk, chunk), chunk)

        def unit_of(j):
            return lax.rem(j, size) * per + lax.div(j, size)

        def mload(k, j, s):
            n = width // pieces
            return [
                pltpu.make_async_copy(
                    full.at[k, lax.div(j, size), lax.rem(j, size), pl.ds(i * n, n)], mbuf.at[s, pl.ds(i * n, n)], msem.at[s, i])
                for i in range(pieces)]

        def depth(which):
            return mbuf.shape[0] // len(which)

        def ahead(which):
            for j in range(min(depth(which) - 1, count)):
                for n, k in enumerate(which):
                    fetch(mload(k, j, j * len(which) + n))

        def streamed(which, body, first=0, stop=count):
            deep = depth(which)

            def one(j, carry):
                slots = [lax.rem(j, deep) * len(which) + n for n in range(len(which))]
                for n, k in enumerate(which):
                    settle(mload(k, j, slots[n]))

                @pl.when(j + deep - 1 < count)
                def _():
                    for n, k in enumerate(which):
                        fetch(mload(k, j + deep - 1, lax.rem(j + deep - 1, deep) * len(which) + n))

                body(j, *slots)
                return carry

            lax.fori_loop(first, stop, one, 0)

        ahead((0,))
        loads[7].wait()

        def norm(r):
            value = xf[own_rows(r, tail)].astype(F32) + (mid[r] + rows12[5:6, :])
            mid[r] = value
            n2[r] = layer_norm(value, rows12[1:2, :], rows12[6:7, :]).astype(BF)
            branch = cot[r].astype(BF)
            gm[r] = branch
            sums[7:8, :] += column_sum(branch.astype(F32))

        loop_rows(rows, tail, norm)

        def turn(value):
            turned[...] = value[...].T
            for i in range(ab):
                for other in range(2):
                    core = lax.rem(spot.c + other, 2)
                    left[other, i * mrows:(i + 1) * mrows, :] = turned[pl.ds(pl.multiple_of((i * 2 + core) * mrows, mrows), mrows), :]

        turn(gm)

        def sending(k, j):
            p, t = lax.div(j, size), lax.rem(j, size)
            return wire.copy(zero[k] + j, snd.at[p, :, :, t], held.at[k * per + p, :, :, t], sibling)

        def give(k, j, right):
            product = nn(left[1], right).astype(BF)
            p, t = lax.div(j, size), lax.rem(j, size)
            for i in range(ab):
                snd[p, i // a_size, i % a_size, t] = product[i * mrows:(i + 1) * mrows, :]
            sending(k, j).start()

        def keep(k, j, right):
            p, t = lax.div(j, size), lax.rem(j, size)
            product = nn(left[0], right)
            sending(k, j).wait_recv()
            for i in range(ab):
                b, a = i // a_size, i % a_size
                held[k * per + p, b, a, t] = (
                    held[k * per + p, b, a, t].astype(F32) + product[i * mrows:(i + 1) * mrows, :]).astype(BF)

        def hidden(j, s):
            cols = cols_of(j)
            row = pl.ds(8 + lax.div(unit_of(j) * chunk, width), 1)
            bcols = pl.ds(pl.multiple_of(lax.rem(unit_of(j) * chunk, width), chunk), chunk)
            value, slope = gelu_parts(nn(n2[...], mbuf[s]) + rows12[row, bcols])
            active = value.astype(BF)
            hmid[:, cols] = active
            da[:, cols] = slope.astype(BF)
            give(1, j, active)

        def keep_down(j, carry):
            keep(1, j, hmid[:, cols_of(j)])
            return carry

        for p in range(per):
            streamed((0,), hidden, p * size, (p + 1) * size)
            gathers[1, p].third()
            lax.fori_loop(p * size, (p + 1) * size, keep_down, 0)
            scatters[1, p].first()
        for p in range(per):
            gathers[1, p].fourth()
        ahead((0, 1))
        dn2[...] = jnp.zeros_like(dn2)

        def hidden_back(j, s, s_down):
            cols = cols_of(j)
            row = pl.ds(8 + lax.div(unit_of(j) * chunk, width), 1)
            bcols = pl.ds(pl.multiple_of(lax.rem(unit_of(j) * chunk, width), chunk), chunk)
            grad = (nn(gm[...], mbuf[s_down]) * da[:, cols].astype(F32)).astype(BF)
            da[:, cols] = grad
            sums[row, bcols] = column_sum(grad.astype(F32))
            dn2[...] += nt(grad, mbuf[s])

        streamed((0, 1), hidden_back)

        def back(r):
            value = mid[r]
            unit_two, scale_two = norm_stats(value)
            grad = dn2[r]
            total = cot[r] + norm_back(grad, unit_two, scale_two, rows12[1:2, :])
            cot[r] = total
            branch = total.astype(BF)
            gaf[own_rows(r, tail)] = branch
            sums[1:2, :] += column_sum(grad * unit_two)
            sums[6:7, :] += column_sum(grad)
            sums[5:6, :] += column_sum(branch.astype(F32))

        loop_rows(rows, tail, back)
        wire.sent(blocks[0].plans())
        gas.start()
        turn(n2)
        def give_up(j, carry):
            sending(1, j).wait_send()
            give(0, j, da[:, cols_of(j)])
            return carry

        lax.fori_loop(0, count, give_up, 0)
        scatters[1, 0].second()

        def keep_up(j, carry):
            keep(0, j, da[:, cols_of(j)])
            return carry

        for p in range(per):
            lax.fori_loop(p * size, (p + 1) * size, keep_up, 0)
            if p:
                scatters[1, p].second()
        scatters[0, 0].first()
        ahead((1,))
        gas.step(1)
        scatters[1, 0].third()
        lines[1, 0].start()
        dn2[...] = jnp.zeros_like(dn2)

        def output(j, s):
            dn2[...] += nt(hmid[:, cols_of(j)], mbuf[s])

        streamed((1,), output)

        def set_out(r):
            dn2[r] = mid[r] + (dn2[r] + rows12[7:8, :])

        loop_rows(rows, tail, set_out)
        out_copy = pltpu.make_async_copy(dn2, out_ref, osem.at[0])
        out_copy.start()
        for p in range(1, per):
            scatters[1, p].third()
            lines[1, p].start()
        for j in range(count):
            sending(0, j).wait_send()
        out_copy.wait()

    ff = size * unit
    pl.run_scoped(
        mlp,
        pltpu.VMEM((6, width, chunk), BF),
        pltpu.VMEM((rows, ff), BF),
        pltpu.VMEM((rows, ff), BF),
        pltpu.VMEM((rows, width), BF),
        pltpu.VMEM((rows, width), BF),
        pltpu.VMEM((width, rows), BF),
        pltpu.VMEM((2, ab * mrows, rows), BF),
        pltpu.VMEM((per, b_size, a_size, size, mrows, chunk), BF),
        pltpu.VMEM((rows, width), F32),
    )

    def attention(gat, do, dqkv, dk, dv, wg):
        def own_line(k):
            for p in range(per):
                here = held.at[k * per + p, spot.b, spot.a, spot.t]

                def set_row(r):
                    gtot[r, p * chunk:(p + 1) * chunk] = here[r].astype(F32)

                loop_rows(mrows, tile, set_row)

        def line_total(p):
            return lambda ref, h: add_tiled(gtot.at[:, pl.ds(p * chunk, chunk)], ref, tile)

        def line_step(k, p, s):
            third = lines[k, p].count() // 3
            lines[k, p].step(s * third, (s + 1) * third, line_total(p))

        def arrived(t):
            r = pl.ds(pl.multiple_of(t * rows, rows), rows)
            value = gaf[r]
            do[r] = nn(value, wf[3]).astype(BF)
            gat[:, r] = value.T

        dk[...] = jnp.zeros_like(dk)
        dv[...] = jnp.zeros_like(dv)

        half = width // 2

        def norm_grad(i):
            r = pl.ds(pl.multiple_of(i * rows, rows), rows)
            dqkv[1, r] = dk[r].astype(BF)
            dqkv[2, r] = dv[r].astype(BF)
            for first in range(0, width, half):
                cols = slice(first, first + half)
                part[r, cols] = sum(nt(dqkv[j, r], wf[j, cols, :]) for j in range(3)).astype(BF)
            blocks[1].start_traced(i)

        plan = {(1, p, n): n + 1 + p for p in range(per) for n in range(end - 1)}
        plan = {key: at for key, at in plan.items() if at < size}

        def arrive_back(k, carry):
            for n in range(1, size):
                @pl.when(k == n)
                def _():
                    if n == 1 and size > 2:
                        gas.step(2)
                    for key, at in plan.items():
                        if at == n:
                            line_step(*key)
                    if n == max(1, end - 1):
                        scatters[0, 0].second()
                        for p in range(1, per):
                            scatters[0, p].first()

            @pl.when((k == end) & (spot.t == 0))
            def _():
                scatters[0, 0].third()
                lines[0, 0].start()

            @pl.when(k >= 3)
            def _():
                gas.step(k)

            def side(i, inner):
                t = spot.t + (2 * i - 1) * k

                @pl.when((t >= 0) & (t < size) & ((i == 0) | (k >= 1)))
                def _():
                    arrived(t)

                return inner

            lax.fori_loop(0, 2, side, 0)
            for i in range(size):
                @pl.when((i == spot.t - k) | (i == spot.t + k))
                def _():
                    start, stop = i * rows, (i + 1) * rows
                    block_bias(seg_col, seg_row, bias, start, rows, stop)
                    attend_block_back(qkv, bias, lse, do, dqkv.at[0], dk, dv, start, rows)

            def ready(n, inner):
                i = jnp.where(lax.rem(n, 2) == 0, end - lax.div(n, 2), lax.div(n, 2))

                @pl.when(jnp.maximum(end - spot.t, spot.t - i) == k)
                def _():
                    norm_grad(i)

                return inner

            lax.fori_loop(0, size, ready, 0)
            return carry

        lax.fori_loop(0, size, arrive_back, 0)
        gas.owe()
        blocks[1].owe_starts()
        blocks[1].start_middle()
        loop_rows(rows, tail, lambda r: set_total(r))
        own_line(1)
        for p in range(per):
            for n in range(end):
                if (1, p, n) not in plan:
                    line_step(1, p, n)
        downg[...] = gtot[...].T
        stores = fetch([pltpu.make_async_copy(downg, downg_ref, osem.at[1])])
        events = blocks[1].count()

        @pl.when(spot.t != 0)
        def _():
            scatters[0, 0].third()
            lines[0, 0].start()

        def first_norm(r):
            unit_one, _ = norm_stats(xf[r].astype(F32))
            term = part[r].astype(F32)
            sums[0:1, :] += column_sum(term * unit_one)
            sums[2:3, :] += column_sum(term)

        loop_rows(seq, tail, first_norm)
        sums[3:4, column] = column_sum(dqkv[0].astype(F32))
        sums[4:5, column] = column_sum(dqkv[2].astype(F32))
        for d in range(geo.dp):
            spart[d] = sums[:, d * piece:(d + 1) * piece]
        for step in range(1, geo.dp):
            to = ring_next(spot.d, step, geo.dp)
            wire.start(small + step - 1, spart.at[to], sland.at[step - 1], spot.at_d(to))
        stot[...] = spart[spot.d]
        blocks[1].step(0, events // 3, mid_total)
        for p in range(1, per):
            scatters[0, p].second()
        def wgrad(r):
            for j in range(3):
                wg[j, r] = nn(n1t[r], dqkv[j]).astype(BF)
            wg[3, r] = nn(gat[r], att[...]).astype(BF)

        loop_rows(width, min(256, width), wgrad)

        def wrows_of(i, core):
            return pl.ds(pl.multiple_of((i * 2 + core) * wrows, wrows), wrows)

        for i in range(ab):
            wire.start(wzero + i, wg.at[:, wrows_of(i, 1 - spot.c)], wheld.at[0, i // a_size, i % a_size], sibling)
        for p in range(1, per):
            scatters[0, p].third()
            lines[0, p].start()
        blocks[1].start_near()
        own_line(0)
        blocks[1].step(events // 3, 2 * events // 3, mid_total)
        for i in range(ab):
            here = wheld.at[0, i // a_size, i % a_size]
            wire.landed(wzero + i, here, sibling)
            wscatter.add(here, wg.at[:, wrows_of(i, spot.c)])
        wscatter.first()
        for step in range(1, geo.dp):
            wire.landed(small + step - 1, sland.at[step - 1], spot.at_d(ring_prev(spot.d, step, geo.dp)))
            stot[...] += sland[step - 1]
        for step in range(1, size):
            wire.start(last + step - 1, stot, tland.at[step - 1], spot.at_t(ring_next(spot.t, step, size)))
        if end > 1:
            line_step(0, 0, 0)
        wscatter.second()
        for n in range(1, end - 1):
            line_step(0, 0, n)
        for p in range(1, per):
            for n in range(end - 1):
                line_step(0, p, n)
        blocks[1].step(2 * events // 3, events, mid_total)

        def back(r):
            unit_one, scale_one = norm_stats(xf[own_rows(r, tail)].astype(F32))
            cot[r] = cot[r] + norm_back(mid[r], unit_one, scale_one, rows12[0:1, :])

        loop_rows(rows, tail, back)
        stores += fetch([pltpu.make_async_copy(cot, igrad_ref, osem.at[0])])
        wscatter.third()
        sums_w = wheld.at[0, spot.b, spot.a]
        for j in range(3):
            awg[j] = sums_w[j].astype(F32)
        owg[...] = sums_w[3].astype(F32).T
        stores += fetch([
            pltpu.make_async_copy(awg, awg_ref, osem.at[2]),
            pltpu.make_async_copy(owg, owg_ref, osem.at[3])])
        for p in range(per):
            line_step(0, p, end - 1)
        stores += fetch([pltpu.make_async_copy(gtot, upg_ref, osem.at[6])])
        for step in range(1, size):
            wire.landed(last + step - 1, tland.at[step - 1], spot.at_t(ring_prev(spot.t, step, size)))
        total = stot[...]
        for step in range(1, size):
            total = total + tland[step - 1]
        gaing[...] = total[0:2, :]
        for i in range(biasg.shape[0]):
            biasg[i] = total[2 + i:3 + i, :]
        stores += fetch([
            pltpu.make_async_copy(gaing, gaing_ref, osem.at[4]),
            pltpu.make_async_copy(biasg, biasg_ref, osem.at[5])])
        wire.drain()
        settle(stores)

    pl.run_scoped(
        attention,
        pltpu.VMEM((width, seq), BF),
        pltpu.VMEM((seq, heads), BF),
        pltpu.VMEM((3, seq, heads), BF),
        pltpu.VMEM((seq, heads), F32),
        pltpu.VMEM((seq, heads), F32),
        pltpu.VMEM((4, width, heads), BF),
    )


def block_kernel(geo, x, aw, ow, up, down, gains, biases, seg_row, cot):
    rows, width = x.shape
    wrows, heads = aw.shape[1:]
    mrows, unit = up.shape
    size = geo.tensor
    seq = size * rows
    chunk = min(512, unit)
    per = unit // chunk
    sems = ((2 * per + 1) * (gather_sems(geo) + scatter_sems(geo)) + (size - 1) * (2 * 4 + 2 * 4 + 4 * per * 2 + 1) + 2 * per * size
            + geo.a_size * geo.b_size + 2 * (geo.dp - 1))
    shared = (2 * per + 1) * gather_sems(geo)
    like = lambda x: pltpu.VMEM(x.shape, x.dtype)
    return pl.pallas_call(
        functools.partial(block_body, geo),
        out_shape=(
            jax.ShapeDtypeStruct((2, unit // chunk, size, width, chunk), BF),
            jax.ShapeDtypeStruct((rows, width), F32),
            jax.ShapeDtypeStruct((rows, width), F32),
            jax.ShapeDtypeStruct((3, wrows, heads), F32),
            jax.ShapeDtypeStruct((heads, wrows), F32),
            jax.ShapeDtypeStruct((mrows, unit), F32),
            jax.ShapeDtypeStruct((unit, mrows), F32),
            jax.ShapeDtypeStruct((2, wrows), F32),
            jax.ShapeDtypeStruct((10, 1, wrows), F32),
        ),
        in_specs=[ANY] * 9,
        out_specs=(ANY,) * 9,
        scratch_shapes=[
            pltpu.VMEM((seq, width), BF),
            pltpu.VMEM((rows, width), BF),
            pltpu.VMEM((width, seq), BF),
            pltpu.VMEM((3, seq, heads), BF),
            pltpu.VMEM((seq, heads), BF),
            pltpu.VMEM((seq, 128), F32),
            pltpu.VMEM((4, width, heads), BF),
            pltpu.VMEM((seq, width), BF),
            pltpu.VMEM((2, size - 1, rows, width), BF),
            pltpu.VMEM((rows, seq), F32),
            pltpu.VMEM((rows, width), F32),
            pltpu.VMEM((rows, width), F32),
            pltpu.VMEM((seq, width), BF),
            pltpu.VMEM((12, width), F32),
            pltpu.VMEM((seq, 128), jnp.int32),
            like(seg_row),
            pltpu.VMEM((geo.dp, 12, wrows), F32),
            pltpu.VMEM((4, wrows, heads), BF),
            like(ow), like(down), pltpu.VMEM((2, unit // chunk, mrows, chunk), BF), like(gains), like(biases),
            pltpu.VMEM((12, wrows), F32),
            pltpu.VMEM((12, width), F32),
            pltpu.VMEM((geo.dp, 12, wrows), F32),
            pltpu.VMEM((geo.dp - 1, 12, wrows), F32),
            pltpu.VMEM((12, wrows), F32),
            pltpu.VMEM((size - 1, 12, wrows), F32),
            *scatter_bufs(geo, 2 * (unit // chunk), 2 * (unit // chunk), size, mrows, chunk),
            *scatter_bufs(geo, 1, 1, 4, wrows, heads),
            pltpu.VMEM((2 * (unit // chunk), 2, size - 1, mrows, chunk), BF),
            pltpu.VMEM((mrows, unit), F32),
            pltpu.VMEM((unit, mrows), F32),
            pltpu.VMEM((3, wrows, heads), F32),
            pltpu.VMEM((heads, wrows), F32),
            pltpu.VMEM((2, wrows), F32),
            pltpu.VMEM((10, 1, wrows), F32),
            pltpu.SemaphoreType.DMA((sems - shared + 2 * per + 1,)), pltpu.SemaphoreType.DMA((sems,)), pltpu.SemaphoreType.DMA((8 + unit // chunk,)),
            pltpu.SemaphoreType.DMA((6, 2)), pltpu.SemaphoreType.DMA((7,))],
        compiler_params=pltpu.CompilerParams(collective_id=1, has_side_effects=True, vmem_limit_bytes=62 * 2**20),
        name="block",
    )(x, aw, ow, up, down, gains, biases, seg_row, cot)


def hand_over_body(*refs):
    *refs, loads, stores = refs
    count = len(refs) // 3
    ins, outs, bufs = refs[:count], refs[count:2 * count], refs[2 * count:]
    coming = fetch([pltpu.make_async_copy(ins[i], bufs[i], loads.at[i]) for i in range(count)])
    going = []
    for i in range(count):
        coming[i].wait()
        going += fetch([pltpu.make_async_copy(bufs[i], outs[i], stores.at[i])])
    settle(going)


def hand_over(parts):
    return pl.pallas_call(
        hand_over_body,
        out_shape=tuple(jax.ShapeDtypeStruct(part.shape, part.dtype) for part in parts),
        in_specs=[ANY] * len(parts),
        out_specs=(ANY,) * len(parts),
        scratch_shapes=[pltpu.VMEM(part.shape, part.dtype) for part in parts] + [pltpu.SemaphoreType.DMA((len(parts),))] * 2,
        name="hand_over",
    )(*parts)


def per_device(geo, activations, segments, attn_weight, out_weight, up_weight, down_weight, norm_gains, bias_rows, cotangent):
    outs = block_kernel(
        geo, activations, attn_weight[0], out_weight[0], up_weight[0], down_weight[0], norm_gains[0], bias_rows[0], segments[None, :],
        cotangent)
    outs = hand_over(outs[1:])
    return outs[:2] + tuple(part[None] for part in outs[2:7]) + (outs[7].reshape(1, 10, -1),)


def solution(mesh):
    geo = Geometry(mesh.shape["dp"], mesh.shape["tensor"])
    return jax.shard_map(
        functools.partial(per_device, geo),
        mesh=mesh,
        in_specs=(
            P(("dp", "tensor"), None),
            P("dp"),
            P(None, None, "dp", "tensor"),
            P(None, "tensor", "dp"),
            P(None, "dp", "tensor"),
            P(None, "tensor", "dp"),
            P(None, None, "dp"),
            P(None, None, "dp"),
            P(("dp", "tensor"), None),
        ),
        out_specs=(
            P(("dp", "tensor"), None),
            P(("dp", "tensor"), None),
            P(None, None, "dp", "tensor"),
            P(None, "tensor", "dp"),
            P(None, "dp", "tensor"),
            P(None, "tensor", "dp"),
            P(None, None, "dp"),
            P(None, None, "dp"),
        ),
        check_vma=False,
    )
```

```python
import functools

import jax
import jax.numpy as jnp
from jax import lax
from jax.experimental import pallas as pl
from jax.experimental.pallas import tpu as pltpu
from jax.sharding import PartitionSpec as P

HD = 64
EPSILON = 1e-05
MASKED = -1e30
MESH_ID = pl.DeviceIdType.MESH
BF = jnp.bfloat16
F32 = jnp.float32
ANY = pl.BlockSpec(memory_space=pl.ANY)
VM = pl.BlockSpec(memory_space=pltpu.VMEM)


def layer_norm(values, gain_row, shift_row):
    center = values - jnp.mean(values, axis=-1, keepdims=True)
    spread = jnp.mean(center * center, axis=-1, keepdims=True)
    return center * lax.rsqrt(spread + EPSILON) * gain_row + shift_row


def norm_stats(values):
    center = values - jnp.mean(values, axis=-1, keepdims=True)
    spread = jnp.mean(center * center, axis=-1, keepdims=True)
    scale = lax.rsqrt(spread + EPSILON)
    return center * scale, scale


def norm_back(grad, unit, scale, gain_row):
    u = grad * gain_row
    mean_u = jnp.mean(u, axis=-1, keepdims=True)
    mean_ux = jnp.mean(u * unit, axis=-1, keepdims=True)
    return scale * (u - mean_u - unit * mean_ux)


def gelu_tanh(values):
    return jax.nn.gelu(values, approximate=True)


class Geometry:
    def __init__(self, dp, tensor):
        self.dp, self.tensor = dp, tensor
        self.c_size = 2
        rest = dp // 2
        self.a_size = 1
        while self.a_size * self.a_size < rest:
            self.a_size *= 2
        self.b_size = rest // self.a_size
        assert self.a_size * self.b_size * 2 == dp

    def bind(self):
        spot = Spot()
        spot.geo = self
        spot.d = lax.axis_index("dp")
        spot.t = lax.axis_index("tensor")
        spot.c = lax.rem(spot.d, 2)
        half = lax.div(spot.d, 2)
        spot.a = lax.rem(half, self.a_size)
        spot.b = lax.div(half, self.a_size)
        return spot


class Spot:
    def rank(self, b, a, c):
        return (b * self.geo.a_size + a) * 2 + c

    def at_t(self, t):
        return (self.d, t)

    def at_d(self, d):
        return (d, self.t)


def ring_next(rank, step, size):
    return lax.rem(rank + step, size)


def ring_prev(rank, step, size):
    return lax.rem(rank + size - step, size)


class Wire:
    def __init__(self, send, recv, base):
        self.send_sems, self.recv_sems, self.base = send, recv, base
        self.count = self.grouped = 0
        self.pending, self.quiet, self.totals, self.group_of = [], [], [], {}

    def take_group(self, n, whole, device):
        first = self.base + self.grouped
        self.grouped += n
        group = self.base + len(self.totals)
        self.group_of.update((i, group) for i in range(first, first + n))
        self.totals.append((group, whole, device))
        return first

    def take(self, n):
        first = self.count
        self.count += n
        return first

    def copy(self, i, src, dst, device):
        return pltpu.make_async_remote_copy(
            src_ref=src, dst_ref=dst, send_sem=self.send_sems.at[self.group_of.get(i, i) if isinstance(i, int) else i], recv_sem=self.recv_sems.at[i],
            device_id=device, device_id_type=MESH_ID)

    def plan(self, i, src, dst, device, when=None):
        planned = self.copy(i, src, dst, device), when
        if isinstance(i, int) and i in self.group_of:
            self.quiet.append(planned)
        return planned

    def go(self, planned):
        copy, when = planned
        if when is None:
            copy.start()
        else:
            pl.when(when)(copy.start)
        self.owe(planned)

    def owe(self, planned):
        if not any(other is planned for other in self.pending + self.quiet):
            self.pending.append(planned)

    def start(self, i, src, dst, device, when=None):
        self.go(self.plan(i, src, dst, device, when))

    def landed(self, i, dst, device, when=None):
        copy = self.copy(i, dst, dst, device)
        if when is None:
            copy.wait_recv()
        else:
            pl.when(when)(copy.wait_recv)

    def sent(self, plans):
        for planned in plans:
            copy, when = planned
            self.pending = [other for other in self.pending if other is not planned]
            if when is None:
                copy.wait_send()
            else:
                pl.when(when)(copy.wait_send)

    def drain(self):
        for copy, when in self.pending:
            if when is None:
                copy.wait_send()
            else:
                pl.when(when)(copy.wait_send)
        for group, whole, device in self.totals:
            pltpu.make_async_remote_copy(
                src_ref=whole, dst_ref=whole, send_sem=self.send_sems.at[group], recv_sem=self.recv_sems.at[group],
                device_id=device, device_id_type=MESH_ID).wait_send()
        self.pending = []


def greet(spot):
    geo = spot.geo
    barrier = pltpu.get_barrier_semaphore()
    total = 0
    for step in range(1, geo.tensor):
        pl.semaphore_signal(barrier, inc=1, device_id=spot.at_t(ring_next(spot.t, step, geo.tensor)), device_id_type=MESH_ID)
        total += 1
    for step in range(1, geo.dp):
        pl.semaphore_signal(barrier, inc=1, device_id=spot.at_d(ring_next(spot.d, step, geo.dp)), device_id_type=MESH_ID)
        total += 1
    return lambda: pl.semaphore_wait(barrier, total)


def halves(ref, count, part):
    rows = ref.shape[-2] // count
    return ref.at[(slice(None),) * (len(ref.shape) - 2) + (pl.ds(part * rows, rows),)]


class LineGather:
    def __init__(self, spot, wire, src, slot, parts=2):
        self.spot, self.wire, self.src, self.slot, self.parts = spot, wire, src, slot, parts
        self.size = size = spot.geo.tensor
        self.base = [wire.take((size - 1) * parts) for _ in range(2)]
        t = spot.t
        self.sends = {}
        for k in range(size - 1):
            for part in range(parts):
                for side in range(2):
                    self.sends[k, part, side] = self.plan(k, part, side)

    def place(self, k, side):
        t = self.spot.t
        origin = t - k if side == 0 else t + k
        there = (origin >= 0) & (origin < self.size)
        onward = t + 1 if side == 0 else t - 1
        return origin, there, t - 1 if side == 0 else t + 1, onward, there & (onward >= 0) & (onward < self.size)

    def plan(self, k, part, side):
        origin, _, _, onward, going = self.place(k, side)
        piece = halves(self.slot(origin), self.parts, part)
        first = isinstance(k, int) and k == 0
        src = halves(self.src, self.parts, part) if first else piece
        return self.wire.plan(self.base[side] + k * self.parts + part, src, piece, self.spot.at_t(onward), when=going)

    def start(self, where=None):
        for part in range(self.parts):
            for side in range(2):
                planned = self.sends[0, part, side]
                if where is None:
                    self.wire.go(planned)
                else:
                    copy, when = planned
                    pl.when(when & self.inner(where))(copy.start)
                    self.wire.owe(planned)

    def inner(self, where):
        inner = (self.spot.t >= 1) & (self.spot.t < self.size - 1)
        return inner if where else jnp.logical_not(inner)

    def step(self, k, where=None):
        for part in range(self.parts):
            for side in range(2):
                origin, there, near, _, _ = self.place(k, side)
                if where is not None:
                    there = there & self.inner(where)
                piece = halves(self.slot(origin), self.parts, part)
                self.wire.landed(self.base[side] + (k - 1) * self.parts + part, piece, self.spot.at_t(near), when=there)
                if not isinstance(k, int):
                    copy, going = self.plan(k, part, side)
                    pl.when(going & (k < self.size - 1))(copy.start)
                elif k < self.size - 1 and where is not False:
                    self.wire.go(self.sends[k, part, side])

    def owe(self):
        for (k, part, side), planned in self.sends.items():
            if k > 0:
                self.wire.owe(planned)


class LineScatter:
    def __init__(self, spot, wire, part, land, add, rising=None, parts=2):
        self.spot, self.wire, self.part, self.land, self.add, self.parts = spot, wire, part, land, add, parts
        self.size = spot.geo.tensor
        base = self.base = [wire.take((self.size - 1) * parts) for _ in range(2)]
        t, end = spot.t, self.size - 1
        self.starts, self.hops = {}, {}
        for h in range(parts):
            for j in range(self.size):
                if j > 0:
                    self.starts[0, j, h] = wire.plan(
                        base[0] + (j - 1) * parts + h, halves(part(j), parts, h), halves(land(0, j), parts, h), spot.at_t(1), when=t == 0)
                if j < end:
                    self.starts[1, j, h] = wire.plan(
                        base[1] + j * parts + h, halves(part(j), parts, h), halves(land(1, j), parts, h), spot.at_t(end - 1), when=t == end)
        self.events = []
        for side in range(2):
            place = t if side == 0 else end - t
            if side == rising:
                for e in range(1, 2 * end):
                    far = e + 1 - place
                    self.events.append((10 * e, side, far if side == 0 else end - far, (place >= 1) & (far >= place) & (far <= end)))
            else:
                for s in range(1, self.size):
                    far = end - s + place
                    at = 10 * s + (0 if rising is None else 15)
                    self.events.append((at, side, far if side == 0 else end - far, (place >= 1) & (s >= place)))
        self.events.sort(key=lambda event: event[0])
        self.hops = []
        for _, side, j, here in self.events:
            near = spot.at_t(t - 1 if side == 0 else t + 1)
            away = spot.at_t(t + 1 if side == 0 else t - 1)
            for h in range(parts):
                held = halves(land(side, j), parts, h)
                i = base[side] + (j - 1 + side) * parts + h
                self.hops.append((here & (j == t), here & (j != t), j, h, held, wire.copy(i, held, held, near),
                                  wire.plan(i, held, held, away, when=here & (j != t))))

    def start_block(self, j):
        for side in range(2):
            for h in range(self.parts):
                if (side, j, h) in self.starts:
                    self.wire.go(self.starts[side, j, h])

    def start_traced(self, j):
        spot, t, end = self.spot, self.spot.t, self.size - 1
        for side in range(2):
            first, to = (0, 1) if side == 0 else (end, end - 1)
            for h in range(self.parts):
                copy, when = self.wire.plan(
                    self.base[side] + (j - 1 + side) * self.parts + h, halves(self.part(j), self.parts, h),
                    halves(self.land(side, j), self.parts, h), spot.at_t(to), when=(t == first) & (j != first) & (j != 1 if side == 0 else (j == 0) | (j == end - 1)))
                pl.when(when)(copy.start)

    def start_middle(self):
        for j in range(1, self.size - 2):
            for h in range(self.parts):
                self.wire.go(self.starts[1, j, h])

    def start_near(self):
        for h in range(self.parts):
            self.wire.go(self.starts[0, 1, h])

    def owe_starts(self):
        for planned in self.starts.values():
            self.wire.owe(planned)

    def start(self):
        for n in range(self.size):
            for side, j in ((0, self.size - 1 - n), (1, n)):
                for h in range(self.parts):
                    if (side, j, h) in self.starts:
                        self.wire.go(self.starts[side, j, h])

    def count(self):
        return len(self.hops)

    def step(self, first, last, total):
        for final, passing, j, h, held, landing, onward in self.hops[first:last]:
            @pl.when(final)
            def _():
                landing.wait_recv()
                total(held, h)

            @pl.when(passing)
            def _():
                landing.wait_recv()
                self.add(held, halves(self.part(j), self.parts, h))

            self.wire.go(onward)

    def plans(self):
        return list(self.starts.values()) + [hop[-1] for hop in self.hops]


def add_tiled(dst, src, tile):
    def step(i, carry):
        rows = pl.ds(pl.multiple_of(i * tile, tile), tile)
        dst[rows] = (dst[rows].astype(F32) + src[rows].astype(F32)).astype(dst.dtype)
        return carry

    lax.fori_loop(0, dst.shape[0] // tile, step, 0)


class WeightGather:
    def __init__(self, spot, wire, rows, full):
        geo = spot.geo
        self.spot, self.wire, self.full, self.rows = spot, wire, full, rows
        self.slots = full.shape[0]
        self.half = self.slots // 2
        a, b = geo.a_size, geo.b_size
        counts = [a - 1, b - 1, (b - 1) * a, (a - 1) * b, 2 * a * b]
        whole = full.at[:, pl.ds(0, sum(counts) // 2 * rows)]
        firsts = [wire.take_group(sum(counts), whole, spot.at_d(spot.rank(spot.b, spot.a, 1 - spot.c)))]
        for n in counts[:-1]:
            firsts.append(firsts[-1] + n)
        self.one_a, self.one_b, self.two_a, self.two_b, self.last = firsts
        self.plan_shares()
        self.plan_hops()

    def span(self, d):
        return pl.ds(pl.multiple_of(d * self.rows, self.rows), self.rows)

    def low(self, d):
        return self.full.at[pl.ds(0, self.half), self.span(d)]

    def high(self, d):
        return self.full.at[pl.ds(self.half, self.slots - self.half), self.span(d)]

    def plan_shares(self):
        spot, geo = self.spot, self.spot.geo
        self.shares = {}
        for j in range(geo.b_size):
            for i in range(geo.a_size):
                held = spot.rank(ring_prev(spot.b, j, geo.b_size), ring_prev(spot.a, i, geo.a_size), spot.c)
                sibling = spot.rank(spot.b, spot.a, 1 - spot.c)
                for part in range(2):
                    half = (self.low, self.high)[part](held)
                    self.shares[part, j, i] = self.wire.plan(
                        self.last + 2 * (j * geo.a_size + i) + part, half, half, spot.at_d(sibling))

    def share(self, part, j, i):
        self.wire.go(self.shares[part, j, i])

    def plan_hops(self):
        spot, geo, wire = self.spot, self.spot.geo, self.wire
        self.ones, self.twos_a, self.twos_b = [], {}, {}
        mine = spot.d
        for j in range(1, geo.a_size):
            to = spot.rank(spot.b, ring_next(spot.a, j, geo.a_size), spot.c)
            self.ones.append(wire.plan(self.one_a + j - 1, self.low(mine), self.low(mine), spot.at_d(to)))
        for j in range(1, geo.b_size):
            to = spot.rank(ring_next(spot.b, j, geo.b_size), spot.a, spot.c)
            self.ones.append(wire.plan(self.one_b + j - 1, self.high(mine), self.high(mine), spot.at_d(to)))
        for i in range(geo.a_size):
            held = spot.rank(spot.b, ring_prev(spot.a, i, geo.a_size), spot.c)
            for j in range(1, geo.b_size):
                to = spot.rank(ring_next(spot.b, j, geo.b_size), spot.a, spot.c)
                self.twos_a[i, j] = wire.plan(self.two_a + (j - 1) * geo.a_size + i, self.low(held), self.low(held), spot.at_d(to))
        for i in range(geo.b_size):
            held = spot.rank(ring_prev(spot.b, i, geo.b_size), spot.a, spot.c)
            for j in range(1, geo.a_size):
                to = spot.rank(spot.b, ring_next(spot.a, j, geo.a_size), spot.c)
                self.twos_b[i, j] = wire.plan(self.two_b + (j - 1) * geo.b_size + i, self.high(held), self.high(held), spot.at_d(to))

    def first(self):
        for planned in self.ones:
            self.wire.go(planned)
        self.share(0, 0, 0)
        self.share(1, 0, 0)

    def second(self):
        spot, geo = self.spot, self.spot.geo
        for i in range(geo.a_size):
            held = spot.rank(spot.b, ring_prev(spot.a, i, geo.a_size), spot.c)
            if i:
                self.wire.landed(self.one_a + i - 1, self.low(held), spot.at_d(held))
                self.share(0, 0, i)
            for j in range(1, geo.b_size):
                self.wire.go(self.twos_a[i, j])
        for i in range(geo.b_size):
            held = spot.rank(ring_prev(spot.b, i, geo.b_size), spot.a, spot.c)
            if i:
                self.wire.landed(self.one_b + i - 1, self.high(held), spot.at_d(held))
                self.share(1, i, 0)
            for j in range(1, geo.a_size):
                self.wire.go(self.twos_b[i, j])

    def third(self):
        spot, geo = self.spot, self.spot.geo
        for j in range(1, geo.b_size):
            for i in range(geo.a_size):
                held = spot.rank(ring_prev(spot.b, j, geo.b_size), ring_prev(spot.a, i, geo.a_size), spot.c)
                source = spot.rank(ring_prev(spot.b, j, geo.b_size), spot.a, spot.c)
                self.wire.landed(self.two_a + (j - 1) * geo.a_size + i, self.low(held), spot.at_d(source))
                self.share(0, j, i)
        for j in range(1, geo.a_size):
            for i in range(geo.b_size):
                held = spot.rank(ring_prev(spot.b, i, geo.b_size), ring_prev(spot.a, j, geo.a_size), spot.c)
                source = spot.rank(spot.b, ring_prev(spot.a, j, geo.a_size), spot.c)
                self.wire.landed(self.two_b + (j - 1) * geo.b_size + i, self.high(held), spot.at_d(source))
                self.share(1, i, j)

    def fourth(self):
        spot, geo = self.spot, self.spot.geo
        sibling = spot.rank(spot.b, spot.a, 1 - spot.c)
        for j in range(geo.b_size):
            for i in range(geo.a_size):
                held = spot.rank(ring_prev(spot.b, j, geo.b_size), ring_prev(spot.a, i, geo.a_size), 1 - spot.c)
                for part in range(2):
                    half = (self.low, self.high)[part](held)
                    self.wire.landed(self.last + 2 * (j * geo.a_size + i) + part, half, spot.at_d(sibling))


def gather_sems(geo):
    return geo.a_size + geo.b_size - 2 + (geo.b_size - 1) * geo.a_size + (geo.a_size - 1) * geo.b_size + 2 * geo.a_size * geo.b_size


class WeightScatter:
    def __init__(self, spot, wire, held, one_a, one_b, two_a, two_b):
        geo = spot.geo
        self.spot, self.wire, self.held = spot, wire, held
        self.one_a_buf, self.one_b_buf, self.two_a_buf, self.two_b_buf = one_a, one_b, two_a, two_b
        self.slots, self.rows = held.shape[2], held.shape[3]
        self.half = self.slots // 2
        self.one_a = wire.take(geo.a_size - 1)
        self.one_b = wire.take(geo.b_size - 1)
        self.two_a = wire.take(geo.b_size - 1)
        self.two_b = wire.take(geo.a_size - 1)
        low, high = pl.ds(0, self.half), pl.ds(self.half, self.half)
        self.sends = []
        for j in range(1, geo.a_size):
            a = ring_next(spot.a, j, geo.a_size)
            self.sends.append(wire.plan(self.one_a + j - 1, held.at[:, a, low], one_a.at[j - 1], spot.at_d(spot.rank(spot.b, a, spot.c))))
        for j in range(1, geo.b_size):
            b = ring_next(spot.b, j, geo.b_size)
            self.sends.append(wire.plan(self.one_b + j - 1, held.at[b, :, high], one_b.at[j - 1], spot.at_d(spot.rank(b, spot.a, spot.c))))
        self.later = []
        for j in range(1, geo.b_size):
            b = ring_next(spot.b, j, geo.b_size)
            self.later.append(wire.plan(self.two_a + j - 1, held.at[b, spot.a, low], two_a.at[j - 1], spot.at_d(spot.rank(b, spot.a, spot.c))))
        for j in range(1, geo.a_size):
            a = ring_next(spot.a, j, geo.a_size)
            self.later.append(wire.plan(self.two_b + j - 1, held.at[spot.b, a, high], two_b.at[j - 1], spot.at_d(spot.rank(spot.b, a, spot.c))))

    def add(self, dst, src):
        tile = min(64, self.rows)
        per = self.rows // tile

        def step(i, carry):
            rows = pl.ds(pl.multiple_of(lax.rem(i, per) * tile, tile), tile)
            j = lax.div(i, per)
            dst[j, rows] = (dst[j, rows].astype(F32) + src[j, rows].astype(F32)).astype(dst.dtype)
            return carry

        lax.fori_loop(0, dst.shape[0] * per, step, 0)

    def first(self):
        for planned in self.sends:
            self.wire.go(planned)

    def second(self):
        spot, geo = self.spot, self.spot.geo
        low, high = pl.ds(0, self.half), pl.ds(self.half, self.half)
        for j in range(1, geo.a_size):
            self.wire.landed(self.one_a + j - 1, self.one_a_buf.at[j - 1], spot.at_d(spot.rank(spot.b, ring_prev(spot.a, j, geo.a_size), spot.c)))
            for b in range(geo.b_size):
                self.add(self.held.at[b, spot.a, low], self.one_a_buf.at[j - 1, b])
        for j in range(1, geo.b_size):
            self.wire.landed(self.one_b + j - 1, self.one_b_buf.at[j - 1], spot.at_d(spot.rank(ring_prev(spot.b, j, geo.b_size), spot.a, spot.c)))
            for a in range(geo.a_size):
                self.add(self.held.at[spot.b, a, high], self.one_b_buf.at[j - 1, a])
        for planned in self.later:
            self.wire.go(planned)

    def third(self):
        spot, geo = self.spot, self.spot.geo
        low, high = pl.ds(0, self.half), pl.ds(self.half, self.half)
        for j in range(1, geo.b_size):
            self.wire.landed(self.two_a + j - 1, self.two_a_buf.at[j - 1], spot.at_d(spot.rank(ring_prev(spot.b, j, geo.b_size), spot.a, spot.c)))
            self.add(self.held.at[spot.b, spot.a, low], self.two_a_buf.at[j - 1])
        for j in range(1, geo.a_size):
            self.wire.landed(self.two_b + j - 1, self.two_b_buf.at[j - 1], spot.at_d(spot.rank(spot.b, ring_prev(spot.a, j, geo.a_size), spot.c)))
            self.add(self.held.at[spot.b, spot.a, high], self.two_b_buf.at[j - 1])


def scatter_sems(geo):
    return 2 * (geo.a_size + geo.b_size - 2)


def scatter_bufs(geo, n, sets, slots, rows, width):
    a, b, half = geo.a_size, geo.b_size, slots // 2
    return [
        pltpu.VMEM((n, b, a, slots, rows, width), BF),
        pltpu.VMEM((sets, a - 1, b, half, rows, width), BF),
        pltpu.VMEM((sets, b - 1, a, half, rows, width), BF),
        pltpu.VMEM((sets, b - 1, half, rows, width), BF),
        pltpu.VMEM((sets, a - 1, half, rows, width), BF),
    ]


def loop_rows(count, tile, body, start=0):
    def step(i, carry):
        body(pl.ds(pl.multiple_of(start + i * tile, tile), tile))
        return carry

    lax.fori_loop(0, count // tile, step, 0)


def fetch(copies):
    for copy in copies:
        copy.start()
    return copies


def settle(copies):
    for copy in copies:
        copy.wait()


PAIR = 2 * HD


def nt(x, w):
    return lax.dot_general(x, w, (((1,), (1,)), ((), ())), preferred_element_type=F32)


def nn(x, w):
    return lax.dot_general(x, w, (((1,), (0,)), ((), ())), preferred_element_type=F32)


def tn(x, w):
    return lax.dot_general(x, w, (((0,), (0,)), ((), ())), preferred_element_type=F32)


def block_bias(seg_col, seg_row, bias, start, rows, keys):
    query = seg_col[start:start + rows, 0:1]
    for first in range(0, keys, rows):
        key = seg_row[:, first:first + rows]
        seen = query == key
        if first + rows > start:
            q_pos = start + lax.broadcasted_iota(jnp.int32, (rows, rows), 0)
            k_pos = first + lax.broadcasted_iota(jnp.int32, (rows, rows), 1)
            seen = seen & (k_pos <= q_pos)
        bias[:, first:first + rows] = jnp.where(seen, 0.0, MASKED).astype(F32)


def one_head(pair, head):
    lane = lax.broadcasted_iota(jnp.int32, pair.shape, 1)
    return jnp.where((lane < HD) if head == 0 else (lane >= HD), pair, jnp.zeros_like(pair))


def attend_block(qkv, bias, att, lse, start, rows):
    keys = start + rows
    width = qkv.shape[2]
    stat_lane = lax.broadcasted_iota(jnp.int32, (rows, 128), 1)
    stats = jnp.zeros((rows, 128), F32)
    for p in range(width // PAIR):
        lanes = slice(p * PAIR, (p + 1) * PAIR)
        query = qkv[0, start:keys, lanes]
        outs = []
        for head in range(2):
            s = nt(one_head(query, head), qkv[1, 0:keys, lanes]) + bias[:, 0:keys]
            top = jnp.max(s, axis=1, keepdims=True)
            e = jnp.exp(s - top)
            total = jnp.sum(e, axis=1, keepdims=True)
            prob = (e * (1.0 / total)).astype(BF)
            outs.append(nn(prob, qkv[2, 0:keys, lanes]))
            stats = jnp.where(stat_lane == 2 * p + head, top + jnp.log(total), stats)
        lane = lax.broadcasted_iota(jnp.int32, outs[0].shape, 1)
        att[start:keys, lanes] = jnp.where(lane < HD, outs[0], outs[1]).astype(BF)
    lse[start:keys, :] = stats


def attend_block_back(qkv, bias, lse, do, dq, dk, dv, start, rows):
    keys = start + rows
    width = qkv.shape[2]
    stat_lane = lax.broadcasted_iota(jnp.int32, (rows, 128), 1)
    stats = lse[start:keys, :]
    for p in range(width // PAIR):
        lanes = slice(p * PAIR, (p + 1) * PAIR)
        query = qkv[0, start:keys, lanes]
        grad = do[start:keys, lanes]
        dqs, dks, dvs = [], [], []
        for head in range(2):
            level = jnp.sum(jnp.where(stat_lane == 2 * p + head, stats, 0.0), axis=1, keepdims=True)
            s = nt(one_head(query, head), qkv[1, 0:keys, lanes]) + bias[:, 0:keys]
            prob = jnp.exp(s - level)
            d_prob = nt(one_head(grad, head), qkv[2, 0:keys, lanes])
            mixed = prob * d_prob
            ds = (mixed - prob * jnp.sum(mixed, axis=1, keepdims=True)).astype(BF)
            dqs.append(nn(ds, qkv[1, 0:keys, lanes]))
            dks.append(tn(ds, query))
            dvs.append(tn(prob.astype(BF), grad))
        lane = lax.broadcasted_iota(jnp.int32, dqs[0].shape, 1)
        dq[start:keys, lanes] = (jnp.where(lane < HD, dqs[0], dqs[1]) * (HD ** -0.5)).astype(dq.dtype)
        lane = lax.broadcasted_iota(jnp.int32, dks[0].shape, 1)
        dk[0:keys, lanes] += jnp.where(lane < HD, dks[0], dks[1])
        dv[0:keys, lanes] += jnp.where(lane < HD, dvs[0], dvs[1])


GELU_C = 0.7978845608028654


def gelu_parts(a):
    square = a * a
    tanh = jnp.tanh(GELU_C * a * (1.0 + 0.044715 * square))
    half = 0.5 * (1.0 + tanh)
    slope = half + 0.5 * a * (1.0 - tanh * tanh) * (GELU_C * (1.0 + 3 * 0.044715 * square))
    return a * half, slope


def column_sum(values):
    return jnp.sum(values, axis=0, keepdims=True)


def block_body(geo, x_ref, aw_ref, ow_ref, up_ref, down_ref, gain_ref, bias_ref, seg_ref, cot_ref,
               full, out_ref, igrad_ref, awg_ref, owg_ref, upg_ref, downg_ref, gaing_ref, biasg_ref,
               xf, n1, n1t, qkv, att, lse, wf, part, land, bias, mid, cot, gaf, rows12, seg_col, seg_row,
               sf, wsend, ow_in, down_in, msend, gain_in, bias_in, ssend,
               sums, spart, sland, stot, tland,
               held, one_a, one_b, two_a, two_b, wheld, wone_a, wone_b, wtwo_a, wtwo_b, mland,
               gtot, downg, awg, owg, gaing, biasg,
               send, recv, local, msem, osem):
    spot = geo.bind()
    groups = 2 * (up_ref.shape[1] // min(512, up_ref.shape[1])) + 1
    wire = Wire(send, recv, send.shape[0] - groups)
    size = geo.tensor
    rows, width = x_ref.shape
    seq = size * rows
    wrows, heads = aw_ref.shape[1:]
    mrows, unit = up_ref.shape
    a_size, b_size = geo.a_size, geo.b_size
    ab = a_size * b_size
    chunk = min(512, unit)
    per = unit // chunk
    pieces = msem.shape[1]
    count = size * per
    tail = min(64, rows)
    tile = min(64, mrows)
    end = size - 1
    sibling = spot.at_d(spot.rank(spot.b, spot.a, 1 - spot.c))
    wspan = pl.ds(pl.multiple_of(spot.d * wrows, wrows), wrows)
    mspan = pl.ds(pl.multiple_of(spot.d * mrows, mrows), mrows)
    column = pl.ds(pl.multiple_of(spot.t * heads, 128), heads)

    def block_of(ref, t):
        return ref.at[pl.ds(pl.multiple_of(t * rows, rows), rows)]

    def own_rows(r, n):
        return pl.ds(pl.multiple_of(spot.t * rows + r.start, n), n)

    weights = WeightGather(spot, wire, wrows, wf)
    halved = [(k, p) for k in range(2) for p in range(per)]
    wlines, gathers = {}, {}
    for k, p in halved:
        wlines[k, p] = LineGather(spot, wire, msend.at[k, p], lambda t, k=k, p=p: full.at[k, p, t, mspan], parts=1)
        gathers[k, p] = WeightGather(spot, wire, mrows, full.at[k, p])
    xs = LineGather(spot, wire, x_ref, lambda t: block_of(xf, t))
    gas = LineGather(spot, wire, block_of(gaf, spot.t), lambda t: block_of(gaf, t))
    blocks = [
        LineScatter(spot, wire, lambda t: block_of(part, t), lambda side, j: land.at[side, j - 1 + side],
                    lambda dst, src: add_tiled(dst, src, tail), rising=(0, None)[k]) for k in range(2)]
    scatters, lines = {}, {}

    def line_of(k, p):
        here = held.at[k * per + p, spot.b, spot.a]
        return LineScatter(spot, wire, lambda t: here.at[t], lambda side, j: mland.at[k * per + p, side, j - 1 + side],
                           lambda dst, src: add_tiled(dst, src, tile), parts=1)

    for k, p in halved:
        scatters[k, p] = WeightScatter(spot, wire, held.at[k * per + p], *(buf.at[k * per + p] for buf in (one_a, one_b, two_a, two_b)))
        lines[k, p] = line_of(k, p)
    wscatter = WeightScatter(spot, wire, wheld.at[0], wone_a.at[0], wone_b.at[0], wtwo_a.at[0], wtwo_b.at[0])
    zero = [wire.take(count) for _ in range(2)]
    wzero = wire.take(ab)
    gains_in = wire.take(geo.dp - 1)
    small = wire.take(geo.dp - 1)
    last = wire.take(size - 1)
    assert wire.count == wire.base and recv.shape[0] == wire.base + wire.grouped

    pairs = [
        (gain_ref, gain_in), (bias_ref, bias_in), (aw_ref, wsend.at[pl.ds(0, 3)]), (ow_ref, ow_in),
        (x_ref, block_of(xf, spot.t)), (down_ref, down_in), (seg_ref, seg_row), (cot_ref, cot)]
    pairs += [(up_ref.at[:, pl.ds(i * chunk, chunk)], msend.at[0, i]) for i in range(per)]
    loads = fetch([pltpu.make_async_copy(src, dst, local.at[i]) for i, (src, dst) in enumerate(pairs)])
    met = greet(spot)
    sums[...] = jnp.zeros_like(sums)
    settle(loads[0:4])
    ssend[0:2, :] = gain_in[...].astype(F32)
    ssend[2:12, :] = bias_in[...].astype(F32)
    sf[spot.d] = ssend[...]
    wsend[3] = ow_in[...].T
    wf[:, wspan] = wsend[...]
    settle(loads[8:])

    def store(k):
        return pltpu.make_async_copy(msend.at[k], full.at[k, :, spot.t, mspan], osem.at[k])

    store(0).start()
    met()
    for p in range(per):
        wlines[0, p].start()
    for step in range(1, geo.dp):
        wire.start(gains_in + step - 1, ssend, sf.at[spot.d], spot.at_d(ring_next(spot.d, step, geo.dp)))
    weights.first()
    loads[5].wait()
    for i in range(per):
        msend[1, i] = down_in[i * chunk:(i + 1) * chunk, :].T
    store(1).start()
    for k in range(1, end):
        for p in range(per):
            wlines[0, p].step(k)
        if k == 1:
            weights.second()
    xs.start()
    weights.third()
    store(0).wait()
    for p in range(per):
        wlines[0, p].step(end)
        gathers[0, p].first()
    for step in range(1, geo.dp):
        source = ring_prev(spot.d, step, geo.dp)
        wire.landed(gains_in + step - 1, sf.at[source], spot.at_d(source))
    piece = ssend.shape[1]
    for d in range(geo.dp):
        rows12[:, d * piece:(d + 1) * piece] = sf[d]
    loads[6].wait()
    seg_col[...] = jnp.broadcast_to(seg_row[...], (128, seq)).T
    weights.fourth()
    loads[4].wait()

    def project(t):
        def norm(r):
            source = pl.ds(pl.multiple_of(t * rows + r.start, tail), tail)
            n1[r] = layer_norm(xf[source].astype(F32), rows12[0:1, :], rows12[2:3, :]).astype(BF)

        loop_rows(rows, tail, norm)
        r = pl.ds(pl.multiple_of(t * rows, rows), rows)
        normed = n1[...]
        n1t[:, r] = normed.T
        qkv[0, r] = ((nn(normed, wf[0]) + rows12[3:4, column]).astype(BF).astype(F32) * HD ** -0.5).astype(BF)
        qkv[1, r] = nn(normed, wf[1]).astype(BF)
        qkv[2, r] = (nn(normed, wf[2]) + rows12[4:5, column]).astype(BF)

    def arrive(k, carry):
        @pl.when(k >= 1)
        def _():
            xs.step(k)

        @pl.when(k == end - 1)
        def _():
            wlines[1, 0].start()
            for p in range(1, per):
                wlines[1, p].start(False)

        def side(i, inner):
            t = spot.t + (2 * i - 1) * k

            @pl.when((t >= 0) & (t < size) & ((i == 0) | (k >= 1)))
            def _():
                project(t)

            return inner

        lax.fori_loop(0, 2, side, 0)

        @pl.when(k == 1)
        def _():
            for p in range(per):
                gathers[0, p].second()

        for i in range(size):
            start = i * rows

            @pl.when(jnp.maximum(spot.t, i - spot.t) == k)
            def _():
                block_bias(seg_col, seg_row, bias, start, rows, start + rows)
                attend_block(qkv, bias, att, lse, start, rows)
                part[start:start + rows, :] = nt(att[start:start + rows, :], wf[3]).astype(BF)
                blocks[0].start_block(i)

        return carry

    lax.fori_loop(0, size, arrive, 0)
    xs.owe()
    for k in range(1, end):
        wlines[1, 0].step(k)
        if k == max(1, end - 1):
            for p in range(1, per):
                wlines[1, p].start(True)
        if k == 1:
            for p in range(per):
                gathers[0, p].third()
    store(1).wait()
    wlines[1, 0].step(end)
    gathers[1, 0].first()
    for p in range(1, per):
        for k in range(1, size):
            wlines[1, p].step(k)
        gathers[1, p].first()

    def set_total(r):
        mid[r] = part[own_rows(r, tail)].astype(F32)

    loop_rows(rows, tail, set_total)

    def mid_total(ref, h):
        n = ref.shape[0]
        add_tiled(mid.at[pl.ds(h * n, n)], ref, tail)

    events = blocks[0].count()
    blocks[0].step(0, 3 * events // 8, mid_total)
    gathers[1, 0].second()
    blocks[0].step(3 * events // 8, 5 * events // 8, mid_total)
    for p in range(per):
        gathers[0, p].fourth()
    for p in range(1, per):
        gathers[1, p].second()
    blocks[0].step(5 * events // 8, events, mid_total)

    def mlp(mbuf, hmid, da, n2, gm, turned, left, snd, dn2):
        def cols_of(j):
            return pl.ds(pl.multiple_of(unit_of(j) * chunk, chunk), chunk)

        def unit_of(j):
            return lax.rem(j, size) * per + lax.div(j, size)

        def mload(k, j, s):
            n = width // pieces
            return [
                pltpu.make_async_copy(
                    full.at[k, lax.div(j, size), lax.rem(j, size), pl.ds(i * n, n)], mbuf.at[s, pl.ds(i * n, n)], msem.at[s, i])
                for i in range(pieces)]

        def depth(which):
            return mbuf.shape[0] // len(which)

        def ahead(which):
            for j in range(min(depth(which) - 1, count)):
                for n, k in enumerate(which):
                    fetch(mload(k, j, j * len(which) + n))

        def streamed(which, body, first=0, stop=count):
            deep = depth(which)

            def one(j, carry):
                slots = [lax.rem(j, deep) * len(which) + n for n in range(len(which))]
                for n, k in enumerate(which):
                    settle(mload(k, j, slots[n]))

                @pl.when(j + deep - 1 < count)
                def _():
                    for n, k in enumerate(which):
                        fetch(mload(k, j + deep - 1, lax.rem(j + deep - 1, deep) * len(which) + n))

                body(j, *slots)
                return carry

            lax.fori_loop(first, stop, one, 0)

        ahead((0,))
        loads[7].wait()

        def norm(r):
            value = xf[own_rows(r, tail)].astype(F32) + (mid[r] + rows12[5:6, :])
            mid[r] = value
            n2[r] = layer_norm(value, rows12[1:2, :], rows12[6:7, :]).astype(BF)
            branch = cot[r].astype(BF)
            gm[r] = branch
            sums[7:8, :] += column_sum(branch.astype(F32))

        loop_rows(rows, tail, norm)

        def turn(value):
            turned[...] = value[...].T
            for i in range(ab):
                for other in range(2):
                    core = lax.rem(spot.c + other, 2)
                    left[other, i * mrows:(i + 1) * mrows, :] = turned[pl.ds(pl.multiple_of((i * 2 + core) * mrows, mrows), mrows), :]

        turn(gm)

        def sending(k, j):
            p, t = lax.div(j, size), lax.rem(j, size)
            return wire.copy(zero[k] + j, snd.at[p, :, :, t], held.at[k * per + p, :, :, t], sibling)

        def give(k, j, right):
            product = nn(left[1], right).astype(BF)
            p, t = lax.div(j, size), lax.rem(j, size)
            for i in range(ab):
                snd[p, i // a_size, i % a_size, t] = product[i * mrows:(i + 1) * mrows, :]
            sending(k, j).start()

        def keep(k, j, right):
            p, t = lax.div(j, size), lax.rem(j, size)
            product = nn(left[0], right)
            sending(k, j).wait_recv()
            for i in range(ab):
                b, a = i // a_size, i % a_size
                held[k * per + p, b, a, t] = (
                    held[k * per + p, b, a, t].astype(F32) + product[i * mrows:(i + 1) * mrows, :]).astype(BF)

        def hidden(j, s):
            cols = cols_of(j)
            row = pl.ds(8 + lax.div(unit_of(j) * chunk, width), 1)
            bcols = pl.ds(pl.multiple_of(lax.rem(unit_of(j) * chunk, width), chunk), chunk)
            value, slope = gelu_parts(nn(n2[...], mbuf[s]) + rows12[row, bcols])
            active = value.astype(BF)
            hmid[:, cols] = active
            da[:, cols] = slope.astype(BF)
            give(1, j, active)

        def keep_down(j, carry):
            keep(1, j, hmid[:, cols_of(j)])
            return carry

        for p in range(per):
            streamed((0,), hidden, p * size, (p + 1) * size)
            gathers[1, p].third()
            lax.fori_loop(p * size, (p + 1) * size, keep_down, 0)
            scatters[1, p].first()
        for p in range(per):
            gathers[1, p].fourth()
        ahead((0, 1))
        dn2[...] = jnp.zeros_like(dn2)

        def hidden_back(j, s, s_down):
            cols = cols_of(j)
            row = pl.ds(8 + lax.div(unit_of(j) * chunk, width), 1)
            bcols = pl.ds(pl.multiple_of(lax.rem(unit_of(j) * chunk, width), chunk), chunk)
            grad = (nn(gm[...], mbuf[s_down]) * da[:, cols].astype(F32)).astype(BF)
            da[:, cols] = grad
            sums[row, bcols] = column_sum(grad.astype(F32))
            dn2[...] += nt(grad, mbuf[s])

        streamed((0, 1), hidden_back)

        def back(r):
            value = mid[r]
            unit_two, scale_two = norm_stats(value)
            grad = dn2[r]
            total = cot[r] + norm_back(grad, unit_two, scale_two, rows12[1:2, :])
            cot[r] = total
            branch = total.astype(BF)
            gaf[own_rows(r, tail)] = branch
            sums[1:2, :] += column_sum(grad * unit_two)
            sums[6:7, :] += column_sum(grad)
            sums[5:6, :] += column_sum(branch.astype(F32))

        loop_rows(rows, tail, back)
        wire.sent(blocks[0].plans())
        gas.start()
        turn(n2)
        def give_up(j, carry):
            sending(1, j).wait_send()
            give(0, j, da[:, cols_of(j)])
            return carry

        lax.fori_loop(0, count, give_up, 0)
        scatters[1, 0].second()

        def keep_up(j, carry):
            keep(0, j, da[:, cols_of(j)])
            return carry

        for p in range(per):
            lax.fori_loop(p * size, (p + 1) * size, keep_up, 0)
            if p:
                scatters[1, p].second()
        scatters[0, 0].first()
        ahead((1,))
        gas.step(1)
        scatters[1, 0].third()
        lines[1, 0].start()
        dn2[...] = jnp.zeros_like(dn2)

        def output(j, s):
            dn2[...] += nt(hmid[:, cols_of(j)], mbuf[s])

        streamed((1,), output)

        def set_out(r):
            dn2[r] = mid[r] + (dn2[r] + rows12[7:8, :])

        loop_rows(rows, tail, set_out)
        out_copy = pltpu.make_async_copy(dn2, out_ref, osem.at[0])
        out_copy.start()
        for p in range(1, per):
            scatters[1, p].third()
            lines[1, p].start()
        for j in range(count):
            sending(0, j).wait_send()
        out_copy.wait()

    ff = size * unit
    pl.run_scoped(
        mlp,
        pltpu.VMEM((6, width, chunk), BF),
        pltpu.VMEM((rows, ff), BF),
        pltpu.VMEM((rows, ff), BF),
        pltpu.VMEM((rows, width), BF),
        pltpu.VMEM((rows, width), BF),
        pltpu.VMEM((width, rows), BF),
        pltpu.VMEM((2, ab * mrows, rows), BF),
        pltpu.VMEM((per, b_size, a_size, size, mrows, chunk), BF),
        pltpu.VMEM((rows, width), F32),
    )

    def attention(gat, do, dqkv, dk, dv, wg):
        def own_line(k):
            for p in range(per):
                here = held.at[k * per + p, spot.b, spot.a, spot.t]

                def set_row(r):
                    gtot[r, p * chunk:(p + 1) * chunk] = here[r].astype(F32)

                loop_rows(mrows, tile, set_row)

        def line_total(p):
            return lambda ref, h: add_tiled(gtot.at[:, pl.ds(p * chunk, chunk)], ref, tile)

        def line_step(k, p, s):
            third = lines[k, p].count() // 3
            lines[k, p].step(s * third, (s + 1) * third, line_total(p))

        def arrived(t):
            r = pl.ds(pl.multiple_of(t * rows, rows), rows)
            value = gaf[r]
            do[r] = nn(value, wf[3]).astype(BF)
            gat[:, r] = value.T

        dk[...] = jnp.zeros_like(dk)
        dv[...] = jnp.zeros_like(dv)

        half = width // 2

        def norm_grad(i):
            r = pl.ds(pl.multiple_of(i * rows, rows), rows)
            dqkv[1, r] = dk[r].astype(BF)
            dqkv[2, r] = dv[r].astype(BF)
            for first in range(0, width, half):
                cols = slice(first, first + half)
                part[r, cols] = sum(nt(dqkv[j, r], wf[j, cols, :]) for j in range(3)).astype(BF)
            blocks[1].start_traced(i)

        plan = {(1, p, n): n + 1 + p for p in range(per) for n in range(end - 1)}
        plan = {key: at for key, at in plan.items() if at < size}

        def arrive_back(k, carry):
            if size > 2:
                @pl.when(k == 0)
                def _():
                    gas.step(2, True)

            for n in range(1, size):
                @pl.when(k == n)
                def _():
                    if n == 1 and size > 2:
                        gas.step(2, False)
                    for key, at in plan.items():
                        if at == n:
                            line_step(*key)
                    if n == max(1, end - 1):
                        scatters[0, 0].second()
                        for p in range(1, per):
                            scatters[0, p].first()

            @pl.when((k == end) & (spot.t == 0))
            def _():
                scatters[0, 0].third()
                lines[0, 0].start()

            @pl.when(k >= 3)
            def _():
                gas.step(k)

            def side(i, inner):
                t = spot.t + (2 * i - 1) * k

                @pl.when((t >= 0) & (t < size) & ((i == 0) | (k >= 1)))
                def _():
                    arrived(t)

                return inner

            lax.fori_loop(0, 2, side, 0)
            for i in range(size):
                @pl.when((i == spot.t - k) | (i == spot.t + k))
                def _():
                    start, stop = i * rows, (i + 1) * rows
                    block_bias(seg_col, seg_row, bias, start, rows, stop)
                    attend_block_back(qkv, bias, lse, do, dqkv.at[0], dk, dv, start, rows)

            def ready(n, inner):
                i = jnp.where(lax.rem(n, 2) == 0, end - lax.div(n, 2), lax.div(n, 2))

                @pl.when(jnp.maximum(end - spot.t, spot.t - i) == k)
                def _():
                    norm_grad(i)

                return inner

            lax.fori_loop(0, size, ready, 0)
            return carry

        lax.fori_loop(0, size, arrive_back, 0)
        gas.owe()
        blocks[1].owe_starts()
        blocks[1].start_middle()
        loop_rows(rows, tail, lambda r: set_total(r))
        own_line(1)
        for p in range(per):
            for n in range(end):
                if (1, p, n) not in plan:
                    line_step(1, p, n)
        downg[...] = gtot[...].T
        stores = fetch([pltpu.make_async_copy(downg, downg_ref, osem.at[1])])
        events = blocks[1].count()

        @pl.when(spot.t != 0)
        def _():
            scatters[0, 0].third()
            lines[0, 0].start()

        def first_norm(r):
            unit_one, _ = norm_stats(xf[r].astype(F32))
            term = part[r].astype(F32)
            sums[0:1, :] += column_sum(term * unit_one)
            sums[2:3, :] += column_sum(term)

        loop_rows(seq, tail, first_norm)
        sums[3:4, column] = column_sum(dqkv[0].astype(F32))
        sums[4:5, column] = column_sum(dqkv[2].astype(F32))
        for d in range(geo.dp):
            spart[d] = sums[:, d * piece:(d + 1) * piece]
        for step in range(1, geo.dp):
            to = ring_next(spot.d, step, geo.dp)
            wire.start(small + step - 1, spart.at[to], sland.at[step - 1], spot.at_d(to))
        stot[...] = spart[spot.d]
        blocks[1].step(0, events // 3, mid_total)
        for p in range(1, per):
            scatters[0, p].second()
        def wgrad(r):
            for j in range(3):
                wg[j, r] = nn(n1t[r], dqkv[j]).astype(BF)
            wg[3, r] = nn(gat[r], att[...]).astype(BF)

        loop_rows(width, min(256, width), wgrad)

        def wrows_of(i, core):
            return pl.ds(pl.multiple_of((i * 2 + core) * wrows, wrows), wrows)

        for i in range(ab):
            wire.start(wzero + i, wg.at[:, wrows_of(i, 1 - spot.c)], wheld.at[0, i // a_size, i % a_size], sibling)
        for p in range(1, per):
            scatters[0, p].third()
            lines[0, p].start()
        blocks[1].start_near()
        own_line(0)
        blocks[1].step(events // 3, 2 * events // 3, mid_total)
        for i in range(ab):
            here = wheld.at[0, i // a_size, i % a_size]
            wire.landed(wzero + i, here, sibling)
            wscatter.add(here, wg.at[:, wrows_of(i, spot.c)])
        wscatter.first()
        for step in range(1, geo.dp):
            wire.landed(small + step - 1, sland.at[step - 1], spot.at_d(ring_prev(spot.d, step, geo.dp)))
            stot[...] += sland[step - 1]
        for step in range(1, size):
            wire.start(last + step - 1, stot, tland.at[step - 1], spot.at_t(ring_next(spot.t, step, size)))
        if end > 1:
            line_step(0, 0, 0)
        wscatter.second()
        for n in range(1, end - 1):
            line_step(0, 0, n)
        for p in range(1, per):
            for n in range(end - 1):
                line_step(0, p, n)
        blocks[1].step(2 * events // 3, events, mid_total)

        def back(r):
            unit_one, scale_one = norm_stats(xf[own_rows(r, tail)].astype(F32))
            cot[r] = cot[r] + norm_back(mid[r], unit_one, scale_one, rows12[0:1, :])

        loop_rows(rows, tail, back)
        stores += fetch([pltpu.make_async_copy(cot, igrad_ref, osem.at[0])])
        wscatter.third()
        sums_w = wheld.at[0, spot.b, spot.a]
        for j in range(3):
            awg[j] = sums_w[j].astype(F32)
        owg[...] = sums_w[3].astype(F32).T
        stores += fetch([
            pltpu.make_async_copy(awg, awg_ref, osem.at[2]),
            pltpu.make_async_copy(owg, owg_ref, osem.at[3])])
        for p in range(per):
            line_step(0, p, end - 1)
        stores += fetch([pltpu.make_async_copy(gtot, upg_ref, osem.at[6])])
        for step in range(1, size):
            wire.landed(last + step - 1, tland.at[step - 1], spot.at_t(ring_prev(spot.t, step, size)))
        total = stot[...]
        for step in range(1, size):
            total = total + tland[step - 1]
        gaing[...] = total[0:2, :]
        for i in range(biasg.shape[0]):
            biasg[i] = total[2 + i:3 + i, :]
        stores += fetch([
            pltpu.make_async_copy(gaing, gaing_ref, osem.at[4]),
            pltpu.make_async_copy(biasg, biasg_ref, osem.at[5])])
        wire.drain()
        settle(stores)

    pl.run_scoped(
        attention,
        pltpu.VMEM((width, seq), BF),
        pltpu.VMEM((seq, heads), BF),
        pltpu.VMEM((3, seq, heads), BF),
        pltpu.VMEM((seq, heads), F32),
        pltpu.VMEM((seq, heads), F32),
        pltpu.VMEM((4, width, heads), BF),
    )


def block_kernel(geo, x, aw, ow, up, down, gains, biases, seg_row, cot):
    rows, width = x.shape
    wrows, heads = aw.shape[1:]
    mrows, unit = up.shape
    size = geo.tensor
    seq = size * rows
    chunk = min(512, unit)
    per = unit // chunk
    sems = ((2 * per + 1) * (gather_sems(geo) + scatter_sems(geo)) + (size - 1) * (2 * 4 + 2 * 4 + 4 * per * 2 + 1) + 2 * per * size
            + geo.a_size * geo.b_size + 2 * (geo.dp - 1))
    shared = (2 * per + 1) * gather_sems(geo)
    like = lambda x: pltpu.VMEM(x.shape, x.dtype)
    return pl.pallas_call(
        functools.partial(block_body, geo),
        out_shape=(
            jax.ShapeDtypeStruct((2, unit // chunk, size, width, chunk), BF),
            jax.ShapeDtypeStruct((rows, width), F32),
            jax.ShapeDtypeStruct((rows, width), F32),
            jax.ShapeDtypeStruct((3, wrows, heads), F32),
            jax.ShapeDtypeStruct((heads, wrows), F32),
            jax.ShapeDtypeStruct((mrows, unit), F32),
            jax.ShapeDtypeStruct((unit, mrows), F32),
            jax.ShapeDtypeStruct((2, wrows), F32),
            jax.ShapeDtypeStruct((10, 1, wrows), F32),
        ),
        in_specs=[ANY] * 9,
        out_specs=(ANY,) * 9,
        scratch_shapes=[
            pltpu.VMEM((seq, width), BF),
            pltpu.VMEM((rows, width), BF),
            pltpu.VMEM((width, seq), BF),
            pltpu.VMEM((3, seq, heads), BF),
            pltpu.VMEM((seq, heads), BF),
            pltpu.VMEM((seq, 128), F32),
            pltpu.VMEM((4, width, heads), BF),
            pltpu.VMEM((seq, width), BF),
            pltpu.VMEM((2, size - 1, rows, width), BF),
            pltpu.VMEM((rows, seq), F32),
            pltpu.VMEM((rows, width), F32),
            pltpu.VMEM((rows, width), F32),
            pltpu.VMEM((seq, width), BF),
            pltpu.VMEM((12, width), F32),
            pltpu.VMEM((seq, 128), jnp.int32),
            like(seg_row),
            pltpu.VMEM((geo.dp, 12, wrows), F32),
            pltpu.VMEM((4, wrows, heads), BF),
            like(ow), like(down), pltpu.VMEM((2, unit // chunk, mrows, chunk), BF), like(gains), like(biases),
            pltpu.VMEM((12, wrows), F32),
            pltpu.VMEM((12, width), F32),
            pltpu.VMEM((geo.dp, 12, wrows), F32),
            pltpu.VMEM((geo.dp - 1, 12, wrows), F32),
            pltpu.VMEM((12, wrows), F32),
            pltpu.VMEM((size - 1, 12, wrows), F32),
            *scatter_bufs(geo, 2 * (unit // chunk), 2 * (unit // chunk), size, mrows, chunk),
            *scatter_bufs(geo, 1, 1, 4, wrows, heads),
            pltpu.VMEM((2 * (unit // chunk), 2, size - 1, mrows, chunk), BF),
            pltpu.VMEM((mrows, unit), F32),
            pltpu.VMEM((unit, mrows), F32),
            pltpu.VMEM((3, wrows, heads), F32),
            pltpu.VMEM((heads, wrows), F32),
            pltpu.VMEM((2, wrows), F32),
            pltpu.VMEM((10, 1, wrows), F32),
            pltpu.SemaphoreType.DMA((sems - shared + 2 * per + 1,)), pltpu.SemaphoreType.DMA((sems,)), pltpu.SemaphoreType.DMA((8 + unit // chunk,)),
            pltpu.SemaphoreType.DMA((6, 2)), pltpu.SemaphoreType.DMA((7,))],
        compiler_params=pltpu.CompilerParams(collective_id=1, has_side_effects=True, vmem_limit_bytes=62 * 2**20),
        name="block",
    )(x, aw, ow, up, down, gains, biases, seg_row, cot)


def hand_over_body(*refs):
    *refs, loads, stores = refs
    count = len(refs) // 3
    ins, outs, bufs = refs[:count], refs[count:2 * count], refs[2 * count:]
    coming = fetch([pltpu.make_async_copy(ins[i], bufs[i], loads.at[i]) for i in range(count)])
    going = []
    for i in range(count):
        coming[i].wait()
        going += fetch([pltpu.make_async_copy(bufs[i], outs[i], stores.at[i])])
    settle(going)


def hand_over(parts):
    return pl.pallas_call(
        hand_over_body,
        out_shape=tuple(jax.ShapeDtypeStruct(part.shape, part.dtype) for part in parts),
        in_specs=[ANY] * len(parts),
        out_specs=(ANY,) * len(parts),
        scratch_shapes=[pltpu.VMEM(part.shape, part.dtype) for part in parts] + [pltpu.SemaphoreType.DMA((len(parts),))] * 2,
        name="hand_over",
    )(*parts)


def per_device(geo, activations, segments, attn_weight, out_weight, up_weight, down_weight, norm_gains, bias_rows, cotangent):
    outs = block_kernel(
        geo, activations, attn_weight[0], out_weight[0], up_weight[0], down_weight[0], norm_gains[0], bias_rows[0], segments[None, :],
        cotangent)
    outs = hand_over(outs[1:])
    return outs[:2] + tuple(part[None] for part in outs[2:7]) + (outs[7].reshape(1, 10, -1),)


def solution(mesh):
    geo = Geometry(mesh.shape["dp"], mesh.shape["tensor"])
    return jax.shard_map(
        functools.partial(per_device, geo),
        mesh=mesh,
        in_specs=(
            P(("dp", "tensor"), None),
            P("dp"),
            P(None, None, "dp", "tensor"),
            P(None, "tensor", "dp"),
            P(None, "dp", "tensor"),
            P(None, "tensor", "dp"),
            P(None, None, "dp"),
            P(None, None, "dp"),
            P(("dp", "tensor"), None),
        ),
        out_specs=(
            P(("dp", "tensor"), None),
            P(("dp", "tensor"), None),
            P(None, None, "dp", "tensor"),
            P(None, "tensor", "dp"),
            P(None, "dp", "tensor"),
            P(None, "tensor", "dp"),
            P(None, None, "dp"),
            P(None, None, "dp"),
        ),
        check_vma=False,
    )
```
